32 devices in a mesh: uly: 4 (over y, core), blk: 8 (over z, x).
Axes of the slice: x: 2, y: 2, z: 4, core: 2. Of those that a mesh axis runs over, the one named last changes fastest.
Arguments:
- hidden: bfloat16 [2, 2048, 1280], P(None, ('uly', 'blk')), may hold values from -0.15625 to 0.15625
- positions: int32 [2, 2048], P(None, ('uly', 'blk')), may hold values from 0 to 2047, as said below
- w_query: bfloat16 [1280, 1280], P(('uly', 'blk')), may hold values from -0.15625 to 0.15625
- w_key: bfloat16 [1280, 1280], P(('uly', 'blk')), may hold values from -0.15625 to 0.15625
- w_value: bfloat16 [1280, 1280], P(('uly', 'blk')), may hold values from -0.15625 to 0.15625
- w_out: bfloat16 [1280, 1280], P(('uly', 'blk')), may hold values from -0.15625 to 0.15625
- w_up: bfloat16 [5120, 1280], P(('uly', 'blk')), may hold values from -0.15625 to 0.15625
- w_gate: bfloat16 [5120, 1280], P(('uly', 'blk')), may hold values from -0.15625 to 0.15625
- w_down: bfloat16 [1280, 5120], P(('uly', 'blk')), may hold values from -0.078125 to 0.078125
- qk_scale: bfloat16 [1280], P(('uly', 'blk')), may hold values from 0.8984375 to 1.59375
- alpha_attn: bfloat16 [1280], P(('uly', 'blk')), may hold values from 0.099609375 to 0.59765625
- alpha_mlp: bfloat16 [1280], P(('uly', 'blk')), may hold values from 0.099609375 to 0.59765625
- up_scale: bfloat16 [5120], P(('uly', 'blk')), may hold values from 0.5 to 2
- gate_scale: bfloat16 [5120], P(('uly', 'blk')), may hold values from 0.5 to 2
- cotangent: bfloat16 [2, 2048, 1280], P(None, ('uly', 'blk')), may hold values from -12 to 12
Outputs:
- layer_out: bfloat16 [2, 2048, 1280], P(None, ('uly', 'blk'))
- grad_hidden: float32 [2, 2048, 1280], P(None, ('uly', 'blk'))
- grad_query: float32 [1280, 1280], P(('uly', 'blk'))
- grad_key: float32 [1280, 1280], P(('uly', 'blk'))
- grad_value: float32 [1280, 1280], P(('uly', 'blk'))
- grad_out: float32 [1280, 1280], P(('uly', 'blk'))
- grad_up: float32 [5120, 1280], P(('uly', 'blk'))
- grad_gate: float32 [5120, 1280], P(('uly', 'blk'))
- down_weight_gradient: float32 [1280, 5120], P(('uly', 'blk'))
- grad_qk_scale: float32 [1280], P(('uly', 'blk'))
- grad_alpha_attn: float32 [1280], P(('uly', 'blk'))
- grad_alpha_mlp: float32 [1280], P(('uly', 'blk'))
- grad_up_scale: float32 [5120], P(('uly', 'blk'))
- grad_gate_scale: float32 [5120], P(('uly', 'blk'))
The draws below stay inside these ranges and needn't reach their ends.
Inputs may be any that keep to these rules, and one draw needn't show every extreme that they name: In each sequence every position occurs once. With spans of 128 consecutive positions, the rows of one index b of blk (over all indices of uly, in order of uly) hold two whole spans, c and 15 - c, each in increasing order, the two spans in either order; every c occurs on one index of blk.
All inputs are finite; a program needn't handle non-finite values.
Results may differ from the reference program's by a relative error of at most 0.029.
Values may be sent and summed in bfloat16 or wider, within the bound.
A program may use at most 320 MiB of HBM per device.

```python
import math
import jax
import jax.numpy as jnp
from jax import lax

D = 1280
HEADS = 20
HEAD_DIM = 64
FF = 5120
SEQS = 2
SEQ_DEV = 64
LENGTH = 2048
GROUP_ROWS = 256


def draw_positions(key, part):
    span_rows = GROUP_ROWS // 2
    blk_groups = LENGTH // GROUP_ROWS
    uly_groups = GROUP_ROWS // SEQ_DEV

    def one_sequence(number):
        sequence_rng_key = jax.random.fold_in(key, number)
        order = jax.random.permutation(jax.random.fold_in(sequence_rng_key, 1), blk_groups).astype(jnp.int32)
        swapped = jax.random.randint(jax.random.fold_in(sequence_rng_key, 2), (blk_groups, 1), 0, 2)
        within = jnp.arange(span_rows, dtype=jnp.int32)[None, :]
        early = order[:, None] * span_rows + within
        later = (2 * blk_groups - 1 - order[:, None]) * span_rows + within
        former = jnp.where(swapped == 1, later, early)
        latter = jnp.where(swapped == 1, early, later)
        joined = jnp.concatenate([former, latter], axis=1).reshape(blk_groups, uly_groups, SEQ_DEV)
        return jnp.transpose(joined, (1, 0, 2)).reshape(LENGTH)
    return jnp.stack([one_sequence(number) for number in range(SEQS)]).astype(jnp.int32)


def with_spikes(array, key, source, target, parts, factor):
    owner, partner = [(jnp.arange(array.shape[dim]) // (array.shape[dim] // parts)).reshape([-1 if axis == dim else 1 for axis in range(array.ndim)]) for dim in (source, target)]
    chosen = jax.random.permutation(key, parts)[partner]
    strong = (owner == chosen) | (owner == (partner + parts // 2) % parts)
    return jnp.where(strong, factor * array, array)


def levels(stream_key, dims, split, low, high):
    gain, own = 1.0, jax.random.fold_in(stream_key, 6)
    for dim, shards_of in split:
        draws = jnp.exp(jax.random.uniform(jax.random.fold_in(own, dim), (shards_of,), jnp.float32, low / len(split), high / len(split)))
        gain = gain * jnp.repeat(draws, dims[dim] // shards_of).reshape([-1 if axis == dim else 1 for axis in range(len(dims))])
    return gain


def bell_draw(rng, dims, width, limit, split=(), held_as=jnp.bfloat16):
    values = jax.random.normal(rng, dims, jnp.float32) * width
    if len(split) > 0:
        values = levels(rng, dims, split, -0.22, 0.18) * values
    return jnp.clip(values, min=-limit, max=limit).astype(held_as)


def heavy_noise(rng, shape, spread, limit, split, heavy, kind=jnp.bfloat16):
    values = spread * jax.random.normal(rng, shape, jnp.float32)
    if split:
        values = values * levels(rng, shape, split, -0.22, 0.18)
    return jnp.clip(with_spikes(values, jax.random.fold_in(rng, 3), *heavy), -limit, limit).astype(kind)


def setup_inputs(seed: int = 0) -> dict:
    splits = jax.random.split(jax.random.key(seed), 16)
    return {
        "hidden": bell_draw(splits[0], (SEQS, LENGTH, D), (D ** -0.5), 0.15625, ((1, 32),)),
        "positions": draw_positions(jax.random.fold_in(splits[15], 71), 0),
        "w_query": bell_draw(splits[2], (D, D), D ** -0.5, 0.15625, ((0, 32),)),
        "w_key": bell_draw(splits[3], (D, D), D ** -0.5, 0.15625, ((0, 32),)),
        "w_value": bell_draw(splits[4], (D, D), D ** -0.5, 0.15625, ((0, 32),)),
        "w_out": bell_draw(splits[5], (D, D), D ** -0.5, 0.15625, ((0, 32),)),
        "w_up": bell_draw(splits[6], (FF, D), D ** -0.5, 0.15625, ((0, 32),)),
        "w_gate": bell_draw(splits[7], (FF, D), D ** -0.5, 0.15625, ((0, 32),)),
        "w_down": bell_draw(splits[8], (D, FF), FF ** -0.5, 0.078125, ((0, 32),)),
        "qk_scale": jnp.clip(jnp.exp(math.log(1.59375) - 0.5731879 * jax.random.uniform(splits[9], (D,), jnp.float32) ** levels(splits[9], (D,), ((0, 32),), -0.2, 0.2)), 0.8984375, 1.59375).astype(jnp.bfloat16),
        "alpha_attn": jnp.clip(jnp.exp(math.log(0.59765625) - 1.7917595 * jax.random.uniform(splits[10], (D,), jnp.float32) ** levels(splits[10], (D,), ((0, 32),), -0.2, 0.2)), 0.099609375, 0.59765625).astype(jnp.bfloat16),
        "alpha_mlp": jnp.clip(jnp.exp(math.log(0.59765625) - 1.7917595 * jax.random.uniform(splits[11], (D,), jnp.float32) ** levels(splits[11], (D,), ((0, 32),), -0.2, 0.2)), 0.099609375, 0.59765625).astype(jnp.bfloat16),
        "up_scale": jnp.clip(jnp.exp(math.log(2.0) - 1.3862944 * jax.random.uniform(splits[12], (FF,), jnp.float32) ** levels(splits[12], (FF,), ((0, 32),), -0.2, 0.2)), 0.5, 2.0).astype(jnp.bfloat16),
        "gate_scale": jnp.clip(jnp.exp(math.log(2.0) - 1.3862944 * jax.random.uniform(splits[13], (FF,), jnp.float32) ** levels(splits[13], (FF,), ((0, 32),), -0.2, 0.2)), 0.5, 2.0).astype(jnp.bfloat16),
        "cotangent": heavy_noise(splits[14], (SEQS, LENGTH, D), 1.0, 12.0, ((1, 32),), (1, 2, 32, 2.75)),
    }


@jax.custom_vjp
def low(v):
    return lax.optimization_barrier(v.astype(jnp.bfloat16)).astype(jnp.float32)

@jax.custom_vjp
def low_back(v):
    return v

def low_keep(v):
    return (low(v), None)

def low_pass(kept, grad):
    return (grad,)

def back_keep(v):
    return (v, None)

def back_low(kept, grad):
    return (low(grad),)
low.defvjp(low_keep, low_pass)
low_back.defvjp(back_keep, back_low)
strict_setting = lax.Precision.HIGHEST
rotary_base = 10000.0
tiny_eps = 1e-06
masked_score = -1e+30

def unit_rows(values):
    entries = values.shape[-1]
    return values * lax.rsqrt(lax.optimization_barrier(jnp.mean(values * values, axis=-1, keepdims=True)) + tiny_eps) * entries ** (-0.5)

def rotate_pairs(values, places):
    half_dim = values.shape[-1] // 2
    freqs = rotary_base ** (-(jnp.arange(half_dim, dtype=jnp.float32) * (2.0 / values.shape[-1])))
    angles = places.astype(jnp.float32)[..., None, None] * freqs
    cosine = jnp.cos(angles)
    sine = jnp.sin(angles)
    former = values[..., :half_dim]
    latter = values[..., half_dim:]
    return jnp.concatenate([former * cosine - latter * sine, latter * cosine + former * sine], axis=-1)

def attend(queries, key_rows, value_rows, places):
    length = queries.shape[0]
    block_rows = min(length, 512)
    total_blocks = length // block_rows
    query_blocks = queries.reshape(total_blocks, block_rows, queries.shape[1], queries.shape[2])
    place_blocks = places.reshape(total_blocks, block_rows)

    def one_block(members):
        query_part, place_part = members
        scores = low_back(jnp.einsum('qhd,khd->hqk', query_part, key_rows, precision=strict_setting))
        allowed = places[None, None, :] <= place_part[None, :, None]
        scores = jnp.where(allowed, scores, masked_score)
        largest = lax.optimization_barrier(jnp.max(scores, axis=-1, keepdims=True))
        log_total = largest + jnp.log(lax.optimization_barrier(jnp.sum(jnp.exp(scores - largest), axis=-1, keepdims=True)))
        weights = low(jnp.exp(scores - log_total))
        return jnp.einsum('hqk,khd->qhd', weights, value_rows, precision=strict_setting)
    outputs = lax.map(jax.checkpoint(one_block), (query_blocks, place_blocks))
    return outputs.reshape(queries.shape)

def forward(hidden, w_query, w_key, w_value, w_out, w_up, w_gate, w_down, qk_scale, alpha_attn, alpha_mlp, up_scale, gate_scale, positions):
    seq_count, length, model_width = hidden.shape

    def project(input_arrays, weight_matrix):
        return jnp.einsum('xom,gm->xog', input_arrays, weight_matrix, precision=strict_setting)
    scale_heads = qk_scale.reshape(HEADS, HEAD_DIM)
    q_raw = low_back(project(hidden, w_query)).reshape(seq_count, length, HEADS, HEAD_DIM)
    k_raw = low_back(project(hidden, w_key)).reshape(seq_count, length, HEADS, HEAD_DIM)
    queries = low(low_back(unit_rows(rotate_pairs(q_raw, positions)) * scale_heads * HEAD_DIM ** 0.5))
    key_rows = low(low_back(unit_rows(rotate_pairs(k_raw, positions)) * scale_heads))
    value_rows = low(low_back(project(hidden, w_value))).reshape(seq_count, length, HEADS, HEAD_DIM)
    attended = lax.map(lambda members: attend(members[0], members[1], members[2], members[3]), (queries, key_rows, value_rows, positions))
    mixed_rows = low(low_back(attended.reshape(seq_count, length, model_width)))
    att_proj = low_back(project(mixed_rows, w_out))
    first_out = unit_rows(hidden + alpha_attn * (unit_rows(att_proj) - hidden))
    mlp_input = low(first_out)
    up_rows = low_back(project(mlp_input, w_up))
    gate_rows = low_back(project(mlp_input, w_gate))
    inner_rows = low(jax.nn.silu(gate_rows * gate_scale * model_width ** 0.5) * (up_rows * up_scale))
    branch_output = low_back(project(inner_rows, w_down))
    return unit_rows(first_out + alpha_mlp * (unit_rows(branch_output) - first_out))

def reference(hidden, positions, w_query, w_key, w_value, w_out, w_up, w_gate, w_down, qk_scale, alpha_attn, alpha_mlp, up_scale, gate_scale, cotangent):
    floats = tuple((member.astype(jnp.float32) for member in (hidden, w_query, w_key, w_value, w_out, w_up, w_gate, w_down, qk_scale, alpha_attn, alpha_mlp, up_scale, gate_scale)))

    def wrapped(*members):
        return forward(*members, positions)
    result, pull_back = jax.vjp(wrapped, *floats)
    grads = pull_back(cotangent.astype(jnp.float32))
    return (result.astype(jnp.bfloat16), grads[0], grads[1], grads[2], grads[3], grads[4], grads[5], grads[6], grads[7], grads[8], grads[9], grads[10], grads[11], grads[12])
```

```python
import math

import jax
import jax.numpy as jnp
from jax import lax
from jax.sharding import PartitionSpec as P

D = 1280
HEADS = 20
HEAD_DIM = 64

rotary_base = 10000.0
tiny_eps = 1e-06
masked_score = -1e30
BF = jnp.bfloat16
F32 = jnp.float32


def unit_rows(values):
    entries = values.shape[-1]
    return (
        values
        * lax.rsqrt(jnp.mean(values * values, axis=-1, keepdims=True) + tiny_eps)
        * entries ** (-0.5)
    )


def rotate_pairs(values, places):
    half_dim = values.shape[-1] // 2
    freqs = rotary_base ** (-(jnp.arange(half_dim, dtype=F32) * (2.0 / values.shape[-1])))
    angles = places.astype(F32)[..., None, None] * freqs
    cosine = jnp.cos(angles)
    sine = jnp.sin(angles)
    former = values[..., :half_dim]
    latter = values[..., half_dim:]
    return jnp.concatenate(
        [former * cosine - latter * sine, latter * cosine + former * sine], axis=-1
    )


def project(rows, weight):
    return lax.dot_general(rows, weight, (((1,), (1,)), ((), ())), preferred_element_type=F32)


def weight_grad(grads, rows):
    return lax.dot_general(grads, rows, (((0,), (0,)), ((), ())), preferred_element_type=F32)


def pull_input(grads, weight):
    return jnp.dot(grads, weight, preferred_element_type=F32)


def residual_step(base, branch_output, rate):
    return unit_rows(base + rate * (unit_rows(branch_output) - base))


def gated(up_rows, gate_rows, up_wide, gate_wide):
    return jax.nn.silu(gate_rows * gate_wide * D**0.5) * (up_rows * up_wide)


def post_heads(raw_rows, scale_row, places, factor):
    seq_count, rows_each = places.shape
    heads = raw_rows.shape[-1] // HEAD_DIM
    shaped = raw_rows.reshape(seq_count, rows_each, heads, HEAD_DIM)
    turned = unit_rows(rotate_pairs(shaped, places)) * scale_row.reshape(heads, HEAD_DIM) * factor
    return turned.reshape(raw_rows.shape)


def local(
    hidden,
    positions,
    w_query,
    w_key,
    w_value,
    w_out,
    w_up,
    w_gate,
    w_down,
    qk_scale,
    alpha_attn,
    alpha_mlp,
    up_scale,
    gate_scale,
    cotangent,
):
    seq_count, rows_each, model_width = hidden.shape
    uly_count = lax.axis_size("uly")
    blk_count = lax.axis_size("blk")
    local_width = model_width // uly_count
    local_heads = HEADS // uly_count
    group_rows = uly_count * rows_each
    token_count = seq_count * rows_each
    group_tokens = seq_count * group_rows
    attn_each = w_query.shape[0]
    ff_each = w_up.shape[0]
    ff_local = ff_each * blk_count

    def uly_gather(rows):
        return lax.all_gather(
            rows.reshape(seq_count, rows_each, model_width), "uly", axis=1, tiled=True
        ).reshape(group_tokens, model_width)

    def uly_reduce(partial):
        return (
            lax.psum_scatter(
                partial.astype(BF).reshape(seq_count, group_rows, model_width),
                "uly",
                scatter_dimension=1,
                tiled=True,
            )
            .reshape(token_count, model_width)
            .astype(F32)
        )

    def by_owner(grad):
        shaped = grad.reshape(uly_count, blk_count, attn_each, grad.shape[1])
        return jnp.transpose(shaped, (1, 0, 2, 3)).reshape(blk_count, -1, grad.shape[1])

    packed = jnp.concatenate([qk_scale, alpha_attn, alpha_mlp, up_scale, gate_scale])[None]
    scales = lax.all_gather(packed, ("uly", "blk"), axis=0, tiled=True)
    cuts = [0, attn_each, 2 * attn_each, 3 * attn_each, 3 * attn_each + ff_each]
    uly_index = lax.axis_index("uly")
    own = lax.dynamic_slice_in_dim(scales, uly_index * blk_count, blk_count, 0)
    scale_wide = own[:, : cuts[1]].reshape(-1).astype(F32)
    attn_rate = scales[:, cuts[1] : cuts[2]].reshape(-1).astype(F32)
    mlp_rate = scales[:, cuts[2] : cuts[3]].reshape(-1).astype(F32)
    up_wide = own[:, cuts[3] : cuts[4]].reshape(-1).astype(F32)
    gate_wide = own[:, cuts[4] :].reshape(-1).astype(F32)

    query_places = lax.all_gather(positions, "uly", axis=1, tiled=True)
    key_places = lax.all_gather(query_places, "blk", axis=1, tiled=True)

    flat_rows = hidden.reshape(token_count, model_width)
    hidden_wide = flat_rows.astype(F32)
    group_hidden = uly_gather(flat_rows)

    qkv_full = lax.all_gather(jnp.stack([w_query, w_key, w_value]), "blk", axis=1, tiled=True)
    query_full, key_full, value_full = qkv_full[0], qkv_full[1], qkv_full[2]

    out_cols = lax.all_to_all(
        jnp.transpose(w_out.reshape(attn_each, uly_count, local_width), (1, 0, 2)),
        "uly", split_axis=0, concat_axis=0, tiled=True,
    )
    down_cols = lax.all_to_all(
        jnp.transpose(w_down.reshape(attn_each, uly_count, ff_local), (1, 0, 2)),
        "uly", split_axis=0, concat_axis=0, tiled=True,
    )
    out_full = lax.all_gather(out_cols, "blk", axis=1, tiled=True).reshape(model_width, local_width)
    down_full = lax.all_gather(down_cols, "blk", axis=1, tiled=True).reshape(model_width, ff_local)
    up_full = lax.all_gather(w_up, "blk", axis=0, tiled=True)
    gate_full = lax.all_gather(w_gate, "blk", axis=0, tiled=True)

    q_raw = project(group_hidden, query_full)
    k_raw = project(group_hidden, key_full)
    query_rows, pull_query = jax.vjp(
        lambda raw, row: post_heads(raw, row, query_places, HEAD_DIM**0.5), q_raw, scale_wide
    )
    key_rows, pull_key = jax.vjp(
        lambda raw, row: post_heads(raw, row, query_places, 1.0), k_raw, scale_wide
    )
    query_heads = query_rows.astype(BF).reshape(seq_count, group_rows, local_width)
    key_heads = key_rows.astype(BF).reshape(seq_count, group_rows, local_width)
    value_heads = (
        project(group_hidden, value_full).astype(BF).reshape(seq_count, group_rows, local_width)
    )
    query_four = query_heads.reshape(seq_count, group_rows, local_heads, HEAD_DIM)
    pieces = lax.all_gather(
        jnp.stack([key_heads, value_heads]), "blk", axis=2, tiled=True
    )

    def block_parts(offset, block_rows):
        both = lax.dynamic_slice_in_dim(pieces, offset, block_rows, 2).reshape(
            2, seq_count, block_rows, local_heads, HEAD_DIM
        )
        key_part, value_part = both[0], both[1]
        place_part = lax.dynamic_slice_in_dim(key_places, offset, block_rows, 1)
        scores = jnp.einsum("sqhd,skhd->shqk", query_four, key_part, preferred_element_type=F32)
        allowed = place_part[:, None, None, :] <= query_places[:, None, :, None]
        return (key_part, value_part, jnp.where(allowed, scores, masked_score), allowed)

    start_state = (
        jnp.full((seq_count, local_heads, group_rows), masked_score, F32),
        jnp.zeros((seq_count, local_heads, group_rows), F32),
        jnp.zeros((seq_count, group_rows, local_heads, HEAD_DIM), F32),
    )
    piece_rows = pieces.shape[2]
    block_rows = math.gcd(piece_rows, 512)

    def forward_step(block_index, running):
        running_max, running_sum, running_acc = running
        key_part, value_part, scores, allowed = block_parts(block_index * block_rows, block_rows)
        new_max = jnp.maximum(running_max, jnp.max(scores, axis=-1))
        weights = jnp.where(allowed, jnp.exp(scores - new_max[..., None]), 0.0)
        shrink = jnp.exp(running_max - new_max)
        running_sum = running_sum * shrink + jnp.sum(weights, axis=-1)
        update = jnp.einsum(
            "shqk,skhd->sqhd", weights.astype(BF), value_part, preferred_element_type=F32
        )
        running_acc = running_acc * jnp.transpose(shrink, (0, 2, 1))[..., None] + update
        return (new_max, running_sum, running_acc)

    running_max, running_sum, running_acc = lax.fori_loop(
        0, piece_rows // block_rows, forward_step, start_state
    )
    log_total = running_max + jnp.log(running_sum)
    attended = running_acc / jnp.transpose(running_sum, (0, 2, 1))[..., None]
    mixed_group = attended.reshape(group_tokens, local_width).astype(BF)
    att_proj = uly_reduce(project(mixed_group, out_full))
    first_out, pull_attn = jax.vjp(residual_step, hidden_wide, att_proj, attn_rate)
    mlp_group = uly_gather(first_out.astype(BF))
    up_rows = project(mlp_group, up_full)
    gate_rows = project(mlp_group, gate_full)
    inner_rows, pull_inner = jax.vjp(gated, up_rows, gate_rows, up_wide, gate_wide)
    inner_send = inner_rows.astype(BF)
    branch_output = uly_reduce(project(inner_send, down_full))
    final_rows, pull_mlp = jax.vjp(residual_step, first_out, branch_output, mlp_rate)
    layer_out = final_rows.astype(BF).reshape(seq_count, rows_each, model_width)
    upstream = cotangent.reshape(token_count, model_width).astype(F32)
    grad_first, grad_branch, grad_alpha_mlp = pull_mlp(upstream)

    branch_low = uly_gather(grad_branch.astype(BF))
    grad_down = weight_grad(branch_low, inner_send)
    grad_inner = pull_input(branch_low, down_full)
    grad_up_rows, grad_gate_rows, grad_up_scale, grad_gate_scale = pull_inner(grad_inner)
    up_low = grad_up_rows.astype(BF)
    gate_low = grad_gate_rows.astype(BF)
    grad_up = weight_grad(up_low, mlp_group)
    grad_gate = weight_grad(gate_low, mlp_group)
    mlp_own = lax.psum_scatter(
        jnp.concatenate(
            [
                grad_up.astype(BF).reshape(blk_count, ff_each, model_width),
                grad_gate.astype(BF).reshape(blk_count, ff_each, model_width),
                by_owner(grad_down.astype(BF)),
            ],
            axis=1,
        ),
        "blk", scatter_dimension=0, tiled=True,
    )[0]
    down_own = lax.all_to_all(
        mlp_own[2 * ff_each :].reshape(uly_count, attn_each, ff_local),
        "uly", split_axis=0, concat_axis=0, tiled=True,
    )
    down_weight_gradient = jnp.transpose(down_own, (1, 0, 2)).reshape(attn_each, -1).astype(F32)

    grad_first = grad_first + uly_reduce(pull_input(up_low, up_full) + pull_input(gate_low, gate_full))
    grad_residual, grad_att, grad_alpha_attn = pull_attn(grad_first)
    att_low = uly_gather(grad_att.astype(BF))
    grad_out = weight_grad(att_low, mixed_group)
    grad_four = (
        pull_input(att_low, out_full).astype(BF).reshape(seq_count, group_rows, local_heads, HEAD_DIM)
    )
    row_delta = jnp.transpose(jnp.sum(grad_four.astype(F32) * attended, axis=-1), (0, 2, 1))
    back_state = (
        jnp.zeros((seq_count, group_rows, local_heads, HEAD_DIM), F32),
        jnp.zeros((2, seq_count, piece_rows, local_width), BF),
    )

    def backward_step(block_index, running):
        grad_query_acc, grad_pairs = running
        offset = block_index * block_rows
        key_part, value_part, scores, allowed = block_parts(offset, block_rows)
        probs = jnp.exp(scores - log_total[..., None])
        grad_values = jnp.einsum(
            "shqk,sqhd->skhd", probs.astype(BF), grad_four, preferred_element_type=F32
        )
        grad_probs = jnp.einsum("sqhd,skhd->shqk", grad_four, value_part, preferred_element_type=F32)
        grad_scores = (probs * (grad_probs - row_delta[..., None])).astype(BF)
        grad_query_acc = grad_query_acc + jnp.einsum(
            "shqk,skhd->sqhd", grad_scores, key_part, preferred_element_type=F32
        )
        grad_keys = jnp.einsum("shqk,sqhd->skhd", grad_scores, query_four, preferred_element_type=F32)
        stacked = (
            jnp.stack([grad_keys, grad_values])
            .reshape(2, seq_count, block_rows, local_width)
            .astype(BF)
        )
        grad_pairs = lax.dynamic_update_slice_in_dim(grad_pairs, stacked, offset, 2)
        return (grad_query_acc, grad_pairs)

    grad_query_acc, grad_pairs = lax.fori_loop(
        0, piece_rows // block_rows, backward_step, back_state
    )
    own_pairs = lax.psum_scatter(grad_pairs, "blk", scatter_dimension=2, tiled=True)
    query_low = grad_query_acc.reshape(group_tokens, local_width).astype(BF)
    key_low = own_pairs[0].reshape(group_tokens, local_width)
    value_low = own_pairs[1].reshape(group_tokens, local_width)
    grad_q_raw, grad_scale_query = pull_query(query_low.astype(F32))
    grad_k_raw, grad_scale_key = pull_key(key_low.astype(F32))
    raw_query_low = grad_q_raw.astype(BF)
    raw_key_low = grad_k_raw.astype(BF)
    grad_query = weight_grad(raw_query_low, group_hidden)
    grad_key = weight_grad(raw_key_low, group_hidden)
    grad_value = weight_grad(value_low, group_hidden)
    grad_hidden = grad_residual + uly_reduce(
        pull_input(raw_query_low, query_full)
        + pull_input(raw_key_low, key_full)
        + pull_input(value_low, value_full)
    )
    attn_own = lax.psum_scatter(
        jnp.concatenate(
            [
                grad.astype(BF).reshape(blk_count, attn_each, model_width)
                for grad in (grad_query, grad_key, grad_value)
            ],
            axis=1,
        ),
        "blk", scatter_dimension=0, tiled=True,
    )[0].reshape(3, attn_each, model_width).astype(F32)
    out_own = lax.psum_scatter(
        by_owner(grad_out.astype(BF)), "blk", scatter_dimension=0, tiled=True
    ).reshape(uly_count, attn_each, local_width)
    out_own = lax.all_to_all(out_own, "uly", split_axis=0, concat_axis=0, tiled=True)
    out_gradient = jnp.transpose(out_own, (1, 0, 2)).reshape(attn_each, -1).astype(F32)

    own_sums = jnp.concatenate(
        [
            (grad_scale_query + grad_scale_key).reshape(blk_count, attn_each),
            grad_up_scale.reshape(blk_count, ff_each),
            grad_gate_scale.reshape(blk_count, ff_each),
        ],
        axis=1,
    )
    alpha_sums = jnp.concatenate(
        [
            grad_alpha_attn.reshape(uly_count, blk_count, attn_each),
            grad_alpha_mlp.reshape(uly_count, blk_count, attn_each),
        ],
        axis=2,
    )
    alpha_sums = lax.all_to_all(alpha_sums, "uly", split_axis=0, concat_axis=0, tiled=True).sum(axis=0)
    sums = jnp.concatenate([own_sums, alpha_sums], axis=1)
    sums = lax.all_to_all(sums, "blk", split_axis=0, concat_axis=0, tiled=True).sum(axis=0)
    c0, c1 = attn_each, attn_each + ff_each
    c2 = c1 + ff_each
    c3 = c2 + attn_each
    return (
        layer_out,
        grad_hidden.reshape(seq_count, rows_each, model_width),
        attn_own[0],
        attn_own[1],
        attn_own[2],
        out_gradient,
        mlp_own[:ff_each].astype(F32),
        mlp_own[ff_each : 2 * ff_each].astype(F32),
        down_weight_gradient,
        sums[:c0],
        sums[c2:c3],
        sums[c3:],
        sums[c0:c1],
        sums[c1:c2],
    )


def solution(mesh):
    both = ("uly", "blk")
    rows, tokens, flat = P(both, None), P(None, both, None), P(both)
    return jax.shard_map(
        local,
        mesh=mesh,
        in_specs=(tokens, P(None, both)) + (rows,) * 7 + (flat,) * 5 + (tokens,),
        out_specs=(tokens, tokens) + (rows,) * 7 + (flat,) * 5,
        check_vma=False,
    )
```

```python
import functools

import jax
import jax.numpy as jnp
from jax import lax
from jax.experimental import pallas as pl
from jax.experimental.pallas import tpu as pltpu
from jax.sharding import Mesh
from jax.sharding import PartitionSpec as P

D = 1280
HEADS = 20
HEAD_DIM = 64
AXES = ("far", "core", "line", "side")
PLANE = ("far", "core", "side")
VMEM_BYTES = 60 * 1024 * 1024

rotary_base = 10000.0
tiny_eps = 1e-06
BF = jnp.bfloat16
F32 = jnp.float32


def place():
    return tuple(lax.axis_index(name) for name in AXES)


def remote(src, dst, send, recv, device):
    return pltpu.make_async_remote_copy(
        src_ref=src,
        dst_ref=dst,
        send_sem=send,
        recv_sem=recv,
        device_id=device,
        device_id_type=pl.DeviceIdType.MESH,
    )


def signal_to(device):
    pl.semaphore_signal(
        pltpu.get_barrier_semaphore(), inc=1, device_id=device, device_id_type=pl.DeviceIdType.MESH
    )


def greet(devices, maybe=()):
    count = len(devices)
    for device in devices:
        signal_to(device)
    for there, device in maybe:
        pl.when(there)(functools.partial(signal_to, device))
        count = count + jnp.where(there, 1, 0)
    pl.semaphore_wait(pltpu.get_barrier_semaphore(), count)


def params(collective_id):
    return pltpu.CompilerParams(
        collective_id=collective_id, has_side_effects=True, vmem_limit_bytes=VMEM_BYTES
    )


class UlyGather:
    sems = staticmethod(lambda parts: [pltpu.SemaphoreType.DMA((3, parts))] * 2 + [pltpu.SemaphoreType.DMA((parts,))])

    def __init__(self, x, o, send, recv, local):
        y, c, z, s = place()
        u, v = y * 2 + c, (1 - y) * 2 + c
        mate, across = (y, 1 - c, z, s), (1 - y, c, z, s)
        self.parts = x.shape[0]
        parts = range(self.parts)
        self.far = [remote(x.at[i], o.at[i, u], send.at[0, i], recv.at[0, i], across) for i in parts]
        self.near = [remote(x.at[i], o.at[i, u], send.at[1, i], recv.at[1, i], mate) for i in parts]
        self.on = [remote(o.at[i, v], o.at[i, v], send.at[2, i], recv.at[2, i], mate) for i in parts]
        self.own = [pltpu.make_async_copy(x.at[i], o.at[i, u], local.at[i]) for i in parts]

    def start_part(self, i):
        self.far[i].start()
        self.near[i].start()
        self.own[i].start()

    def start(self):
        for i in range(self.parts):
            self.start_part(i)

    def forward(self):
        for i in range(self.parts):
            self.far[i].wait_recv()
            self.on[i].start()

    def finish(self):
        for i in range(self.parts):
            self.near[i].wait_recv()
            self.on[i].wait_recv()
            self.own[i].wait()
            self.far[i].wait_send()
            self.near[i].wait_send()
            self.on[i].wait_send()


def uly_peers():
    y, c, z, s = place()
    return [(y, 1 - c, z, s), (1 - y, c, z, s)]


def add_low(*terms):
    total = terms[0].astype(F32)
    for term in terms[1:]:
        total = total + term.astype(F32)
    return total


class UlyReduce:
    @staticmethod
    def scratch(x):
        parts, _, rows, width = x.shape
        return [
            pltpu.VMEM((parts, 2, rows, width), x.dtype),
            pltpu.VMEM((parts, rows, width), x.dtype),
            pltpu.VMEM((parts, rows, width), x.dtype),
            pltpu.SemaphoreType.DMA((3, parts)),
            pltpu.SemaphoreType.DMA((3, parts)),
        ]

    def __init__(self, x, near, mid, far_in, send, recv):
        y, c, z, s = place()
        mate, across = uly_peers()
        self.x, self.near_ref, self.mid, self.far_in = x, near, mid, far_in
        self.y, self.c, self.parts = y, c, x.shape[0]
        parts = range(self.parts)
        self.near = [
            [
                remote(x.at[i, f * 2 + 1 - c], near.at[i, k], send.at[k, i], recv.at[k, i], mate)
                for k, f in enumerate((1 - y, y))
            ]
            for i in parts
        ]
        self.far = [remote(mid.at[i], far_in.at[i], send.at[2, i], recv.at[2, i], across) for i in parts]

    def start(self):
        for i in range(self.parts):
            for copy in self.near[i]:
                copy.start()

    def middle(self):
        for i in range(self.parts):
            self.near[i][0].wait_recv()
            self.mid[i] = add_low(self.x[i, (1 - self.y) * 2 + self.c], self.near_ref[i, 0]).astype(BF)
            self.far[i].start()

    def result(self, i):
        self.near[i][1].wait_recv()
        self.far[i].wait_recv()
        return add_low(self.x[i, self.y * 2 + self.c], self.near_ref[i, 1], self.far_in[i])

    def finish(self):
        for i in range(self.parts):
            for copy in self.near[i] + [self.far[i]]:
                copy.wait_send()


def plane_peers():
    y, c, z, s = place()
    return [(y, 1 - c, z, s), (1 - y, c, z, s), (y, c, z, 1 - s)]


def plane_index(y, c, s):
    return (y * 2 + c) * 2 + s


class PlaneGather:
    sems = [pltpu.SemaphoreType.DMA((14,))] * 2 + [pltpu.SemaphoreType.DMA((2,))]

    def __init__(self, x, o, send, recv, local):
        y, c, z, s = place()
        mate, across, cross = plane_peers()
        me, py, px, pd = (
            plane_index(y, c, s),
            plane_index(1 - y, c, s),
            plane_index(y, c, 1 - s),
            plane_index(1 - y, c, 1 - s),
        )

        def copy(source, target, slot, device):
            return remote(source, target, send.at[slot], recv.at[slot], device)

        def on(p, i, slot, device):
            return copy(o.at[p, i], o.at[p, i], slot, device)

        self.by_y = [copy(x.at[i], o.at[me, i], i, across) for i in (0, 1)]
        self.by_x = [copy(x.at[i], o.at[me, i], 2 + i, cross) for i in (0, 1)]
        self.near = [copy(x.at[i], o.at[me, i], 4 + i, mate) for i in (0, 1)]
        self.corner = [on(py, 0, 6, cross), on(px, 1, 7, across)]
        self.pass_y = [on(py, 0, 8, mate), on(py, 1, 10, mate)]
        self.pass_x = [on(px, 0, 11, mate), on(px, 1, 9, mate)]
        self.pass_d = [on(pd, 0, 12, mate), on(pd, 1, 13, mate)]
        self.own = [pltpu.make_async_copy(x.at[i], o.at[me, i], local.at[i]) for i in (0, 1)]

    def start_part(self, i):
        for copy in (self.by_y[i], self.by_x[i], self.near[i], self.own[i]):
            copy.start()

    def forward_part(self, i):
        first, then = ((self.by_y, self.pass_y), (self.by_x, self.pass_x))[:: 1 - 2 * i]
        first[0][i].wait_recv()
        self.corner[i].start()
        first[1][i].start()
        then[0][i].wait_recv()
        then[1][i].start()

    def finish(self):
        for i in (0, 1):
            self.corner[i].wait_recv()
            self.pass_d[i].start()
        for i in (0, 1):
            for copy in (self.near[i], self.pass_y[i], self.pass_x[i], self.pass_d[i]):
                copy.wait()
            for copy in (self.by_y[i], self.by_x[i], self.corner[i]):
                copy.wait_send()
            self.own[i].wait()


class PlaneReduce:
    @staticmethod
    def scratch(x):
        one = pltpu.VMEM(x.shape[1:], x.dtype)
        return [pltpu.VMEM((4,) + x.shape[1:], x.dtype)] + [one] * 6 + [pltpu.SemaphoreType.DMA((14,))] * 2

    def __init__(self, x, near, out_x, out_y, out_d, in_x, in_y, in_d, send, recv):
        y, c, z, s = place()
        mate, across, cross = plane_peers()
        self.c = c
        self.spots = ((1 - y, 1 - s), (y, 1 - s), (1 - y, s), (y, s))
        self.x, self.near_ref = x, near
        self.out_x, self.out_y, self.out_d = out_x, out_y, out_d
        self.in_x, self.in_y, self.in_d = in_x, in_y, in_d

        def copy(source, target, slot, device):
            return remote(source, target, send.at[slot], recv.at[slot], device)

        self.near = [
            [copy(x.at[plane_index(sy, 1 - c, ss), i], near.at[k, i], 2 * k + i, mate) for i in (0, 1)]
            for k, (sy, ss) in enumerate(self.spots)
        ]
        self.corner = [
            copy(out_d.at[0], in_d.at[0], 8, cross),
            copy(out_d.at[1], in_d.at[1], 9, across),
        ]
        self.by_x = [copy(out_x.at[i], in_x.at[i], 10 + i, cross) for i in (0, 1)]
        self.by_y = [copy(out_y.at[i], in_y.at[i], 12 + i, across) for i in (0, 1)]

    def pair(self, k, i):
        sy, ss = self.spots[k]
        self.near[k][i].wait_recv()
        return add_low(self.x[plane_index(sy, self.c, ss), i], self.near_ref[k, i])

    def start(self):
        for spot in self.near:
            for copy in spot:
                copy.start()

    def middle(self):
        for i in (0, 1):
            self.out_d[i] = self.pair(0, i).astype(BF)
            self.corner[i].start()
        self.out_x[0] = self.pair(1, 0).astype(BF)
        self.by_x[0].start()
        self.out_y[1] = self.pair(2, 1).astype(BF)
        self.by_y[1].start()

    def last(self):
        part = self.pair(2, 0)
        self.corner[0].wait_recv()
        self.out_y[0] = (part + self.in_d[0].astype(F32)).astype(BF)
        self.by_y[0].start()
        part = self.pair(1, 1)
        self.corner[1].wait_recv()
        self.out_x[1] = (part + self.in_d[1].astype(F32)).astype(BF)
        self.by_x[1].start()

    def result(self, i):
        own = self.pair(3, i)
        self.by_x[i].wait_recv()
        self.by_y[i].wait_recv()
        return own + add_low(self.in_x[i], self.in_y[i])

    def finish(self):
        for copy in [c for spot in self.near for c in spot] + self.corner + self.by_x + self.by_y:
            copy.wait_send()


def plane_corners():
    y, c, z, s = place()
    return [
        (y, 1 - c, s), (1 - y, c, s), (1 - y, 1 - c, s),
        (y, c, 1 - s), (y, 1 - c, 1 - s), (1 - y, c, 1 - s), (1 - y, 1 - c, 1 - s),
    ]


def line_ends(n_line):
    y, c, z, s = place()
    return (z > 0, (y, c, z - 1, s)), (z < n_line - 1, (y, c, z + 1, s)), (y, c, z, 1 - s)


class BlkGather:
    @staticmethod
    def sems(n_line):
        return [
            pltpu.SemaphoreType.DMA((3,)),
            pltpu.SemaphoreType.DMA((1,)),
            pltpu.SemaphoreType.DMA((4, n_line)),
            pltpu.SemaphoreType.DMA((4, n_line)),
            pltpu.SemaphoreType.DMA((1,)),
        ]

    def __init__(self, n_line, pick_x, pick_o, own_send, own_recv, send, recv, local):
        y, c, z, s = place()
        self.z, self.s, self.n = z, s, n_line
        (self.has_low, self.low), (self.has_high, self.high), self.cross = line_ends(n_line)
        self.pick_x, self.pick_o = pick_x, pick_o
        self.sem = (own_send, own_recv, send, recv, local)

    def block(self, way, k):
        z = self.z - k if way == 0 else self.z + k
        return self.pick_o(z * 2 + self.s)

    def own(self, way):
        own_send, own_recv, send, recv, local = self.sem
        arrival = own_recv.at[0] if way == 2 else recv.at[way, 0]
        target = (self.high, self.low, self.cross)[way]
        return remote(self.pick_x(), self.pick_o(self.z * 2 + self.s), own_send.at[way], arrival, target)

    def keep(self):
        return pltpu.make_async_copy(self.pick_x(), self.pick_o(self.z * 2 + self.s), self.sem[4].at[0])

    def onward(self, way, k):
        send, recv = self.sem[2:4]
        target = self.high if way == 0 else self.low
        return remote(self.block(way, k), self.block(way, k), send.at[way, k], recv.at[way, k], target)

    def over(self, way, k):
        send, recv = self.sem[2:4]
        return remote(self.block(way, k), self.block(way, k), send.at[2 + way, k], recv.at[2 + way, k], self.cross)

    def arrive(self, way, k):
        send, recv = self.sem[2:4]
        return remote(self.block(way, k), self.block(way, k), send.at[way, k], recv.at[way, k - 1], self.cross)

    def there(self, way, k):
        return self.z >= k if way == 0 else self.z + k < self.n

    def start(self):
        pl.when(self.has_high)(lambda: self.own(0).start())
        pl.when(self.has_low)(lambda: self.own(1).start())
        self.own(2).start()
        self.keep().start()

    def step(self, k):
        for way in (0, 1):
            @pl.when(self.there(way, k))
            def _():
                self.arrive(way, k).wait_recv()

                @pl.when((self.has_high, self.has_low)[way])
                def _():
                    self.onward(way, k).start()

                self.over(way, k).start()

    def finish_arrivals(self):
        self.own(2).wait_recv()
        for k in range(1, self.n):
            for way in (0, 1):
                pl.when(self.there(way, k))(lambda: self.over(way, k).wait_recv())
        self.keep().wait()

    def finish_sends(self):
        pl.when(self.has_high)(lambda: self.own(0).wait_send())
        pl.when(self.has_low)(lambda: self.own(1).wait_send())
        self.own(2).wait_send()
        for k in range(1, self.n):
            for way in (0, 1):
                @pl.when(self.there(way, k))
                def _():
                    self.over(way, k).wait_send()

                    @pl.when((self.has_high, self.has_low)[way])
                    def _():
                        self.onward(way, k).wait_send()


def blk_greet(n_line):
    low, high, cross = line_ends(n_line)
    greet([cross], [low, high])


def blk_gather_kernel(n_line, count, *refs):
    ins, outs, sems = refs[:count], refs[count : 2 * count], refs[2 * count :]
    blk_greet(n_line)
    jobs, at = [], 0
    for x, o in zip(ins, outs):
        for i in range(x.shape[0]):
            jobs.append(
                BlkGather(
                    n_line,
                    lambda x=x, i=i: x.at[i],
                    lambda block, o=o, i=i: o.at[block, i],
                    *sems[5 * at : 5 * at + 5],
                )
            )
            at += 1
    for job in jobs:
        job.start()
    for k in range(1, n_line):
        for job in jobs:
            job.step(k)
    for job in jobs:
        job.finish_arrivals()
    for job in jobs:
        job.finish_sends()


def blk_gather(n_line, *arrays):
    count = len(arrays)
    chunks = sum(a.shape[0] for a in arrays)
    return pl.pallas_call(
        functools.partial(blk_gather_kernel, n_line, count),
        out_shape=[jax.ShapeDtypeStruct((2 * n_line,) + a.shape, a.dtype) for a in arrays],
        in_specs=[pl.BlockSpec(memory_space=pltpu.VMEM)] * count,
        out_specs=[pl.BlockSpec(memory_space=pl.ANY)] * count,
        scratch_shapes=BlkGather.sems(n_line) * chunks,
        compiler_params=params(5),
        cost_estimate=pl.CostEstimate(flops=0, bytes_accessed=70 * 3_000_000, transcendentals=0),
        name="blk_gather",
    )(*arrays)


class BlkReduce:
    @staticmethod
    def scratch(n_line, a):
        return [
            pltpu.VMEM((n_line,) + a.shape[1:], a.dtype),
            pltpu.VMEM((n_line + 1,) + a.shape[1:], a.dtype),
            pltpu.SemaphoreType.DMA((n_line,)),
            pltpu.SemaphoreType.DMA((n_line,)),
            pltpu.SemaphoreType.DMA((2, n_line)),
            pltpu.SemaphoreType.DMA((2, n_line)),
        ]

    def __init__(self, n_line, x, side_in, line_in, side_send, side_recv, send, recv):
        y, c, self.z, self.s = place()
        self.n = n_line
        (self.has_low, self.low), (self.has_high, self.high), self.cross = line_ends(n_line)
        self.x, self.side_in, self.line_in = x, side_in, line_in
        self.sem = (side_send, side_recv, send, recv)

    def spot(self, way, k):
        return self.z + k if way == 0 else self.z - k

    def exists(self, way, k):
        return self.z + k < self.n if way == 0 else self.z >= k

    def side(self, zz):
        side_send, side_recv = self.sem[:2]
        return remote(
            self.x.at[zz * 2 + 1 - self.s], self.side_in.at[zz], side_send.at[zz], side_recv.at[zz], self.cross
        )

    def slot(self, way, k):
        return self.n if way == 1 and k == 0 else self.spot(way, k)

    def move(self, way, k):
        send, recv = self.sem[2:]
        target = self.high if way == 0 else self.low
        zz = self.spot(way, k)
        there = self.n if way == 1 and k == 1 else zz
        return remote(
            self.side_in.at[zz], self.line_in.at[there], send.at[way, k], recv.at[way, k - 1], target
        )

    def arrive(self, way, k):
        send, recv = self.sem[2:]
        there = self.line_in.at[self.slot(way, k)]
        return remote(there, there, send.at[way, k], recv.at[way, k], self.cross)

    def start(self, k):
        for way in (0, 1) if k > 0 else (0,):
            pl.when(self.exists(way, k))(lambda: self.side(self.spot(way, k)).start())

    def step(self, k):
        for way in (0, 1):
            @pl.when(self.exists(way, k))
            def _():
                zz = self.spot(way, k)
                self.side(zz).wait_recv()
                passed = self.has_low if way == 0 else self.has_high

                @pl.when(passed)
                def _():
                    self.arrive(way, k).wait_recv()
                    self.side_in[zz] = add_low(
                        self.x[zz * 2 + self.s], self.side_in[zz], self.line_in[zz]
                    ).astype(self.side_in.dtype)

                @pl.when(jnp.logical_not(passed))
                def _():
                    self.side_in[zz] = add_low(self.x[zz * 2 + self.s], self.side_in[zz]).astype(
                        self.side_in.dtype
                    )

                self.move(way, k).start()

    def result(self, o):
        z = self.z
        self.side(z).wait_recv()
        pl.when(self.has_low)(lambda: self.arrive(0, 0).wait_recv())
        pl.when(self.has_high)(lambda: self.arrive(1, 0).wait_recv())
        own = add_low(self.x[z * 2 + self.s], self.side_in[z])

        @pl.when(jnp.logical_and(self.has_low, self.has_high))
        def _():
            o[...] = (own + add_low(self.line_in[z], self.line_in[self.n])).astype(o.dtype)

        @pl.when(jnp.logical_not(self.has_low))
        def _():
            o[...] = (own + self.line_in[self.n].astype(F32)).astype(o.dtype)

        @pl.when(jnp.logical_not(self.has_high))
        def _():
            o[...] = (own + self.line_in[z].astype(F32)).astype(o.dtype)

    def finish(self):
        for k in range(self.n - 1, -1, -1):
            for way in (0, 1) if k > 0 else (0,):
                @pl.when(self.exists(way, k))
                def _():
                    self.side(self.spot(way, k)).wait_send()
                    if k > 0:
                        self.move(way, k).wait_send()


def blk_reduce_kernel(n_line, count, *refs):
    ins, outs, scratch = refs[:count], refs[count : 2 * count], refs[2 * count :]
    blk_greet(n_line)
    jobs, places = [], []
    for x, o in zip(ins, outs):
        for i in range(x.shape[1]):
            at = 6 * len(jobs)
            jobs.append(BlkReduce(n_line, x.at[:, i], *scratch[at : at + 6]))
            places.append(o.at[i])
    for k in range(n_line - 1, -1, -1):
        for job in jobs:
            job.start(k)
    for k in range(n_line - 1, 0, -1):
        for job in jobs:
            job.step(k)
    for job, o in zip(jobs, places):
        job.result(o)
    for job in jobs:
        job.finish()


def blk_reduce(n_line, *arrays):
    count, scratch = len(arrays), []
    for x in arrays:
        one = jax.ShapeDtypeStruct(x.shape[:1] + x.shape[2:], x.dtype)
        scratch += BlkReduce.scratch(n_line, one) * x.shape[1]
    return pl.pallas_call(
        functools.partial(blk_reduce_kernel, n_line, count),
        out_shape=[jax.ShapeDtypeStruct(x.shape[1:], x.dtype) for x in arrays],
        in_specs=[pl.BlockSpec(memory_space=pltpu.VMEM)] * count,
        out_specs=[pl.BlockSpec(memory_space=pltpu.VMEM)] * count,
        scratch_shapes=scratch,
        compiler_params=params(7),
        cost_estimate=pl.CostEstimate(flops=0, bytes_accessed=70 * 3_000_000, transcendentals=0),
        name="blk_reduce",
    )(*arrays)


def exit_kernel(
    n_line, gq, gk, gv, gh, res, oc, dc, alpha, rest,
    gq_o, gk_o, gv_o, gh_o, oc_o, dc_o, sum_o,
    alpha_in, line_out, line_all, oc_s, oc_r, dc_s, dc_r, al_s, al_r, su_s, su_r, keep, *scratch,
):
    y, c, z, s = place()
    u, p, b, n_blk = y * 2 + c, plane_index(y, c, s), z * 2 + s, 2 * n_line
    low, high, cross = line_ends(n_line)
    corners = plane_corners()
    others = []
    for i in range(1, n_blk):
        to = lax.rem(b + i, n_blk)
        others.append((y, c, to // 2, lax.rem(to, 2)))
    once = [(to[3] != 1 - s) | (to[2] != z) for to in others]
    greet([(yy, cc, z, ss) for yy, cc, ss in corners], list(zip(once, others)))
    heads = 6
    jobs = [BlkReduce(n_line, x, *scratch[heads * i : heads * (i + 1)]) for i, x in enumerate((gq, gk, gv))]
    hid = UlyReduce(gh, *scratch[heads * 3 :])
    small, cols = [], []
    for k, (yy, cc, ss) in enumerate(corners):
        target = (yy, cc, z, ss)
        cols.append(remote(dc.at[plane_index(yy, cc, ss)], dc_o.at[p], dc_s.at[k], dc_r.at[k], target))
        if k < 3:
            cols.append(remote(oc.at[yy * 2 + cc], oc_o.at[u], oc_s.at[k], oc_r.at[k], target))
            small.append(remote(alpha.at[yy * 2 + cc], alpha_in.at[k], al_s.at[k], al_r.at[k], target))
    for job in small:
        job.start()
    hid.start()
    for k in range(n_line - 1, -1, -1):
        for job in jobs:
            job.start(k)
    mine = [
        pltpu.make_async_copy(dc.at[p], dc_o.at[p], keep.at[0]),
        pltpu.make_async_copy(oc.at[u], oc_o.at[u], keep.at[1]),
    ]
    for job in mine:
        job.start()
    hid.middle()
    for job in cols:
        job.start()
    for job in small:
        job.wait_recv()
    line_out[...] = rest[...]
    line_out[:, :, :128] = rest[:, :, :128] + alpha[u] + alpha_in[0] + alpha_in[1] + alpha_in[2]
    line_jobs = []
    for i in range(1, n_blk):
        to = lax.rem(b + i, n_blk)
        line_jobs.append(
            remote(line_out.at[to], line_all.at[i - 1], su_s.at[i - 1], su_r.at[i - 1], others[i - 1])
        )
    for job in line_jobs:
        job.start()
    for k in range(n_line - 1, 0, -1):
        for job in jobs:
            job.step(k)
    for i in range(gh.shape[0]):
        gh_o[i] = res[i] + hid.result(i)
    total = line_out[b]
    for i, job in enumerate(line_jobs):
        job.wait_recv()
        total = total + line_all[i]
    sum_o[...] = total
    for job, o in zip(jobs, (gq_o, gk_o, gv_o)):
        job.result(o)
    hid.finish()
    for job in jobs:
        job.finish()
    for job in line_jobs + small:
        job.wait_send()
    for job in cols + mine:
        job.wait()


def leave(n_line, gq, gk, gv, gh, res, oc, dc, alpha, rest):
    n_blk = 2 * n_line
    vmem = pl.BlockSpec(memory_space=pltpu.VMEM)
    dma = pltpu.SemaphoreType.DMA
    scratch = [
        pltpu.VMEM((3,) + alpha.shape[1:], F32),
        pltpu.VMEM(rest.shape, F32),
        pltpu.VMEM((n_blk - 1,) + rest.shape[1:], F32),
        dma((3,)), dma((3,)), dma((7,)), dma((7,)), dma((3,)), dma((3,)),
        dma((n_blk - 1,)), dma((n_blk - 1,)), dma((2,)),
    ]
    for g in (gq, gk, gv):
        scratch += BlkReduce.scratch(n_line, g)
    scratch += UlyReduce.scratch(gh)
    grad = jax.ShapeDtypeStruct(gq.shape[1:], F32)
    return pl.pallas_call(
        functools.partial(exit_kernel, n_line),
        out_shape=[
            grad, grad, grad,
            jax.ShapeDtypeStruct(res.shape, F32),
            jax.ShapeDtypeStruct(oc.shape, oc.dtype),
            jax.ShapeDtypeStruct(dc.shape, dc.dtype),
            jax.ShapeDtypeStruct(rest.shape[1:], F32),
        ],
        in_specs=[vmem] * 9,
        out_specs=[vmem] * 7,
        scratch_shapes=scratch,
        compiler_params=params(8),
        cost_estimate=pl.CostEstimate(flops=0, bytes_accessed=40 * 3_000_000, transcendentals=0),
        name="leave",
    )(gq, gk, gv, gh, res, oc, dc, alpha, rest)


def entry_kernel(
    n_line, hid, small, wq, wk, wv, oc, dc, hid_o, small_o, wq_o, wk_o, wv_o, oc_o, dc_o, *sems
):
    y, c, z, s = place()
    u, p = y * 2 + c, plane_index(y, c, s)
    low, high, cross = line_ends(n_line)
    corners = plane_corners()
    greet([(yy, cc, z, ss) for yy, cc, ss in corners], [low, high])
    hid_job = UlyGather(hid, hid_o, *sems[:3])
    at, jobs = 3, []
    for x, pick in (
        (small, lambda block: small_o.at[u, block]),
        (wq, lambda block: wq_o.at[block]),
        (wk, lambda block: wk_o.at[block]),
        (wv, lambda block: wv_o.at[block]),
    ):
        jobs.append(BlkGather(n_line, lambda x=x: x, pick, *sems[at : at + 5]))
        at += 5
    oc_s, oc_r, dc_s, dc_r, sm_s, sm_r, keep = sems[at:]
    jobs[0].start()
    for job in jobs[1:]:
        job.start()
    hid_job.start()
    col_jobs = []
    for k, (yy, cc, ss) in enumerate(corners):
        target = (yy, cc, z, ss)
        col_jobs.append(
            remote(dc.at[plane_index(yy, cc, ss)], dc_o.at[p], dc_s.at[k], dc_r.at[k], target)
        )
        if k < 3:
            col_jobs.append(remote(oc.at[yy * 2 + cc], oc_o.at[u], oc_s.at[k], oc_r.at[k], target))
    for job in col_jobs:
        job.start()
    mine = [
        pltpu.make_async_copy(dc.at[p], dc_o.at[p], keep.at[0]),
        pltpu.make_async_copy(oc.at[u], oc_o.at[u], keep.at[1]),
    ]
    for job in mine:
        job.start()
    for k in range(1, n_line):
        for job in jobs:
            job.step(k)
        if k == 1:
            hid_job.forward()
    jobs[0].finish_arrivals()
    small_jobs = [
        remote(small_o.at[u], small_o.at[u], sm_s.at[k], sm_r.at[k], (yy, cc, z, ss))
        for k, (yy, cc, ss) in enumerate(corners[:3])
    ]
    for job in small_jobs:
        job.start()
    for job in jobs[1:]:
        job.finish_arrivals()
    hid_job.finish()
    for job in small_jobs + col_jobs:
        job.wait()
    for job in mine:
        job.wait()
    for job in jobs:
        job.finish_sends()


def entry(n_line, hid, small, wq, wk, wv, oc, dc):
    n_blk = 2 * n_line
    parts = hid.shape[0]
    vmem, anyway = pl.BlockSpec(memory_space=pltpu.VMEM), pl.BlockSpec(memory_space=pl.ANY)

    def out(shape, like):
        return jax.ShapeDtypeStruct(shape, like.dtype)

    return pl.pallas_call(
        functools.partial(entry_kernel, n_line),
        out_shape=[
            out((parts, 4) + hid.shape[1:], hid),
            out((4, n_blk) + small.shape, small),
            out((n_blk,) + wq.shape, wq),
            out((n_blk,) + wk.shape, wk),
            out((n_blk,) + wv.shape, wv),
            out(oc.shape, oc),
            out(dc.shape, dc),
        ],
        in_specs=[vmem] * 7,
        out_specs=[vmem, vmem, anyway, anyway, anyway, vmem, vmem],
        scratch_shapes=UlyGather.sems(parts)
        + BlkGather.sems(n_line) * 4
        + [pltpu.SemaphoreType.DMA((3,))] * 2
        + [pltpu.SemaphoreType.DMA((7,))] * 2
        + [pltpu.SemaphoreType.DMA((3,))] * 2
        + [pltpu.SemaphoreType.DMA((2,))],
        compiler_params=params(6),
        cost_estimate=pl.CostEstimate(flops=0, bytes_accessed=40 * 3_000_000, transcendentals=0),
        name="entry",
    )(hid, small, wq, wk, wv, oc, dc)
def dot_nt(a, b):
    return lax.dot_general(a, b, (((1,), (1,)), ((), ())), preferred_element_type=F32)


def dot_nn(a, b):
    return lax.dot_general(a, b, (((1,), (0,)), ((), ())), preferred_element_type=F32)


def dot_tn(a, b):
    return lax.dot_general(a, b, (((0,), (0,)), ((), ())), preferred_element_type=F32)


def lanes_of(shape):
    return lax.broadcasted_iota(jnp.int32, shape, len(shape) - 1)


def halves(x):
    row = lax.broadcasted_iota(jnp.int32, (128, 128), 0) // HEAD_DIM
    same = jnp.where(row == lanes_of((128, 128)) // HEAD_DIM, 1.0, 0.0).astype(BF)
    high = x.astype(BF)
    rest = (x - high.astype(F32)).astype(BF)
    return dot_nn(high, same) + dot_nn(rest, same)


def turn(x):
    first = lanes_of(x.shape) % HEAD_DIM < HEAD_DIM // 2
    return jnp.where(first, pltpu.roll(x, 128 - 32, 1), pltpu.roll(x, 32, 1))


def heads_kernel(x_ref, wq_ref, wk_ref, wv_ref, cos_ref, sin_ref, scale_ref, qz_ref, kv_ref, y_ref, c_ref):
    x = x_ref[...]
    wqk = jnp.concatenate([wq_ref[0], wk_ref[0]], axis=0)
    wv = wv_ref[0]
    raw = dot_nt(x, wqk)
    value = dot_nt(x, jnp.concatenate([jnp.zeros_like(wv), wv], axis=0))
    low = lanes_of(raw.shape) < HEAD_DIM
    turned = raw * cos_ref[...] + turn(raw) * sin_ref[...]
    c = lax.rsqrt(halves(turned * turned) + HEAD_DIM * tiny_eps)
    y = turned * c
    both = y * scale_ref[0]
    qz_ref[...] = jnp.where(low, both, 0.0).astype(BF)
    kv_ref[...] = jnp.where(low, pltpu.roll(both, HEAD_DIM, 1), value).astype(BF)
    y_ref[...] = y
    c_ref[...] = c


def heads_forward(x, wq, wk, wv, cos, sin, scale):
    rows, width = x.shape
    heads = wq.shape[0]
    whole = lambda shape: pl.BlockSpec(shape, lambda h: (0,) * len(shape))
    weight = pl.BlockSpec((1, HEAD_DIM, width), lambda h: (h, 0, 0))
    head = pl.BlockSpec((rows, 128), lambda h: (0, h))
    wide = lambda dtype: jax.ShapeDtypeStruct((rows, heads * 128), dtype)
    return pl.pallas_call(
        heads_kernel,
        grid=(heads,),
        out_shape=[wide(BF), wide(BF), wide(F32), wide(F32)],
        in_specs=[whole((rows, width)), weight, weight, weight, whole((rows, 128)), whole((rows, 128)),
                  pl.BlockSpec((1, 1, 128), lambda h: (h, 0, 0))],
        out_specs=[head] * 4,
        compiler_params=pltpu.CompilerParams(vmem_limit_bytes=VMEM_BYTES),
        cost_estimate=pl.CostEstimate(flops=rows * width * heads * 384, bytes_accessed=rows * width * 8, transcendentals=0),
        name="heads_forward",
    )(x, wq, wk, wv, cos, sin, scale)


def attend_kernel(blocks, q_ref, kv_ref, qp_ref, kp_ref, o_ref, low_ref, inv_ref):
    q = q_ref[0]
    rows = q.shape[0]
    acc = jnp.zeros((rows, 128), F32)
    total = jnp.zeros((rows, 128), F32)
    q_place = qp_ref[0]

    def step(b, state):
        acc, total = state
        kv = kv_ref[b, 0]
        allowed = kp_ref[0, b] <= q_place
        p = jnp.where(allowed, jnp.exp(dot_nt(q, kv)), 0.0)
        for i in range(p.shape[1] // 128):
            total = total + p[:, i * 128 : (i + 1) * 128]
        return acc + dot_nn(p.astype(BF), kv), total

    if blocks <= 8:
        for b in range(blocks):
            acc, total = step(b, (acc, total))
    else:
        acc, total = lax.fori_loop(0, blocks, step, (acc, total))
    inverse = 1.0 / jnp.broadcast_to(jnp.sum(total, axis=-1, keepdims=True), (rows, 128))
    out = acc * inverse
    o_ref[0] = out
    low_ref[0] = out.astype(BF)
    inv_ref[0, 0] = jnp.transpose(inverse)[:8]


def attend(q, kv, q_places, k_places):
    seqs, rows, wide = q.shape
    blocks, heads = kv.shape[0], wide // 128
    mine = pl.BlockSpec((1, rows, 128), lambda s, h: (s, 0, h))
    return pl.pallas_call(
        functools.partial(attend_kernel, blocks),
        grid=(seqs, heads),
        out_shape=[
            jax.ShapeDtypeStruct(q.shape, F32),
            jax.ShapeDtypeStruct(q.shape, BF),
            jax.ShapeDtypeStruct((seqs, heads, 8, rows), F32),
        ],
        in_specs=[
            mine,
            pl.BlockSpec((blocks, 1, rows, 128), lambda s, h: (0, s, 0, h)),
            pl.BlockSpec((1, rows, 1), lambda s, h: (s, 0, 0)),
            pl.BlockSpec((1, blocks, 1, rows), lambda s, h: (s, 0, 0, 0)),
        ],
        out_specs=[mine, mine, pl.BlockSpec((1, 1, 8, rows), lambda s, h: (s, h, 0, 0))],
        compiler_params=pltpu.CompilerParams(vmem_limit_bytes=VMEM_BYTES),
        cost_estimate=pl.CostEstimate(
            flops=4 * blocks * seqs * rows * rows * wide, bytes_accessed=2 * blocks * seqs * rows * wide,
            transcendentals=blocks * seqs * rows * rows * heads,
        ),
        name="attend",
    )(q, kv, q_places, k_places)


def attend_back_kernel(blocks, q_ref, d_ref, o_ref, inv_ref, kv_ref, qp_ref, kp_ref, dq_ref, dkv_ref):
    q, d = q_ref[0], d_ref[0]
    rows = q.shape[0]
    delta = jnp.sum(d.astype(F32) * o_ref[0], axis=-1, keepdims=True)
    delta = jnp.transpose(jnp.broadcast_to(delta, (rows, 128)))[:1]
    inverse = inv_ref[0, 0][:1]
    pair = jnp.concatenate([q, d], axis=0)
    q_place = qp_ref[0]

    def step(b, dq):
        kv = kv_ref[b, 0]
        scores = dot_nt(kv, pair)
        allowed = kp_ref[0, b] <= q_place
        p = jnp.where(allowed, jnp.exp(scores[:, :rows]) * inverse, 0.0)
        ds = (p * (scores[:, rows:] - delta)).astype(BF)
        dkv_ref[b, 0] = dot_nn(jnp.concatenate([ds, p.astype(BF)], axis=1), pair).astype(BF)
        return dq + dot_tn(ds, kv)

    dq = jnp.zeros((rows, 128), F32)
    if blocks <= 8:
        for b in range(blocks):
            dq = step(b, dq)
    else:
        dq = lax.fori_loop(0, blocks, step, dq)
    dq_ref[0] = dq.astype(BF)


def attend_back(q, d, o, inv, kv, q_places, k_places):
    seqs, rows, wide = q.shape
    blocks, heads = kv.shape[0], wide // 128
    mine = pl.BlockSpec((1, rows, 128), lambda s, h: (s, 0, h))
    keys = pl.BlockSpec((blocks, 1, rows, 128), lambda s, h: (0, s, 0, h))
    return pl.pallas_call(
        functools.partial(attend_back_kernel, blocks),
        grid=(seqs, heads),
        out_shape=[jax.ShapeDtypeStruct(q.shape, BF), jax.ShapeDtypeStruct(kv.shape, BF)],
        in_specs=[
            mine, mine, mine,
            pl.BlockSpec((1, 1, 8, rows), lambda s, h: (s, h, 0, 0)),
            keys,
            pl.BlockSpec((1, 1, rows), lambda s, h: (s, 0, 0)),
            pl.BlockSpec((1, blocks, rows, 1), lambda s, h: (s, 0, 0, 0)),
        ],
        out_specs=[mine, keys],
        compiler_params=pltpu.CompilerParams(vmem_limit_bytes=VMEM_BYTES),
        cost_estimate=pl.CostEstimate(
            flops=10 * blocks * seqs * rows * rows * wide, bytes_accessed=4 * blocks * seqs * rows * wide,
            transcendentals=blocks * seqs * rows * rows * heads,
        ),
        name="attend_back",
    )(q, d, o, inv, kv, q_places, k_places)


def heads_back_kernel(
    x_ref, dq_ref, dkv_ref, y_ref, c_ref, cos_ref, sin_ref, scale_ref, wq_ref, wk_ref, wv_ref,
    gq_ref, gk_ref, gv_ref, gs_ref, gh_ref, acc_ref,
):
    h = pl.program_id(0)
    dq, dkv = dq_ref[...], dkv_ref[...]
    low = lanes_of(dq.shape) < HEAD_DIM
    dy = jnp.where(low, dq.astype(F32), pltpu.roll(dkv.astype(F32), HEAD_DIM, 1))
    y = y_ref[...]
    factor = jnp.where(lanes_of((1, 128)) < HEAD_DIM, HEAD_DIM**0.5, 1.0)
    gs_ref[0] = jnp.sum(dy * y, axis=0, keepdims=True) * factor
    dy = dy * scale_ref[0]
    dr = c_ref[...] * (dy - y * halves(y * dy))
    raw = (dr * cos_ref[...] - turn(dr) * sin_ref[...]).astype(BF)
    x = x_ref[...]
    grad = dot_tn(raw, x)
    gq_ref[0] = grad[:HEAD_DIM].astype(BF)
    gk_ref[0] = grad[HEAD_DIM:].astype(BF)
    value = jnp.where(low, jnp.zeros_like(dkv), dkv)
    gv_ref[0] = dot_tn(value, x)[HEAD_DIM:].astype(BF)
    wqk = jnp.concatenate([wq_ref[0], wk_ref[0]], axis=0)
    wv = wv_ref[0]
    more = dot_nn(raw, wqk) + dot_nn(value, jnp.concatenate([jnp.zeros_like(wv), wv], axis=0))

    @pl.when(h == 0)
    def _():
        acc_ref[...] = more

    @pl.when(h > 0)
    def _():
        acc_ref[...] = acc_ref[...] + more

    @pl.when(h == pl.num_programs(0) - 1)
    def _():
        gh_ref[...] = acc_ref[...].astype(BF)


def heads_back(x, dq, dkv, y, c, cos, sin, scale, wq, wk, wv):
    rows, width = x.shape
    heads = wq.shape[0]
    whole = lambda shape: pl.BlockSpec(shape, lambda h: (0,) * len(shape))
    weight = pl.BlockSpec((1, HEAD_DIM, width), lambda h: (h, 0, 0))
    head = pl.BlockSpec((rows, 128), lambda h: (0, h))
    row = pl.BlockSpec((1, 1, 128), lambda h: (h, 0, 0))
    return pl.pallas_call(
        heads_back_kernel,
        grid=(heads,),
        out_shape=[jax.ShapeDtypeStruct(wq.shape, BF)] * 3
        + [jax.ShapeDtypeStruct((heads, 1, 128), F32), jax.ShapeDtypeStruct((rows, width), BF)],
        in_specs=[whole((rows, width))] + [head] * 4 + [whole((rows, 128))] * 2 + [row] + [weight] * 3,
        out_specs=[weight] * 3 + [row, whole((rows, width))],
        scratch_shapes=[pltpu.VMEM((rows, width), F32)],
        compiler_params=pltpu.CompilerParams(vmem_limit_bytes=VMEM_BYTES),
        cost_estimate=pl.CostEstimate(flops=rows * width * heads * 1024, bytes_accessed=rows * width * 12, transcendentals=0),
        name="heads_back",
    )(x, dq, dkv, y, c, cos, sin, scale, wq, wk, wv)


def ff_kernel(x_ref, wu_ref, wg_ref, us_ref, gs_ref, inner_ref, up_ref, gate_ref):
    x = x_ref[...]
    up = dot_nt(x, wu_ref[...])
    gate = dot_nt(x, wg_ref[...])
    z = gate * gs_ref[...] * D**0.5
    inner_ref[...] = (z / (1.0 + jnp.exp(-z)) * (up * us_ref[...])).astype(BF)
    up_ref[...] = up
    gate_ref[...] = gate


def ff_forward(x, wu, wg, us, gs):
    rows, width = x.shape
    columns = wu.shape[0]
    block = rows // 4
    whole = lambda a: pl.BlockSpec(a.shape, lambda i: (0, 0))
    part = lambda n: pl.BlockSpec((block, n), lambda i: (i, 0))
    out = lambda dtype: jax.ShapeDtypeStruct((rows, columns), dtype)
    return pl.pallas_call(
        ff_kernel,
        grid=(4,),
        out_shape=[out(BF), out(F32), out(F32)],
        in_specs=[part(width)] + [whole(a) for a in (wu, wg, us, gs)],
        out_specs=[part(columns)] * 3,
        compiler_params=pltpu.CompilerParams(vmem_limit_bytes=VMEM_BYTES),
        cost_estimate=pl.CostEstimate(
            flops=4 * rows * width * columns, bytes_accessed=2 * rows * width + 10 * rows * columns,
            transcendentals=rows * columns,
        ),
        name="ff_forward",
    )(x, wu, wg, us, gs)


def ff_back_kernel(d_ref, wd_ref, up_ref, gate_ref, us_ref, gs_ref, du_ref, dg_ref, sum_ref):
    d = dot_nn(d_ref[...], wd_ref[...])
    up, gate = up_ref[...], gate_ref[...]
    us, gs = us_ref[...], gs_ref[...] * D**0.5
    z = gate * gs
    sig = 1.0 / (1.0 + jnp.exp(-z))
    du = d * (z * sig)
    dz = d * (up * us) * sig * (1.0 + z * (1.0 - sig))
    du_ref[...] = (du * us).astype(BF)
    dg_ref[...] = (dz * gs).astype(BF)
    sums = jnp.concatenate(
        [
            jnp.sum(du * up, axis=0, keepdims=True),
            jnp.sum(dz * gate, axis=0, keepdims=True) * D**0.5,
        ],
        axis=0,
    )
    i = pl.program_id(0)

    @pl.when(i == 0)
    def _():
        sum_ref[...] = sums

    @pl.when(i > 0)
    def _():
        sum_ref[...] = sum_ref[...] + sums


def ff_back(d, wd, up, gate, us, gs):
    rows, width = d.shape
    columns = wd.shape[1]
    block = rows // 4
    whole = lambda a: pl.BlockSpec(a.shape, lambda i: (0, 0))
    part = lambda n: pl.BlockSpec((block, n), lambda i: (i, 0))
    out = jax.ShapeDtypeStruct((rows, columns), BF)
    return pl.pallas_call(
        ff_back_kernel,
        grid=(4,),
        out_shape=[out, out, jax.ShapeDtypeStruct((2, columns), F32)],
        in_specs=[part(width), whole(wd), part(columns), part(columns), whole(us), whole(gs)],
        out_specs=[part(columns), part(columns), pl.BlockSpec((2, columns), lambda i: (0, 0))],
        compiler_params=pltpu.CompilerParams(vmem_limit_bytes=VMEM_BYTES),
        cost_estimate=pl.CostEstimate(
            flops=2 * rows * width * columns, bytes_accessed=2 * rows * width + 14 * rows * columns,
            transcendentals=rows * columns,
        ),
        name="ff_back",
    )(d, wd, up, gate, us, gs)


def unit_of(x):
    c = lax.rsqrt(jnp.sum(x * x, axis=-1, keepdims=True) + x.shape[-1] * tiny_eps)
    return x * c, c


def unit_back(y, c, dy):
    return c * (dy - y * jnp.sum(y * dy, axis=-1, keepdims=True))


def comm_call(kernel, name, collective_id, args, outs, scratch, micros):
    vmem = pl.BlockSpec(memory_space=pltpu.VMEM)
    return pl.pallas_call(
        kernel,
        out_shape=[jax.ShapeDtypeStruct(shape, dtype) for shape, dtype in outs],
        in_specs=[vmem] * len(args),
        out_specs=[vmem] * len(outs),
        scratch_shapes=scratch,
        compiler_params=params(collective_id),
        cost_estimate=pl.CostEstimate(flops=0, bytes_accessed=micros * 3_000_000, transcendentals=0),
        name=name,
    )(*args)


def attn_joint_kernel(mixed, w, hid, rate, first_o, ua_o, ca_o, cv_o, all_o, part, low, *scratch):
    mate, across, cross = plane_peers()
    greet([mate, across, cross])
    split = len(UlyReduce.scratch(part))
    job = UlyReduce(part, *scratch[:split])
    out = PlaneGather(low, all_o, *scratch[split:])
    seqs, _, rows, width = part.shape
    for i in range(seqs):
        part[i] = dot_nt(mixed[i], w[...]).astype(BF).reshape(4, rows, width)
        for copy in job.near[i]:
            copy.start()
    job.middle()
    for i in range(seqs):
        ua, ca = unit_of(job.result(i))
        h = hid[i].astype(F32)
        first, cv = unit_of(h + rate[...] * (ua - h))
        low[i] = first.astype(BF)
        out.start_part(i)
        first_o[i], ua_o[i] = first, ua
        ca_o[i] = jnp.broadcast_to(ca, (rows, 128))
        cv_o[i] = jnp.broadcast_to(cv, (rows, 128))
        if i > 0:
            out.forward_part(i - 1)
    out.forward_part(seqs - 1)
    out.finish()
    job.finish()


def attn_joint(mixed, w, hid, rate):
    seqs, rows, width = hid.shape
    part = jax.ShapeDtypeStruct((seqs, 4, rows, width), BF)
    thin = ((seqs, rows, 128), F32)
    return comm_call(
        attn_joint_kernel, "attn_joint", 1, (mixed, w, hid, rate),
        [(hid.shape, F32), (hid.shape, F32), thin, thin, ((8, seqs, rows, width), BF)],
        [pltpu.VMEM(part.shape, BF), pltpu.VMEM(hid.shape, BF)] + UlyReduce.scratch(part) + PlaneGather.sems,
        25,
    )


def plane_products(job, part, c, product):
    _, seqs, rows, width = part.shape
    for cc, first in ((1 - c, True), (c, False)):
        got = product(cc).astype(BF).reshape(2, 2, seqs, rows, width)
        for yy in (0, 1):
            for ss in (0, 1):
                part[plane_index(yy, cc, ss)] = got[yy, ss]
        if first:
            job.start()


def ff_joint_kernel(inner, w, first, rate, cot, out_o, d1_o, sum_o, all_o, part, low, *scratch):
    y, c, z, s = place()
    greet(plane_peers())
    split = len(PlaneReduce.scratch(part))
    job = PlaneReduce(part, *scratch[:split])
    out = PlaneGather(low, all_o, *scratch[split:])
    _, seqs, rows, width = part.shape
    columns = inner.shape[-1]
    plane_products(
        job, part, c, lambda cc: dot_nt(inner[:, cc].reshape(4 * seqs * rows, columns), w[...])
    )
    job.middle()
    job.last()
    for i in range(seqs):
        ub, cb = unit_of(job.result(i))
        f, b = first[i], rate[...]
        o, cw = unit_of(f + b * (ub - f))
        dw = unit_back(o, cw, cot[i].astype(F32))
        step = b * dw
        low[i] = unit_back(ub, cb, step).astype(BF)
        out.start_part(i)
        out_o[i] = o.astype(BF)
        d1_o[i] = dw - step
        total = jnp.sum(dw * (ub - f), axis=0, keepdims=True)
        sum_o[...] = total if i == 0 else sum_o[...] + total
        if i > 0:
            out.forward_part(i - 1)
    out.forward_part(seqs - 1)
    out.finish()
    job.finish()


def ff_joint(inner, w, first, rate, cot):
    seqs, rows, width = first.shape
    part = jax.ShapeDtypeStruct((8, seqs, rows, width), BF)
    return comm_call(
        ff_joint_kernel, "ff_joint", 2,
        (inner.reshape(2, 2, 2, seqs * rows, inner.shape[-1]), w, first, rate, cot),
        [(first.shape, BF), (first.shape, F32), ((1, width), F32), (part.shape, BF)],
        [pltpu.VMEM(part.shape, BF), pltpu.VMEM(first.shape, BF)] + PlaneReduce.scratch(part) + PlaneGather.sems,
        30,
    )


def back_joint_kernel(
    du, dg, wu, wg, d1, first, ua, ca, cv, hid, rate, res_o, sum_o, all_o, part, low, *scratch
):
    y, c, z, s = place()
    greet(plane_peers())
    split = len(PlaneReduce.scratch(part))
    job = PlaneReduce(part, *scratch[:split])
    out = UlyGather(low, all_o, *scratch[split:])
    _, seqs, rows, width = part.shape
    columns = du.shape[-1]
    tokens = 8 * seqs * rows
    half = lambda ref, cc: ref[:, cc].reshape(tokens // 2, columns)
    plane_products(
        job, part, c, lambda cc: dot_nn(half(du, cc), wu[...]) + dot_nn(half(dg, cc), wg[...])
    )
    job.middle()
    job.last()
    for i in range(seqs):
        f, h, u, a = first[i], hid[i].astype(F32), ua[i], rate[...]
        dv = unit_back(f, cv[i][:, :1], d1[i] + job.result(i))
        step = a * dv
        low[i] = unit_back(u, ca[i][:, :1], step).astype(BF)
        out.start_part(i)
        res_o[i] = dv - step
        total = jnp.sum(dv * (u - h), axis=0, keepdims=True)
        sum_o[...] = total if i == 0 else sum_o[...] + total
    out.forward()
    out.finish()
    job.finish()


def back_joint(du, dg, wu, wg, d1, first, ua, ca, cv, hid, rate):
    seqs, rows, width = first.shape
    part = jax.ShapeDtypeStruct((8, seqs, rows, width), BF)
    wide = lambda a: a.reshape(2, 2, 2, seqs * rows, a.shape[-1])
    return comm_call(
        back_joint_kernel, "back_joint", 3,
        (wide(du), wide(dg), wu, wg, d1, first, ua, ca, cv, hid, rate),
        [(first.shape, F32), ((1, width), F32), ((seqs, 4, rows, width), BF)],
        [pltpu.VMEM(part.shape, BF), pltpu.VMEM(first.shape, BF)]
        + PlaneReduce.scratch(part) + UlyGather.sems(seqs),
        30,
    )


def down_grad_kernel(d_ref, inner_ref, o_ref):
    grad = dot_tn(d_ref[...], inner_ref[...]).astype(BF)
    n_line, groups, each, _ = o_ref.shape
    for v in range(groups):
        for k in range(n_line):
            at = (v * n_line + k) * each
            o_ref[k, v] = grad[at : at + each]


def down_grad(n_line, d, inner):
    rows, width = d.shape
    columns = inner.shape[1]
    each = width // (4 * n_line)
    return pl.pallas_call(
        down_grad_kernel,
        grid=(2,),
        out_shape=jax.ShapeDtypeStruct((n_line, 4, each, columns), BF),
        in_specs=[
            pl.BlockSpec((rows, width // 2), lambda i: (0, i)),
            pl.BlockSpec((rows, columns), lambda i: (0, 0)),
        ],
        out_specs=pl.BlockSpec((n_line, 2, each, columns), lambda i: (0, i, 0, 0)),
        compiler_params=pltpu.CompilerParams(vmem_limit_bytes=VMEM_BYTES),
        cost_estimate=pl.CostEstimate(flops=2 * rows * width * columns, bytes_accessed=8_000_000, transcendentals=0),
        name="down_grad",
    )(d, inner)


def ff_grad_kernel(du_ref, dg_ref, x_ref, o_ref):
    n_line, both, _ = o_ref.shape
    each = both // 2
    for j, ref in enumerate((du_ref, dg_ref)):
        grad = dot_tn(ref[...], x_ref[...]).astype(BF)
        for k in range(n_line):
            o_ref[k, j * each : (j + 1) * each] = grad[k * each : (k + 1) * each]


def ff_grad(n_line, du, dg, x):
    rows, width = x.shape
    columns = du.shape[1]
    whole = pl.BlockSpec((rows, columns), lambda i: (0, 0))
    shape = (n_line, 2 * columns // n_line, width)
    return pl.pallas_call(
        ff_grad_kernel,
        grid=(2,),
        out_shape=jax.ShapeDtypeStruct(shape, BF),
        in_specs=[whole, whole, pl.BlockSpec((rows, width // 2), lambda i: (0, i))],
        out_specs=pl.BlockSpec(shape[:2] + (width // 2,), lambda i: (0, 0, i)),
        compiler_params=pltpu.CompilerParams(vmem_limit_bytes=VMEM_BYTES),
        cost_estimate=pl.CostEstimate(flops=4 * rows * width * columns, bytes_accessed=10_000_000, transcendentals=0),
        name="ff_grad",
    )(du, dg, x)
def local(
    hidden, positions, w_query, w_key, w_value, w_out, w_up, w_gate, w_down,
    qk_scale, alpha_attn, alpha_mlp, up_scale, gate_scale, cotangent,
):
    seqs, rows_each, width = hidden.shape
    n_line = lax.axis_size("line")
    n_blk = 2 * n_line
    heads = HEADS // 4
    local_width = heads * HEAD_DIM
    group_rows = 4 * rows_each
    tokens = seqs * rows_each
    group_tokens = 4 * tokens
    plane_tokens = 8 * tokens
    attn_each, ff_each = w_query.shape[0], w_up.shape[0]
    ff_local = ff_each * n_line
    far, core, line, side = place()
    uly = far * 2 + core

    pieces = [v.astype(F32) for v in (qk_scale, alpha_attn, alpha_mlp, up_scale, gate_scale)]
    pieces.append(positions.reshape(-1).astype(F32))
    used = sum(v.shape[0] for v in pieces)
    room, at, small = used + -used % 1024, 0, 0.0
    for v in pieces:
        small = small + jnp.pad(v, (at, room - at - v.shape[0]))
        at += v.shape[0]
    small = small.reshape(-1, 128)

    out_send = jnp.transpose(w_out.reshape(attn_each, 4, local_width), (1, 0, 2))
    down_send = jnp.transpose(
        w_down.reshape(attn_each, 4, n_line, 2, ff_each), (1, 3, 0, 2, 4)
    ).reshape(8, attn_each, ff_local)

    up_full = lax.all_gather(w_up, "line", axis=0, tiled=True)

    hid_all, small_all, wq_all, wk_all, wv_all, out_cols, down_cols = entry(
        n_line, hidden, small, w_query, w_key, w_value, out_send, down_send
    )
    w_gate, up_full, hid_all = lax.optimization_barrier((w_gate, up_full, hid_all))
    gate_full = lax.all_gather(w_gate, "line", axis=0, tiled=True)

    flat = small_all.reshape(4, n_blk, -1)
    cut = [0, attn_each, 2 * attn_each, 3 * attn_each, 3 * attn_each + ff_each, 3 * attn_each + 2 * ff_each, used]
    own = lax.dynamic_slice_in_dim(flat, uly, 1, 0)[0]
    scale_wide = own[:, : cut[1]].reshape(heads, HEAD_DIM)
    attn_rate = flat[:, :, cut[1] : cut[2]].reshape(-1)
    mlp_rate = flat[:, :, cut[2] : cut[3]].reshape(-1)
    mine = lax.dynamic_slice_in_dim(own.reshape(n_line, 2, -1), side, 1, 1)[:, 0]
    up_wide = mine[:, cut[3] : cut[4]].reshape(-1)
    gate_wide = mine[:, cut[4] : cut[5]].reshape(-1)
    places = jnp.transpose(
        flat[:, :, cut[5] : cut[6]].astype(jnp.int32).reshape(4, n_blk, seqs, rows_each), (2, 1, 0, 3)
    ).reshape(seqs, n_blk, group_rows)
    q_places = lax.dynamic_slice_in_dim(places, line * 2 + side, 1, 1)[:, 0]

    lane = jnp.arange(128) % HEAD_DIM
    freqs = rotary_base ** (-((lane % 32).astype(F32) * (2.0 / HEAD_DIM)))
    angles = q_places.reshape(group_tokens, 1).astype(F32) * freqs
    cos = jnp.cos(angles)
    sin = jnp.where(lane < 32, -1.0, 1.0) * jnp.sin(angles)
    scale_both = jnp.concatenate([scale_wide * HEAD_DIM**0.5, scale_wide], axis=1)[:, None]

    group_hidden = hid_all.reshape(group_tokens, width)
    wq = wq_all.reshape(heads, HEAD_DIM, width)
    wk = wk_all.reshape(heads, HEAD_DIM, width)
    wv = wv_all.reshape(heads, HEAD_DIM, width)
    qz, kv, y_both, c_both = heads_forward(group_hidden, wq, wk, wv, cos, sin, scale_both)
    qz = qz.reshape(seqs, group_rows, heads * 128)

    kv_all, out_all = blk_gather(
        n_line, kv.reshape(seqs, group_rows, heads * 128), out_cols.reshape(1, 4 * attn_each, local_width)
    )
    kv_all, out_all, gate_full, down_cols = lax.optimization_barrier(
        (kv_all, out_all, gate_full, down_cols)
    )
    down_all = lax.all_gather(down_cols.reshape(8 * attn_each, ff_local), "line", axis=0, tiled=False)
    down_full = jnp.transpose(
        down_all.reshape(n_line, 4, 2, attn_each, ff_local), (1, 0, 2, 3, 4)
    ).reshape(width, ff_local)

    out_full = jnp.transpose(
        out_all.reshape(n_blk, 4, attn_each, local_width), (1, 0, 2, 3)
    ).reshape(width, local_width)

    attended, mixed, inverse = attend(qz, kv_all, q_places[:, :, None], places[:, :, None, :])
    mixed = mixed.reshape(group_tokens, heads, 128)[:, :, HEAD_DIM:].reshape(
        seqs, group_rows, local_width
    )

    first, unit_att, att_c, first_c, mlp_in = attn_joint(mixed, out_full, hidden, attn_rate[None])
    mlp_in = mlp_in.reshape(plane_tokens, width)
    inner, up_rows, gate_rows = ff_forward(mlp_in, up_full, gate_full, up_wide[None], gate_wide[None])
    layer_out, grad_first, grad_alpha_mlp, branch_low = ff_joint(
        inner, down_full, first, mlp_rate[None], cotangent
    )
    branch_low = branch_low.reshape(plane_tokens, width)
    grad_down = down_grad(n_line, branch_low, inner)
    down_own = lax.psum_scatter(
        grad_down.reshape(n_line, 8 * attn_each, ff_local), "line", scatter_dimension=0, tiled=True
    ).reshape(8, attn_each, ff_local)
    up_low, gate_low, ff_scales = ff_back(
        branch_low, down_full, up_rows, gate_rows, up_wide[None], gate_wide[None]
    )
    grad_up_scale, grad_gate_scale = ff_scales[0], ff_scales[1]
    grad_ug = ff_grad(n_line, up_low, gate_low, mlp_in)
    mlp_own = lax.psum_scatter(grad_ug, "line", scatter_dimension=0, tiled=True)[0]
    up_low, grad_ug = lax.optimization_barrier((up_low, grad_ug))
    grad_residual, grad_alpha_attn, att_low = back_joint(
        up_low, gate_low, up_full, gate_full, grad_first, first, unit_att, att_c, first_c,
        hidden, attn_rate[None],
    )

    att_low = att_low.reshape(group_tokens, width)
    grad_mixed = jnp.pad(
        dot_nn(att_low, out_full).astype(BF).reshape(seqs, group_rows, heads, HEAD_DIM),
        ((0, 0), (0, 0), (0, 0), (HEAD_DIM, 0)),
    ).reshape(seqs, group_rows, heads * 128)
    grad_out = (
        dot_tn(att_low, mixed.reshape(group_tokens, local_width))
        .astype(BF)
        .reshape(4, n_blk, attn_each, local_width)
    )
    grad_out = jnp.transpose(grad_out, (1, 0, 2, 3)).reshape(n_blk, 1, 4 * attn_each, local_width)
    dq, dkv_all = attend_back(
        qz, grad_mixed, attended, inverse, kv_all, q_places[:, None, :], places[..., None]
    )
    dkv, out_own = blk_reduce(n_line, dkv_all, grad_out)
    out_own = out_own.reshape(4, attn_each, local_width)
    gq, gk, gv, gs, gh = heads_back(
        group_hidden, dq.reshape(group_tokens, -1), dkv.reshape(group_tokens, -1), y_both, c_both,
        cos, sin, scale_both, wq, wk, wv,
    )
    def row(x, wide):
        return jnp.pad(x, ((0, 0),) * (x.ndim - 1) + ((0, wide - x.shape[-1]),))

    alpha = jnp.concatenate(
        [grad_alpha_attn.reshape(4, n_blk, attn_each), grad_alpha_mlp.reshape(4, n_blk, attn_each)], axis=2
    )
    grad_scale = gs[:, 0, :HEAD_DIM] + gs[:, 0, HEAD_DIM:]
    ff_sums = jnp.concatenate(
        [grad_up_scale.reshape(n_line, ff_each), grad_gate_scale.reshape(n_line, ff_each)], axis=1
    )
    sides = (jnp.arange(2) == side)[None, :, None]
    ff_sums = jnp.where(sides, ff_sums[:, None], 0.0).reshape(n_blk, 2 * ff_each)
    rest = jnp.concatenate(
        [jnp.zeros((n_blk, 128), F32), row(grad_scale.reshape(n_blk, attn_each), 128), row(ff_sums, 384)], axis=1
    )
    mlp_own = mlp_own.astype(F32)
    gq, gk, gv, grad_hidden, out_own, down_own, sums = leave(
        n_line,
        *(g.reshape(n_blk, attn_each, width) for g in (gq, gk, gv)),
        gh.reshape(seqs, 4, rows_each, width),
        grad_residual,
        out_own, down_own, row(alpha, 128)[:, :, None], rest[:, None],
    )
    out_gradient = jnp.transpose(out_own, (1, 0, 2)).reshape(attn_each, width).astype(F32)
    down_gradient = jnp.transpose(
        down_own.reshape(4, 2, attn_each, n_line, ff_each), (2, 0, 3, 1, 4)
    ).reshape(attn_each, -1).astype(F32)
    sums = sums[0]
    return (
        layer_out,
        grad_hidden,
        gq,
        gk,
        gv,
        out_gradient,
        mlp_own[:ff_each],
        mlp_own[ff_each:],
        down_gradient,
        sums[128 : 128 + attn_each],
        sums[:attn_each],
        sums[attn_each : 2 * attn_each],
        sums[256 : 256 + ff_each],
        sums[256 + ff_each : 256 + 2 * ff_each],
    )


def solution(mesh):
    far = mesh.shape["uly"] // 2
    line = mesh.shape["blk"] // 2
    finer = Mesh(mesh.devices.reshape(far, 2, line, 2), AXES)
    rows, tokens, flat = P(AXES, None), P(None, AXES, None), P(AXES)
    return jax.shard_map(
        local,
        mesh=finer,
        in_specs=(tokens, P(None, AXES)) + (rows,) * 7 + (flat,) * 5 + (tokens,),
        out_specs=(tokens, tokens) + (rows,) * 7 + (flat,) * 5,
        check_vma=False,
    )
```

```python
import functools

import jax
import jax.numpy as jnp
from jax import lax
from jax.experimental import pallas as pl
from jax.experimental.pallas import tpu as pltpu
from jax.sharding import Mesh
from jax.sharding import PartitionSpec as P

D = 1280
HEADS = 20
HEAD_DIM = 64
AXES = ("far", "core", "line", "side")
PLANE = ("far", "core", "side")
VMEM_BYTES = 60 * 1024 * 1024

rotary_base = 10000.0
tiny_eps = 1e-06
BF = jnp.bfloat16
F32 = jnp.float32


def place():
    return tuple(lax.axis_index(name) for name in AXES)


def remote(src, dst, send, recv, device):
    return pltpu.make_async_remote_copy(
        src_ref=src,
        dst_ref=dst,
        send_sem=send,
        recv_sem=recv,
        device_id=device,
        device_id_type=pl.DeviceIdType.MESH,
    )


def signal_to(device):
    pl.semaphore_signal(
        pltpu.get_barrier_semaphore(), inc=1, device_id=device, device_id_type=pl.DeviceIdType.MESH
    )


def greet(devices, maybe=()):
    count = len(devices)
    for device in devices:
        signal_to(device)
    for there, device in maybe:
        pl.when(there)(functools.partial(signal_to, device))
        count = count + jnp.where(there, 1, 0)
    pl.semaphore_wait(pltpu.get_barrier_semaphore(), count)


def params(collective_id, room=VMEM_BYTES):
    return pltpu.CompilerParams(
        collective_id=collective_id, has_side_effects=True, vmem_limit_bytes=room
    )


class UlyGather:
    sems = staticmethod(lambda parts: [pltpu.SemaphoreType.DMA((3, parts))] * 2 + [pltpu.SemaphoreType.DMA((parts,))])

    def __init__(self, x, o, send, recv, local):
        y, c, z, s = place()
        u, v = y * 2 + c, (1 - y) * 2 + c
        mate, across = (y, 1 - c, z, s), (1 - y, c, z, s)
        self.parts = x.shape[0]
        parts = range(self.parts)
        self.far = [remote(x.at[i], o.at[i, u], send.at[0, i], recv.at[0, i], across) for i in parts]
        self.near = [remote(x.at[i], o.at[i, u], send.at[1, i], recv.at[1, i], mate) for i in parts]
        self.on = [remote(o.at[i, v], o.at[i, v], send.at[2, i], recv.at[2, i], mate) for i in parts]
        self.own = [pltpu.make_async_copy(x.at[i], o.at[i, u], local.at[i]) for i in parts]

    def start_part(self, i):
        self.far[i].start()
        self.near[i].start()
        self.own[i].start()

    def start(self):
        for i in range(self.parts):
            self.start_part(i)

    def forward(self):
        for i in range(self.parts):
            self.far[i].wait_recv()
            self.on[i].start()

    def finish(self):
        for i in range(self.parts):
            self.near[i].wait_recv()
            self.on[i].wait_recv()
            self.own[i].wait()
            self.far[i].wait_send()
            self.near[i].wait_send()
            self.on[i].wait_send()


def uly_peers():
    y, c, z, s = place()
    return [(y, 1 - c, z, s), (1 - y, c, z, s)]


def add_low(*terms):
    total = terms[0].astype(F32)
    for term in terms[1:]:
        total = total + term.astype(F32)
    return total


class UlyReduce:
    @staticmethod
    def scratch(x):
        parts, _, rows, width = x.shape
        return [
            pltpu.VMEM((parts, 2, rows, width), x.dtype),
            pltpu.VMEM((parts, rows, width), x.dtype),
            pltpu.VMEM((parts, rows, width), x.dtype),
            pltpu.SemaphoreType.DMA((3, parts)),
            pltpu.SemaphoreType.DMA((3, parts)),
        ]

    def __init__(self, x, near, mid, far_in, send, recv):
        y, c, z, s = place()
        mate, across = uly_peers()
        self.x, self.near_ref, self.mid, self.far_in = x, near, mid, far_in
        self.y, self.c, self.parts = y, c, x.shape[0]
        parts = range(self.parts)
        self.near = [
            [
                remote(x.at[i, f * 2 + 1 - c], near.at[i, k], send.at[k, i], recv.at[k, i], mate)
                for k, f in enumerate((1 - y, y))
            ]
            for i in parts
        ]
        self.far = [remote(mid.at[i], far_in.at[i], send.at[2, i], recv.at[2, i], across) for i in parts]

    def start(self):
        for i in range(self.parts):
            for copy in self.near[i]:
                copy.start()

    def middle(self):
        for i in range(self.parts):
            self.near[i][0].wait_recv()
            self.mid[i] = add_low(self.x[i, (1 - self.y) * 2 + self.c], self.near_ref[i, 0]).astype(BF)
            self.far[i].start()

    def result(self, i):
        self.near[i][1].wait_recv()
        self.far[i].wait_recv()
        return add_low(self.x[i, self.y * 2 + self.c], self.near_ref[i, 1], self.far_in[i])

    def finish(self):
        for i in range(self.parts):
            for copy in self.near[i] + [self.far[i]]:
                copy.wait_send()


def plane_peers():
    y, c, z, s = place()
    return [(y, 1 - c, z, s), (1 - y, c, z, s), (y, c, z, 1 - s)]


def plane_index(y, c, s):
    return (y * 2 + c) * 2 + s


class PlaneGather:
    sems = [pltpu.SemaphoreType.DMA((14,))] * 2 + [pltpu.SemaphoreType.DMA((2,))]

    def __init__(self, x, o, send, recv, local):
        y, c, z, s = place()
        mate, across, cross = plane_peers()
        me, py, px, pd = (
            plane_index(y, c, s),
            plane_index(1 - y, c, s),
            plane_index(y, c, 1 - s),
            plane_index(1 - y, c, 1 - s),
        )

        def copy(source, target, slot, device):
            return remote(source, target, send.at[slot], recv.at[slot], device)

        def on(p, i, slot, device):
            return copy(o.at[p, i], o.at[p, i], slot, device)

        self.by_y = [copy(x.at[i], o.at[me, i], i, across) for i in (0, 1)]
        self.by_x = [copy(x.at[i], o.at[me, i], 2 + i, cross) for i in (0, 1)]
        self.near = [copy(x.at[i], o.at[me, i], 4 + i, mate) for i in (0, 1)]
        self.corner = [on(py, 0, 6, cross), on(px, 1, 7, across)]
        self.pass_y = [on(py, 0, 8, mate), on(py, 1, 10, mate)]
        self.pass_x = [on(px, 0, 11, mate), on(px, 1, 9, mate)]
        self.pass_d = [on(pd, 0, 12, mate), on(pd, 1, 13, mate)]
        self.own = [pltpu.make_async_copy(x.at[i], o.at[me, i], local.at[i]) for i in (0, 1)]

    def start_part(self, i):
        for copy in (self.by_y[i], self.by_x[i], self.near[i], self.own[i]):
            copy.start()

    def forward_part(self, i):
        first, then = ((self.by_y, self.pass_y), (self.by_x, self.pass_x))[:: 1 - 2 * i]
        first[0][i].wait_recv()
        self.corner[i].start()
        first[1][i].start()
        then[0][i].wait_recv()
        then[1][i].start()

    def finish(self):
        for i in (0, 1):
            self.corner[i].wait_recv()
            self.pass_d[i].start()
        for i in (0, 1):
            for copy in (self.near[i], self.pass_y[i], self.pass_x[i], self.pass_d[i]):
                copy.wait()
            for copy in (self.by_y[i], self.by_x[i], self.corner[i]):
                copy.wait_send()
            self.own[i].wait()


class PlaneReduce:
    @staticmethod
    def scratch(x):
        one = pltpu.VMEM(x.shape[1:], x.dtype)
        return [pltpu.VMEM((4,) + x.shape[1:], x.dtype)] + [one] * 6 + [pltpu.SemaphoreType.DMA((14,))] * 2

    def __init__(self, x, near, out_x, out_y, out_d, in_x, in_y, in_d, send, recv):
        y, c, z, s = place()
        mate, across, cross = plane_peers()
        self.c = c
        self.spots = ((1 - y, 1 - s), (y, 1 - s), (1 - y, s), (y, s))
        self.x, self.near_ref = x, near
        self.out_x, self.out_y, self.out_d = out_x, out_y, out_d
        self.in_x, self.in_y, self.in_d = in_x, in_y, in_d

        def copy(source, target, slot, device):
            return remote(source, target, send.at[slot], recv.at[slot], device)

        self.near = [
            [copy(x.at[plane_index(sy, 1 - c, ss), i], near.at[k, i], 2 * k + i, mate) for i in (0, 1)]
            for k, (sy, ss) in enumerate(self.spots)
        ]
        self.corner = [
            copy(out_d.at[0], in_d.at[0], 8, cross),
            copy(out_d.at[1], in_d.at[1], 9, across),
        ]
        self.by_x = [copy(out_x.at[i], in_x.at[i], 10 + i, cross) for i in (0, 1)]
        self.by_y = [copy(out_y.at[i], in_y.at[i], 12 + i, across) for i in (0, 1)]

    def pair(self, k, i):
        sy, ss = self.spots[k]
        self.near[k][i].wait_recv()
        return add_low(self.x[plane_index(sy, self.c, ss), i], self.near_ref[k, i])

    def start(self):
        for spot in self.near:
            for copy in spot:
                copy.start()

    def middle(self):
        for i in (0, 1):
            self.out_d[i] = self.pair(0, i).astype(BF)
            self.corner[i].start()
        self.out_x[0] = self.pair(1, 0).astype(BF)
        self.by_x[0].start()
        self.out_y[1] = self.pair(2, 1).astype(BF)
        self.by_y[1].start()

    def last(self):
        part = self.pair(2, 0)
        self.corner[0].wait_recv()
        self.out_y[0] = (part + self.in_d[0].astype(F32)).astype(BF)
        self.by_y[0].start()
        part = self.pair(1, 1)
        self.corner[1].wait_recv()
        self.out_x[1] = (part + self.in_d[1].astype(F32)).astype(BF)
        self.by_x[1].start()

    def result(self, i):
        own = self.pair(3, i)
        self.by_x[i].wait_recv()
        self.by_y[i].wait_recv()
        return own + add_low(self.in_x[i], self.in_y[i])

    def finish(self):
        for copy in [c for spot in self.near for c in spot] + self.corner + self.by_x + self.by_y:
            copy.wait_send()


def plane_corners():
    y, c, z, s = place()
    return [
        (y, 1 - c, s), (1 - y, c, s), (1 - y, 1 - c, s),
        (y, c, 1 - s), (y, 1 - c, 1 - s), (1 - y, c, 1 - s), (1 - y, 1 - c, 1 - s),
    ]


def line_ends(n_line):
    y, c, z, s = place()
    return (z > 0, (y, c, z - 1, s)), (z < n_line - 1, (y, c, z + 1, s)), (y, c, z, 1 - s)


class BlkGather:
    @staticmethod
    def sems(n_line):
        return [
            pltpu.SemaphoreType.DMA((3,)),
            pltpu.SemaphoreType.DMA((1,)),
            pltpu.SemaphoreType.DMA((4, n_line)),
            pltpu.SemaphoreType.DMA((4, n_line)),
            pltpu.SemaphoreType.DMA((1,)),
        ]

    def __init__(self, n_line, pick_x, pick_o, own_send, own_recv, send, recv, local):
        y, c, z, s = place()
        self.z, self.s, self.n = z, s, n_line
        (self.has_low, self.low), (self.has_high, self.high), self.cross = line_ends(n_line)
        self.pick_x, self.pick_o = pick_x, pick_o
        self.sem = (own_send, own_recv, send, recv, local)

    def block(self, way, k):
        z = self.z - k if way == 0 else self.z + k
        return self.pick_o(z * 2 + self.s)

    def own(self, way):
        own_send, own_recv, send, recv, local = self.sem
        arrival = own_recv.at[0] if way == 2 else recv.at[way, 0]
        target = (self.high, self.low, self.cross)[way]
        return remote(self.pick_x(), self.pick_o(self.z * 2 + self.s), own_send.at[way], arrival, target)

    def keep(self):
        return pltpu.make_async_copy(self.pick_x(), self.pick_o(self.z * 2 + self.s), self.sem[4].at[0])

    def onward(self, way, k):
        send, recv = self.sem[2:4]
        target = self.high if way == 0 else self.low
        return remote(self.block(way, k), self.block(way, k), send.at[way, k], recv.at[way, k], target)

    def over(self, way, k):
        send, recv = self.sem[2:4]
        return remote(self.block(way, k), self.block(way, k), send.at[2 + way, k], recv.at[2 + way, k], self.cross)

    def arrive(self, way, k):
        send, recv = self.sem[2:4]
        return remote(self.block(way, k), self.block(way, k), send.at[way, k], recv.at[way, k - 1], self.cross)

    def there(self, way, k):
        return self.z >= k if way == 0 else self.z + k < self.n

    def start(self):
        pl.when(self.has_high)(lambda: self.own(0).start())
        pl.when(self.has_low)(lambda: self.own(1).start())
        self.own(2).start()
        self.keep().start()

    def take(self, way, k):
        self.arrive(way, k).wait_recv()
        pl.when((self.has_high, self.has_low)[way])(lambda: self.onward(way, k).start())
        self.over(way, k).start()

    def step(self, k):
        for way in (0, 1):
            pl.when(self.there(way, k))(lambda: self.take(way, k))

    def finish_arrivals(self):
        self.own(2).wait_recv()
        for k in range(1, self.n):
            for way in (0, 1):
                pl.when(self.there(way, k))(lambda: self.over(way, k).wait_recv())
        self.keep().wait()

    def finish_sends(self):
        pl.when(self.has_high)(lambda: self.own(0).wait_send())
        pl.when(self.has_low)(lambda: self.own(1).wait_send())
        self.own(2).wait_send()
        for k in range(1, self.n):
            for way in (0, 1):
                @pl.when(self.there(way, k))
                def _():
                    self.over(way, k).wait_send()

                    @pl.when((self.has_high, self.has_low)[way])
                    def _():
                        self.onward(way, k).wait_send()


def blk_greet(n_line):
    low, high, cross = line_ends(n_line)
    greet([cross], [low, high])


class BlkReduce:
    @staticmethod
    def scratch(n_line, a):
        return [
            pltpu.VMEM((n_line,) + a.shape[1:], a.dtype),
            pltpu.VMEM((n_line + 1,) + a.shape[1:], a.dtype),
            pltpu.SemaphoreType.DMA((n_line,)),
            pltpu.SemaphoreType.DMA((n_line,)),
            pltpu.SemaphoreType.DMA((2, n_line)),
            pltpu.SemaphoreType.DMA((2, n_line)),
        ]

    def __init__(self, n_line, x, side_in, line_in, side_send, side_recv, send, recv):
        y, c, self.z, self.s = place()
        self.n = n_line
        (self.has_low, self.low), (self.has_high, self.high), self.cross = line_ends(n_line)
        s = self.s
        if isinstance(x, tuple):
            self.leaves, self.stays = (lambda zz: x[0].at[zz]), (lambda zz: x[1][...])
        else:
            self.leaves, self.stays = (lambda zz: x.at[zz * 2 + 1 - s]), (lambda zz: x[zz * 2 + s])
        self.side_in, self.line_in = side_in, line_in
        self.sem = (side_send, side_recv, send, recv)

    def spot(self, way, k):
        return self.z + k if way == 0 else self.z - k

    def exists(self, way, k):
        return self.z + k < self.n if way == 0 else self.z >= k

    def side(self, zz):
        side_send, side_recv = self.sem[:2]
        return remote(
            self.leaves(zz), self.side_in.at[zz], side_send.at[zz], side_recv.at[zz], self.cross
        )

    def slot(self, way, k):
        return jnp.where(k == 0, self.n, self.spot(way, k)) if way == 1 else self.spot(way, k)

    def move(self, way, k):
        send, recv = self.sem[2:]
        target = self.high if way == 0 else self.low
        zz = self.spot(way, k)
        there = jnp.where(k == 1, self.n, zz) if way == 1 else zz
        return remote(
            self.side_in.at[zz], self.line_in.at[there], send.at[way, k], recv.at[way, k - 1], target
        )

    def arrive(self, way, k):
        send, recv = self.sem[2:]
        there = self.line_in.at[self.slot(way, k)]
        return remote(there, there, send.at[way, k], recv.at[way, k], self.cross)

    def start(self, k):
        for way in (0, 1) if k > 0 else (0,):
            pl.when(self.exists(way, k))(lambda: self.side(self.spot(way, k)).start())

    def move_on(self, way, k):
        zz = self.spot(way, k)
        self.side(zz).wait_recv()
        passed = self.has_low if way == 0 else self.has_high

        @pl.when(passed)
        def _():
            self.arrive(way, k).wait_recv()
            self.side_in[zz] = add_low(
                self.stays(zz), self.side_in[zz], self.line_in[zz]
            ).astype(self.side_in.dtype)

        @pl.when(jnp.logical_not(passed))
        def _():
            self.side_in[zz] = add_low(self.stays(zz), self.side_in[zz]).astype(
                self.side_in.dtype
            )

        self.move(way, k).start()

    def step(self, k):
        for way in (0, 1):
            pl.when(self.exists(way, k))(lambda: self.move_on(way, k))

    def result(self, o):
        z = self.z
        self.side(z).wait_recv()
        pl.when(self.has_low)(lambda: self.arrive(0, 0).wait_recv())
        pl.when(self.has_high)(lambda: self.arrive(1, 0).wait_recv())
        own = add_low(self.stays(z), self.side_in[z])

        @pl.when(jnp.logical_and(self.has_low, self.has_high))
        def _():
            o[...] = (own + add_low(self.line_in[z], self.line_in[self.n])).astype(o.dtype)

        @pl.when(jnp.logical_not(self.has_low))
        def _():
            o[...] = (own + self.line_in[self.n].astype(F32)).astype(o.dtype)

        @pl.when(jnp.logical_not(self.has_high))
        def _():
            o[...] = (own + self.line_in[z].astype(F32)).astype(o.dtype)

    def finish(self):
        for k in range(self.n - 1, -1, -1):
            for way in (0, 1) if k > 0 else (0,):
                @pl.when(self.exists(way, k))
                def _():
                    self.side(self.spot(way, k)).wait_send()
                    if k > 0:
                        self.move(way, k).wait_send()


def exit_kernel(
    n_line, gq, gk, gv, gh, res, oc, dc, alpha, rest,
    gq_o, gk_o, gv_o, gh_o, go_o, gd_o, sum_o, oc_o, dc_o,
    alpha_in, line_out, line_all, oc_s, oc_r, dc_s, dc_r, al_s, al_r, su_s, su_r, keep, *scratch,
):
    y, c, z, s = place()
    u, p, b, n_blk = y * 2 + c, plane_index(y, c, s), z * 2 + s, 2 * n_line
    low, high, cross = line_ends(n_line)
    corners = plane_corners()
    others = []
    for i in range(1, n_blk):
        to = lax.rem(b + i, n_blk)
        others.append((y, c, to // 2, lax.rem(to, 2)))
    once = [(to[3] != 1 - s) | (to[2] != z) for to in others]
    greet([(yy, cc, z, ss) for yy, cc, ss in corners], list(zip(once, others)))
    heads = 6
    jobs = [BlkReduce(n_line, x, *scratch[heads * i : heads * (i + 1)]) for i, x in enumerate((gq, gk, gv))]
    hid = UlyReduce(gh, *scratch[heads * 3 :])
    small, cols = [], []
    for k, (yy, cc, ss) in enumerate(corners):
        target = (yy, cc, z, ss)
        cols.append(remote(dc.at[plane_index(yy, cc, ss)], dc_o.at[p], dc_s.at[k], dc_r.at[k], target))
        if k < 3:
            cols.append(remote(oc.at[yy * 2 + cc], oc_o.at[u], oc_s.at[k], oc_r.at[k], target))
            small.append(remote(alpha.at[yy * 2 + cc], alpha_in.at[k], al_s.at[k], al_r.at[k], target))
    for job in small:
        job.start()
    hid.start()
    for k in range(n_line - 1, -1, -1):
        for job in jobs:
            job.start(k)
    mine = [
        pltpu.make_async_copy(dc.at[p], dc_o.at[p], keep.at[0]),
        pltpu.make_async_copy(oc.at[u], oc_o.at[u], keep.at[1]),
    ]
    for job in mine:
        job.start()
    hid.middle()
    for job in cols:
        job.start()
    for job in small:
        job.wait_recv()
    line_out[...] = rest[...]
    line_out[:, :, :128] = rest[:, :, :128] + alpha[u] + alpha_in[0] + alpha_in[1] + alpha_in[2]
    line_jobs = []
    for i in range(1, n_blk):
        to = lax.rem(b + i, n_blk)
        line_jobs.append(
            remote(line_out.at[to], line_all.at[i - 1], su_s.at[i - 1], su_r.at[i - 1], others[i - 1])
        )
    for job in line_jobs:
        job.start()
    for k in range(n_line - 1, 0, -1):
        for job in jobs:
            job.step(k)
    for i in range(gh.shape[0]):
        gh_o[i] = res[i] + hid.result(i)
    for job in cols:
        job.wait_recv()
    for job in mine:
        job.wait()
    wide, ff_each = oc.shape[-1], dc.shape[-1] // n_line
    for v in range(4):
        go_o[:, v * wide : (v + 1) * wide] = oc_o[v].astype(F32)
        for t in (0, 1):
            for k in range(n_line):
                at = ((v * n_line + k) * 2 + t) * ff_each
                gd_o[:, at : at + ff_each] = dc_o[v * 2 + t, :, k * ff_each : (k + 1) * ff_each].astype(F32)
    total = line_out[b]
    for i, job in enumerate(line_jobs):
        job.wait_recv()
        total = total + line_all[i]
    sum_o[...] = total
    for job, o in zip(jobs, (gq_o, gk_o, gv_o)):
        job.result(o)
    hid.finish()
    for job in jobs:
        job.finish()
    for job in line_jobs + small:
        job.wait_send()
    for job in cols:
        job.wait_send()


def leave(n_line, gq, gk, gv, gh, res, oc, dc, alpha, rest):
    n_blk = 2 * n_line
    vmem = pl.BlockSpec(memory_space=pltpu.VMEM)
    dma = pltpu.SemaphoreType.DMA
    scratch = [
        pltpu.VMEM(oc.shape, oc.dtype),
        pltpu.VMEM(dc.shape, dc.dtype),
        pltpu.VMEM((3,) + alpha.shape[1:], F32),
        pltpu.VMEM(rest.shape, F32),
        pltpu.VMEM((n_blk - 1,) + rest.shape[1:], F32),
        dma((3,)), dma((3,)), dma((7,)), dma((7,)), dma((3,)), dma((3,)),
        dma((n_blk - 1,)), dma((n_blk - 1,)), dma((2,)),
    ]
    for g in (gq, gk, gv):
        scratch += BlkReduce.scratch(n_line, g)
    scratch += UlyReduce.scratch(gh)
    grad = jax.ShapeDtypeStruct(gq.shape[1:], F32)
    return pl.pallas_call(
        functools.partial(exit_kernel, n_line),
        out_shape=[
            grad, grad, grad,
            jax.ShapeDtypeStruct(res.shape, F32),
            jax.ShapeDtypeStruct((oc.shape[1], 4 * oc.shape[2]), F32),
            jax.ShapeDtypeStruct((dc.shape[1], 8 * dc.shape[2]), F32),
            jax.ShapeDtypeStruct(rest.shape[1:], F32),
        ],
        in_specs=[vmem] * 9,
        out_specs=[vmem] * 7,
        scratch_shapes=scratch,
        compiler_params=params(8),
        cost_estimate=pl.CostEstimate(flops=0, bytes_accessed=40 * 3_000_000, transcendentals=0),
        name="leave",
    )(gq, gk, gv, gh, res, oc, dc, alpha, rest)


def entry_kernel(
    n_line, hid, small, wq, wk, wv, wo, wd, hid_o, small_o, wq_o, wk_o, wv_o, oc_o, dc_o, oc, dc, *sems
):
    y, c, z, s = place()
    u, p = y * 2 + c, plane_index(y, c, s)
    low, high, cross = line_ends(n_line)
    corners = plane_corners()
    greet([(yy, cc, z, ss) for yy, cc, ss in corners], [low, high])
    hid_job = UlyGather(hid, hid_o, *sems[:3])
    at, jobs = 3, []
    for x, pick in (
        (small, lambda block: small_o.at[u, block]),
        (wq, lambda block: wq_o.at[block]),
        (wk, lambda block: wk_o.at[block]),
        (wv, lambda block: wv_o.at[block]),
    ):
        jobs.append(BlkGather(n_line, lambda x=x: x, pick, *sems[at : at + 5]))
        at += 5
    oc_s, oc_r, dc_s, dc_r, sm_s, sm_r, keep = sems[at:]
    jobs[0].start()
    for job in jobs[1:]:
        job.start()
    hid_job.start()
    for v in range(4):
        wide = oc.shape[-1]
        oc[v] = wo[:, v * wide : (v + 1) * wide]
        ff_each = dc.shape[-1] // n_line
        for t in (0, 1):
            for k in range(n_line):
                at = ((v * n_line + k) * 2 + t) * ff_each
                dc[v * 2 + t, :, k * ff_each : (k + 1) * ff_each] = wd[:, at : at + ff_each]
    col_jobs = []
    for k, (yy, cc, ss) in enumerate(corners):
        target = (yy, cc, z, ss)
        col_jobs.append(
            remote(dc.at[plane_index(yy, cc, ss)], dc_o.at[p], dc_s.at[k], dc_r.at[k], target)
        )
        if k < 3:
            col_jobs.append(remote(oc.at[yy * 2 + cc], oc_o.at[u], oc_s.at[k], oc_r.at[k], target))
    for job in col_jobs:
        job.start()
    mine = [
        pltpu.make_async_copy(dc.at[p], dc_o.at[p], keep.at[0]),
        pltpu.make_async_copy(oc.at[u], oc_o.at[u], keep.at[1]),
    ]
    for job in mine:
        job.start()
    for k in range(1, n_line):
        for job in jobs:
            job.step(k)
        if k == 1:
            hid_job.forward()
    jobs[0].finish_arrivals()
    small_jobs = [
        remote(small_o.at[u], small_o.at[u], sm_s.at[k], sm_r.at[k], (yy, cc, z, ss))
        for k, (yy, cc, ss) in enumerate(corners[:3])
    ]
    for job in small_jobs:
        job.start()
    for job in jobs[1:]:
        job.finish_arrivals()
    hid_job.finish()
    for job in small_jobs + col_jobs:
        job.wait()
    for job in mine:
        job.wait()
    for job in jobs:
        job.finish_sends()


def entry(n_line, hid, small, wq, wk, wv, wo, wd):
    n_blk = 2 * n_line
    oc = jax.ShapeDtypeStruct((4, wo.shape[0], wo.shape[1] // 4), wo.dtype)
    dc = jax.ShapeDtypeStruct((8, wd.shape[0], wd.shape[1] // 8), wd.dtype)
    parts = hid.shape[0]
    vmem, anyway = pl.BlockSpec(memory_space=pltpu.VMEM), pl.BlockSpec(memory_space=pl.ANY)

    def out(shape, like):
        return jax.ShapeDtypeStruct(shape, like.dtype)

    return pl.pallas_call(
        functools.partial(entry_kernel, n_line),
        out_shape=[
            out((parts, 4) + hid.shape[1:], hid),
            out((4, n_blk) + small.shape, small),
            out((n_blk,) + wq.shape, wq),
            out((n_blk,) + wk.shape, wk),
            out((n_blk,) + wv.shape, wv),
            out(oc.shape, oc),
            out(dc.shape, dc),
        ],
        in_specs=[vmem] * 7,
        out_specs=[vmem, vmem, anyway, anyway, anyway, vmem, vmem],
        scratch_shapes=[pltpu.VMEM(oc.shape, oc.dtype), pltpu.VMEM(dc.shape, dc.dtype)]
        + UlyGather.sems(parts)
        + BlkGather.sems(n_line) * 4
        + [pltpu.SemaphoreType.DMA((3,))] * 2
        + [pltpu.SemaphoreType.DMA((7,))] * 2
        + [pltpu.SemaphoreType.DMA((3,))] * 2
        + [pltpu.SemaphoreType.DMA((2,))],
        compiler_params=params(6),
        cost_estimate=pl.CostEstimate(flops=0, bytes_accessed=40 * 3_000_000, transcendentals=0),
        name="entry",
    )(hid, small, wq, wk, wv, wo, wd)
def dot_nt(a, b):
    return lax.dot_general(a, b, (((1,), (1,)), ((), ())), preferred_element_type=F32)


def dot_nn(a, b):
    return lax.dot_general(a, b, (((1,), (0,)), ((), ())), preferred_element_type=F32)


def dot_tn(a, b):
    return lax.dot_general(a, b, (((0,), (0,)), ((), ())), preferred_element_type=F32)


def lanes_of(shape):
    return lax.broadcasted_iota(jnp.int32, shape, len(shape) - 1)


def halves(x):
    row = lax.broadcasted_iota(jnp.int32, (128, 128), 0) // HEAD_DIM
    same = jnp.where(row == lanes_of((128, 128)) // HEAD_DIM, 1.0, 0.0).astype(BF)
    high = x.astype(BF)
    rest = (x - high.astype(F32)).astype(BF)
    return dot_nn(high, same) + dot_nn(rest, same)


def turn(x):
    first = lanes_of(x.shape) % HEAD_DIM < HEAD_DIM // 2
    return jnp.where(first, pltpu.roll(x, 128 - 32, 1), pltpu.roll(x, 32, 1))


def heads_kernel(x_ref, wq_ref, wk_ref, wv_ref, cos_ref, sin_ref, scale_ref, qz_ref, kv_ref, y_ref, c_ref):
    x = x_ref[...]
    wv = wv_ref[0]
    got = dot_nt(x, jnp.concatenate([wq_ref[0], wk_ref[0], jnp.zeros_like(wv), wv], axis=0))
    raw, value = got[:, :128], got[:, 128:]
    low = lanes_of(raw.shape) < HEAD_DIM
    turned = raw * cos_ref[...] + turn(raw) * sin_ref[...]
    c = lax.rsqrt(halves(turned * turned) + HEAD_DIM * tiny_eps)
    y = turned * c
    both = y * scale_ref[0]
    qz_ref[...] = jnp.where(low, both, 0.0).astype(BF)
    kv_ref[...] = jnp.where(low, pltpu.roll(both, HEAD_DIM, 1), value).astype(BF)
    y_ref[...] = y
    c_ref[...] = c


def heads_forward(x, wq, wk, wv, cos, sin, scale):
    rows, width = x.shape
    heads = wq.shape[0]
    whole = lambda shape: pl.BlockSpec(shape, lambda h: (0,) * len(shape))
    weight = pl.BlockSpec((1, HEAD_DIM, width), lambda h: (h, 0, 0))
    head = pl.BlockSpec((rows, 128), lambda h: (0, h))
    wide = lambda dtype: jax.ShapeDtypeStruct((rows, heads * 128), dtype)
    return pl.pallas_call(
        heads_kernel,
        grid=(heads,),
        out_shape=[wide(BF), wide(BF), wide(F32), wide(F32)],
        in_specs=[whole((rows, width)), weight, weight, weight, whole((rows, 128)), whole((rows, 128)),
                  pl.BlockSpec((1, 1, 128), lambda h: (h, 0, 0))],
        out_specs=[head] * 4,
        compiler_params=pltpu.CompilerParams(vmem_limit_bytes=VMEM_BYTES),
        cost_estimate=pl.CostEstimate(flops=rows * width * heads * 384, bytes_accessed=rows * width * 8, transcendentals=0),
        name="heads_forward",
    )(x, wq, wk, wv, cos, sin, scale)


def down_columns(row):
    n = row.shape[1]
    one = jnp.transpose(jnp.broadcast_to(row, (128, n)))
    return jnp.concatenate([one] * (n // 128), axis=1)


def arrivals(n_line, body):
    each = 2 * n_line - 1

    def step(t, carry):
        stage, r = t // each, lax.rem(t, each)
        body(stage, (r + 1) // 2, lax.rem(r + 1, 2))
        return carry

    lax.fori_loop(0, 2 * each, step, 0)


def attend_kernel(
    n_line, q_ref, kv_ref, oc_ref, qp_ref, kp_ref,
    kv_o, oc_o, o_ref, mixed_ref, inv_ref, acc, total, place_q, *sems,
):
    y, c, z, s = place()
    blk_greet(n_line)
    seqs, rows, wide = q_ref.shape
    heads = wide // 128
    each = len(BlkGather.sems(n_line))
    picks = [
        (lambda i=i: kv_ref.at[i], lambda block, i=i: kv_o.at[block, i]) for i in range(seqs)
    ] + [(lambda: oc_ref.at[0], lambda block: oc_o.at[block, 0])]
    jobs = [
        BlkGather(n_line, *pick, *sems[each * i : each * (i + 1)]) for i, pick in enumerate(picks)
    ]
    for job in jobs:
        job.start()
    acc[...] = jnp.zeros_like(acc)
    total[...] = jnp.zeros_like(total)
    for i in range(seqs):
        place_q[i] = down_columns(qp_ref[i])

    def attend_to(i, block, keys):
        allowed = kp_ref[i, block] <= place_q[i]
        for h in range(heads):
            kv = keys(h)
            p = jnp.where(allowed, jnp.exp(dot_nt(q_ref[i, :, h * 128 : (h + 1) * 128], kv)), 0.0)
            part = p[:, :128]
            for j in range(1, rows // 128):
                part = part + p[:, j * 128 : (j + 1) * 128]
            total[i, h] = total[i, h] + part
            acc[i, h] = acc[i, h] + dot_nn(p.astype(BF), kv)

    def body(stage, k, way):
        there = (k == 0) | jnp.where(way == 0, z >= k, z + k < n_line)

        @pl.when(there)
        def _():
            for job in jobs:
                for w in (0, 1):
                    pl.when((stage == 0) & (k > 0) & (way == w))(lambda: job.take(w, k))
                    pl.when((stage == 1) & (k > 0) & (way == w))(lambda: job.over(w, k).wait_recv())
                pl.when((stage == 1) & (k == 0))(lambda: job.own(2).wait_recv())
                pl.when((stage == 0) & (k == 0))(lambda: job.keep().wait())
            zz = jnp.where(way == 0, z - k, z + k)
            block = zz * 2 + jnp.where(stage == 0, s, 1 - s)
            for i in range(seqs):
                attend_to(i, block, lambda h: kv_o[block, i, :, h * 128 : (h + 1) * 128])

    arrivals(n_line, body)
    low = lanes_of((rows, 128)) < HEAD_DIM
    for i in range(seqs):
        outs = []
        for h in range(heads):
            inverse = 1.0 / jnp.broadcast_to(jnp.sum(total[i, h], axis=-1, keepdims=True), (rows, 128))
            out = acc[i, h] * inverse
            o_ref[i, h] = out
            inv_ref[i, h] = jnp.transpose(inverse)[:8]
            outs.append(out)
        for h in range(0, heads - 1, 2):
            mixed_ref[i, :, h * HEAD_DIM : (h + 2) * HEAD_DIM] = jnp.where(
                low, pltpu.roll(outs[h], HEAD_DIM, 1), outs[h + 1]
            ).astype(BF)
        if heads % 2 == 1:
            mixed_ref[i, :, (heads - 1) * HEAD_DIM :] = pltpu.roll(outs[-1], HEAD_DIM, 1)[:, :HEAD_DIM].astype(BF)
    for job in jobs:
        job.finish_sends()


def attend(n_line, q, kv, oc, q_places, k_places):
    seqs, rows, wide = q.shape
    n_blk, heads = 2 * n_line, wide // 128
    head = (seqs, heads, rows, 128)
    return comm_call(
        functools.partial(attend_kernel, n_line), "attend", 5, (q, kv, oc, q_places, k_places),
        [
            ((n_blk,) + kv.shape, BF), ((n_blk,) + oc.shape, BF), (head, F32),
            ((seqs, rows, heads * HEAD_DIM), BF), ((seqs, heads, 8, rows), F32),
        ],
        [pltpu.VMEM(head, F32), pltpu.VMEM(head, F32), pltpu.VMEM((seqs, rows, rows), F32)]
        + BlkGather.sems(n_line) * (seqs + 1),
        75,
    )


def attend_back_kernel(
    n_line, q_ref, low_ref, w_ref, mixed_ref, o_ref, inv_ref, kv_ref, qp_ref, kp_ref,
    dq_ref, dkv_ref, oc_ref, dz, delta, dq, parts, oparts, *scratch,
):
    y, c, z, s = place()
    blk_greet(n_line)
    seqs, rows, wide = q_ref.shape
    heads, width = wide // 128, low_ref.shape[-1]
    low_rows = low_ref[...].reshape(seqs * rows, width)
    grad = dot_tn(low_rows, mixed_ref[...].reshape(seqs * rows, mixed_ref.shape[-1])).astype(BF)
    n_blk, each_out = 2 * n_line, width // (8 * n_line)
    for b in range(n_blk):
        for v in range(4):
            at = (v * n_blk + b) * each_out
            oparts[b, v * each_out : (v + 1) * each_out] = grad[at : at + each_out]
    each = 6
    jobs = [
        BlkReduce(n_line, (parts.at[:, i], parts.at[n_line, i]), *scratch[each * i : each * (i + 1)])
        for i in range(seqs)
    ]
    out_job = BlkReduce(n_line, oparts, *scratch[each * seqs :])
    for k in range(n_line - 1, -1, -1):
        out_job.start(k)
    low = lanes_of((rows, 128)) < HEAD_DIM
    for i in range(seqs):
        d = dot_nn(low_rows[i * rows : (i + 1) * rows], w_ref[...]).astype(BF).astype(F32)
        for h in range(heads):
            at = h // 2 * 128
            if h == heads - 1 and heads % 2 == 1:
                tile = jnp.concatenate([jnp.zeros((rows, HEAD_DIM), F32), d[:, at:]], axis=1)
            else:
                tile = d[:, at : at + 128]
                if h % 2 == 0:
                    tile = pltpu.roll(tile, HEAD_DIM, 1)
                tile = jnp.where(low, 0.0, tile)
            dz[i, h] = tile.astype(BF)
            row = jnp.sum(tile * o_ref[i, h], axis=-1, keepdims=True)
            delta[i, h] = jnp.transpose(jnp.broadcast_to(row, (rows, 128)))[:8]
    dq[...] = jnp.zeros_like(dq)

    def block_of(block, spot):
        for i in range(seqs):
            allowed = down_columns(kp_ref[i, block]) <= qp_ref[i]
            for h in range(heads):
                lanes = slice(h * 128, (h + 1) * 128)
                kv = kv_ref[block, i, :, lanes]
                pair = jnp.concatenate([q_ref[i, :, lanes], dz[i, h]], axis=0)
                scores = dot_nt(kv, pair)
                p = jnp.where(allowed, jnp.exp(scores[:, :rows]) * inv_ref[i, h][:1], 0.0)
                ds = (p * (scores[:, rows:] - delta[i, h][:1])).astype(BF)
                parts[spot, i, :, lanes] = dot_nn(
                    jnp.concatenate([ds, p.astype(BF)], axis=1), pair
                ).astype(BF)
                dq[i, h] = dq[i, h] + dot_tn(ds, kv)

    def body(stage, k, way):
        there = jnp.where(k == 0, way == 0, jnp.where(way == 0, z + k < n_line, z >= k))

        @pl.when(there)
        def _():
            zz = jnp.where(way == 0, z + k, z - k)
            block_of(zz * 2 + jnp.where(stage == 0, 1 - s, s), jnp.where(stage == 0, zz, n_line))

            @pl.when(stage == 0)
            def _():
                for job in jobs:
                    job.side(zz).start()

            for w in (0, 1):
                @pl.when((stage == 1) & (k > 0) & (way == w))
                def _():
                    for job in jobs + [out_job]:
                        job.move_on(w, k)

    def step(t, carry):
        r = lax.rem(t, 2 * n_line)
        body(t // (2 * n_line), n_line - 1 - r // 2, lax.rem(r, 2))
        return carry

    lax.fori_loop(0, 4 * n_line, step, 0)
    for i in range(seqs):
        for h in range(heads):
            dq_ref[i, :, h * 128 : (h + 1) * 128] = dq[i, h].astype(BF)
    out_job.result(oc_ref)
    for i, job in enumerate(jobs):
        job.result(dkv_ref.at[i])
    for job in jobs + [out_job]:
        job.finish()


def attend_back(n_line, q, low, w, mixed, o, inv, kv, q_places, k_places):
    seqs, rows, wide = q.shape
    n_blk, heads = 2 * n_line, wide // 128
    head = (seqs, heads, rows, 128)
    width, columns = w.shape
    out_shape = (width // n_blk, columns)
    one = jax.ShapeDtypeStruct((n_blk,) + kv.shape[2:], BF)
    out_one = jax.ShapeDtypeStruct((n_blk,) + out_shape, BF)
    return comm_call(
        functools.partial(attend_back_kernel, n_line), "attend_back", 7,
        (q, low, w, mixed, o, inv, kv, q_places, k_places),
        [(q.shape, BF), (kv.shape[1:], BF), (out_shape, BF)],
        [
            pltpu.VMEM(head, BF), pltpu.VMEM((seqs, heads, 8, rows), F32), pltpu.VMEM(head, F32),
            pltpu.VMEM((n_line + 1,) + kv.shape[1:], BF), pltpu.VMEM(out_one.shape, BF),
        ]
        + BlkReduce.scratch(n_line, one) * seqs + BlkReduce.scratch(n_line, out_one),
        75, 67_000_000,
    )


def heads_back_kernel(
    x_ref, dq_ref, dkv_ref, y_ref, c_ref, cos_ref, sin_ref, scale_ref, wq_ref, wk_ref, wv_ref,
    gq_ref, gk_ref, gv_ref, gs_ref, gh_ref, acc_ref,
):
    h = pl.program_id(0)
    dq, dkv = dq_ref[...], dkv_ref[...]
    low = lanes_of(dq.shape) < HEAD_DIM
    dy = jnp.where(low, dq.astype(F32), pltpu.roll(dkv.astype(F32), HEAD_DIM, 1))
    y = y_ref[...]
    factor = jnp.where(lanes_of((1, 128)) < HEAD_DIM, HEAD_DIM**0.5, 1.0)
    gs_ref[0] = jnp.sum(dy * y, axis=0, keepdims=True) * factor
    dy = dy * scale_ref[0]
    dr = c_ref[...] * (dy - y * halves(y * dy))
    raw = (dr * cos_ref[...] - turn(dr) * sin_ref[...]).astype(BF)
    x = x_ref[...]
    value = jnp.where(low, jnp.zeros_like(dkv), dkv)
    both = jnp.concatenate([raw, value], axis=1)
    grad = dot_tn(both, x)
    gq_ref[0] = grad[:HEAD_DIM].astype(BF)
    gk_ref[0] = grad[HEAD_DIM : 2 * HEAD_DIM].astype(BF)
    gv_ref[0] = grad[3 * HEAD_DIM :].astype(BF)
    wv = wv_ref[0]
    more = dot_nn(both, jnp.concatenate([wq_ref[0], wk_ref[0], jnp.zeros_like(wv), wv], axis=0))

    @pl.when(h == 0)
    def _():
        acc_ref[...] = more

    @pl.when(h > 0)
    def _():
        acc_ref[...] = acc_ref[...] + more

    @pl.when(h == pl.num_programs(0) - 1)
    def _():
        gh_ref[...] = acc_ref[...].astype(BF)


def heads_back(x, dq, dkv, y, c, cos, sin, scale, wq, wk, wv):
    rows, width = x.shape
    heads = wq.shape[0]
    whole = lambda shape: pl.BlockSpec(shape, lambda h: (0,) * len(shape))
    weight = pl.BlockSpec((1, HEAD_DIM, width), lambda h: (h, 0, 0))
    head = pl.BlockSpec((rows, 128), lambda h: (0, h))
    row = pl.BlockSpec((1, 1, 128), lambda h: (h, 0, 0))
    return pl.pallas_call(
        heads_back_kernel,
        grid=(heads,),
        out_shape=[jax.ShapeDtypeStruct(wq.shape, BF)] * 3
        + [jax.ShapeDtypeStruct((heads, 1, 128), F32), jax.ShapeDtypeStruct((rows, width), BF)],
        in_specs=[whole((rows, width))] + [head] * 4 + [whole((rows, 128))] * 2 + [row] + [weight] * 3,
        out_specs=[weight] * 3 + [row, whole((rows, width))],
        scratch_shapes=[pltpu.VMEM((rows, width), F32)],
        compiler_params=pltpu.CompilerParams(vmem_limit_bytes=VMEM_BYTES),
        cost_estimate=pl.CostEstimate(flops=rows * width * heads * 1024, bytes_accessed=rows * width * 12, transcendentals=0),
        name="heads_back",
    )(x, dq, dkv, y, c, cos, sin, scale, wq, wk, wv)


def ff_kernel(x_ref, wu_ref, wg_ref, us_ref, gs_ref, inner_ref, up_ref, gate_ref):
    x = x_ref[...]
    up = dot_nt(x, wu_ref[...])
    gate = dot_nt(x, wg_ref[...])
    z = gate * gs_ref[...] * D**0.5
    inner_ref[...] = (z / (1.0 + jnp.exp(-z)) * (up * us_ref[...])).astype(BF)
    up_ref[...] = up
    gate_ref[...] = gate


def ff_forward(x, wu, wg, us, gs):
    rows, width = x.shape
    columns = wu.shape[0]
    block = rows // 4
    whole = lambda a: pl.BlockSpec(a.shape, lambda i: (0, 0))
    part = lambda n: pl.BlockSpec((block, n), lambda i: (i, 0))
    out = lambda dtype: jax.ShapeDtypeStruct((rows, columns), dtype)
    return pl.pallas_call(
        ff_kernel,
        grid=(4,),
        out_shape=[out(BF), out(F32), out(F32)],
        in_specs=[part(width)] + [whole(a) for a in (wu, wg, us, gs)],
        out_specs=[part(columns)] * 3,
        compiler_params=pltpu.CompilerParams(vmem_limit_bytes=VMEM_BYTES),
        cost_estimate=pl.CostEstimate(
            flops=4 * rows * width * columns, bytes_accessed=2 * rows * width + 10 * rows * columns,
            transcendentals=rows * columns,
        ),
        name="ff_forward",
    )(x, wu, wg, us, gs)


def ff_back_kernel(d_ref, wd_ref, up_ref, gate_ref, us_ref, gs_ref, du_ref, dg_ref, sum_ref):
    d = dot_nn(d_ref[...], wd_ref[...])
    up, gate = up_ref[...], gate_ref[...]
    us, gs = us_ref[...], gs_ref[...] * D**0.5
    z = gate * gs
    sig = 1.0 / (1.0 + jnp.exp(-z))
    du = d * (z * sig)
    dz = d * (up * us) * sig * (1.0 + z * (1.0 - sig))
    du_ref[...] = (du * us).astype(BF)
    dg_ref[...] = (dz * gs).astype(BF)
    sums = jnp.concatenate(
        [
            jnp.sum(du * up, axis=0, keepdims=True),
            jnp.sum(dz * gate, axis=0, keepdims=True) * D**0.5,
        ],
        axis=0,
    )
    i = pl.program_id(0)

    @pl.when(i == 0)
    def _():
        sum_ref[...] = sums

    @pl.when(i > 0)
    def _():
        sum_ref[...] = sum_ref[...] + sums


def ff_back(d, wd, up, gate, us, gs):
    rows, width = d.shape
    columns = wd.shape[1]
    block = rows // 4
    whole = lambda a: pl.BlockSpec(a.shape, lambda i: (0, 0))
    part = lambda n: pl.BlockSpec((block, n), lambda i: (i, 0))
    out = jax.ShapeDtypeStruct((rows, columns), BF)
    return pl.pallas_call(
        ff_back_kernel,
        grid=(4,),
        out_shape=[out, out, jax.ShapeDtypeStruct((2, columns), F32)],
        in_specs=[part(width), whole(wd), part(columns), part(columns), whole(us), whole(gs)],
        out_specs=[part(columns), part(columns), pl.BlockSpec((2, columns), lambda i: (0, 0))],
        compiler_params=pltpu.CompilerParams(vmem_limit_bytes=VMEM_BYTES),
        cost_estimate=pl.CostEstimate(
            flops=2 * rows * width * columns, bytes_accessed=2 * rows * width + 14 * rows * columns,
            transcendentals=rows * columns,
        ),
        name="ff_back",
    )(d, wd, up, gate, us, gs)


def unit_of(x):
    c = lax.rsqrt(jnp.sum(x * x, axis=-1, keepdims=True) + x.shape[-1] * tiny_eps)
    return x * c, c


def unit_back(y, c, dy):
    return c * (dy - y * jnp.sum(y * dy, axis=-1, keepdims=True))


def comm_call(kernel, name, collective_id, args, outs, scratch, micros, room=VMEM_BYTES):
    vmem = pl.BlockSpec(memory_space=pltpu.VMEM)
    return pl.pallas_call(
        kernel,
        out_shape=[jax.ShapeDtypeStruct(shape, dtype) for shape, dtype in outs],
        in_specs=[vmem] * len(args),
        out_specs=[vmem] * len(outs),
        scratch_shapes=scratch,
        compiler_params=params(collective_id, room),
        cost_estimate=pl.CostEstimate(flops=0, bytes_accessed=micros * 3_000_000, transcendentals=0),
        name=name,
    )(*args)


def attn_joint_kernel(mixed, w, hid, rate, first_o, ua_o, ca_o, cv_o, all_o, part, low, *scratch):
    mate, across, cross = plane_peers()
    greet([mate, across, cross])
    split = len(UlyReduce.scratch(part))
    job = UlyReduce(part, *scratch[:split])
    out = PlaneGather(low, all_o, *scratch[split:])
    seqs, _, rows, width = part.shape
    for i in range(seqs):
        part[i] = dot_nt(mixed[i], w[...]).astype(BF).reshape(4, rows, width)
        for copy in job.near[i]:
            copy.start()
    job.middle()
    for i in range(seqs):
        ua, ca = unit_of(job.result(i))
        h = hid[i].astype(F32)
        first, cv = unit_of(h + rate[...] * (ua - h))
        low[i] = first.astype(BF)
        out.start_part(i)
        first_o[i], ua_o[i] = first, ua
        ca_o[i] = jnp.broadcast_to(ca, (rows, 128))
        cv_o[i] = jnp.broadcast_to(cv, (rows, 128))
        if i > 0:
            out.forward_part(i - 1)
    out.forward_part(seqs - 1)
    out.finish()
    job.finish()


def attn_joint(mixed, w, hid, rate):
    seqs, rows, width = hid.shape
    part = jax.ShapeDtypeStruct((seqs, 4, rows, width), BF)
    thin = ((seqs, rows, 128), F32)
    return comm_call(
        attn_joint_kernel, "attn_joint", 1, (mixed, w, hid, rate),
        [(hid.shape, F32), (hid.shape, F32), thin, thin, ((8, seqs, rows, width), BF)],
        [pltpu.VMEM(part.shape, BF), pltpu.VMEM(hid.shape, BF)] + UlyReduce.scratch(part) + PlaneGather.sems,
        25,
    )


def plane_products(job, part, c, product):
    _, seqs, rows, width = part.shape
    for cc, first in ((1 - c, True), (c, False)):
        got = product(cc).astype(BF).reshape(2, 2, seqs, rows, width)
        for yy in (0, 1):
            for ss in (0, 1):
                part[plane_index(yy, cc, ss)] = got[yy, ss]
        if first:
            job.start()


def ff_joint_kernel(inner, w, first, rate, cot, out_o, d1_o, sum_o, all_o, part, low, *scratch):
    y, c, z, s = place()
    greet(plane_peers())
    split = len(PlaneReduce.scratch(part))
    job = PlaneReduce(part, *scratch[:split])
    out = PlaneGather(low, all_o, *scratch[split:])
    _, seqs, rows, width = part.shape
    columns = inner.shape[-1]
    plane_products(
        job, part, c, lambda cc: dot_nt(inner[:, cc].reshape(4 * seqs * rows, columns), w[...])
    )
    job.middle()
    job.last()
    for i in range(seqs):
        ub, cb = unit_of(job.result(i))
        f, b = first[i], rate[...]
        o, cw = unit_of(f + b * (ub - f))
        dw = unit_back(o, cw, cot[i].astype(F32))
        step = b * dw
        low[i] = unit_back(ub, cb, step).astype(BF)
        out.start_part(i)
        out_o[i] = o.astype(BF)
        d1_o[i] = dw - step
        total = jnp.sum(dw * (ub - f), axis=0, keepdims=True)
        sum_o[...] = total if i == 0 else sum_o[...] + total
        if i > 0:
            out.forward_part(i - 1)
    out.forward_part(seqs - 1)
    out.finish()
    job.finish()


def ff_joint(inner, w, first, rate, cot):
    seqs, rows, width = first.shape
    part = jax.ShapeDtypeStruct((8, seqs, rows, width), BF)
    return comm_call(
        ff_joint_kernel, "ff_joint", 2,
        (inner.reshape(2, 2, 2, seqs * rows, inner.shape[-1]), w, first, rate, cot),
        [(first.shape, BF), (first.shape, F32), ((1, width), F32), (part.shape, BF)],
        [pltpu.VMEM(part.shape, BF), pltpu.VMEM(first.shape, BF)] + PlaneReduce.scratch(part) + PlaneGather.sems,
        30,
    )


def back_joint_kernel(
    du, dg, wu, wg, d1, first, ua, ca, cv, hid, rate, res_o, sum_o, all_o, part, low, *scratch
):
    y, c, z, s = place()
    greet(plane_peers())
    split = len(PlaneReduce.scratch(part))
    job = PlaneReduce(part, *scratch[:split])
    out = UlyGather(low, all_o, *scratch[split:])
    _, seqs, rows, width = part.shape
    columns = du.shape[-1]
    tokens = 8 * seqs * rows
    half = lambda ref, cc: ref[:, cc].reshape(tokens // 2, columns)
    plane_products(
        job, part, c, lambda cc: dot_nn(half(du, cc), wu[...]) + dot_nn(half(dg, cc), wg[...])
    )
    job.middle()
    job.last()
    for i in range(seqs):
        f, h, u, a = first[i], hid[i].astype(F32), ua[i], rate[...]
        dv = unit_back(f, cv[i][:, :1], d1[i] + job.result(i))
        step = a * dv
        low[i] = unit_back(u, ca[i][:, :1], step).astype(BF)
        out.start_part(i)
        res_o[i] = dv - step
        total = jnp.sum(dv * (u - h), axis=0, keepdims=True)
        sum_o[...] = total if i == 0 else sum_o[...] + total
    out.forward()
    out.finish()
    job.finish()


def back_joint(du, dg, wu, wg, d1, first, ua, ca, cv, hid, rate):
    seqs, rows, width = first.shape
    part = jax.ShapeDtypeStruct((8, seqs, rows, width), BF)
    wide = lambda a: a.reshape(2, 2, 2, seqs * rows, a.shape[-1])
    return comm_call(
        back_joint_kernel, "back_joint", 3,
        (wide(du), wide(dg), wu, wg, d1, first, ua, ca, cv, hid, rate),
        [(first.shape, F32), ((1, width), F32), ((seqs, 4, rows, width), BF)],
        [pltpu.VMEM(part.shape, BF), pltpu.VMEM(first.shape, BF)]
        + PlaneReduce.scratch(part) + UlyGather.sems(seqs),
        30,
    )


def down_grad_kernel(d_ref, inner_ref, o_ref):
    grad = dot_tn(d_ref[...], inner_ref[...]).astype(BF)
    n_line, groups, each, _ = o_ref.shape
    for v in range(groups):
        for k in range(n_line):
            at = (v * n_line + k) * each
            o_ref[k, v] = grad[at : at + each]


def down_grad(n_line, d, inner):
    rows, width = d.shape
    columns = inner.shape[1]
    each = width // (4 * n_line)
    return pl.pallas_call(
        down_grad_kernel,
        grid=(2,),
        out_shape=jax.ShapeDtypeStruct((n_line, 4, each, columns), BF),
        in_specs=[
            pl.BlockSpec((rows, width // 2), lambda i: (0, i)),
            pl.BlockSpec((rows, columns), lambda i: (0, 0)),
        ],
        out_specs=pl.BlockSpec((n_line, 2, each, columns), lambda i: (0, i, 0, 0)),
        compiler_params=pltpu.CompilerParams(vmem_limit_bytes=VMEM_BYTES),
        cost_estimate=pl.CostEstimate(flops=2 * rows * width * columns, bytes_accessed=8_000_000, transcendentals=0),
        name="down_grad",
    )(d, inner)


def ff_grad_kernel(du_ref, dg_ref, x_ref, u_ref, g_ref):
    n_line, each, _ = u_ref.shape
    for ref, o_ref in ((du_ref, u_ref), (dg_ref, g_ref)):
        grad = dot_tn(ref[...], x_ref[...]).astype(BF)
        for k in range(n_line):
            o_ref[k] = grad[k * each : (k + 1) * each]


def ff_grad(n_line, du, dg, x):
    rows, width = x.shape
    columns = du.shape[1]
    whole = pl.BlockSpec((rows, columns), lambda i: (0, 0))
    shape = (n_line, columns // n_line, width)
    return pl.pallas_call(
        ff_grad_kernel,
        grid=(2,),
        out_shape=[jax.ShapeDtypeStruct(shape, BF)] * 2,
        in_specs=[whole, whole, pl.BlockSpec((rows, width // 2), lambda i: (0, i))],
        out_specs=[pl.BlockSpec(shape[:2] + (width // 2,), lambda i: (0, 0, i))] * 2,
        compiler_params=pltpu.CompilerParams(vmem_limit_bytes=VMEM_BYTES),
        cost_estimate=pl.CostEstimate(flops=4 * rows * width * columns, bytes_accessed=10_000_000, transcendentals=0),
        name="ff_grad",
    )(du, dg, x)
def local(
    hidden, positions, w_query, w_key, w_value, w_out, w_up, w_gate, w_down,
    qk_scale, alpha_attn, alpha_mlp, up_scale, gate_scale, cotangent,
):
    seqs, rows_each, width = hidden.shape
    n_line = lax.axis_size("line")
    n_blk = 2 * n_line
    heads = HEADS // 4
    local_width = heads * HEAD_DIM
    group_rows = 4 * rows_each
    tokens = seqs * rows_each
    group_tokens = 4 * tokens
    plane_tokens = 8 * tokens
    attn_each, ff_each = w_query.shape[0], w_up.shape[0]
    ff_local = ff_each * n_line
    far, core, line, side = place()
    uly = far * 2 + core

    pieces = [v.astype(F32) for v in (qk_scale, alpha_attn, alpha_mlp, up_scale, gate_scale)]
    pieces.append(positions.reshape(-1).astype(F32))
    used = sum(v.shape[0] for v in pieces)
    room, at, small = used + -used % 1024, 0, 0.0
    for v in pieces:
        small = small + jnp.pad(v, (at, room - at - v.shape[0]))
        at += v.shape[0]
    small = small.reshape(-1, 128)

    up_full = lax.all_gather(w_up, "line", axis=0, tiled=True)

    hid_all, small_all, wq_all, wk_all, wv_all, out_cols, down_cols = entry(
        n_line, hidden, small, w_query, w_key, w_value, w_out, w_down
    )
    w_gate, up_full, hid_all = lax.optimization_barrier((w_gate, up_full, hid_all))
    gate_full = lax.all_gather(w_gate, "line", axis=0, tiled=True)

    flat = small_all.reshape(4, n_blk, -1)
    cut = [0, attn_each, 2 * attn_each, 3 * attn_each, 3 * attn_each + ff_each, 3 * attn_each + 2 * ff_each, used]
    own = lax.dynamic_slice_in_dim(flat, uly, 1, 0)[0]
    scale_wide = own[:, : cut[1]].reshape(heads, HEAD_DIM)
    attn_rate = flat[:, :, cut[1] : cut[2]].reshape(-1)
    mlp_rate = flat[:, :, cut[2] : cut[3]].reshape(-1)
    mine = lax.dynamic_slice_in_dim(own.reshape(n_line, 2, -1), side, 1, 1)[:, 0]
    up_wide = mine[:, cut[3] : cut[4]].reshape(-1)
    gate_wide = mine[:, cut[4] : cut[5]].reshape(-1)
    places = jnp.transpose(
        flat[:, :, cut[5] : cut[6]].reshape(4, n_blk, seqs, rows_each), (2, 1, 0, 3)
    ).reshape(seqs, n_blk, 1, group_rows)
    q_places = lax.dynamic_slice_in_dim(places, line * 2 + side, 1, 1)[:, 0]

    lane = jnp.arange(128) % HEAD_DIM
    freqs = rotary_base ** (-((lane % 32).astype(F32) * (2.0 / HEAD_DIM)))
    angles = q_places.reshape(group_tokens, 1) * freqs
    cos = jnp.cos(angles)
    sin = jnp.where(lane < 32, -1.0, 1.0) * jnp.sin(angles)
    scale_both = jnp.concatenate([scale_wide * HEAD_DIM**0.5, scale_wide], axis=1)[:, None]

    group_hidden = hid_all.reshape(group_tokens, width)
    wq = wq_all.reshape(heads, HEAD_DIM, width)
    wk = wk_all.reshape(heads, HEAD_DIM, width)
    wv = wv_all.reshape(heads, HEAD_DIM, width)
    qz, kv, y_both, c_both = heads_forward(group_hidden, wq, wk, wv, cos, sin, scale_both)
    qz = qz.reshape(seqs, group_rows, heads * 128)

    kv_all, out_all, attended, mixed, inverse = attend(
        n_line, qz, kv.reshape(seqs, group_rows, heads * 128),
        out_cols.reshape(1, 4 * attn_each, local_width), q_places, places,
    )
    out_all, gate_full, down_cols = lax.optimization_barrier((out_all, gate_full, down_cols))
    down_all = lax.all_gather(down_cols.reshape(8 * attn_each, ff_local), "line", axis=0, tiled=False)
    down_full = jnp.transpose(
        down_all.reshape(n_line, 4, 2, attn_each, ff_local), (1, 0, 2, 3, 4)
    ).reshape(width, ff_local)
    out_full = jnp.transpose(
        out_all.reshape(n_blk, 4, attn_each, local_width), (1, 0, 2, 3)
    ).reshape(width, local_width)

    first, unit_att, att_c, first_c, mlp_in = attn_joint(mixed, out_full, hidden, attn_rate[None])
    mlp_in = mlp_in.reshape(plane_tokens, width)
    inner, up_rows, gate_rows = ff_forward(mlp_in, up_full, gate_full, up_wide[None], gate_wide[None])
    layer_out, grad_first, grad_alpha_mlp, branch_low = ff_joint(
        inner, down_full, first, mlp_rate[None], cotangent
    )
    branch_low = branch_low.reshape(plane_tokens, width)
    grad_down = down_grad(n_line, branch_low, inner)
    branch_low, grad_down = lax.optimization_barrier((branch_low, grad_down))
    down_own = lax.psum_scatter(
        grad_down.reshape(n_line, 8 * attn_each, ff_local), "line", scatter_dimension=0, tiled=True
    ).reshape(8, attn_each, ff_local)
    up_low, gate_low, ff_scales = ff_back(
        branch_low, down_full, up_rows, gate_rows, up_wide[None], gate_wide[None]
    )
    grad_up_scale, grad_gate_scale = ff_scales[0], ff_scales[1]
    grad_up, grad_gate = ff_grad(n_line, up_low, gate_low, mlp_in)
    up_own = lax.psum_scatter(grad_up, "line", scatter_dimension=0, tiled=True)[0]
    up_low, grad_up, grad_gate = lax.optimization_barrier((up_low, grad_up, grad_gate))
    grad_residual, grad_alpha_attn, att_low = back_joint(
        up_low, gate_low, up_full, gate_full, grad_first, first, unit_att, att_c, first_c,
        hidden, attn_rate[None],
    )

    att_low, down_own = lax.optimization_barrier((att_low, down_own))
    dq, dkv, out_own = attend_back(
        n_line, qz, att_low.reshape(seqs, group_rows, width), out_full, mixed, attended, inverse,
        kv_all, q_places, places,
    )
    dkv, grad_gate, up_own = lax.optimization_barrier((dkv, grad_gate, up_own))
    gate_own = lax.psum_scatter(grad_gate, "line", scatter_dimension=0, tiled=True)[0].astype(F32)
    out_own = out_own.reshape(4, attn_each, local_width)
    gq, gk, gv, gs, gh = heads_back(
        group_hidden, dq.reshape(group_tokens, -1), dkv.reshape(group_tokens, -1), y_both, c_both,
        cos, sin, scale_both, wq, wk, wv,
    )
    def row(x, wide):
        return jnp.pad(x, ((0, 0),) * (x.ndim - 1) + ((0, wide - x.shape[-1]),))

    alpha = jnp.concatenate(
        [grad_alpha_attn.reshape(4, n_blk, attn_each), grad_alpha_mlp.reshape(4, n_blk, attn_each)], axis=2
    )
    grad_scale = gs[:, 0, :HEAD_DIM] + gs[:, 0, HEAD_DIM:]
    ff_sums = jnp.concatenate(
        [grad_up_scale.reshape(n_line, ff_each), grad_gate_scale.reshape(n_line, ff_each)], axis=1
    )
    sides = (jnp.arange(2) == side)[None, :, None]
    ff_sums = jnp.where(sides, ff_sums[:, None], 0.0).reshape(n_blk, 2 * ff_each)
    rest = jnp.concatenate(
        [jnp.zeros((n_blk, 128), F32), row(grad_scale.reshape(n_blk, attn_each), 128), row(ff_sums, 384)], axis=1
    )
    gq, gk, gv, grad_hidden, out_gradient, down_gradient, sums = leave(
        n_line,
        *(g.reshape(n_blk, attn_each, width) for g in (gq, gk, gv)),
        gh.reshape(seqs, 4, rows_each, width),
        grad_residual,
        out_own, down_own, row(alpha, 128)[:, :, None], rest[:, None],
    )
    sums = sums[0]
    return (
        layer_out,
        grad_hidden,
        gq,
        gk,
        gv,
        out_gradient,
        up_own.astype(F32),
        gate_own,
        down_gradient,
        sums[128 : 128 + attn_each],
        sums[:attn_each],
        sums[attn_each : 2 * attn_each],
        sums[256 : 256 + ff_each],
        sums[256 + ff_each : 256 + 2 * ff_each],
    )


def solution(mesh):
    far = mesh.shape["uly"] // 2
    line = mesh.shape["blk"] // 2
    finer = Mesh(mesh.devices.reshape(far, 2, line, 2), AXES)
    rows, tokens, flat = P(AXES, None), P(None, AXES, None), P(AXES)
    return jax.shard_map(
        local,
        mesh=finer,
        in_specs=(tokens, P(None, AXES)) + (rows,) * 7 + (flat,) * 5 + (tokens,),
        out_specs=(tokens, tokens) + (rows,) * 7 + (flat,) * 5,
        check_vma=False,
    )
```

```python
import functools

import jax
import jax.numpy as jnp
from jax import lax
from jax.experimental import pallas as pl
from jax.experimental.pallas import tpu as pltpu
from jax.sharding import Mesh
from jax.sharding import PartitionSpec as P

D = 1280
HEADS = 20
HEAD_DIM = 64
AXES = ("far", "core", "line", "side")
PLANE = ("far", "core", "side")
VMEM_BYTES = 60 * 1024 * 1024

rotary_base = 10000.0
tiny_eps = 1e-06
BF = jnp.bfloat16
F32 = jnp.float32


def place():
    return tuple(lax.axis_index(name) for name in AXES)


def remote(src, dst, send, recv, device):
    return pltpu.make_async_remote_copy(
        src_ref=src,
        dst_ref=dst,
        send_sem=send,
        recv_sem=recv,
        device_id=device,
        device_id_type=pl.DeviceIdType.MESH,
    )


def signal_to(device):
    pl.semaphore_signal(
        pltpu.get_barrier_semaphore(), inc=1, device_id=device, device_id_type=pl.DeviceIdType.MESH
    )


def greet(devices, maybe=()):
    count = len(devices)
    for device in devices:
        signal_to(device)
    for there, device in maybe:
        pl.when(there)(functools.partial(signal_to, device))
        count = count + jnp.where(there, 1, 0)
    pl.semaphore_wait(pltpu.get_barrier_semaphore(), count)


def params(collective_id, room=VMEM_BYTES):
    return pltpu.CompilerParams(
        collective_id=collective_id, has_side_effects=True, vmem_limit_bytes=room
    )


class UlyGather:
    sems = staticmethod(lambda parts: [pltpu.SemaphoreType.DMA((3, parts))] * 2 + [pltpu.SemaphoreType.DMA((parts,))])

    def __init__(self, x, o, send, recv, local, pick=None):
        pick = pick or (lambda i, u: o.at[i, u])
        y, c, z, s = place()
        u, v = y * 2 + c, (1 - y) * 2 + c
        mate, across = (y, 1 - c, z, s), (1 - y, c, z, s)
        self.parts = x.shape[0]
        parts = range(self.parts)
        self.far = [remote(x.at[i], pick(i, u), send.at[0, i], recv.at[0, i], across) for i in parts]
        self.near = [remote(x.at[i], pick(i, u), send.at[1, i], recv.at[1, i], mate) for i in parts]
        self.on = [remote(pick(i, v), pick(i, v), send.at[2, i], recv.at[2, i], mate) for i in parts]
        self.own = [pltpu.make_async_copy(x.at[i], pick(i, u), local.at[i]) for i in parts]

    def start_part(self, i):
        self.far[i].start()
        self.near[i].start()
        self.own[i].start()

    def start(self):
        for i in range(self.parts):
            self.start_part(i)

    def forward(self):
        for i in range(self.parts):
            self.far[i].wait_recv()
            self.on[i].start()

    def finish(self):
        for i in range(self.parts):
            self.near[i].wait_recv()
            self.on[i].wait_recv()
            self.own[i].wait()
            self.far[i].wait_send()
            self.near[i].wait_send()
            self.on[i].wait_send()


def uly_peers():
    y, c, z, s = place()
    return [(y, 1 - c, z, s), (1 - y, c, z, s)]


def add_low(*terms):
    total = terms[0].astype(F32)
    for term in terms[1:]:
        total = total + term.astype(F32)
    return total


class UlyReduce:
    @staticmethod
    def scratch(x):
        parts, _, rows, width = x.shape
        return [
            pltpu.VMEM((parts, 2, rows, width), x.dtype),
            pltpu.VMEM((parts, rows, width), x.dtype),
            pltpu.VMEM((parts, rows, width), x.dtype),
            pltpu.SemaphoreType.DMA((3, parts)),
            pltpu.SemaphoreType.DMA((3, parts)),
        ]

    def __init__(self, x, near, mid, far_in, send, recv):
        y, c, z, s = place()
        mate, across = uly_peers()
        self.x, self.near_ref, self.mid, self.far_in = x, near, mid, far_in
        self.y, self.c, self.parts = y, c, x.shape[0]
        parts = range(self.parts)
        self.near = [
            [
                remote(x.at[i, f * 2 + 1 - c], near.at[i, k], send.at[k, i], recv.at[k, i], mate)
                for k, f in enumerate((1 - y, y))
            ]
            for i in parts
        ]
        self.far = [remote(mid.at[i], far_in.at[i], send.at[2, i], recv.at[2, i], across) for i in parts]

    def start(self):
        for i in range(self.parts):
            for copy in self.near[i]:
                copy.start()

    def middle(self):
        for i in range(self.parts):
            self.near[i][0].wait_recv()
            self.mid[i] = add_low(self.x[i, (1 - self.y) * 2 + self.c], self.near_ref[i, 0]).astype(BF)
            self.far[i].start()

    def result(self, i):
        self.near[i][1].wait_recv()
        self.far[i].wait_recv()
        return add_low(self.x[i, self.y * 2 + self.c], self.near_ref[i, 1], self.far_in[i])

    def finish(self):
        for i in range(self.parts):
            for copy in self.near[i] + [self.far[i]]:
                copy.wait_send()


def plane_peers():
    y, c, z, s = place()
    return [(y, 1 - c, z, s), (1 - y, c, z, s), (y, c, z, 1 - s)]


def plane_index(y, c, s):
    return (y * 2 + c) * 2 + s


class PlaneGather:
    @staticmethod
    def sems(parts):
        return [pltpu.SemaphoreType.DMA((7, parts))] * 2 + [pltpu.SemaphoreType.DMA((parts,))]

    def __init__(self, x, o, send, recv, local):
        y, c, z, s = place()
        mate, across, cross = plane_peers()
        self.parts = parts = range(x.shape[0])
        me, py, px, pd = (
            plane_index(y, c, s),
            plane_index(1 - y, c, s),
            plane_index(y, c, 1 - s),
            plane_index(1 - y, c, 1 - s),
        )

        def copy(source, p, i, slot, device):
            return remote(source, o.at[p, i], send.at[slot, i], recv.at[slot, i], device)

        def on(p, i, slot, device):
            return copy(o.at[p, i], p, i, slot, device)

        self.by_y = [copy(x.at[i], me, i, 0, across) for i in parts]
        self.by_x = [copy(x.at[i], me, i, 1, cross) for i in parts]
        self.near = [copy(x.at[i], me, i, 2, mate) for i in parts]
        self.corner = [on(px, i, 3, across) if i % 2 else on(py, i, 3, cross) for i in parts]
        self.pass_y = [on(py, i, 4, mate) for i in parts]
        self.pass_x = [on(px, i, 5, mate) for i in parts]
        self.pass_d = [on(pd, i, 6, mate) for i in parts]
        self.own = [pltpu.make_async_copy(x.at[i], o.at[me, i], local.at[i]) for i in parts]

    def start_part(self, i):
        for copy in (self.by_y[i], self.by_x[i], self.near[i], self.own[i]):
            copy.start()

    def forward_part(self, i):
        ways = [(self.by_y[i], self.pass_y[i]), (self.by_x[i], self.pass_x[i])]
        first, then = ways[:: 1 - 2 * (i % 2)]
        first[0].wait_recv()
        self.corner[i].start()
        first[1].start()
        then[0].wait_recv()
        then[1].start()

    def finish(self):
        for i in self.parts:
            self.corner[i].wait_recv()
            self.pass_d[i].start()
        for i in self.parts:
            for copy in (self.near[i], self.pass_y[i], self.pass_x[i], self.pass_d[i]):
                copy.wait()
            for copy in (self.by_y[i], self.by_x[i], self.corner[i]):
                copy.wait_send()
            self.own[i].wait()


class PlaneReduce:
    @staticmethod
    def scratch(x):
        one = pltpu.VMEM(x.shape[1:], x.dtype)
        sems = pltpu.SemaphoreType.DMA((7, x.shape[1]))
        return [pltpu.VMEM((4,) + x.shape[1:], x.dtype)] + [one] * 6 + [sems] * 2

    def __init__(self, x, near, out_x, out_y, out_d, in_x, in_y, in_d, send, recv):
        y, c, z, s = place()
        mate, across, cross = plane_peers()
        self.c = c
        self.parts = parts = range(x.shape[1])
        self.spots = ((1 - y, 1 - s), (y, 1 - s), (1 - y, s), (y, s))
        self.x, self.near_ref = x, near
        self.out_x, self.out_y, self.out_d = out_x, out_y, out_d
        self.in_x, self.in_y, self.in_d = in_x, in_y, in_d

        def copy(source, target, i, slot, device):
            return remote(source, target, send.at[slot, i], recv.at[slot, i], device)

        self.near = [
            [copy(x.at[plane_index(sy, 1 - c, ss), i], near.at[k, i], i, k, mate) for i in parts]
            for k, (sy, ss) in enumerate(self.spots)
        ]
        self.corner = [copy(out_d.at[i], in_d.at[i], i, 4, across if i % 2 else cross) for i in parts]
        self.by_x = [copy(out_x.at[i], in_x.at[i], i, 5, cross) for i in parts]
        self.by_y = [copy(out_y.at[i], in_y.at[i], i, 6, across) for i in parts]

    def pair(self, k, i):
        sy, ss = self.spots[k]
        self.near[k][i].wait_recv()
        return add_low(self.x[plane_index(sy, self.c, ss), i], self.near_ref[k, i])

    def start(self):
        for spot in self.near:
            for copy in spot:
                copy.start()

    def middle(self):
        for i in self.parts:
            self.out_d[i] = self.pair(0, i).astype(BF)
            self.corner[i].start()
            if i % 2 == 0:
                self.out_x[i] = self.pair(1, i).astype(BF)
                self.by_x[i].start()
            else:
                self.out_y[i] = self.pair(2, i).astype(BF)
                self.by_y[i].start()

    def last(self):
        for i in self.parts:
            k, out, by = (1, self.out_x, self.by_x) if i % 2 else (2, self.out_y, self.by_y)
            part = self.pair(k, i)
            self.corner[i].wait_recv()
            out[i] = (part + self.in_d[i].astype(F32)).astype(BF)
            by[i].start()

    def result(self, i):
        own = self.pair(3, i)
        self.by_x[i].wait_recv()
        self.by_y[i].wait_recv()
        return own + add_low(self.in_x[i], self.in_y[i])

    def finish(self):
        for copy in [c for spot in self.near for c in spot] + self.corner + self.by_x + self.by_y:
            copy.wait_send()


def plane_corners():
    y, c, z, s = place()
    return [
        (y, 1 - c, s), (1 - y, c, s), (1 - y, 1 - c, s),
        (y, c, 1 - s), (y, 1 - c, 1 - s), (1 - y, c, 1 - s), (1 - y, 1 - c, 1 - s),
    ]


def line_ends(n_line):
    y, c, z, s = place()
    return (z > 0, (y, c, z - 1, s)), (z < n_line - 1, (y, c, z + 1, s)), (y, c, z, 1 - s)


class BlkGather:
    @staticmethod
    def sems(n_line):
        return [
            pltpu.SemaphoreType.DMA((3,)),
            pltpu.SemaphoreType.DMA((1,)),
            pltpu.SemaphoreType.DMA((4, n_line)),
            pltpu.SemaphoreType.DMA((4, n_line)),
            pltpu.SemaphoreType.DMA((1,)),
        ]

    def __init__(self, n_line, pick_x, pick_o, own_send, own_recv, send, recv, local):
        y, c, z, s = place()
        self.z, self.s, self.n = z, s, n_line
        (self.has_low, self.low), (self.has_high, self.high), self.cross = line_ends(n_line)
        self.pick_x, self.pick_o = pick_x, pick_o
        self.sem = (own_send, own_recv, send, recv, local)

    def block(self, way, k):
        z = self.z - k if way == 0 else self.z + k
        return self.pick_o(z * 2 + self.s)

    def own(self, way):
        own_send, own_recv, send, recv, local = self.sem
        arrival = own_recv.at[0] if way == 2 else recv.at[way, 0]
        target = (self.high, self.low, self.cross)[way]
        return remote(self.pick_x(), self.pick_o(self.z * 2 + self.s), own_send.at[way], arrival, target)

    def keep(self):
        return pltpu.make_async_copy(self.pick_x(), self.pick_o(self.z * 2 + self.s), self.sem[4].at[0])

    def onward(self, way, k):
        send, recv = self.sem[2:4]
        target = self.high if way == 0 else self.low
        return remote(self.block(way, k), self.block(way, k), send.at[way, k], recv.at[way, k], target)

    def over(self, way, k):
        send, recv = self.sem[2:4]
        return remote(self.block(way, k), self.block(way, k), send.at[2 + way, k], recv.at[2 + way, k], self.cross)

    def arrive(self, way, k):
        send, recv = self.sem[2:4]
        return remote(self.block(way, k), self.block(way, k), send.at[way, k], recv.at[way, k - 1], self.cross)

    def there(self, way, k):
        return self.z >= k if way == 0 else self.z + k < self.n

    def start(self):
        pl.when(self.has_high)(lambda: self.own(0).start())
        pl.when(self.has_low)(lambda: self.own(1).start())
        self.own(2).start()
        self.keep().start()

    def take(self, way, k):
        self.arrive(way, k).wait_recv()
        pl.when((self.has_high, self.has_low)[way])(lambda: self.onward(way, k).start())
        self.over(way, k).start()

    def step(self, k):
        for way in (0, 1):
            pl.when(self.there(way, k))(lambda: self.take(way, k))

    def finish_arrivals(self):
        self.own(2).wait_recv()
        for k in range(1, self.n):
            for way in (0, 1):
                pl.when(self.there(way, k))(lambda: self.over(way, k).wait_recv())
        self.keep().wait()

    def finish_sends(self):
        pl.when(self.has_high)(lambda: self.own(0).wait_send())
        pl.when(self.has_low)(lambda: self.own(1).wait_send())
        self.own(2).wait_send()
        for k in range(1, self.n):
            for way in (0, 1):
                @pl.when(self.there(way, k))
                def _():
                    self.over(way, k).wait_send()

                    @pl.when((self.has_high, self.has_low)[way])
                    def _():
                        self.onward(way, k).wait_send()


def blk_greet(n_line):
    low, high, cross = line_ends(n_line)
    greet([cross], [low, high])


class BlkReduce:
    @staticmethod
    def scratch(n_line, a):
        return [
            pltpu.VMEM((n_line,) + a.shape[1:], a.dtype),
            pltpu.VMEM((n_line + 1,) + a.shape[1:], a.dtype),
            pltpu.SemaphoreType.DMA((n_line,)),
            pltpu.SemaphoreType.DMA((n_line,)),
            pltpu.SemaphoreType.DMA((2, n_line)),
            pltpu.SemaphoreType.DMA((2, n_line)),
        ]

    def __init__(self, n_line, x, side_in, line_in, side_send, side_recv, send, recv):
        y, c, self.z, self.s = place()
        self.n = n_line
        (self.has_low, self.low), (self.has_high, self.high), self.cross = line_ends(n_line)
        self.x = x
        self.side_in, self.line_in = side_in, line_in
        self.sem = (side_send, side_recv, send, recv)

    def spot(self, way, k):
        return self.z + k if way == 0 else self.z - k

    def exists(self, way, k):
        return self.z + k < self.n if way == 0 else self.z >= k

    def side(self, zz):
        side_send, side_recv = self.sem[:2]
        return remote(
            self.x.at[zz * 2 + 1 - self.s], self.side_in.at[zz], side_send.at[zz], side_recv.at[zz], self.cross
        )

    def slot(self, way, k):
        return jnp.where(k == 0, self.n, self.spot(way, k)) if way == 1 else self.spot(way, k)

    def move(self, way, k):
        send, recv = self.sem[2:]
        target = self.high if way == 0 else self.low
        zz = self.spot(way, k)
        there = jnp.where(k == 1, self.n, zz) if way == 1 else zz
        return remote(
            self.side_in.at[zz], self.line_in.at[there], send.at[way, k], recv.at[way, k - 1], target
        )

    def arrive(self, way, k):
        send, recv = self.sem[2:]
        there = self.line_in.at[self.slot(way, k)]
        return remote(there, there, send.at[way, k], recv.at[way, k], self.cross)

    def start(self, k):
        for way in (0, 1) if k > 0 else (0,):
            pl.when(self.exists(way, k))(lambda: self.side(self.spot(way, k)).start())

    def move_on(self, way, k):
        zz = self.spot(way, k)
        self.side(zz).wait_recv()
        passed = self.has_low if way == 0 else self.has_high

        @pl.when(passed)
        def _():
            self.arrive(way, k).wait_recv()
            self.side_in[zz] = add_low(
                self.x[zz * 2 + self.s], self.side_in[zz], self.line_in[zz]
            ).astype(self.side_in.dtype)

        @pl.when(jnp.logical_not(passed))
        def _():
            self.side_in[zz] = add_low(self.x[zz * 2 + self.s], self.side_in[zz]).astype(
                self.side_in.dtype
            )

        self.move(way, k).start()

    def step(self, k):
        for way in (0, 1):
            pl.when(self.exists(way, k))(lambda: self.move_on(way, k))

    def result(self, o):
        z = self.z
        self.side(z).wait_recv()
        pl.when(self.has_low)(lambda: self.arrive(0, 0).wait_recv())
        pl.when(self.has_high)(lambda: self.arrive(1, 0).wait_recv())
        own = add_low(self.x[z * 2 + self.s], self.side_in[z])

        @pl.when(jnp.logical_and(self.has_low, self.has_high))
        def _():
            o[...] = (own + add_low(self.line_in[z], self.line_in[self.n])).astype(o.dtype)

        @pl.when(jnp.logical_not(self.has_low))
        def _():
            o[...] = (own + self.line_in[self.n].astype(F32)).astype(o.dtype)

        @pl.when(jnp.logical_not(self.has_high))
        def _():
            o[...] = (own + self.line_in[z].astype(F32)).astype(o.dtype)

    def finish(self):
        for k in range(self.n - 1, -1, -1):
            for way in (0, 1) if k > 0 else (0,):
                @pl.when(self.exists(way, k))
                def _():
                    self.side(self.spot(way, k)).wait_send()
                    if k > 0:
                        self.move(way, k).wait_send()


class LineGather:
    @staticmethod
    def sems(n_line):
        dma = pltpu.SemaphoreType.DMA
        return [dma((2,)), dma((2, n_line)), dma((2, n_line)), dma((1,))]

    def __init__(self, n_line, pick_x, pick_o, own_send, send, recv, local):
        y, c, self.z, s = place()
        self.n = n_line
        (self.has_low, self.low), (self.has_high, self.high), _ = line_ends(n_line)
        self.pick_x, self.pick_o = pick_x, pick_o
        self.own_send, self.send, self.recv, self.local = own_send, send, recv, local

    def goes(self, way):
        return (self.has_high, self.has_low)[way]

    def own(self, way):
        target = (self.high, self.low)[way]
        return remote(self.pick_x(), self.pick_o(self.z), self.own_send.at[way], self.recv.at[way, 0], target)

    def keep(self):
        return pltpu.make_async_copy(self.pick_x(), self.pick_o(self.z), self.local.at[0])

    def onward(self, way, k):
        block = self.pick_o(self.z - k if way == 0 else self.z + k)
        target = (self.high, self.low)[way]
        return remote(block, block, self.send.at[way, k], self.recv.at[way, k], target)

    def arrive(self, way, k):
        block = self.pick_o(self.z - k if way == 0 else self.z + k)
        return remote(block, block, self.send.at[way, k], self.recv.at[way, k - 1], (self.low, self.high)[way])

    def there(self, way, k):
        return self.z >= k if way == 0 else self.z + k < self.n

    def start(self):
        for way in (0, 1):
            pl.when(self.goes(way))(lambda: self.own(way).start())
        self.keep().start()

    def step(self, k):
        for way in (0, 1):
            @pl.when(self.there(way, k))
            def _():
                self.arrive(way, k).wait_recv()
                pl.when(self.goes(way))(lambda: self.onward(way, k).start())

    def finish(self):
        self.keep().wait()
        for way in (0, 1):
            pl.when(self.goes(way))(lambda: self.own(way).wait_send())
            for k in range(1, self.n):
                pl.when(self.there(way, k) & self.goes(way))(lambda: self.onward(way, k).wait_send())


class LineReduce:
    @staticmethod
    def scratch(n_line, a):
        dma = pltpu.SemaphoreType.DMA
        return [
            pltpu.VMEM((n_line,) + a.shape[1:], a.dtype),
            pltpu.VMEM((n_line + 1,) + a.shape[1:], a.dtype),
            dma((2, n_line)), dma((2, n_line)),
        ]

    def __init__(self, n_line, x, sums, line_in, send, recv):
        y, c, self.z, s = place()
        self.n, self.x, self.sums, self.line_in, self.send, self.recv = n_line, x, sums, line_in, send, recv
        (self.has_low, self.low), (self.has_high, self.high), _ = line_ends(n_line)

    def spot(self, way, k):
        return self.z + k if way == 0 else self.z - k

    def exists(self, way, k):
        return self.z + k < self.n if way == 0 else self.z >= k

    def slot(self, way, k):
        return jnp.where(k == 0, self.n, self.spot(way, k)) if way == 1 else self.spot(way, k)

    def move(self, way, k):
        zz = self.spot(way, k)
        there = jnp.where(k == 1, self.n, zz) if way == 1 else zz
        return remote(
            self.sums.at[zz], self.line_in.at[there], self.send.at[way, k], self.recv.at[way, k - 1],
            (self.high, self.low)[way],
        )

    def arrive(self, way, k):
        there = self.line_in.at[self.slot(way, k)]
        return remote(there, there, self.send.at[way, k], self.recv.at[way, k], (self.low, self.high)[way])

    def step(self, k):
        for way in (0, 1):
            @pl.when(self.exists(way, k))
            def _():
                zz = self.spot(way, k)
                passed = (self.has_low, self.has_high)[way]

                @pl.when(passed)
                def _():
                    self.arrive(way, k).wait_recv()
                    self.sums[zz] = add_low(self.x[zz], self.line_in[zz]).astype(self.sums.dtype)

                @pl.when(jnp.logical_not(passed))
                def _():
                    self.sums[zz] = self.x[zz]

                self.move(way, k).start()

    def result(self, o):
        z = self.z
        pl.when(self.has_low)(lambda: self.arrive(0, 0).wait_recv())
        pl.when(self.has_high)(lambda: self.arrive(1, 0).wait_recv())

        @pl.when(self.has_low & self.has_high)
        def _():
            o[...] = add_low(self.x[z], self.line_in[z], self.line_in[self.n]).astype(o.dtype)

        @pl.when(jnp.logical_not(self.has_low))
        def _():
            o[...] = add_low(self.x[z], self.line_in[self.n]).astype(o.dtype)

        @pl.when(jnp.logical_not(self.has_high))
        def _():
            o[...] = add_low(self.x[z], self.line_in[z]).astype(o.dtype)

    def finish(self):
        for k in range(self.n - 1, 0, -1):
            for way in (0, 1):
                pl.when(self.exists(way, k))(lambda: self.move(way, k).wait_send())


def lane_chunks(width):
    cut = width // 256 * 128
    return [slice(0, cut), slice(cut, width)]


LINE_CHUNKS = 2


def line_gathers(n_line, x, pick_o, sems):
    jobs = []
    for i, lanes in enumerate(lane_chunks(x.shape[-1])):
        cut = (slice(None),) * (len(x.shape) - 1) + (lanes,)
        jobs.append(
            LineGather(
                n_line, lambda cut=cut: x.at[cut], lambda z, cut=cut: pick_o(z).at[cut],
                *sems[4 * i : 4 * i + 4],
            )
        )
    return jobs


def line_gather_sems(n_line):
    return LineGather.sems(n_line) * LINE_CHUNKS


def line_reduces(n_line, x, scratch):
    jobs = []
    for i, lanes in enumerate(lane_chunks(x.shape[-1])):
        cut = (slice(None),) * (len(x.shape) - 1) + (lanes,)
        jobs.append((LineReduce(n_line, x.at[cut], *scratch[4 * i : 4 * i + 4]), cut[1:]))
    return jobs


def line_reduce_scratch(n_line, a):
    scratch = []
    for lanes in lane_chunks(a.shape[-1]):
        one = jax.ShapeDtypeStruct(a.shape[:-1] + (lanes.stop - lanes.start,), a.dtype)
        scratch += LineReduce.scratch(n_line, one)
    return scratch


def exit_kernel(
    n_line, gq, gk, gv, gh, res, oc, dc, alpha, rest, gg,
    gq_o, gk_o, gv_o, gh_o, go_o, gd_o, sum_o, gg_o, oc_o, dc_o,
    alpha_in, line_out, line_all, oc_s, oc_r, dc_s, dc_r, al_s, al_r, su_s, su_r, keep, *scratch,
):
    y, c, z, s = place()
    u, p, b, n_blk = y * 2 + c, plane_index(y, c, s), z * 2 + s, 2 * n_line
    low, high, cross = line_ends(n_line)
    corners = plane_corners()
    others = []
    for i in range(1, n_blk):
        to = lax.rem(b + i, n_blk)
        others.append((y, c, to // 2, lax.rem(to, 2)))
    once = [(to[3] != 1 - s) | (to[2] != z) for to in others]
    greet([(yy, cc, z, ss) for yy, cc, ss in corners], list(zip(once, others)))
    heads = 6
    jobs = [BlkReduce(n_line, x, *scratch[heads * i : heads * (i + 1)]) for i, x in enumerate((gq, gk, gv))]
    split = heads * 3 + len(UlyReduce.scratch(gh))
    hid = UlyReduce(gh, *scratch[heads * 3 : split])
    gates = line_reduces(n_line, gg, scratch[split:])
    small, cols = [], []
    for k, (yy, cc, ss) in enumerate(corners):
        target = (yy, cc, z, ss)
        cols.append(remote(dc.at[plane_index(yy, cc, ss)], dc_o.at[p], dc_s.at[k], dc_r.at[k], target))
        if k < 3:
            cols.append(remote(oc.at[yy * 2 + cc], oc_o.at[u], oc_s.at[k], oc_r.at[k], target))
            small.append(remote(alpha.at[yy * 2 + cc], alpha_in.at[k], al_s.at[k], al_r.at[k], target))
    for job in small:
        job.start()
    hid.start()
    for k in range(n_line - 1, -1, -1):
        for job in jobs:
            job.start(k)
    mine = [
        pltpu.make_async_copy(dc.at[p], dc_o.at[p], keep.at[0]),
        pltpu.make_async_copy(oc.at[u], oc_o.at[u], keep.at[1]),
    ]
    for job in mine:
        job.start()
    hid.middle()
    for job in cols:
        job.start()
    for job in small:
        job.wait_recv()
    line_out[...] = rest[...]
    line_out[:, :, :128] = rest[:, :, :128] + alpha[u] + alpha_in[0] + alpha_in[1] + alpha_in[2]
    line_jobs = []
    for i in range(1, n_blk):
        to = lax.rem(b + i, n_blk)
        line_jobs.append(
            remote(line_out.at[to], line_all.at[i - 1], su_s.at[i - 1], su_r.at[i - 1], others[i - 1])
        )
    for job in line_jobs:
        job.start()
    for job, _ in gates:
        job.step(n_line - 1)
    for k in range(n_line - 1, 0, -1):
        for job in jobs:
            job.step(k)
        if k > 1:
            for job, _ in gates:
                job.step(k - 1)
    for i in range(gh.shape[0]):
        gh_o[i] = res[i] + hid.result(i)
    for job in cols:
        job.wait_recv()
    for job in mine:
        job.wait()
    wide, ff_each = oc.shape[-1], dc.shape[-1] // n_line
    for v in range(4):
        go_o[:, v * wide : (v + 1) * wide] = oc_o[v].astype(F32)
        for t in (0, 1):
            for k in range(n_line):
                at = ((v * n_line + k) * 2 + t) * ff_each
                gd_o[:, at : at + ff_each] = dc_o[v * 2 + t, :, k * ff_each : (k + 1) * ff_each].astype(F32)
    total = line_out[b]
    for i, job in enumerate(line_jobs):
        job.wait_recv()
        total = total + line_all[i]
    sum_o[...] = total
    for job, o in zip(jobs, (gq_o, gk_o, gv_o)):
        job.result(o)
    for job, cut in gates:
        job.result(gg_o.at[cut])
        job.finish()
    hid.finish()
    for job in jobs:
        job.finish()
    for job in line_jobs + small:
        job.wait_send()
    for job in cols:
        job.wait_send()


def leave(n_line, gq, gk, gv, gh, res, oc, dc, alpha, rest, gg):
    n_blk = 2 * n_line
    vmem = pl.BlockSpec(memory_space=pltpu.VMEM)
    dma = pltpu.SemaphoreType.DMA
    scratch = [
        pltpu.VMEM(oc.shape, oc.dtype),
        pltpu.VMEM(dc.shape, dc.dtype),
        pltpu.VMEM((3,) + alpha.shape[1:], F32),
        pltpu.VMEM(rest.shape, F32),
        pltpu.VMEM((n_blk - 1,) + rest.shape[1:], F32),
        dma((3,)), dma((3,)), dma((7,)), dma((7,)), dma((3,)), dma((3,)),
        dma((n_blk - 1,)), dma((n_blk - 1,)), dma((2,)),
    ]
    for g in (gq, gk, gv):
        scratch += BlkReduce.scratch(n_line, g)
    scratch += UlyReduce.scratch(gh) + line_reduce_scratch(n_line, gg)
    grad = jax.ShapeDtypeStruct(gq.shape[1:], F32)
    return pl.pallas_call(
        functools.partial(exit_kernel, n_line),
        out_shape=[
            grad, grad, grad,
            jax.ShapeDtypeStruct(res.shape, F32),
            jax.ShapeDtypeStruct((oc.shape[1], 4 * oc.shape[2]), F32),
            jax.ShapeDtypeStruct((dc.shape[1], 8 * dc.shape[2]), F32),
            jax.ShapeDtypeStruct(rest.shape[1:], F32),
            jax.ShapeDtypeStruct(gg.shape[1:], F32),
        ],
        in_specs=[vmem] * 10,
        out_specs=[vmem] * 8,
        scratch_shapes=scratch,
        compiler_params=params(8),
        cost_estimate=pl.CostEstimate(flops=0, bytes_accessed=40 * 3_000_000, transcendentals=0),
        name="leave",
    )(gq, gk, gv, gh, res, oc, dc, alpha, rest, gg)


def entry_kernel(
    n_line, hid, small, wq, wk, wv, wo, wd, wu,
    hid_o, small_o, wq_o, wk_o, wv_o, oc_o, dc_o, wu_o, oc, dc, *sems
):
    y, c, z, s = place()
    u, p = y * 2 + c, plane_index(y, c, s)
    low, high, cross = line_ends(n_line)
    corners = plane_corners()
    greet([(yy, cc, z, ss) for yy, cc, ss in corners], [low, high])
    hid_job = UlyGather(hid, hid_o, *sems[:3])
    at, jobs = 3, []
    for x, pick in (
        (small, lambda block: small_o.at[u, block]),
        (wq, lambda block: wq_o.at[block]),
        (wk, lambda block: wk_o.at[block]),
        (wv, lambda block: wv_o.at[block]),
    ):
        jobs.append(BlkGather(n_line, lambda x=x: x, pick, *sems[at : at + 5]))
        at += 5
    line_count = 4 * LINE_CHUNKS
    up_jobs = line_gathers(n_line, wu, lambda z: wu_o.at[z], sems[at : at + line_count])
    oc_s, oc_r, dc_s, dc_r, sm_s, sm_r, keep = sems[at + line_count :]
    jobs[0].start()
    for job in jobs[1:]:
        job.start()
    hid_job.start()
    for v in range(4):
        wide = oc.shape[-1]
        oc[v] = wo[:, v * wide : (v + 1) * wide]
        ff_each = dc.shape[-1] // n_line
        for t in (0, 1):
            for k in range(n_line):
                at = ((v * n_line + k) * 2 + t) * ff_each
                dc[v * 2 + t, :, k * ff_each : (k + 1) * ff_each] = wd[:, at : at + ff_each]
    col_jobs = []
    for k, (yy, cc, ss) in enumerate(corners):
        target = (yy, cc, z, ss)
        col_jobs.append(
            remote(dc.at[plane_index(yy, cc, ss)], dc_o.at[p], dc_s.at[k], dc_r.at[k], target)
        )
        if k < 3:
            col_jobs.append(remote(oc.at[yy * 2 + cc], oc_o.at[u], oc_s.at[k], oc_r.at[k], target))
    for job in col_jobs:
        job.start()
    for job in up_jobs:
        job.start()
    mine = [
        pltpu.make_async_copy(dc.at[p], dc_o.at[p], keep.at[0]),
        pltpu.make_async_copy(oc.at[u], oc_o.at[u], keep.at[1]),
    ]
    for job in mine:
        job.start()
    for k in range(1, n_line):
        for job in jobs:
            job.step(k)
        if k == 1:
            hid_job.forward()
    jobs[0].finish_arrivals()
    small_jobs = [
        remote(small_o.at[u], small_o.at[u], sm_s.at[k], sm_r.at[k], (yy, cc, z, ss))
        for k, (yy, cc, ss) in enumerate(corners[:3])
    ]
    for job in small_jobs:
        job.start()
    for k in range(1, n_line):
        for job in up_jobs:
            job.step(k)
    for job in jobs[1:]:
        job.finish_arrivals()
    hid_job.finish()
    for job in up_jobs:
        job.finish()
    for job in small_jobs + col_jobs:
        job.wait()
    for job in mine:
        job.wait()
    for job in jobs:
        job.finish_sends()


def entry(n_line, hid, small, wq, wk, wv, wo, wd, wu):
    n_blk = 2 * n_line
    oc = jax.ShapeDtypeStruct((4, wo.shape[0], wo.shape[1] // 4), wo.dtype)
    dc = jax.ShapeDtypeStruct((8, wd.shape[0], wd.shape[1] // 8), wd.dtype)
    parts = hid.shape[0]
    vmem, anyway = pl.BlockSpec(memory_space=pltpu.VMEM), pl.BlockSpec(memory_space=pl.ANY)

    def out(shape, like):
        return jax.ShapeDtypeStruct(shape, like.dtype)

    return pl.pallas_call(
        functools.partial(entry_kernel, n_line),
        out_shape=[
            out((parts, 4) + hid.shape[1:], hid),
            out((4, n_blk) + small.shape, small),
            out((n_blk,) + wq.shape, wq),
            out((n_blk,) + wk.shape, wk),
            out((n_blk,) + wv.shape, wv),
            out(oc.shape, oc),
            out(dc.shape, dc),
            out((n_line,) + wu.shape, wu),
        ],
        in_specs=[vmem] * 8,
        out_specs=[vmem, vmem, anyway, anyway, anyway, vmem, vmem, anyway],
        scratch_shapes=[pltpu.VMEM(oc.shape, oc.dtype), pltpu.VMEM(dc.shape, dc.dtype)]
        + UlyGather.sems(parts)
        + BlkGather.sems(n_line) * 4
        + line_gather_sems(n_line)
        + [pltpu.SemaphoreType.DMA((3,))] * 2
        + [pltpu.SemaphoreType.DMA((7,))] * 2
        + [pltpu.SemaphoreType.DMA((3,))] * 2
        + [pltpu.SemaphoreType.DMA((2,))],
        compiler_params=params(6),
        cost_estimate=pl.CostEstimate(flops=0, bytes_accessed=40 * 3_000_000, transcendentals=0),
        name="entry",
    )(hid, small, wq, wk, wv, wo, wd, wu)
def dot_nt(a, b):
    return lax.dot_general(a, b, (((1,), (1,)), ((), ())), preferred_element_type=F32)


def dot_nn(a, b):
    return lax.dot_general(a, b, (((1,), (0,)), ((), ())), preferred_element_type=F32)


def dot_tn(a, b):
    return lax.dot_general(a, b, (((0,), (0,)), ((), ())), preferred_element_type=F32)


def lanes_of(shape):
    return lax.broadcasted_iota(jnp.int32, shape, len(shape) - 1)


def halves(x):
    row = lax.broadcasted_iota(jnp.int32, (128, 128), 0) // HEAD_DIM
    same = jnp.where(row == lanes_of((128, 128)) // HEAD_DIM, 1.0, 0.0).astype(BF)
    high = x.astype(BF)
    rest = (x - high.astype(F32)).astype(BF)
    return dot_nn(high, same) + dot_nn(rest, same)


def turn(x):
    first = lanes_of(x.shape) % HEAD_DIM < HEAD_DIM // 2
    return jnp.where(first, pltpu.roll(x, 128 - 32, 1), pltpu.roll(x, 32, 1))


def heads_kernel(x_ref, wq_ref, wk_ref, wv_ref, cos_ref, sin_ref, scale_ref, qz_ref, kv_ref, y_ref, c_ref):
    x = x_ref[...]
    wv = wv_ref[0]
    got = dot_nt(x, jnp.concatenate([wq_ref[0], wk_ref[0], jnp.zeros_like(wv), wv], axis=0))
    raw, value = got[:, :128], got[:, 128:]
    low = lanes_of(raw.shape) < HEAD_DIM
    turned = raw * cos_ref[...] + turn(raw) * sin_ref[...]
    c = lax.rsqrt(halves(turned * turned) + HEAD_DIM * tiny_eps)
    y = turned * c
    both = y * scale_ref[0]
    qz_ref[...] = jnp.where(low, both, 0.0).astype(BF)
    kv_ref[...] = jnp.where(low, pltpu.roll(both, HEAD_DIM, 1), value).astype(BF)
    y_ref[...] = y
    c_ref[...] = c


def heads_forward(x, wq, wk, wv, cos, sin, scale):
    rows, width = x.shape
    heads = wq.shape[0]
    whole = lambda shape: pl.BlockSpec(shape, lambda h: (0,) * len(shape))
    weight = pl.BlockSpec((1, HEAD_DIM, width), lambda h: (h, 0, 0))
    head = pl.BlockSpec((rows, 128), lambda h: (0, h))
    wide = lambda dtype: jax.ShapeDtypeStruct((rows, heads * 128), dtype)
    return pl.pallas_call(
        heads_kernel,
        grid=(heads,),
        out_shape=[wide(BF), wide(BF), wide(F32), wide(F32)],
        in_specs=[whole((rows, width)), weight, weight, weight, whole((rows, 128)), whole((rows, 128)),
                  pl.BlockSpec((1, 1, 128), lambda h: (h, 0, 0))],
        out_specs=[head] * 4,
        compiler_params=pltpu.CompilerParams(vmem_limit_bytes=VMEM_BYTES),
        cost_estimate=pl.CostEstimate(flops=rows * width * heads * 384, bytes_accessed=rows * width * 8, transcendentals=0),
        name="heads_forward",
    )(x, wq, wk, wv, cos, sin, scale)


def down_columns(row):
    n = row.shape[1]
    one = jnp.transpose(jnp.broadcast_to(row, (128, n)))
    return jnp.concatenate([one] * (n // 128), axis=1)


def arrivals(n_line, body):
    each = 2 * n_line - 1

    def step(t, carry):
        stage, r = t // each, lax.rem(t, each)
        body(stage, (r + 1) // 2, lax.rem(r + 1, 2))
        return carry

    lax.fori_loop(0, 2 * each, step, 0)


def attend_kernel(
    n_line, q_ref, kv_ref, oc_ref, wg_ref, qp_ref, kp_ref,
    kv_o, oc_o, wg_o, o_ref, mixed_ref, inv_ref, acc, total, place_q, *sems,
):
    y, c, z, s = place()
    blk_greet(n_line)
    seqs, rows, wide = q_ref.shape
    heads = wide // 128
    each = len(BlkGather.sems(n_line))
    picks = [
        (lambda i=i: kv_ref.at[i], lambda block, i=i: kv_o.at[block, i]) for i in range(seqs)
    ] + [(lambda: oc_ref, lambda block: oc_o.at[:, block])]
    jobs = [
        BlkGather(n_line, *pick, *sems[each * i : each * (i + 1)]) for i, pick in enumerate(picks)
    ]
    gates = line_gathers(n_line, wg_ref, lambda z: wg_o.at[z], sems[each * (seqs + 1) :])
    for job in jobs:
        job.start()
    for job in gates:
        job.keep().start()
    acc[...] = jnp.zeros_like(acc)
    total[...] = jnp.zeros_like(total)
    for i in range(seqs):
        place_q[i] = down_columns(qp_ref[i])

    def attend_to(i, block, keys):
        allowed = kp_ref[i, block] <= place_q[i]
        for h in range(heads):
            lanes = slice(h * 128, (h + 1) * 128)
            kv = keys(lanes)
            p = jnp.where(allowed, jnp.exp(dot_nt(q_ref[i, :, lanes], kv)), 0.0)
            part = p[:, :128]
            for j in range(1, rows // 128):
                part = part + p[:, j * 128 : (j + 1) * 128]
            total[i, h] = total[i, h] + part
            acc[i, h] = acc[i, h] + dot_nn(p.astype(BF), kv)

    def body(stage, k, way):
        ahead = jnp.where(k == 0, 1, k + 1)

        @pl.when((stage == 1) & ((k == 0) | (way == 1)) & (ahead < n_line))
        def _():
            for job in gates:
                job.step(ahead)

        there = (k == 0) | jnp.where(way == 0, z >= k, z + k < n_line)

        @pl.when(there)
        def _():
            for job in jobs:
                for w in (0, 1):
                    pl.when((stage == 0) & (k > 0) & (way == w))(lambda: job.take(w, k))
                    pl.when((stage == 1) & (k > 0) & (way == w))(lambda: job.over(w, k).wait_recv())
                pl.when((stage == 1) & (k == 0))(lambda: job.own(2).wait_recv())
                pl.when((stage == 0) & (k == 0))(lambda: job.keep().wait())
            for w, last in ((0, z), (1, n_line - 1 - z)):
                @pl.when((stage == 0) & (k == last) & ((k == 0) | (way == w)))
                def _():
                    for job in gates:
                        pl.when(job.goes(w))(lambda: job.own(w).start())
            zz = jnp.where(way == 0, z - k, z + k)
            block = zz * 2 + jnp.where(stage == 0, s, 1 - s)
            for i in range(seqs):
                attend_to(i, block, lambda lanes: kv_o[block, i, :, lanes])

    arrivals(n_line, body)
    low = lanes_of((rows, 128)) < HEAD_DIM
    for i in range(seqs):
        outs = []
        for h in range(heads):
            inverse = 1.0 / jnp.broadcast_to(jnp.sum(total[i, h], axis=-1, keepdims=True), (rows, 128))
            out = acc[i, h] * inverse
            o_ref[i, h] = out
            inv_ref[i, h] = jnp.transpose(inverse)[:8]
            outs.append(out)
        for h in range(0, heads - 1, 2):
            mixed_ref[i, :, h * HEAD_DIM : (h + 2) * HEAD_DIM] = jnp.where(
                low, pltpu.roll(outs[h], HEAD_DIM, 1), outs[h + 1]
            ).astype(BF)
        if heads % 2 == 1:
            mixed_ref[i, :, (heads - 1) * HEAD_DIM :] = pltpu.roll(outs[-1], HEAD_DIM, 1)[:, :HEAD_DIM].astype(BF)
    for job in jobs:
        job.finish_sends()
    for job in gates:
        job.finish()


def attend(n_line, q, kv, oc, wg, q_places, k_places):
    seqs, rows, wide = q.shape
    n_blk, heads = 2 * n_line, wide // 128
    head = (seqs, heads, rows, 128)
    return comm_call(
        functools.partial(attend_kernel, n_line), "attend", 5, (q, kv, oc, wg, q_places, k_places),
        [
            ((n_blk,) + kv.shape, BF), (oc.shape[:1] + (n_blk,) + oc.shape[1:], BF),
            ((n_line,) + wg.shape, BF), (head, F32),
            ((seqs, rows, heads * HEAD_DIM), BF), ((seqs, heads, 8, rows), F32),
        ],
        [pltpu.VMEM(head, F32), pltpu.VMEM(head, F32), pltpu.VMEM((seqs, rows, rows), F32)]
        + BlkGather.sems(n_line) * (seqs + 1) + line_gather_sems(n_line),
        75, far_outs=(1, 2),
    )


def attend_back_kernel(
    n_line, fits, q_ref, low_ref, w_ref, mixed_ref, o_ref, inv_ref, kv_ref, qp_ref, kp_ref, gu_ref,
    dq_ref, dkv_ref, oc_ref, gu_o, dz, delta, dq, parts, oparts, key_s, key_sem, *scratch,
):
    y, c, z, s = place()
    blk_greet(n_line)
    seqs, rows, wide = q_ref.shape
    heads, width = wide // 128, low_ref.shape[-1]
    low_rows = low_ref[...].reshape(seqs * rows, width)
    grad = dot_tn(low_rows, mixed_ref[...].reshape(seqs * rows, mixed_ref.shape[-1])).astype(BF)
    n_blk, each_out = 2 * n_line, width // (8 * n_line)
    for b in range(n_blk):
        for v in range(4):
            at = (v * n_blk + b) * each_out
            oparts[b, v * each_out : (v + 1) * each_out] = grad[at : at + each_out]
    each = 6
    jobs = [BlkReduce(n_line, parts.at[:, i], *scratch[each * i : each * (i + 1)]) for i in range(seqs)]
    out_job = BlkReduce(n_line, oparts, *scratch[each * seqs : each * (seqs + 1)])
    ups = line_reduces(n_line, gu_ref, scratch[each * (seqs + 1) :])
    for k in range(n_line - 1, -1, -1):
        out_job.start(k)
    low = lanes_of((rows, 128)) < HEAD_DIM
    for i in range(seqs):
        d = dot_nn(low_rows[i * rows : (i + 1) * rows], w_ref[...]).astype(BF).astype(F32)
        for h in range(heads):
            at = h // 2 * 128
            if h == heads - 1 and heads % 2 == 1:
                tile = jnp.concatenate([jnp.zeros((rows, HEAD_DIM), F32), d[:, at:]], axis=1)
            else:
                tile = d[:, at : at + 128]
                if h % 2 == 0:
                    tile = pltpu.roll(tile, HEAD_DIM, 1)
                tile = jnp.where(low, 0.0, tile)
            dz[i, h] = tile.astype(BF)
            row = jnp.sum(tile * o_ref[i, h], axis=-1, keepdims=True)
            delta[i, h] = jnp.transpose(jnp.broadcast_to(row, (rows, 128)))[:8]
    dq[...] = jnp.zeros_like(dq)

    def block_of(block):
        if fits:
            keys = kv_ref.at[block]
        else:
            keys = key_s
            copy = pltpu.make_async_copy(kv_ref.at[block], key_s, key_sem.at[0])
            copy.start()
            copy.wait()
        for i in range(seqs):
            allowed = down_columns(kp_ref[i, block]) <= qp_ref[i]
            for h in range(heads):
                lanes = slice(h * 128, (h + 1) * 128)
                kv = keys[i, :, lanes]
                pair = jnp.concatenate([q_ref[i, :, lanes], dz[i, h]], axis=0)
                scores = dot_nt(kv, pair)
                p = jnp.where(allowed, jnp.exp(scores[:, :rows]) * inv_ref[i, h][:1], 0.0)
                ds = (p * (scores[:, rows:] - delta[i, h][:1])).astype(BF)
                parts[block, i, :, lanes] = dot_nn(
                    jnp.concatenate([ds, p.astype(BF)], axis=1), pair
                ).astype(BF)
                dq[i, h] = dq[i, h] + dot_tn(ds, kv)

    def step(t, carry):
        k, r = n_line - 1 - t // 4, lax.rem(t, 4)
        way, stays = r // 2, lax.rem(r, 2)

        @pl.when((r == 0) & (k > 0))
        def _():
            for line_job, _ in ups:
                line_job.step(k)

        there = jnp.where(k == 0, way == 0, jnp.where(way == 0, z + k < n_line, z >= k))

        @pl.when(there)
        def _():
            zz = jnp.where(way == 0, z + k, z - k)
            block_of(zz * 2 + jnp.where(stays == 0, 1 - s, s))

            @pl.when(stays == 0)
            def _():
                for job in jobs:
                    job.side(zz).start()

        @pl.when((r == 3) & (k + 1 < n_line))
        def _():
            for w in (0, 1):
                @pl.when(jobs[0].exists(w, k + 1))
                def _():
                    for job in jobs + [out_job]:
                        job.move_on(w, k + 1)

        return carry

    lax.fori_loop(0, 4 * n_line, step, 0)
    for i in range(seqs):
        for h in range(heads):
            dq_ref[i, :, h * 128 : (h + 1) * 128] = dq[i, h].astype(BF)
    out_job.result(oc_ref)
    for i, job in enumerate(jobs):
        job.result(dkv_ref.at[i])
    for job, cut in ups:
        job.result(gu_o.at[cut])
    for job in jobs + [out_job] + [job for job, _ in ups]:
        job.finish()


def attend_back(n_line, q, low, w, mixed, o, inv, kv, q_places, k_places, gu):
    seqs, rows, wide = q.shape
    n_blk, heads = 2 * n_line, wide // 128
    head = (seqs, heads, rows, 128)
    width, columns = w.shape
    out_shape = (width // n_blk, columns)
    one = jax.ShapeDtypeStruct((n_blk,) + kv.shape[2:], BF)
    out_one = jax.ShapeDtypeStruct((n_blk,) + out_shape, BF)
    fits = kv.size * 2 <= 8_000_000
    return comm_call(
        functools.partial(attend_back_kernel, n_line, fits), "attend_back", 7,
        (q, low, w, mixed, o, inv, kv, q_places, k_places, gu),
        [(q.shape, BF), (kv.shape[1:], BF), (out_shape, BF), (gu.shape[1:], F32)],
        [
            pltpu.VMEM(head, BF), pltpu.VMEM((seqs, heads, 8, rows), F32), pltpu.VMEM(head, F32),
            pltpu.VMEM(kv.shape, BF), pltpu.VMEM(out_one.shape, BF),
            pltpu.VMEM((16, 128) if fits else kv.shape[1:], BF), pltpu.SemaphoreType.DMA((1,)),
        ]
        + BlkReduce.scratch(n_line, one) * seqs + BlkReduce.scratch(n_line, out_one)
        + line_reduce_scratch(n_line, gu),
        75, 67_000_000, () if fits else (6,),
    )


def heads_back_kernel(
    x_ref, dq_ref, dkv_ref, y_ref, c_ref, cos_ref, sin_ref, scale_ref, wq_ref, wk_ref, wv_ref,
    gq_ref, gk_ref, gv_ref, gs_ref, gh_ref, acc_ref,
):
    h = pl.program_id(0)
    dq, dkv = dq_ref[...], dkv_ref[...]
    low = lanes_of(dq.shape) < HEAD_DIM
    dy = jnp.where(low, dq.astype(F32), pltpu.roll(dkv.astype(F32), HEAD_DIM, 1))
    y = y_ref[...]
    factor = jnp.where(lanes_of((1, 128)) < HEAD_DIM, HEAD_DIM**0.5, 1.0)
    gs_ref[0] = jnp.sum(dy * y, axis=0, keepdims=True) * factor
    dy = dy * scale_ref[0]
    dr = c_ref[...] * (dy - y * halves(y * dy))
    raw = (dr * cos_ref[...] - turn(dr) * sin_ref[...]).astype(BF)
    x = x_ref[...]
    value = jnp.where(low, jnp.zeros_like(dkv), dkv)
    both = jnp.concatenate([raw, value], axis=1)
    grad = dot_tn(both, x)
    gq_ref[0] = grad[:HEAD_DIM].astype(BF)
    gk_ref[0] = grad[HEAD_DIM : 2 * HEAD_DIM].astype(BF)
    gv_ref[0] = grad[3 * HEAD_DIM :].astype(BF)
    wv = wv_ref[0]
    more = dot_nn(both, jnp.concatenate([wq_ref[0], wk_ref[0], jnp.zeros_like(wv), wv], axis=0))

    @pl.when(h == 0)
    def _():
        acc_ref[...] = more

    @pl.when(h > 0)
    def _():
        acc_ref[...] = acc_ref[...] + more

    @pl.when(h == pl.num_programs(0) - 1)
    def _():
        gh_ref[...] = acc_ref[...].astype(BF)


def heads_back(x, dq, dkv, y, c, cos, sin, scale, wq, wk, wv):
    rows, width = x.shape
    heads = wq.shape[0]
    whole = lambda shape: pl.BlockSpec(shape, lambda h: (0,) * len(shape))
    weight = pl.BlockSpec((1, HEAD_DIM, width), lambda h: (h, 0, 0))
    head = pl.BlockSpec((rows, 128), lambda h: (0, h))
    row = pl.BlockSpec((1, 1, 128), lambda h: (h, 0, 0))
    return pl.pallas_call(
        heads_back_kernel,
        grid=(heads,),
        out_shape=[jax.ShapeDtypeStruct(wq.shape, BF)] * 3
        + [jax.ShapeDtypeStruct((heads, 1, 128), F32), jax.ShapeDtypeStruct((rows, width), BF)],
        in_specs=[whole((rows, width))] + [head] * 4 + [whole((rows, 128))] * 2 + [row] + [weight] * 3,
        out_specs=[weight] * 3 + [row, whole((rows, width))],
        scratch_shapes=[pltpu.VMEM((rows, width), F32)],
        compiler_params=pltpu.CompilerParams(vmem_limit_bytes=VMEM_BYTES),
        cost_estimate=pl.CostEstimate(flops=rows * width * heads * 1024, bytes_accessed=rows * width * 12, transcendentals=0),
        name="heads_back",
    )(x, dq, dkv, y, c, cos, sin, scale, wq, wk, wv)


def ff_kernel(x_ref, wu_ref, wg_ref, us_ref, gs_ref, inner_ref, up_ref, gate_ref):
    x = x_ref[...]
    up = dot_nt(x, wu_ref[...])
    gate = dot_nt(x, wg_ref[...])
    z = gate * gs_ref[...] * D**0.5
    inner_ref[...] = (z / (1.0 + jnp.exp(-z)) * (up * us_ref[...])).astype(BF)
    up_ref[...] = up
    gate_ref[...] = gate


def ff_forward(x, wu, wg, us, gs):
    rows, width = x.shape
    columns = wu.shape[0]
    block = rows // 4
    whole = lambda a: pl.BlockSpec(a.shape, lambda i: (0, 0))
    part = lambda n: pl.BlockSpec((block, n), lambda i: (i, 0))
    out = lambda dtype: jax.ShapeDtypeStruct((rows, columns), dtype)
    return pl.pallas_call(
        ff_kernel,
        grid=(4,),
        out_shape=[out(BF), out(F32), out(F32)],
        in_specs=[part(width)] + [whole(a) for a in (wu, wg, us, gs)],
        out_specs=[part(columns)] * 3,
        compiler_params=pltpu.CompilerParams(vmem_limit_bytes=VMEM_BYTES),
        cost_estimate=pl.CostEstimate(
            flops=4 * rows * width * columns, bytes_accessed=2 * rows * width + 10 * rows * columns,
            transcendentals=rows * columns,
        ),
        name="ff_forward",
    )(x, wu, wg, us, gs)


def unit_of(x):
    c = lax.rsqrt(jnp.sum(x * x, axis=-1, keepdims=True) + x.shape[-1] * tiny_eps)
    return x * c, c


def unit_back(y, c, dy):
    return c * (dy - y * jnp.sum(y * dy, axis=-1, keepdims=True))


class Late:
    @staticmethod
    def scratch(arrays):
        return [pltpu.VMEM(a.shape, a.dtype) for a in arrays] + [pltpu.SemaphoreType.DMA((len(arrays),))]

    def __init__(self, refs, scratch):
        *self.bufs, sem = scratch
        self.copies = [
            pltpu.make_async_copy(ref, buf, sem.at[i]) for i, (ref, buf) in enumerate(zip(refs, self.bufs))
        ]
        for copy in self.copies:
            copy.start()

    def __call__(self, i):
        self.copies[i].wait()
        return self.bufs[i]


def comm_call(kernel, name, collective_id, args, outs, scratch, micros, room=VMEM_BYTES, far_args=(), far_outs=()):
    vmem, anyway = pl.BlockSpec(memory_space=pltpu.VMEM), pl.BlockSpec(memory_space=pl.ANY)
    return pl.pallas_call(
        kernel,
        out_shape=[jax.ShapeDtypeStruct(shape, dtype) for shape, dtype in outs],
        in_specs=[anyway if i in far_args else vmem for i in range(len(args))],
        out_specs=[anyway if i in far_outs else vmem for i in range(len(outs))],
        scratch_shapes=scratch,
        compiler_params=params(collective_id, room),
        cost_estimate=pl.CostEstimate(flops=0, bytes_accessed=micros * 3_000_000, transcendentals=0),
        name=name,
    )(*args)


def attn_joint_kernel(
    n_line, mixed, w, hid, rate, dc, first_o, ua_o, ca_o, cv_o, all_o, down_o, part, low, *scratch
):
    ends = line_ends(n_line)
    greet(plane_peers(), ends[:2])
    split = len(UlyReduce.scratch(part))
    job = UlyReduce(part, *scratch[:split])
    out = PlaneGather(low, all_o, *scratch[split : split + 3])
    downs = line_gathers(n_line, dc, lambda z: down_o.at[:, z], scratch[split + 3 :])
    for line_job in downs:
        line_job.start()
    steps = [(k, line_job) for k in range(1, n_line) for line_job in downs]
    parts, _, rows, width = part.shape
    seqs = mixed.shape[0]
    each = parts // seqs
    for i in range(seqs):
        got = dot_nt(mixed[i], w[...]).astype(BF)
        for k in range(each):
            for u in range(4):
                at = (u * each + k) * rows
                part[i * each + k, u] = got[at : at + rows]
            for copy in job.near[i * each + k]:
                copy.start()
    job.middle()
    k, line_job = steps.pop(0)
    line_job.step(k)
    for i in range(parts):
        ua, ca = unit_of(job.result(i))
        h = hid[i].astype(F32)
        first, cv = unit_of(h + rate[...] * (ua - h))
        low[i] = first.astype(BF)
        out.start_part(i)
        first_o[i], ua_o[i] = first, ua
        ca_o[i] = jnp.broadcast_to(ca, (rows, 128))
        cv_o[i] = jnp.broadcast_to(cv, (rows, 128))
        if i > 0:
            out.forward_part(i - 1)
        if len(steps) > 0:
            k, line_job = steps.pop(0)
            line_job.step(k)
    out.forward_part(parts - 1)
    for k, line_job in steps:
        line_job.step(k)
    out.finish()
    job.finish()
    for line_job in downs:
        line_job.finish()


def attn_joint(n_line, mixed, w, hid, rate, dc):
    parts, rows, width = hid.shape
    part = jax.ShapeDtypeStruct((parts, 4, rows, width), BF)
    thin = ((parts, rows, 128), F32)
    return comm_call(
        functools.partial(attn_joint_kernel, n_line), "attn_joint", 1, (mixed, w, hid, rate, dc),
        [
            (hid.shape, F32), (hid.shape, F32), thin, thin, ((8, parts, rows, width), BF),
            (dc.shape[:1] + (n_line,) + dc.shape[1:], BF),
        ],
        [pltpu.VMEM(part.shape, BF), pltpu.VMEM(hid.shape, BF)]
        + UlyReduce.scratch(part) + PlaneGather.sems(parts) + line_gather_sems(n_line),
        25, far_outs=(5,),
    )


def plane_products(job, part, c, product, between=lambda: None):
    _, seqs, rows, width = part.shape
    for cc, first in ((1 - c, True), (c, False)):
        got = product(cc).astype(BF).reshape(2, 2, seqs, rows, width)
        for yy in (0, 1):
            for ss in (0, 1):
                part[plane_index(yy, cc, ss)] = got[yy, ss]
        if first:
            job.start()
            between()


def ff_joint_kernel(inner, w, first, rate, cot, out_o, d1_o, sum_o, all_o, part, low, *scratch):
    y, c, z, s = place()
    greet(plane_peers())
    split = len(PlaneReduce.scratch(part))
    job = PlaneReduce(part, *scratch[:split])
    out = PlaneGather(low, all_o, *scratch[split:])
    _, seqs, rows, width = part.shape
    columns = inner.shape[-1]
    plane_products(
        job, part, c, lambda cc: dot_nt(inner[:, cc].reshape(4 * seqs * rows, columns), w[...])
    )
    job.middle()
    job.last()
    for i in range(seqs):
        ub, cb = unit_of(job.result(i))
        f, b = first[i], rate[...]
        o, cw = unit_of(f + b * (ub - f))
        dw = unit_back(o, cw, cot[i].astype(F32))
        step = b * dw
        low[i] = unit_back(ub, cb, step).astype(BF)
        out.start_part(i)
        out_o[i] = o.astype(BF)
        d1_o[i] = dw - step
        total = jnp.sum(dw * (ub - f), axis=0, keepdims=True)
        sum_o[...] = total if i == 0 else sum_o[...] + total
        if i > 0:
            out.forward_part(i - 1)
    out.forward_part(seqs - 1)
    out.finish()
    job.finish()


def ff_joint(inner, w, first, rate, cot):
    seqs, rows, width = first.shape
    part = jax.ShapeDtypeStruct((8, seqs, rows, width), BF)
    return comm_call(
        ff_joint_kernel, "ff_joint", 2,
        (inner.reshape(2, 2, 2, seqs * rows, inner.shape[-1]), w, first, rate, cot),
        [(first.shape, BF), (first.shape, F32), ((1, width), F32), (part.shape, BF)],
        [pltpu.VMEM(part.shape, BF), pltpu.VMEM(first.shape, BF)] + PlaneReduce.scratch(part) + PlaneGather.sems(seqs),
        30,
    )


def back_joint_kernel(
    n_line, d, inner, us, gs, d1, first, ua, ca, cv, hid, rate, wd_h, up_h, gate_h, wu_h, wg_h, x_h,
    res_o, sum_o, ff_sum_o, all_o, up_o, gate_o, down_o, part, low, down_s, du, dg, *scratch,
):
    y, c, z, s = place()
    late = Late((wd_h, up_h, gate_h, wu_h, wg_h, x_h), scratch[:7])
    scratch = scratch[7:]
    greet(plane_peers(), line_ends(n_line)[:2])
    split = len(PlaneReduce.scratch(part))
    job = PlaneReduce(part, *scratch[:split])
    _, parts, rows, width = part.shape
    columns = du.shape[-1]
    tokens = 8 * parts * rows
    each = parts // all_o.shape[0]
    out = UlyGather(
        low, all_o, *scratch[split : split + 3],
        pick=lambda i, u: all_o.at[i // each, u, pl.ds(i % each * rows, rows)],
    )
    downs = line_reduces(n_line, down_s, scratch[split + 3 :])
    flat = lambda ref: ref[...].reshape(tokens, ref.shape[-1])

    grad = dot_tn(flat(d), flat(inner)).astype(BF)
    deep = width // (4 * n_line)
    for v in range(4):
        for k in range(n_line):
            at = (v * n_line + k) * deep
            down_s[k, v] = grad[at : at + deep]
    for line_job, _ in downs:
        line_job.step(n_line - 1)

    wd, up_ref, gate_ref = late(0), late(1), late(2)
    u_scale, g_scale = us[...], gs[...] * D**0.5

    def gated_back(yy, cc):
        got = dot_nn(d[yy, cc].reshape(tokens // 4, width), wd[...])
        up, gate = up_ref[yy, cc].reshape(got.shape), gate_ref[yy, cc].reshape(got.shape)
        gz = gate * g_scale
        sig = 1.0 / (1.0 + jnp.exp(-gz))
        d_up = got * (gz * sig)
        d_gate = got * (up * u_scale) * sig * (1.0 + gz * (1.0 - sig))
        du[yy, cc] = (d_up * u_scale).astype(BF).reshape(du.shape[2:])
        dg[yy, cc] = (d_gate * g_scale).astype(BF).reshape(dg.shape[2:])
        return jnp.sum(d_up * up, axis=0, keepdims=True), jnp.sum(d_gate * gate, axis=0, keepdims=True)

    sums = [gated_back(0, 1 - c), gated_back(1, 1 - c)]
    wu, wg = late(3), late(4)

    def product(cc):
        half = lambda ref: ref[:, cc].reshape(tokens // 2, columns)
        return dot_nn(half(du), wu[...]) + dot_nn(half(dg), wg[...])

    def rest():
        sums.extend([gated_back(0, c), gated_back(1, c)])
        ff_sum_o[0:1] = sum(a for a, _ in sums)
        ff_sum_o[1:2] = sum(b for _, b in sums) * D**0.5

    plane_products(job, part, c, product, rest)
    job.middle()
    steps = [(k, line_job) for k in range(n_line - 2, 0, -1) for line_job, _ in downs]
    job.last()
    x = late(5)

    def by_line(o, grad):
        n = columns // n_line
        for k in range(n_line):
            o[k] = grad[k * n : (k + 1) * n].astype(BF)

    by_line(up_o, dot_tn(flat(du), x[...]))
    for i in range(parts):
        f, h, u, a = first[i], hid[i].astype(F32), ua[i], rate[...]
        dv = unit_back(f, cv[i][:, :1], d1[i] + job.result(i))
        step = a * dv
        low[i] = unit_back(u, ca[i][:, :1], step).astype(BF)
        out.start_part(i)
        res_o[i] = dv - step
        total = jnp.sum(dv * (u - h), axis=0, keepdims=True)
        sum_o[...] = total if i == 0 else sum_o[...] + total
        if len(steps) > 0:
            k, line_job = steps.pop(0)
            line_job.step(k)
    for k, line_job in steps:
        line_job.step(k)
    by_line(gate_o, dot_tn(flat(dg), x[...]))
    out.forward()
    out.finish()
    job.finish()
    for line_job, cut in downs:
        line_job.result(down_o.at[cut])
        line_job.finish()


def back_joint(n_line, seqs, d, wd, up, gate, us, gs, wu, wg, x, inner, d1, first, ua, ca, cv, hid, rate):
    parts, rows, width = first.shape
    columns = wd.shape[1]
    part = jax.ShapeDtypeStruct((8, parts, rows, width), BF)
    down = jax.ShapeDtypeStruct((n_line, 4, width // (4 * n_line), columns), BF)
    by_line = ((n_line, columns // n_line, width), BF)
    wide = lambda a: a.reshape(2, 2, 2, parts * rows, a.shape[-1])
    thin = pltpu.VMEM((2, 2, 2, parts * rows, columns), BF)
    late = (wd, wide(up), wide(gate), wu, wg, x)
    return comm_call(
        functools.partial(back_joint_kernel, n_line), "back_joint", 3,
        (wide(d), wide(inner), us, gs, d1, first, ua, ca, cv, hid, rate) + late,
        [
            (first.shape, F32), ((1, width), F32), ((2, columns), F32),
            ((seqs, 4, parts * rows // seqs, width), BF), by_line, by_line, (down.shape[1:], BF),
        ],
        [pltpu.VMEM(part.shape, BF), pltpu.VMEM(first.shape, BF), pltpu.VMEM(down.shape, BF), thin, thin]
        + Late.scratch(late) + PlaneReduce.scratch(part) + UlyGather.sems(parts)
        + line_reduce_scratch(n_line, down),
        40, VMEM_BYTES, tuple(range(11, 17)),
    )


def settle_kernel(*refs):
    count = len(refs) // 2
    for x, o in zip(refs[:count], refs[count:]):
        o[...] = x[...]


def settle(*arrays):
    vmem = pl.BlockSpec(memory_space=pltpu.VMEM)
    return pl.pallas_call(
        settle_kernel,
        out_shape=[jax.ShapeDtypeStruct(a.shape, a.dtype) for a in arrays],
        in_specs=[vmem] * len(arrays),
        out_specs=[vmem] * len(arrays),
        compiler_params=pltpu.CompilerParams(vmem_limit_bytes=VMEM_BYTES),
        name="settle",
    )(*arrays)
def local(
    hidden, positions, w_query, w_key, w_value, w_out, w_up, w_gate, w_down,
    qk_scale, alpha_attn, alpha_mlp, up_scale, gate_scale, cotangent,
):
    seqs, rows_each, width = hidden.shape
    n_line = lax.axis_size("line")
    n_blk = 2 * n_line
    heads = HEADS // 4
    local_width = heads * HEAD_DIM
    group_rows = 4 * rows_each
    tokens = seqs * rows_each
    group_tokens = 4 * tokens
    plane_tokens = 8 * tokens
    attn_each, ff_each = w_query.shape[0], w_up.shape[0]
    ff_local = ff_each * n_line
    far, core, line, side = place()
    uly = far * 2 + core

    pieces = [v.astype(F32) for v in (qk_scale, alpha_attn, alpha_mlp, up_scale, gate_scale)]
    pieces.append(positions.reshape(-1).astype(F32))
    used = sum(v.shape[0] for v in pieces)
    room, at, small = used + -used % 1024, 0, 0.0
    for v in pieces:
        small = small + jnp.pad(v, (at, room - at - v.shape[0]))
        at += v.shape[0]
    small = small.reshape(-1, 128)

    hid_all, small_all, wq_all, wk_all, wv_all, out_cols, down_cols, up_full = entry(
        n_line, hidden, small, w_query, w_key, w_value, w_out, w_down, w_up
    )
    up_full = up_full.reshape(ff_local, width)

    flat = small_all.reshape(4, n_blk, -1)
    cut = [0, attn_each, 2 * attn_each, 3 * attn_each, 3 * attn_each + ff_each, 3 * attn_each + 2 * ff_each, used]
    own = lax.dynamic_slice_in_dim(flat, uly, 1, 0)[0]
    scale_wide = own[:, : cut[1]].reshape(heads, HEAD_DIM)
    attn_rate = flat[:, :, cut[1] : cut[2]].reshape(-1)
    mlp_rate = flat[:, :, cut[2] : cut[3]].reshape(-1)
    mine = lax.dynamic_slice_in_dim(own.reshape(n_line, 2, -1), side, 1, 1)[:, 0]
    up_wide = mine[:, cut[3] : cut[4]].reshape(-1)
    gate_wide = mine[:, cut[4] : cut[5]].reshape(-1)
    places = jnp.transpose(
        flat[:, :, cut[5] : cut[6]].reshape(4, n_blk, seqs, rows_each), (2, 1, 0, 3)
    ).reshape(seqs, n_blk, 1, group_rows)
    q_places = lax.dynamic_slice_in_dim(places, line * 2 + side, 1, 1)[:, 0]

    lane = jnp.arange(128) % HEAD_DIM
    freqs = rotary_base ** (-((lane % 32).astype(F32) * (2.0 / HEAD_DIM)))
    angles = q_places.reshape(group_tokens, 1) * freqs
    cos = jnp.cos(angles)
    sin = jnp.where(lane < 32, -1.0, 1.0) * jnp.sin(angles)
    scale_both = jnp.concatenate([scale_wide * HEAD_DIM**0.5, scale_wide], axis=1)[:, None]

    group_hidden = hid_all.reshape(group_tokens, width)
    wq = wq_all.reshape(heads, HEAD_DIM, width)
    wk = wk_all.reshape(heads, HEAD_DIM, width)
    wv = wv_all.reshape(heads, HEAD_DIM, width)
    qz, kv, y_both, c_both = heads_forward(group_hidden, wq, wk, wv, cos, sin, scale_both)
    qz = qz.reshape(seqs, group_rows, heads * 128)

    kv_all, out_all, gate_full, attended, mixed, inverse = attend(
        n_line, qz, kv.reshape(seqs, group_rows, heads * 128),
        out_cols, w_gate, q_places, places,
    )
    gate_full = gate_full.reshape(ff_local, width)
    out_full = out_all.reshape(width, local_width)

    fine = (2 * seqs, rows_each // 2, width)
    hidden_fine = hidden.reshape(fine)
    first, unit_att, att_c, first_c, mlp_in, down_full = attn_joint(
        n_line, mixed, out_full, hidden_fine, attn_rate[None],
        down_cols.reshape(4, 2 * attn_each, ff_local),
    )
    down_full = down_full.reshape(width, ff_local)
    mlp_in = mlp_in.reshape(plane_tokens, width)
    inner, up_rows, gate_rows = ff_forward(mlp_in, up_full, gate_full, up_wide[None], gate_wide[None])
    layer_out, grad_first, grad_alpha_mlp, branch_low = ff_joint(
        inner, down_full, first, mlp_rate[None], cotangent.reshape(fine)
    )
    branch_low = branch_low.reshape(plane_tokens, width)
    grad_residual, grad_alpha_attn, ff_scales, att_low, grad_up, grad_gate, down_own = back_joint(
        n_line, seqs, branch_low, down_full, up_rows, gate_rows, up_wide[None], gate_wide[None],
        up_full, gate_full, mlp_in, inner, grad_first, first, unit_att, att_c, first_c, hidden_fine,
        attn_rate[None],
    )
    grad_up_scale, grad_gate_scale = ff_scales[0], ff_scales[1]
    down_own = down_own.reshape(8, attn_each, ff_local)

    dq, dkv, out_own, up_own = attend_back(
        n_line, qz, att_low.reshape(seqs, group_rows, width), out_full, mixed, attended, inverse,
        kv_all, q_places, places, grad_up,
    )
    out_own = out_own.reshape(4, attn_each, local_width)
    gq, gk, gv, gs, gh = heads_back(
        group_hidden, dq.reshape(group_tokens, -1), dkv.reshape(group_tokens, -1), y_both, c_both,
        cos, sin, scale_both, wq, wk, wv,
    )
    def row(x, wide):
        return jnp.pad(x, ((0, 0),) * (x.ndim - 1) + ((0, wide - x.shape[-1]),))

    alpha = jnp.concatenate(
        [grad_alpha_attn.reshape(4, n_blk, attn_each), grad_alpha_mlp.reshape(4, n_blk, attn_each)], axis=2
    )
    grad_scale = gs[:, 0, :HEAD_DIM] + gs[:, 0, HEAD_DIM:]
    ff_sums = jnp.concatenate(
        [grad_up_scale.reshape(n_line, ff_each), grad_gate_scale.reshape(n_line, ff_each)], axis=1
    )
    sides = (jnp.arange(2) == side)[None, :, None]
    ff_sums = jnp.where(sides, ff_sums[:, None], 0.0).reshape(n_blk, 2 * ff_each)
    rest = jnp.concatenate(
        [jnp.zeros((n_blk, 128), F32), row(grad_scale.reshape(n_blk, attn_each), 128), row(ff_sums, 384)], axis=1
    )
    gq, gk, gv, grad_hidden, out_gradient, down_gradient, sums, gate_own = leave(
        n_line,
        *(g.reshape(n_blk, attn_each, width) for g in (gq, gk, gv)),
        gh.reshape(seqs, 4, rows_each, width),
        grad_residual.reshape(seqs, rows_each, width),
        out_own, down_own, row(alpha, 128)[:, :, None], rest[:, None], grad_gate,
    )
    sums = sums[0]
    layer_out, grad_hidden, gq, gk, gv, out_gradient, up_own, gate_own, down_gradient = settle(
        layer_out.reshape(hidden.shape), grad_hidden, gq, gk, gv, out_gradient, up_own, gate_own,
        down_gradient,
    )
    return (
        layer_out,
        grad_hidden,
        gq,
        gk,
        gv,
        out_gradient,
        up_own,
        gate_own,
        down_gradient,
        sums[128 : 128 + attn_each],
        sums[:attn_each],
        sums[attn_each : 2 * attn_each],
        sums[256 : 256 + ff_each],
        sums[256 + ff_each : 256 + 2 * ff_each],
    )


def solution(mesh):
    far = mesh.shape["uly"] // 2
    line = mesh.shape["blk"] // 2
    finer = Mesh(mesh.devices.reshape(far, 2, line, 2), AXES)
    rows, tokens, flat = P(AXES, None), P(None, AXES, None), P(AXES)
    return jax.shard_map(
        local,
        mesh=finer,
        in_specs=(tokens, P(None, AXES)) + (rows,) * 7 + (flat,) * 5 + (tokens,),
        out_specs=(tokens, tokens) + (rows,) * 7 + (flat,) * 5,
        check_vma=False,
    )
```

```python
import functools

import jax
import jax.numpy as jnp
from jax import lax
from jax.experimental import pallas as pl
from jax.experimental.pallas import tpu as pltpu
from jax.sharding import Mesh
from jax.sharding import PartitionSpec as P

D = 1280
HEADS = 20
HEAD_DIM = 64
AXES = ("far", "core", "line", "side")
PLANE = ("far", "core", "side")
VMEM_BYTES = 60 * 1024 * 1024

rotary_base = 10000.0
tiny_eps = 1e-06
BF = jnp.bfloat16
F32 = jnp.float32


def place():
    return tuple(lax.axis_index(name) for name in AXES)


def remote(src, dst, send, recv, device):
    return pltpu.make_async_remote_copy(
        src_ref=src,
        dst_ref=dst,
        send_sem=send,
        recv_sem=recv,
        device_id=device,
        device_id_type=pl.DeviceIdType.MESH,
    )


def signal_to(device):
    pl.semaphore_signal(
        pltpu.get_barrier_semaphore(), inc=1, device_id=device, device_id_type=pl.DeviceIdType.MESH
    )


def greet(devices, maybe=()):
    count = len(devices)
    for device in devices:
        signal_to(device)
    for there, device in maybe:
        pl.when(there)(functools.partial(signal_to, device))
        count = count + jnp.where(there, 1, 0)
    pl.semaphore_wait(pltpu.get_barrier_semaphore(), count)


def params(collective_id, room=VMEM_BYTES):
    return pltpu.CompilerParams(
        collective_id=collective_id, has_side_effects=True, vmem_limit_bytes=room
    )


class UlyGather:
    sems = staticmethod(lambda parts: [pltpu.SemaphoreType.DMA((3, parts))] * 2 + [pltpu.SemaphoreType.DMA((parts,))])

    def __init__(self, x, o, send, recv, local, pick=None):
        pick = pick or (lambda i, u: o.at[i, u])
        y, c, z, s = place()
        u, v = y * 2 + c, (1 - y) * 2 + c
        mate, across = (y, 1 - c, z, s), (1 - y, c, z, s)
        self.parts = x.shape[0]
        parts = range(self.parts)
        self.far = [remote(x.at[i], pick(i, u), send.at[0, i], recv.at[0, i], across) for i in parts]
        self.near = [remote(x.at[i], pick(i, u), send.at[1, i], recv.at[1, i], mate) for i in parts]
        self.on = [remote(pick(i, v), pick(i, v), send.at[2, i], recv.at[2, i], mate) for i in parts]
        self.own = [pltpu.make_async_copy(x.at[i], pick(i, u), local.at[i]) for i in parts]

    def start_part(self, i):
        self.far[i].start()
        self.near[i].start()
        self.own[i].start()

    def start(self):
        for i in range(self.parts):
            self.start_part(i)

    def forward(self):
        for i in range(self.parts):
            self.far[i].wait_recv()
            self.on[i].start()

    def finish(self):
        for i in range(self.parts):
            self.near[i].wait_recv()
            self.on[i].wait_recv()
            self.own[i].wait()
            self.far[i].wait_send()
            self.near[i].wait_send()
            self.on[i].wait_send()


def uly_peers():
    y, c, z, s = place()
    return [(y, 1 - c, z, s), (1 - y, c, z, s)]


def add_low(*terms):
    total = terms[0].astype(F32)
    for term in terms[1:]:
        total = total + term.astype(F32)
    return total


class UlyReduce:
    @staticmethod
    def scratch(x):
        parts, _, rows, width = x.shape
        return [
            pltpu.VMEM((parts, 2, rows, width), x.dtype),
            pltpu.VMEM((parts, rows, width), x.dtype),
            pltpu.VMEM((parts, rows, width), x.dtype),
            pltpu.SemaphoreType.DMA((3, parts)),
            pltpu.SemaphoreType.DMA((3, parts)),
        ]

    def __init__(self, x, near, mid, far_in, send, recv):
        y, c, z, s = place()
        mate, across = uly_peers()
        self.x, self.near_ref, self.mid, self.far_in = x, near, mid, far_in
        self.y, self.c, self.parts = y, c, x.shape[0]
        parts = range(self.parts)
        self.near = [
            [
                remote(x.at[i, f * 2 + 1 - c], near.at[i, k], send.at[k, i], recv.at[k, i], mate)
                for k, f in enumerate((1 - y, y))
            ]
            for i in parts
        ]
        self.far = [remote(mid.at[i], far_in.at[i], send.at[2, i], recv.at[2, i], across) for i in parts]

    def start(self):
        for i in range(self.parts):
            for copy in self.near[i]:
                copy.start()

    def middle(self):
        for i in range(self.parts):
            self.near[i][0].wait_recv()
            self.mid[i] = add_low(self.x[i, (1 - self.y) * 2 + self.c], self.near_ref[i, 0]).astype(BF)
            self.far[i].start()

    def result(self, i):
        self.near[i][1].wait_recv()
        self.far[i].wait_recv()
        return add_low(self.x[i, self.y * 2 + self.c], self.near_ref[i, 1], self.far_in[i])

    def finish(self):
        for i in range(self.parts):
            for copy in self.near[i] + [self.far[i]]:
                copy.wait_send()


def plane_peers():
    y, c, z, s = place()
    return [(y, 1 - c, z, s), (1 - y, c, z, s), (y, c, z, 1 - s)]


def plane_index(y, c, s):
    return (y * 2 + c) * 2 + s


class PlaneGather:
    @staticmethod
    def sems(parts):
        return [pltpu.SemaphoreType.DMA((7, parts))] * 2 + [pltpu.SemaphoreType.DMA((parts,))]

    def __init__(self, x, o, send, recv, local):
        y, c, z, s = place()
        mate, across, cross = plane_peers()
        self.parts = parts = range(x.shape[0])
        me, py, px, pd = (
            plane_index(y, c, s),
            plane_index(1 - y, c, s),
            plane_index(y, c, 1 - s),
            plane_index(1 - y, c, 1 - s),
        )

        def copy(source, p, i, slot, device):
            return remote(source, o.at[p, i], send.at[slot, i], recv.at[slot, i], device)

        def on(p, i, slot, device):
            return copy(o.at[p, i], p, i, slot, device)

        self.by_y = [copy(x.at[i], me, i, 0, across) for i in parts]
        self.by_x = [copy(x.at[i], me, i, 1, cross) for i in parts]
        self.near = [copy(x.at[i], me, i, 2, mate) for i in parts]
        self.corner = [on(px, i, 3, across) if i % 2 else on(py, i, 3, cross) for i in parts]
        self.pass_y = [on(py, i, 4, mate) for i in parts]
        self.pass_x = [on(px, i, 5, mate) for i in parts]
        self.pass_d = [on(pd, i, 6, mate) for i in parts]
        self.own = [pltpu.make_async_copy(x.at[i], o.at[me, i], local.at[i]) for i in parts]

    def start_part(self, i):
        for copy in (self.by_y[i], self.by_x[i], self.near[i], self.own[i]):
            copy.start()

    def forward_part(self, i):
        ways = [(self.by_y[i], self.pass_y[i]), (self.by_x[i], self.pass_x[i])]
        first, then = ways[:: 1 - 2 * (i % 2)]
        first[0].wait_recv()
        self.corner[i].start()
        first[1].start()
        then[0].wait_recv()
        then[1].start()

    def finish(self):
        for i in self.parts:
            self.corner[i].wait_recv()
            self.pass_d[i].start()
        for i in self.parts:
            for copy in (self.near[i], self.pass_y[i], self.pass_x[i], self.pass_d[i]):
                copy.wait()
            for copy in (self.by_y[i], self.by_x[i], self.corner[i]):
                copy.wait_send()
            self.own[i].wait()


class PlaneReduce:
    @staticmethod
    def scratch(x):
        one = pltpu.VMEM(x.shape[1:], x.dtype)
        sems = pltpu.SemaphoreType.DMA((7, x.shape[1]))
        return [pltpu.VMEM((4,) + x.shape[1:], x.dtype)] + [one] * 6 + [sems] * 2

    def __init__(self, x, near, out_x, out_y, out_d, in_x, in_y, in_d, send, recv):
        y, c, z, s = place()
        mate, across, cross = plane_peers()
        self.c = c
        self.parts = parts = range(x.shape[1])
        self.spots = ((1 - y, 1 - s), (y, 1 - s), (1 - y, s), (y, s))
        self.x, self.near_ref = x, near
        self.out_x, self.out_y, self.out_d = out_x, out_y, out_d
        self.in_x, self.in_y, self.in_d = in_x, in_y, in_d

        def copy(source, target, i, slot, device):
            return remote(source, target, send.at[slot, i], recv.at[slot, i], device)

        self.near = [
            [copy(x.at[plane_index(sy, 1 - c, ss), i], near.at[k, i], i, k, mate) for i in parts]
            for k, (sy, ss) in enumerate(self.spots)
        ]
        self.corner = [copy(out_d.at[i], in_d.at[i], i, 4, across if i % 2 else cross) for i in parts]
        self.by_x = [copy(out_x.at[i], in_x.at[i], i, 5, cross) for i in parts]
        self.by_y = [copy(out_y.at[i], in_y.at[i], i, 6, across) for i in parts]

    def pair(self, k, i):
        sy, ss = self.spots[k]
        self.near[k][i].wait_recv()
        return add_low(self.x[plane_index(sy, self.c, ss), i], self.near_ref[k, i])

    def start(self):
        for spot in self.near:
            for copy in spot:
                copy.start()

    def middle(self):
        for i in self.parts:
            self.out_d[i] = self.pair(0, i).astype(BF)
            self.corner[i].start()
            if i % 2 == 0:
                self.out_x[i] = self.pair(1, i).astype(BF)
                self.by_x[i].start()
            else:
                self.out_y[i] = self.pair(2, i).astype(BF)
                self.by_y[i].start()

    def last(self):
        for i in self.parts:
            k, out, by = (1, self.out_x, self.by_x) if i % 2 else (2, self.out_y, self.by_y)
            part = self.pair(k, i)
            self.corner[i].wait_recv()
            out[i] = (part + self.in_d[i].astype(F32)).astype(BF)
            by[i].start()

    def result(self, i):
        own = self.pair(3, i)
        self.by_x[i].wait_recv()
        self.by_y[i].wait_recv()
        return own + add_low(self.in_x[i], self.in_y[i])

    def finish(self):
        for copy in [c for spot in self.near for c in spot] + self.corner + self.by_x + self.by_y:
            copy.wait_send()


def plane_corners():
    y, c, z, s = place()
    return [
        (y, 1 - c, s), (1 - y, c, s), (1 - y, 1 - c, s),
        (y, c, 1 - s), (y, 1 - c, 1 - s), (1 - y, c, 1 - s), (1 - y, 1 - c, 1 - s),
    ]


def line_ends(n_line):
    y, c, z, s = place()
    return (z > 0, (y, c, z - 1, s)), (z < n_line - 1, (y, c, z + 1, s)), (y, c, z, 1 - s)


class BlkGather:
    @staticmethod
    def sems(n_line):
        return [
            pltpu.SemaphoreType.DMA((3,)),
            pltpu.SemaphoreType.DMA((1,)),
            pltpu.SemaphoreType.DMA((4, n_line)),
            pltpu.SemaphoreType.DMA((4, n_line)),
            pltpu.SemaphoreType.DMA((1,)),
        ]

    def __init__(self, n_line, pick_x, pick_o, own_send, own_recv, send, recv, local):
        y, c, z, s = place()
        self.z, self.s, self.n = z, s, n_line
        (self.has_low, self.low), (self.has_high, self.high), self.cross = line_ends(n_line)
        self.pick_x, self.pick_o = pick_x, pick_o
        self.sem = (own_send, own_recv, send, recv, local)

    def block(self, way, k):
        z = self.z - k if way == 0 else self.z + k
        return self.pick_o(z * 2 + self.s)

    def own(self, way):
        own_send, own_recv, send, recv, local = self.sem
        arrival = own_recv.at[0] if way == 2 else recv.at[way, 0]
        target = (self.high, self.low, self.cross)[way]
        return remote(self.pick_x(), self.pick_o(self.z * 2 + self.s), own_send.at[way], arrival, target)

    def keep(self):
        return pltpu.make_async_copy(self.pick_x(), self.pick_o(self.z * 2 + self.s), self.sem[4].at[0])

    def onward(self, way, k):
        send, recv = self.sem[2:4]
        target = self.high if way == 0 else self.low
        return remote(self.block(way, k), self.block(way, k), send.at[way, k], recv.at[way, k], target)

    def over(self, way, k):
        send, recv = self.sem[2:4]
        return remote(self.block(way, k), self.block(way, k), send.at[2 + way, k], recv.at[2 + way, k], self.cross)

    def arrive(self, way, k):
        send, recv = self.sem[2:4]
        return remote(self.block(way, k), self.block(way, k), send.at[way, k], recv.at[way, k - 1], self.cross)

    def there(self, way, k):
        return self.z >= k if way == 0 else self.z + k < self.n

    def start(self):
        pl.when(self.has_high)(lambda: self.own(0).start())
        pl.when(self.has_low)(lambda: self.own(1).start())
        self.own(2).start()
        self.keep().start()

    def take(self, way, k):
        self.arrive(way, k).wait_recv()
        pl.when((self.has_high, self.has_low)[way])(lambda: self.onward(way, k).start())
        self.over(way, k).start()

    def step(self, k):
        for way in (0, 1):
            pl.when(self.there(way, k))(lambda: self.take(way, k))

    def finish_arrivals(self):
        self.own(2).wait_recv()
        for k in range(1, self.n):
            for way in (0, 1):
                pl.when(self.there(way, k))(lambda: self.over(way, k).wait_recv())
        self.keep().wait()

    def finish_sends(self):
        pl.when(self.has_high)(lambda: self.own(0).wait_send())
        pl.when(self.has_low)(lambda: self.own(1).wait_send())
        self.own(2).wait_send()
        for k in range(1, self.n):
            for way in (0, 1):
                @pl.when(self.there(way, k))
                def _():
                    self.over(way, k).wait_send()

                    @pl.when((self.has_high, self.has_low)[way])
                    def _():
                        self.onward(way, k).wait_send()


def blk_greet(n_line):
    low, high, cross = line_ends(n_line)
    greet([cross], [low, high])


class BlkReduce:
    @staticmethod
    def scratch(n_line, a):
        return [
            pltpu.VMEM((n_line,) + a.shape[1:], a.dtype),
            pltpu.VMEM((n_line + 1,) + a.shape[1:], a.dtype),
            pltpu.SemaphoreType.DMA((n_line,)),
            pltpu.SemaphoreType.DMA((n_line,)),
            pltpu.SemaphoreType.DMA((2, n_line)),
            pltpu.SemaphoreType.DMA((2, n_line)),
        ]

    def __init__(self, n_line, x, side_in, line_in, side_send, side_recv, send, recv):
        y, c, self.z, self.s = place()
        self.n = n_line
        (self.has_low, self.low), (self.has_high, self.high), self.cross = line_ends(n_line)
        self.x = x
        self.side_in, self.line_in = side_in, line_in
        self.sem = (side_send, side_recv, send, recv)

    def spot(self, way, k):
        return self.z + k * (1 - 2 * way)

    def exists(self, way, k):
        return (self.spot(way, k) >= 0) & (self.spot(way, k) < self.n)

    def toward(self, way):
        y, c, z, s = place()
        return (y, c, z + 1 - 2 * way, s)

    def side(self, zz):
        side_send, side_recv = self.sem[:2]
        return remote(
            self.x.at[zz * 2 + 1 - self.s], self.side_in.at[zz], side_send.at[zz], side_recv.at[zz], self.cross
        )

    def slot(self, way, k):
        return jnp.where((way == 1) & (k == 0), self.n, self.spot(way, k))

    def move(self, way, k):
        send, recv = self.sem[2:]
        zz = self.spot(way, k)
        there = jnp.where((way == 1) & (k == 1), self.n, zz)
        return remote(
            self.side_in.at[zz], self.line_in.at[there], send.at[way, k], recv.at[way, k - 1], self.toward(way)
        )

    def arrive(self, way, k):
        send, recv = self.sem[2:]
        there = self.line_in.at[self.slot(way, k)]
        return remote(there, there, send.at[way, k], recv.at[way, k], self.toward(1 - way))

    def start(self, k):
        for way in (0, 1) if k > 0 else (0,):
            pl.when(self.exists(way, k))(lambda: self.side(self.spot(way, k)).start())

    def move_on(self, way, k):
        zz = self.spot(way, k)
        self.side(zz).wait_recv()
        passed = jnp.where(way == 0, self.has_low, self.has_high)

        @pl.when(passed)
        def _():
            self.arrive(way, k).wait_recv()
            self.side_in[zz] = add_low(
                self.x[zz * 2 + self.s], self.side_in[zz], self.line_in[zz]
            ).astype(self.side_in.dtype)

        @pl.when(jnp.logical_not(passed))
        def _():
            self.side_in[zz] = add_low(self.x[zz * 2 + self.s], self.side_in[zz]).astype(
                self.side_in.dtype
            )

        self.move(way, k).start()

    def step(self, k):
        def one(way, carry):
            pl.when(self.exists(way, k))(lambda: self.move_on(way, k))
            return carry

        lax.fori_loop(0, 2, one, 0)

    def result(self, o):
        z = self.z
        self.side(z).wait_recv()
        pl.when(self.has_low)(lambda: self.arrive(0, 0).wait_recv())
        pl.when(self.has_high)(lambda: self.arrive(1, 0).wait_recv())
        own = lambda: add_low(self.x[z * 2 + self.s], self.side_in[z])
        both = self.has_low & self.has_high

        @pl.when(both)
        def _():
            o[...] = (own() + add_low(self.line_in[z], self.line_in[self.n])).astype(o.dtype)

        @pl.when(jnp.logical_not(both))
        def _():
            other = self.line_in[jnp.where(self.has_low, z, self.n)].astype(F32)
            o[...] = (own() + other).astype(o.dtype)

    def finish(self):
        for k in range(self.n - 1, -1, -1):
            for way in (0, 1) if k > 0 else (0,):
                @pl.when(self.exists(way, k))
                def _():
                    self.side(self.spot(way, k)).wait_send()
                    if k > 0:
                        self.move(way, k).wait_send()


class LineGather:
    @staticmethod
    def sems(n_line):
        dma = pltpu.SemaphoreType.DMA
        return [dma((2,)), dma((2, n_line)), dma((2, n_line)), dma((1,))]

    def __init__(self, n_line, pick_x, pick_o, own_send, send, recv, local):
        y, c, self.z, s = place()
        self.n = n_line
        (self.has_low, self.low), (self.has_high, self.high), _ = line_ends(n_line)
        self.pick_x, self.pick_o = pick_x, pick_o
        self.own_send, self.send, self.recv, self.local = own_send, send, recv, local

    def goes(self, way):
        return (self.has_high, self.has_low)[way]

    def own(self, way):
        target = (self.high, self.low)[way]
        return remote(self.pick_x(), self.pick_o(self.z), self.own_send.at[way], self.recv.at[way, 0], target)

    def keep(self):
        return pltpu.make_async_copy(self.pick_x(), self.pick_o(self.z), self.local.at[0])

    def onward(self, way, k):
        block = self.pick_o(self.z - k if way == 0 else self.z + k)
        target = (self.high, self.low)[way]
        return remote(block, block, self.send.at[way, k], self.recv.at[way, k], target)

    def arrive(self, way, k):
        block = self.pick_o(self.z - k if way == 0 else self.z + k)
        return remote(block, block, self.send.at[way, k], self.recv.at[way, k - 1], (self.low, self.high)[way])

    def there(self, way, k):
        return self.z >= k if way == 0 else self.z + k < self.n

    def start(self):
        for way in (0, 1):
            pl.when(self.goes(way))(lambda: self.own(way).start())
        self.keep().start()

    def step(self, k):
        for way in (0, 1):
            @pl.when(self.there(way, k))
            def _():
                self.arrive(way, k).wait_recv()
                pl.when(self.goes(way))(lambda: self.onward(way, k).start())

    def finish(self):
        self.keep().wait()
        for way in (0, 1):
            pl.when(self.goes(way))(lambda: self.own(way).wait_send())
            for k in range(1, self.n):
                pl.when(self.there(way, k) & self.goes(way))(lambda: self.onward(way, k).wait_send())


class LineReduce:
    @staticmethod
    def scratch(n_line, a):
        dma = pltpu.SemaphoreType.DMA
        return [
            pltpu.VMEM((n_line,) + a.shape[1:], a.dtype),
            pltpu.VMEM((n_line + 1,) + a.shape[1:], a.dtype),
            dma((2, n_line)), dma((2, n_line)),
        ]

    def __init__(self, n_line, x, sums, line_in, send, recv):
        y, c, self.z, s = place()
        self.n, self.x, self.sums, self.line_in, self.send, self.recv = n_line, x, sums, line_in, send, recv
        (self.has_low, self.low), (self.has_high, self.high), _ = line_ends(n_line)

    def spot(self, way, k):
        return self.z + k * (1 - 2 * way)

    def exists(self, way, k):
        return (self.spot(way, k) >= 0) & (self.spot(way, k) < self.n)

    def passed(self, way):
        return jnp.where(way == 0, self.has_low, self.has_high)

    def slot(self, way, k):
        return jnp.where((way == 1) & (k == 0), self.n, self.spot(way, k))

    def toward(self, way):
        y, c, z, s = place()
        return (y, c, z + 1 - 2 * way, s)

    def move(self, way, k, source):
        zz = self.spot(way, k)
        there = jnp.where((way == 1) & (k == 1), self.n, zz)
        return remote(
            source.at[zz], self.line_in.at[there], self.send.at[way, k], self.recv.at[way, k - 1], self.toward(way)
        )

    def arrive(self, way, k):
        there = self.line_in.at[self.slot(way, k)]
        return remote(there, there, self.send.at[way, k], self.recv.at[way, k], self.toward(1 - way))

    def step(self, k):
        def one(way, carry):
            exists, passed = self.exists(way, k), self.passed(way)

            @pl.when(exists & passed)
            def _():
                zz = self.spot(way, k)
                self.arrive(way, k).wait_recv()
                self.sums[zz] = add_low(self.x[zz], self.line_in[zz]).astype(self.sums.dtype)
                self.move(way, k, self.sums).start()

            pl.when(exists & jnp.logical_not(passed))(lambda: self.move(way, k, self.x).start())
            return carry

        lax.fori_loop(0, 2, one, 0)

    def result(self, o):
        z = self.z
        pl.when(self.has_low)(lambda: self.arrive(0, 0).wait_recv())
        pl.when(self.has_high)(lambda: self.arrive(1, 0).wait_recv())
        both = self.has_low & self.has_high

        @pl.when(both)
        def _():
            o[...] = add_low(self.x[z], self.line_in[z], self.line_in[self.n]).astype(o.dtype)

        @pl.when(jnp.logical_not(both))
        def _():
            o[...] = add_low(self.x[z], self.line_in[jnp.where(self.has_low, z, self.n)]).astype(o.dtype)

    def finish(self):
        for k in range(self.n - 1, 0, -1):
            for way in (0, 1):
                pl.when(self.exists(way, k))(lambda: self.move(way, k, self.sums).wait_send())


def lane_chunks(width):
    cut = width // 256 * 128
    return [slice(0, cut), slice(cut, width)]


LINE_CHUNKS = 2


def line_gathers(n_line, x, pick_o, sems):
    jobs = []
    for i, lanes in enumerate(lane_chunks(x.shape[-1])):
        cut = (slice(None),) * (len(x.shape) - 1) + (lanes,)
        jobs.append(
            LineGather(
                n_line, lambda cut=cut: x.at[cut], lambda z, cut=cut: pick_o(z).at[cut],
                *sems[4 * i : 4 * i + 4],
            )
        )
    return jobs


def line_gather_sems(n_line):
    return LineGather.sems(n_line) * LINE_CHUNKS


def line_reduces(n_line, x, scratch):
    jobs = []
    for i, lanes in enumerate(lane_chunks(x.shape[-1])):
        cut = (slice(None),) * (len(x.shape) - 1) + (lanes,)
        jobs.append((LineReduce(n_line, x.at[cut], *scratch[4 * i : 4 * i + 4]), cut[1:]))
    return jobs


def line_reduce_scratch(n_line, a):
    scratch = []
    for lanes in lane_chunks(a.shape[-1]):
        one = jax.ShapeDtypeStruct(a.shape[:-1] + (lanes.stop - lanes.start,), a.dtype)
        scratch += LineReduce.scratch(n_line, one)
    return scratch


def exit_kernel(
    n_line, x, dq, dkv, yy_ref, cc_ref, cos, sin, scale, wq, wk, wv, res, oc, dc, alpha, rest, gg,
    gq_o, gk_o, gv_o, gh_o, go_o, gd_o, sum_o, gg_o, oc_o, dc_o,
    flat, acc, gq, gk, gv, gh, scale_s,
    alpha_in, line_out, line_all, oc_s, oc_r, dc_s, dc_r, al_s, al_r, su_s, su_r, keep, *scratch,
):
    y, c, z, s = place()
    u, p, b, n_blk = y * 2 + c, plane_index(y, c, s), z * 2 + s, 2 * n_line
    low, high, cross = line_ends(n_line)
    corners = plane_corners()
    others = []
    for i in range(1, n_blk):
        to = lax.rem(b + i, n_blk)
        others.append((y, c, to // 2, lax.rem(to, 2)))
    once = [(to[3] != 1 - s) | (to[2] != z) for to in others]
    greet([(yy, cc, z, ss) for yy, cc, ss in corners], list(zip(once, others)))
    each = 6
    jobs = [BlkReduce(n_line, g, *scratch[each * i : each * (i + 1)]) for i, g in enumerate((gq, gk, gv))]
    split = each * 3 + len(UlyReduce.scratch(gh))
    hid = UlyReduce(gh, *scratch[each * 3 : split])
    gates = line_reduces(n_line, gg, scratch[split:])
    small, cols = [], []
    for k, (yy, cc, ss) in enumerate(corners):
        target = (yy, cc, z, ss)
        cols.append(remote(dc.at[plane_index(yy, cc, ss)], dc_o.at[p], dc_s.at[k], dc_r.at[k], target))
        if k < 3:
            cols.append(remote(oc.at[yy * 2 + cc], oc_o.at[u], oc_s.at[k], oc_r.at[k], target))
            small.append(remote(alpha.at[yy * 2 + cc], alpha_in.at[k], al_s.at[k], al_r.at[k], target))
    for job in small:
        job.start()
    for job, _ in gates:
        job.step(n_line - 1)
    rows_all = x[...]
    seqs, group_rows, wide = dq.shape
    heads = wide // 128
    factor = jnp.where(lanes_of((1, 128)) < HEAD_DIM, HEAD_DIM**0.5, 1.0)
    late_steps = [(min(1 + 2 * i, heads - 1), k) for i, k in enumerate(range(n_line - 2, 0, -1))]

    def head(h, carry):
        lanes = pl.ds(pl.multiple_of(h * 128, 128), 128)
        queries = jnp.concatenate([dq[i, :, lanes] for i in range(seqs)], axis=0)
        pairs = jnp.concatenate([dkv[i, :, lanes] for i in range(seqs)], axis=0)
        low_half = lanes_of(queries.shape) < HEAD_DIM
        dy = jnp.where(low_half, queries.astype(F32), pltpu.roll(pairs.astype(F32), HEAD_DIM, 1))
        unit = yy_ref[:, lanes]
        scale_s[h] = jnp.sum(dy * unit, axis=0, keepdims=True) * factor
        dy = dy * scale[pl.ds(h, 1)]
        dr = cc_ref[:, lanes] * (dy - unit * halves(unit * dy))
        raw = (dr * cos[...] - turn(dr) * sin[...]).astype(BF)
        both = jnp.concatenate([raw, jnp.where(low_half, jnp.zeros_like(pairs), pairs)], axis=1)
        grad = dot_tn(both, rows_all).astype(BF)
        at = pl.ds(pl.multiple_of(h * HEAD_DIM, HEAD_DIM), HEAD_DIM)
        for j, lo in enumerate((0, HEAD_DIM, 3 * HEAD_DIM)):
            flat[j, at] = grad[lo : lo + HEAD_DIM]
        w_value = wv[h]
        more = dot_nn(both, jnp.concatenate([wq[h], wk[h], jnp.zeros_like(w_value), w_value], axis=0))

        @pl.when(h == 0)
        def _():
            acc[...] = more

        @pl.when(h > 0)
        def _():
            acc[...] = acc[...] + more

        for when, k in late_steps:
            @pl.when(h == when)
            def _():
                for job, _ in gates:
                    job.step(k)

        return carry

    lax.fori_loop(0, heads, head, 0)
    each_rows = gq.shape[1]
    for i, g in enumerate((gq, gk, gv)):
        for k in range(n_blk):
            g[k] = flat[i, k * each_rows : (k + 1) * each_rows]
    for i in range(seqs):
        gh[i] = acc[i * group_rows : (i + 1) * group_rows].astype(BF).reshape(gh.shape[1:])
    hid.start()
    for k in range(n_line - 1, -1, -1):
        for job in jobs:
            job.start(k)
    mine = [
        pltpu.make_async_copy(dc.at[p], dc_o.at[p], keep.at[0]),
        pltpu.make_async_copy(oc.at[u], oc_o.at[u], keep.at[1]),
    ]
    for job in mine:
        job.start()
    hid.middle()
    for job in cols:
        job.start()
    for job in small:
        job.wait_recv()
    line_out[...] = rest[...]
    line_out[:, :, :128] = alpha[u] + alpha_in[0] + alpha_in[1] + alpha_in[2]
    scales = jnp.concatenate(
        [scale_s[h][:, :HEAD_DIM] + scale_s[h][:, HEAD_DIM:] for h in range(heads)], axis=1
    )
    for k in range(n_blk):
        line_out[k, :, 128 : 128 + each_rows] = scales[:, k * each_rows : (k + 1) * each_rows]
    line_jobs = []
    for i in range(1, n_blk):
        to = lax.rem(b + i, n_blk)
        line_jobs.append(
            remote(line_out.at[to], line_all.at[i - 1], su_s.at[i - 1], su_r.at[i - 1], others[i - 1])
        )
    for job in line_jobs:
        job.start()
    for k in range(n_line - 1, 0, -1):
        for job in jobs:
            job.step(k)
    for i in range(gh.shape[0]):
        gh_o[i] = res[i] + hid.result(i)
    for job in cols:
        job.wait_recv()
    for job in mine:
        job.wait()
    wide, ff_each = oc.shape[-1], dc.shape[-1] // n_line
    for v in range(4):
        go_o[:, v * wide : (v + 1) * wide] = oc_o[v].astype(F32)
        for t in (0, 1):
            for k in range(n_line):
                at = ((v * n_line + k) * 2 + t) * ff_each
                gd_o[:, at : at + ff_each] = dc_o[v * 2 + t, :, k * ff_each : (k + 1) * ff_each].astype(F32)
    total = line_out[b]
    for i, job in enumerate(line_jobs):
        job.wait_recv()
        total = total + line_all[i]
    sum_o[...] = total
    for job, o in zip(jobs, (gq_o, gk_o, gv_o)):
        job.result(o)
    for job, cut in gates:
        job.result(gg_o.at[cut])
        job.finish()
    hid.finish()
    for job in jobs:
        job.finish()
    for job in line_jobs + small:
        job.wait_send()
    for job in cols:
        job.wait_send()


def leave(n_line, x, dq, dkv, y, c, cos, sin, scale, wq, wk, wv, res, oc, dc, alpha, rest, gg):
    n_blk = 2 * n_line
    heads, _, width = wq.shape
    seqs, rows, _ = res.shape
    vmem = pl.BlockSpec(memory_space=pltpu.VMEM)
    dma = pltpu.SemaphoreType.DMA
    grad = jax.ShapeDtypeStruct((n_blk, heads * HEAD_DIM // n_blk, width), BF)
    gh = jax.ShapeDtypeStruct((seqs, 4, rows, width), BF)
    scratch = [
        pltpu.VMEM(oc.shape, oc.dtype),
        pltpu.VMEM(dc.shape, dc.dtype),
        pltpu.VMEM((3, heads * HEAD_DIM, width), BF),
        pltpu.VMEM(x.shape, F32),
        pltpu.VMEM(grad.shape, BF), pltpu.VMEM(grad.shape, BF), pltpu.VMEM(grad.shape, BF),
        pltpu.VMEM(gh.shape, BF),
        pltpu.VMEM((heads, 1, 128), F32),
        pltpu.VMEM((3,) + alpha.shape[1:], F32),
        pltpu.VMEM(rest.shape, F32),
        pltpu.VMEM((n_blk - 1,) + rest.shape[1:], F32),
        dma((3,)), dma((3,)), dma((7,)), dma((7,)), dma((3,)), dma((3,)),
        dma((n_blk - 1,)), dma((n_blk - 1,)), dma((2,)),
    ]
    scratch += BlkReduce.scratch(n_line, grad) * 3
    scratch += UlyReduce.scratch(gh) + line_reduce_scratch(n_line, gg)
    args = (x, dq, dkv, y, c, cos, sin, scale, wq, wk, wv, res, oc, dc, alpha, rest, gg)
    outs = [grad.shape[1:]] * 3 + [
        res.shape, (oc.shape[1], 4 * oc.shape[2]), (dc.shape[1], 8 * dc.shape[2]), rest.shape[1:], gg.shape[1:]
    ]
    return pl.pallas_call(
        functools.partial(exit_kernel, n_line),
        out_shape=[jax.ShapeDtypeStruct(shape, F32) for shape in outs],
        in_specs=[vmem] * len(args),
        out_specs=[vmem] * len(outs),
        scratch_shapes=scratch,
        compiler_params=params(8),
        name="leave",
    )(*args)


def entry_kernel(
    n_line, hid, small, wq, wk, wv, wo, wd, wu,
    hid_o, small_o, wq_o, wk_o, wv_o, oc_o, dc_o, wu_o, oc, dc, *sems
):
    y, c, z, s = place()
    u, p = y * 2 + c, plane_index(y, c, s)
    low, high, cross = line_ends(n_line)
    corners = plane_corners()
    greet([(yy, cc, z, ss) for yy, cc, ss in corners], [low, high])
    hid_job = UlyGather(hid, hid_o, *sems[:3])
    at, jobs = 3, []
    for x, pick in (
        (small, lambda block: small_o.at[u, block]),
        (wq, lambda block: wq_o.at[block]),
        (wk, lambda block: wk_o.at[block]),
        (wv, lambda block: wv_o.at[block]),
    ):
        jobs.append(BlkGather(n_line, lambda x=x: x, pick, *sems[at : at + 5]))
        at += 5
    first = wu_o.shape[-1]
    up_jobs = [
        LineGather(n_line, lambda: wu.at[:, slice(0, first)], lambda z: wu_o.at[z], *sems[at : at + 4])
    ]
    oc_s, oc_r, dc_s, dc_r, sm_s, sm_r, keep = sems[at + 4 :]
    jobs[0].start()
    for job in jobs[1:]:
        job.start()
    hid_job.start()
    for v in range(4):
        wide = oc.shape[-1]
        oc[v] = wo[:, v * wide : (v + 1) * wide]
        ff_each = dc.shape[-1] // n_line
        for t in (0, 1):
            for k in range(n_line):
                at = ((v * n_line + k) * 2 + t) * ff_each
                dc[v * 2 + t, :, k * ff_each : (k + 1) * ff_each] = wd[:, at : at + ff_each]
    col_jobs = []
    for k, (yy, cc, ss) in enumerate(corners):
        target = (yy, cc, z, ss)
        col_jobs.append(
            remote(dc.at[plane_index(yy, cc, ss)], dc_o.at[p], dc_s.at[k], dc_r.at[k], target)
        )
        if k < 3:
            col_jobs.append(remote(oc.at[yy * 2 + cc], oc_o.at[u], oc_s.at[k], oc_r.at[k], target))
    for job in col_jobs:
        job.start()
    for job in up_jobs:
        job.start()
    mine = [
        pltpu.make_async_copy(dc.at[p], dc_o.at[p], keep.at[0]),
        pltpu.make_async_copy(oc.at[u], oc_o.at[u], keep.at[1]),
    ]
    for job in mine:
        job.start()
    for k in range(1, n_line):
        for job in jobs:
            job.step(k)
        if k == 1:
            hid_job.forward()
    jobs[0].finish_arrivals()
    small_jobs = [
        remote(small_o.at[u], small_o.at[u], sm_s.at[k], sm_r.at[k], (yy, cc, z, ss))
        for k, (yy, cc, ss) in enumerate(corners[:3])
    ]
    for job in small_jobs:
        job.start()
    for k in range(1, n_line):
        for job in up_jobs:
            job.step(k)
    for job in jobs[1:]:
        job.finish_arrivals()
    hid_job.finish()
    for job in up_jobs:
        job.finish()
    for job in small_jobs + col_jobs:
        job.wait()
    for job in mine:
        job.wait()
    for job in jobs:
        job.finish_sends()


def entry(n_line, hid, small, wq, wk, wv, wo, wd, wu):
    n_blk = 2 * n_line
    oc = jax.ShapeDtypeStruct((4, wo.shape[0], wo.shape[1] // 4), wo.dtype)
    dc = jax.ShapeDtypeStruct((8, wd.shape[0], wd.shape[1] // 8), wd.dtype)
    parts = hid.shape[0]
    vmem, anyway = pl.BlockSpec(memory_space=pltpu.VMEM), pl.BlockSpec(memory_space=pl.ANY)

    def out(shape, like):
        return jax.ShapeDtypeStruct(shape, like.dtype)

    return pl.pallas_call(
        functools.partial(entry_kernel, n_line),
        out_shape=[
            out((parts, 4) + hid.shape[1:], hid),
            out((4, n_blk) + small.shape, small),
            out((n_blk,) + wq.shape, wq),
            out((n_blk,) + wk.shape, wk),
            out((n_blk,) + wv.shape, wv),
            out(oc.shape, oc),
            out(dc.shape, dc),
            out((n_line, wu.shape[0], lane_chunks(wu.shape[1])[0].stop), wu),
        ],
        in_specs=[vmem] * 8,
        out_specs=[vmem, vmem, anyway, anyway, anyway, vmem, vmem, anyway],
        scratch_shapes=[pltpu.VMEM(oc.shape, oc.dtype), pltpu.VMEM(dc.shape, dc.dtype)]
        + UlyGather.sems(parts)
        + BlkGather.sems(n_line) * 4
        + LineGather.sems(n_line)
        + [pltpu.SemaphoreType.DMA((3,))] * 2
        + [pltpu.SemaphoreType.DMA((7,))] * 2
        + [pltpu.SemaphoreType.DMA((3,))] * 2
        + [pltpu.SemaphoreType.DMA((2,))],
        compiler_params=params(6),
        cost_estimate=pl.CostEstimate(flops=0, bytes_accessed=40 * 3_000_000, transcendentals=0),
        name="entry",
    )(hid, small, wq, wk, wv, wo, wd, wu)
def dot_nt(a, b):
    return lax.dot_general(a, b, (((1,), (1,)), ((), ())), preferred_element_type=F32)


def dot_nn(a, b):
    return lax.dot_general(a, b, (((1,), (0,)), ((), ())), preferred_element_type=F32)


def dot_tn(a, b):
    return lax.dot_general(a, b, (((0,), (0,)), ((), ())), preferred_element_type=F32)


def lanes_of(shape):
    return lax.broadcasted_iota(jnp.int32, shape, len(shape) - 1)


def halves(x):
    row = lax.broadcasted_iota(jnp.int32, (128, 128), 0) // HEAD_DIM
    same = jnp.where(row == lanes_of((128, 128)) // HEAD_DIM, 1.0, 0.0).astype(BF)
    high = x.astype(BF)
    rest = (x - high.astype(F32)).astype(BF)
    return dot_nn(high, same) + dot_nn(rest, same)


def turn(x):
    first = lanes_of(x.shape) % HEAD_DIM < HEAD_DIM // 2
    return jnp.where(first, pltpu.roll(x, 128 - 32, 1), pltpu.roll(x, 32, 1))


def down_columns(row):
    n = row.shape[1]
    one = jnp.transpose(jnp.broadcast_to(row, (128, n)))
    return jnp.concatenate([one] * (n // 128), axis=1)


def arrivals(n_line, body):
    each = 2 * n_line - 1

    def step(t, carry):
        stage, r = t // each, lax.rem(t, each)
        body(stage, (r + 1) // 2, lax.rem(r + 1, 2))
        return carry

    lax.fori_loop(0, 2 * each, step, 0)


def attend_kernel(
    n_line, x_ref, wq_ref, wk_ref, wv_ref, cos_ref, sin_ref, scale_ref, oc_ref, wg_ref, wu_ref, kp_ref,
    q_ref, y_ref, c_ref, kv_o, oc_o, wg_o, wu_o, o_ref, mixed_ref, inv_ref, kv_ref, acc, total, place_q, *sems,
):
    y, c, z, s = place()
    blk_greet(n_line)
    seqs, rows, wide = q_ref.shape
    heads = wide // 128
    chunk = 4 * LINE_CHUNKS
    cut = wu_ref.shape[-1] - wu_o.shape[-1]
    up = LineGather(
        n_line, lambda: wu_ref.at[:, slice(cut, wu_ref.shape[-1])], lambda zz: wu_o.at[zz], *sems[-4:]
    )
    up.start()
    x = x_ref[...]

    def make(h, carry):
        lanes = pl.ds(pl.multiple_of(h * 128, 128), 128)
        wv = wv_ref[h]
        got = dot_nt(x, jnp.concatenate([wq_ref[h], wk_ref[h], jnp.zeros_like(wv), wv], axis=0))
        raw, value = got[:, :128], got[:, 128:]
        low = lanes_of(raw.shape) < HEAD_DIM
        turned = raw * cos_ref[...] + turn(raw) * sin_ref[...]
        norm = lax.rsqrt(halves(turned * turned) + HEAD_DIM * tiny_eps)
        unit = turned * norm
        both = unit * scale_ref[pl.ds(h, 1)]
        query = jnp.where(low, both, 0.0).astype(BF)
        kv = jnp.where(low, pltpu.roll(both, HEAD_DIM, 1), value).astype(BF)
        for i in range(seqs):
            q_ref[i, :, lanes] = query[i * rows : (i + 1) * rows]
            kv_ref[i, :, lanes] = kv[i * rows : (i + 1) * rows]
        y_ref[:, lanes] = unit
        c_ref[:, lanes] = norm
        return carry

    lax.fori_loop(0, heads, make, 0)
    each = len(BlkGather.sems(n_line))
    picks = [
        (lambda i=i: kv_ref.at[i], lambda block, i=i: kv_o.at[block, i]) for i in range(seqs)
    ] + [(lambda: oc_ref, lambda block: oc_o.at[:, block])]
    jobs = [
        BlkGather(n_line, *pick, *sems[each * i : each * (i + 1)]) for i, pick in enumerate(picks)
    ]
    gates = line_gathers(
        n_line, wg_ref, lambda z: wg_o.at[z], sems[each * (seqs + 1) : each * (seqs + 1) + chunk]
    )
    for job in jobs:
        job.start()
    for job in gates:
        job.keep().start()
    acc[...] = jnp.zeros_like(acc)
    total[...] = jnp.zeros_like(total)
    for i in range(seqs):
        place_q[i] = down_columns(kp_ref[i, z * 2 + s])

    def attend_to(i, block, keys):
        allowed = kp_ref[i, block] <= place_q[i]
        for h in range(heads):
            lanes = slice(h * 128, (h + 1) * 128)
            kv = keys(lanes)
            p = jnp.where(allowed, jnp.exp(dot_nt(q_ref[i, :, lanes], kv)), 0.0)
            part = p[:, :128]
            for j in range(1, rows // 128):
                part = part + p[:, j * 128 : (j + 1) * 128]
            total[i, h] = total[i, h] + part
            acc[i, h] = acc[i, h] + dot_nn(p.astype(BF), kv)

    def body(stage, k, way):
        ahead = jnp.where(k == 0, 1, k + 1)

        @pl.when((stage == 1) & ((k == 0) | (way == 1)) & (ahead < n_line))
        def _():
            for job in gates + [up]:
                job.step(ahead)

        there = (k == 0) | jnp.where(way == 0, z >= k, z + k < n_line)

        @pl.when(there)
        def _():
            for job in jobs:
                for w in (0, 1):
                    pl.when((stage == 0) & (k > 0) & (way == w))(lambda: job.take(w, k))
                    pl.when((stage == 1) & (k > 0) & (way == w))(lambda: job.over(w, k).wait_recv())
                pl.when((stage == 1) & (k == 0))(lambda: job.own(2).wait_recv())
                pl.when((stage == 0) & (k == 0))(lambda: job.keep().wait())
            for w, last in ((0, z), (1, n_line - 1 - z)):
                @pl.when((stage == 0) & (k == last) & ((k == 0) | (way == w)))
                def _():
                    for job in gates:
                        pl.when(job.goes(w))(lambda: job.own(w).start())
            zz = jnp.where(way == 0, z - k, z + k)
            block = zz * 2 + jnp.where(stage == 0, s, 1 - s)
            for i in range(seqs):
                attend_to(i, block, lambda lanes: kv_o[block, i, :, lanes])

    arrivals(n_line, body)
    low = lanes_of((rows, 128)) < HEAD_DIM
    for i in range(seqs):
        outs = []
        for h in range(heads):
            inverse = 1.0 / jnp.broadcast_to(jnp.sum(total[i, h], axis=-1, keepdims=True), (rows, 128))
            out = acc[i, h] * inverse
            o_ref[i, h] = out
            inv_ref[i, h] = jnp.transpose(inverse)[:8]
            outs.append(out)
        for h in range(0, heads - 1, 2):
            mixed_ref[i, :, h * HEAD_DIM : (h + 2) * HEAD_DIM] = jnp.where(
                low, pltpu.roll(outs[h], HEAD_DIM, 1), outs[h + 1]
            ).astype(BF)
        if heads % 2 == 1:
            mixed_ref[i, :, (heads - 1) * HEAD_DIM :] = pltpu.roll(outs[-1], HEAD_DIM, 1)[:, :HEAD_DIM].astype(BF)
    for job in jobs:
        job.finish_sends()
    for job in gates + [up]:
        job.finish()


def attend(n_line, seqs, x, wq, wk, wv, cos, sin, scale, oc, wg, wu, k_places):
    tokens, width = x.shape
    n_blk, heads, rows = 2 * n_line, wq.shape[0], tokens // seqs
    head, wide = (seqs, heads, rows, 128), (seqs, rows, heads * 128)
    flat = ((tokens, heads * 128), F32)
    first = lane_chunks(width)[0].stop
    return comm_call(
        functools.partial(attend_kernel, n_line), "attend", 5,
        (x, wq, wk, wv, cos, sin, scale, oc, wg, wu, k_places),
        [
            (wide, BF), flat, flat, ((n_blk,) + wide, BF), (oc.shape[:1] + (n_blk,) + oc.shape[1:], BF),
            ((n_line,) + wg.shape, BF), ((n_line, wu.shape[0], width - first), BF), (head, F32),
            ((seqs, rows, heads * HEAD_DIM), BF), ((seqs, heads, 8, rows), F32),
        ],
        [pltpu.VMEM(wide, BF), pltpu.VMEM(head, F32), pltpu.VMEM(head, F32), pltpu.VMEM((seqs, rows, rows), F32)]
        + BlkGather.sems(n_line) * (seqs + 1) + line_gather_sems(n_line) + LineGather.sems(n_line),
        90, far_outs=(4, 5, 6),
    )


def attend_back_kernel(
    n_line, fits, q_ref, low_ref, w_ref, mixed_ref, o_ref, inv_ref, kv_ref, kp_ref, gu_ref,
    dq_ref, dkv_ref, oc_ref, gu_o, dz, delta, dq, parts, oparts, key_s, key_sem, *scratch,
):
    y, c, z, s = place()
    blk_greet(n_line)
    seqs, rows, wide = q_ref.shape
    heads, width = wide // 128, low_ref.shape[-1]
    low_rows = low_ref[...].reshape(seqs * rows, width)
    grad = dot_tn(low_rows, mixed_ref[...].reshape(seqs * rows, mixed_ref.shape[-1])).astype(BF)
    n_blk, each_out = 2 * n_line, width // (8 * n_line)
    for b in range(n_blk):
        for v in range(4):
            at = (v * n_blk + b) * each_out
            oparts[b, v * each_out : (v + 1) * each_out] = grad[at : at + each_out]
    each = 6
    jobs = [BlkReduce(n_line, parts.at[:, i], *scratch[each * i : each * (i + 1)]) for i in range(seqs)]
    out_job = BlkReduce(n_line, oparts, *scratch[each * seqs : each * (seqs + 1)])
    ups = line_reduces(n_line, gu_ref, scratch[each * (seqs + 1) :])
    for k in range(n_line - 1, -1, -1):
        out_job.start(k)
    low = lanes_of((rows, 128)) < HEAD_DIM
    for i in range(seqs):
        d = dot_nn(low_rows[i * rows : (i + 1) * rows], w_ref[...]).astype(BF).astype(F32)
        for h in range(heads):
            at = h // 2 * 128
            if h == heads - 1 and heads % 2 == 1:
                tile = jnp.concatenate([jnp.zeros((rows, HEAD_DIM), F32), d[:, at:]], axis=1)
            else:
                tile = d[:, at : at + 128]
                if h % 2 == 0:
                    tile = pltpu.roll(tile, HEAD_DIM, 1)
                tile = jnp.where(low, 0.0, tile)
            dz[i, h] = tile.astype(BF)
            row = jnp.sum(tile * o_ref[i, h], axis=-1, keepdims=True)
            delta[i, h] = jnp.transpose(jnp.broadcast_to(row, (rows, 128)))[:8]
    dq[...] = jnp.zeros_like(dq)

    def block_of(block):
        if fits:
            keys = kv_ref.at[block]
        else:
            keys = key_s
            copy = pltpu.make_async_copy(kv_ref.at[block], key_s, key_sem.at[0])
            copy.start()
            copy.wait()
        for i in range(seqs):
            allowed = down_columns(kp_ref[i, block]) <= kp_ref[i, z * 2 + s]
            for h in range(heads):
                lanes = slice(h * 128, (h + 1) * 128)
                kv = keys[i, :, lanes]
                pair = jnp.concatenate([q_ref[i, :, lanes], dz[i, h]], axis=0)
                scores = dot_nt(kv, pair)
                p = jnp.where(allowed, jnp.exp(scores[:, :rows]) * inv_ref[i, h][:1], 0.0)
                ds = (p * (scores[:, rows:] - delta[i, h][:1])).astype(BF)
                parts[block, i, :, lanes] = dot_nn(
                    jnp.concatenate([ds, p.astype(BF)], axis=1), pair
                ).astype(BF)
                dq[i, h] = dq[i, h] + dot_tn(ds, kv)

    def step(t, carry):
        k, r = n_line - 1 - t // 4, lax.rem(t, 4)
        way, stays = r // 2, lax.rem(r, 2)

        @pl.when((r == 0) & (k > 0))
        def _():
            for line_job, _ in ups:
                line_job.step(k)

        there = jnp.where(k == 0, way == 0, jnp.where(way == 0, z + k < n_line, z >= k))

        @pl.when(there)
        def _():
            zz = jnp.where(way == 0, z + k, z - k)
            block_of(zz * 2 + jnp.where(stays == 0, 1 - s, s))

            @pl.when(stays == 0)
            def _():
                for job in jobs:
                    job.side(zz).start()

        @pl.when((r == 3) & (k + 1 < n_line))
        def _():
            for w in (0, 1):
                @pl.when(jobs[0].exists(w, k + 1))
                def _():
                    for job in jobs + [out_job]:
                        job.move_on(w, k + 1)

        return carry

    lax.fori_loop(0, 4 * n_line, step, 0)
    for i in range(seqs):
        for h in range(heads):
            dq_ref[i, :, h * 128 : (h + 1) * 128] = dq[i, h].astype(BF)
    out_job.result(oc_ref)
    for i, job in enumerate(jobs):
        job.result(dkv_ref.at[i])
    for job, cut in ups:
        job.result(gu_o.at[cut])
    for job in jobs + [out_job] + [job for job, _ in ups]:
        job.finish()


def attend_back(n_line, q, low, w, mixed, o, inv, kv, k_places, gu):
    seqs, rows, wide = q.shape
    n_blk, heads = 2 * n_line, wide // 128
    head = (seqs, heads, rows, 128)
    width, columns = w.shape
    out_shape = (width // n_blk, columns)
    one = jax.ShapeDtypeStruct((n_blk,) + kv.shape[2:], BF)
    out_one = jax.ShapeDtypeStruct((n_blk,) + out_shape, BF)
    fits = kv.size * 2 <= 8_000_000
    return comm_call(
        functools.partial(attend_back_kernel, n_line, fits), "attend_back", 7,
        (q, low, w, mixed, o, inv, kv, k_places, gu),
        [(q.shape, BF), (kv.shape[1:], BF), (out_shape, BF), (gu.shape[1:], F32)],
        [
            pltpu.VMEM(head, BF), pltpu.VMEM((seqs, heads, 8, rows), F32), pltpu.VMEM(head, F32),
            pltpu.VMEM(kv.shape, BF), pltpu.VMEM(out_one.shape, BF),
            pltpu.VMEM((16, 128) if fits else kv.shape[1:], BF), pltpu.SemaphoreType.DMA((1,)),
        ]
        + BlkReduce.scratch(n_line, one) * seqs + BlkReduce.scratch(n_line, out_one)
        + line_reduce_scratch(n_line, gu),
        75, 67_000_000, () if fits else (6,),
    )


def ff_kernel(x_ref, wu_ref, wu2_ref, wg_ref, vec_ref, inner_ref, up_ref, gate_ref):
    x = x_ref[...]
    cut = wu_ref.shape[1]
    up = dot_nt(x[:, :cut], wu_ref[...]) + dot_nt(x[:, cut:], wu2_ref[...])
    gate = dot_nt(x, wg_ref[...])
    columns = up.shape[1]
    z = gate * vec_ref[3:4, :columns] * D**0.5
    inner_ref[...] = (z / (1.0 + jnp.exp(-z)) * (up * vec_ref[2:3, :columns])).astype(BF)
    up_ref[...] = up
    gate_ref[...] = gate


def ff_forward(x, wu, wu2, wg, vec):
    rows, width = x.shape
    columns = wu.shape[0]
    block = rows // 4
    whole = lambda a: pl.BlockSpec(a.shape, lambda i: (0, 0))
    part = lambda n: pl.BlockSpec((block, n), lambda i: (i, 0))
    out = lambda dtype: jax.ShapeDtypeStruct((rows, columns), dtype)
    return pl.pallas_call(
        ff_kernel,
        grid=(4,),
        out_shape=[out(BF), out(F32), out(F32)],
        in_specs=[part(width)] + [whole(a) for a in (wu, wu2, wg, vec)],
        out_specs=[part(columns)] * 3,
        compiler_params=pltpu.CompilerParams(vmem_limit_bytes=VMEM_BYTES),
        cost_estimate=pl.CostEstimate(
            flops=4 * rows * width * columns, bytes_accessed=2 * rows * width + 10 * rows * columns,
            transcendentals=rows * columns,
        ),
        name="ff_forward",
    )(x, wu, wu2, wg, vec)


def unit_of(x):
    c = lax.rsqrt(jnp.sum(x * x, axis=-1, keepdims=True) + x.shape[-1] * tiny_eps)
    return x * c, c


def unit_back(y, c, dy):
    return c * (dy - y * jnp.sum(y * dy, axis=-1, keepdims=True))


class Late:
    @staticmethod
    def scratch(arrays):
        return [pltpu.VMEM(a.shape, a.dtype) for a in arrays] + [pltpu.SemaphoreType.DMA((len(arrays),))]

    def __init__(self, refs, scratch):
        *self.bufs, sem = scratch
        self.copies = [
            pltpu.make_async_copy(ref, buf, sem.at[i]) for i, (ref, buf) in enumerate(zip(refs, self.bufs))
        ]
        for copy in self.copies:
            copy.start()

    def __call__(self, i):
        self.copies[i].wait()
        return self.bufs[i]


def comm_call(kernel, name, collective_id, args, outs, scratch, micros, room=VMEM_BYTES, far_args=(), far_outs=()):
    vmem, anyway = pl.BlockSpec(memory_space=pltpu.VMEM), pl.BlockSpec(memory_space=pl.ANY)
    return pl.pallas_call(
        kernel,
        out_shape=[jax.ShapeDtypeStruct(shape, dtype) for shape, dtype in outs],
        in_specs=[anyway if i in far_args else vmem for i in range(len(args))],
        out_specs=[anyway if i in far_outs else vmem for i in range(len(outs))],
        scratch_shapes=scratch,
        compiler_params=params(collective_id, room),
        cost_estimate=pl.CostEstimate(flops=0, bytes_accessed=micros * 3_000_000, transcendentals=0),
        name=name,
    )(*args)


def attn_joint_kernel(
    n_line, mixed, w, hid, rate, dc, first_o, ua_o, ca_o, cv_o, all_o, down_o, part, low, *scratch
):
    ends = line_ends(n_line)
    greet(plane_peers(), ends[:2])
    split = len(UlyReduce.scratch(part))
    job = UlyReduce(part, *scratch[:split])
    out = PlaneGather(low, all_o, *scratch[split : split + 3])
    downs = line_gathers(n_line, dc, lambda z: down_o.at[:, z], scratch[split + 3 :])
    for line_job in downs:
        line_job.start()
    steps = [(k, line_job) for k in range(1, n_line) for line_job in downs]
    parts, _, rows, width = part.shape
    seqs = mixed.shape[0]
    each = parts // seqs
    for i in range(seqs):
        got = dot_nt(mixed[i], w[...]).astype(BF)
        for k in range(each):
            for u in range(4):
                at = (u * each + k) * rows
                part[i * each + k, u] = got[at : at + rows]
            for copy in job.near[i * each + k]:
                copy.start()
    job.middle()
    k, line_job = steps.pop(0)
    line_job.step(k)
    for i in range(parts):
        ua, ca = unit_of(job.result(i))
        h = hid[i].astype(F32)
        first, cv = unit_of(h + rate[0:1] * (ua - h))
        low[i] = first.astype(BF)
        out.start_part(i)
        first_o[i], ua_o[i] = first, ua
        ca_o[i] = jnp.broadcast_to(ca, (rows, 128))
        cv_o[i] = jnp.broadcast_to(cv, (rows, 128))
        if i > 0:
            out.forward_part(i - 1)
        if len(steps) > 0:
            k, line_job = steps.pop(0)
            line_job.step(k)
    out.forward_part(parts - 1)
    for k, line_job in steps:
        line_job.step(k)
    out.finish()
    job.finish()
    for line_job in downs:
        line_job.finish()


def attn_joint(n_line, mixed, w, hid, rate, dc):
    parts, rows, width = hid.shape
    part = jax.ShapeDtypeStruct((parts, 4, rows, width), BF)
    thin = ((parts, rows, 128), F32)
    return comm_call(
        functools.partial(attn_joint_kernel, n_line), "attn_joint", 1, (mixed, w, hid, rate, dc),
        [
            (hid.shape, F32), (hid.shape, F32), thin, thin, ((8, parts, rows, width), BF),
            (dc.shape[:1] + (n_line,) + dc.shape[1:], BF),
        ],
        [pltpu.VMEM(part.shape, BF), pltpu.VMEM(hid.shape, BF)]
        + UlyReduce.scratch(part) + PlaneGather.sems(parts) + line_gather_sems(n_line),
        25, far_outs=(5,),
    )


def plane_products(job, part, c, product, between=lambda: None):
    _, parts, rows, width = part.shape
    for cc, first in ((1 - c, True), (c, False)):
        def one(yy, carry):
            got = product(yy, cc).astype(BF).reshape(2, parts, rows, width)
            for ss in (0, 1):
                part[plane_index(yy, cc, ss)] = got[ss]
            return carry

        lax.fori_loop(0, 2, one, 0)
        if first:
            job.start()
            between()


def ff_joint_kernel(inner, w, first, rate, cot, out_o, d1_o, sum_o, all_o, part, low, *scratch):
    y, c, z, s = place()
    greet(plane_peers())
    split = len(PlaneReduce.scratch(part))
    job = PlaneReduce(part, *scratch[:split])
    out = PlaneGather(low, all_o, *scratch[split:])
    _, seqs, rows, width = part.shape
    columns = inner.shape[-1]
    plane_products(
        job, part, c, lambda yy, cc: dot_nt(inner[yy, cc].reshape(2 * seqs * rows, columns), w[...])
    )
    job.middle()
    job.last()
    for i in range(seqs):
        ub, cb = unit_of(job.result(i))
        f, b = first[i], rate[1:2]
        o, cw = unit_of(f + b * (ub - f))
        dw = unit_back(o, cw, cot[i].astype(F32))
        step = b * dw
        low[i] = unit_back(ub, cb, step).astype(BF)
        out.start_part(i)
        out_o[i] = o.astype(BF)
        d1_o[i] = dw - step
        total = jnp.sum(dw * (ub - f), axis=0, keepdims=True)
        sum_o[...] = total if i == 0 else sum_o[...] + total
        if i > 0:
            out.forward_part(i - 1)
    out.forward_part(seqs - 1)
    out.finish()
    job.finish()


def ff_joint(inner, w, first, rate, cot):
    seqs, rows, width = first.shape
    part = jax.ShapeDtypeStruct((8, seqs, rows, width), BF)
    return comm_call(
        ff_joint_kernel, "ff_joint", 2,
        (inner.reshape(2, 2, 2, seqs * rows, inner.shape[-1]), w, first, rate, cot),
        [(first.shape, BF), (first.shape, F32), ((1, width), F32), (part.shape, BF)],
        [pltpu.VMEM(part.shape, BF), pltpu.VMEM(first.shape, BF)] + PlaneReduce.scratch(part) + PlaneGather.sems(seqs),
        30,
    )


def back_joint_kernel(
    n_line, d, inner, rate, d1, first, ua, ca, cv, hid, wd_h, up_h, gate_h, wu_h, wu2_h, wg_h, x_h,
    res_o, sum_o, ff_sum_o, all_o, up_o, gate_o, down_o, part, low, down_s, du, dg, *scratch,
):
    y, c, z, s = place()
    late = Late((wd_h, up_h, gate_h, wu_h, wu2_h, wg_h, x_h), scratch[:8])
    scratch = scratch[8:]
    greet(plane_peers(), line_ends(n_line)[:2])
    split = len(PlaneReduce.scratch(part))
    job = PlaneReduce(part, *scratch[:split])
    _, parts, rows, width = part.shape
    columns = du.shape[-1]
    tokens = 8 * parts * rows
    each = parts // all_o.shape[0]
    out = UlyGather(
        low, all_o, *scratch[split : split + 3],
        pick=lambda i, u: all_o.at[i // each, u, pl.ds(i % each * rows, rows)],
    )
    downs = line_reduces(n_line, down_s, scratch[split + 3 :])
    flat = lambda ref: ref[...].reshape(tokens, ref.shape[-1])

    deep = width // (4 * n_line)
    inner_all = flat(inner)

    def down_half(i, carry):
        lanes = pl.ds(pl.multiple_of(i * (width // 2), 128), width // 2)
        grad = dot_tn(d[:, :, :, :, lanes].reshape(tokens, width // 2), inner_all).astype(BF)
        for v in (0, 1):
            for k in range(n_line):
                at = (v * n_line + k) * deep
                down_s[k, 2 * i + v] = grad[at : at + deep]
        return carry

    lax.fori_loop(0, 2, down_half, 0)
    for line_job, _ in downs:
        line_job.step(n_line - 1)

    wd, up_ref, gate_ref = late(0), late(1), late(2)
    u_scale, g_scale = rate[2:3, :columns], rate[3:4, :columns] * D**0.5

    ff_sum_o[...] = jnp.zeros_like(ff_sum_o)

    def gated_back(cc):
        def one(yy, carry):
            got = dot_nn(d[yy, cc].reshape(tokens // 4, width), wd[...])
            up, gate = up_ref[yy, cc].reshape(got.shape), gate_ref[yy, cc].reshape(got.shape)
            gz = gate * g_scale
            sig = 1.0 / (1.0 + jnp.exp(-gz))
            d_up = got * (gz * sig)
            d_gate = got * (up * u_scale) * sig * (1.0 + gz * (1.0 - sig))
            du[yy, cc] = (d_up * u_scale).astype(BF).reshape(du.shape[2:])
            dg[yy, cc] = (d_gate * g_scale).astype(BF).reshape(dg.shape[2:])
            ff_sum_o[0:1] = ff_sum_o[0:1] + jnp.sum(d_up * up, axis=0, keepdims=True)
            ff_sum_o[1:2] = ff_sum_o[1:2] + jnp.sum(d_gate * gate, axis=0, keepdims=True) * D**0.5
            return carry

        lax.fori_loop(0, 2, one, 0)

    gated_back(1 - c)
    wu, wu2, wg = late(3), late(4), late(5)

    def product(yy, cc):
        u, g = du[yy, cc].reshape(tokens // 4, columns), dg[yy, cc].reshape(tokens // 4, columns)
        got = jnp.concatenate([dot_nn(u, wu[...]), dot_nn(u, wu2[...])], axis=1)
        return got + dot_nn(g, wg[...])

    plane_products(job, part, c, product, lambda: gated_back(c))
    job.middle()
    steps = [(k, line_job) for k in range(n_line - 2, 0, -1) for line_job, _ in downs]
    job.last()
    x = late(6)

    def by_line(o, ref):
        n, rows_all = columns // n_line, flat(ref)

        def half(i, carry):
            lanes = pl.ds(pl.multiple_of(i * (width // 2), 128), width // 2)
            grad = dot_tn(rows_all, x[:, lanes]).astype(BF)
            for k in range(n_line):
                o[k, :, lanes] = grad[k * n : (k + 1) * n]
            return carry

        lax.fori_loop(0, 2, half, 0)

    by_line(up_o, du)
    for i in range(parts):
        f, h, u, a = first[i], hid[i].astype(F32), ua[i], rate[0:1]
        dv = unit_back(f, cv[i][:, :1], d1[i] + job.result(i))
        step = a * dv
        low[i] = unit_back(u, ca[i][:, :1], step).astype(BF)
        out.start_part(i)
        res_o[i] = dv - step
        total = jnp.sum(dv * (u - h), axis=0, keepdims=True)
        sum_o[...] = total if i == 0 else sum_o[...] + total
        if len(steps) > 0:
            k, line_job = steps.pop(0)
            line_job.step(k)
    for k, line_job in steps:
        line_job.step(k)
    by_line(gate_o, dg)
    out.forward()
    out.finish()
    job.finish()
    for line_job, cut in downs:
        line_job.result(down_o.at[cut])
        line_job.finish()


def back_joint(n_line, seqs, d, wd, up, gate, rate, wu, wu2, wg, x, inner, d1, first, ua, ca, cv, hid):
    parts, rows, width = first.shape
    columns = wd.shape[1]
    part = jax.ShapeDtypeStruct((8, parts, rows, width), BF)
    down = jax.ShapeDtypeStruct((n_line, 4, width // (4 * n_line), columns), BF)
    by_line = ((n_line, columns // n_line, width), BF)
    wide = lambda a: a.reshape(2, 2, 2, parts * rows, a.shape[-1])
    thin = pltpu.VMEM((2, 2, 2, parts * rows, columns), BF)
    late = (wd, wide(up), wide(gate), wu, wu2, wg, x)
    return comm_call(
        functools.partial(back_joint_kernel, n_line), "back_joint", 3,
        (wide(d), wide(inner), rate, d1, first, ua, ca, cv, hid) + late,
        [
            (first.shape, F32), ((1, width), F32), ((2, columns), F32),
            ((seqs, 4, parts * rows // seqs, width), BF), by_line, by_line, (down.shape[1:], BF),
        ],
        [pltpu.VMEM(part.shape, BF), pltpu.VMEM(first.shape, BF), pltpu.VMEM(down.shape, BF), thin, thin]
        + Late.scratch(late) + PlaneReduce.scratch(part) + UlyGather.sems(parts)
        + line_reduce_scratch(n_line, down),
        40, VMEM_BYTES, tuple(range(9, 16)),
    )


def settle_kernel(*refs):
    count = len(refs) // 2
    for x, o in zip(refs[:count], refs[count:]):
        o[...] = x[...]


def settle(*arrays):
    vmem = pl.BlockSpec(memory_space=pltpu.VMEM)
    return pl.pallas_call(
        settle_kernel,
        out_shape=[jax.ShapeDtypeStruct(a.shape, a.dtype) for a in arrays],
        in_specs=[vmem] * len(arrays),
        out_specs=[vmem] * len(arrays),
        compiler_params=pltpu.CompilerParams(vmem_limit_bytes=VMEM_BYTES),
        name="settle",
    )(*arrays)
def local(
    hidden, positions, w_query, w_key, w_value, w_out, w_up, w_gate, w_down,
    qk_scale, alpha_attn, alpha_mlp, up_scale, gate_scale, cotangent,
):
    seqs, rows_each, width = hidden.shape
    n_line = lax.axis_size("line")
    n_blk = 2 * n_line
    heads = HEADS // 4
    local_width = heads * HEAD_DIM
    group_rows = 4 * rows_each
    tokens = seqs * rows_each
    group_tokens = 4 * tokens
    plane_tokens = 8 * tokens
    attn_each, ff_each = w_query.shape[0], w_up.shape[0]
    ff_local = ff_each * n_line
    far, core, line, side = place()
    uly = far * 2 + core

    def row(x, wide):
        return jnp.pad(x, ((0, 0),) * (x.ndim - 1) + ((0, wide - x.shape[-1]),))

    pieces = [v.astype(F32) for v in (qk_scale, alpha_attn, alpha_mlp, up_scale, gate_scale)]
    pieces.append(positions.reshape(-1).astype(F32))
    used = sum(v.shape[0] for v in pieces)
    room, at, small = used + -used % 1024, 0, 0.0
    for v in pieces:
        small = small + jnp.pad(v, (at, room - at - v.shape[0]))
        at += v.shape[0]
    small = small.reshape(-1, 128)

    hid_all, small_all, wq_all, wk_all, wv_all, out_cols, down_cols, up_first = entry(
        n_line, hidden, small, w_query, w_key, w_value, w_out, w_down, w_up
    )
    up_first = up_first.reshape(ff_local, -1)

    flat = small_all.reshape(4, n_blk, -1)
    cut = [0, attn_each, 2 * attn_each, 3 * attn_each, 3 * attn_each + ff_each, 3 * attn_each + 2 * ff_each, used]
    own = lax.dynamic_slice_in_dim(flat, uly, 1, 0)[0]
    scale_wide = own[:, : cut[1]].reshape(heads, HEAD_DIM)
    attn_rate = flat[:, :, cut[1] : cut[2]].reshape(-1)
    mlp_rate = flat[:, :, cut[2] : cut[3]].reshape(-1)
    mine = lax.dynamic_slice_in_dim(own.reshape(n_line, 2, -1), side, 1, 1)[:, 0]
    up_wide = mine[:, cut[3] : cut[4]].reshape(-1)
    gate_wide = mine[:, cut[4] : cut[5]].reshape(-1)
    assert ff_local <= width
    rates = jnp.pad(
        jnp.stack([attn_rate, mlp_rate, row(up_wide, width), row(gate_wide, width)]), ((0, 4), (0, 0))
    )
    places = jnp.transpose(
        flat[:, :, cut[5] : cut[6]].reshape(4, n_blk, seqs, rows_each), (2, 1, 0, 3)
    ).reshape(seqs, n_blk, 1, group_rows)
    q_places = lax.dynamic_slice_in_dim(places, line * 2 + side, 1, 1)[:, 0]

    lane = jnp.arange(128) % HEAD_DIM
    freqs = rotary_base ** (-((lane % 32).astype(F32) * (2.0 / HEAD_DIM)))
    angles = q_places.reshape(group_tokens, 1) * freqs
    cos = jnp.cos(angles)
    sin = jnp.where(lane < 32, -1.0, 1.0) * jnp.sin(angles)
    scale_both = jnp.concatenate([scale_wide * HEAD_DIM**0.5, scale_wide], axis=1)

    group_hidden = hid_all.reshape(group_tokens, width)
    wq = wq_all.reshape(heads, HEAD_DIM, width)
    wk = wk_all.reshape(heads, HEAD_DIM, width)
    wv = wv_all.reshape(heads, HEAD_DIM, width)
    qz, y_both, c_both, kv_all, out_all, gate_full, up_last, attended, mixed, inverse = attend(
        n_line, seqs, group_hidden, wq, wk, wv, cos, sin, scale_both, out_cols, w_gate, w_up,
        places,
    )
    up_last = up_last.reshape(ff_local, -1)
    gate_full = gate_full.reshape(ff_local, width)
    out_full = out_all.reshape(width, local_width)

    fine = (2 * seqs, rows_each // 2, width)
    hidden_fine = hidden.reshape(fine)
    first, unit_att, att_c, first_c, mlp_in, down_full = attn_joint(
        n_line, mixed, out_full, hidden_fine, rates,
        down_cols.reshape(4, 2 * attn_each, ff_local),
    )
    down_full = down_full.reshape(width, ff_local)
    mlp_in = mlp_in.reshape(plane_tokens, width)
    inner, up_rows, gate_rows = ff_forward(mlp_in, up_first, up_last, gate_full, rates)
    layer_out, grad_first, grad_alpha_mlp, branch_low = ff_joint(
        inner, down_full, first, rates, cotangent.reshape(fine)
    )
    branch_low = branch_low.reshape(plane_tokens, width)
    grad_residual, grad_alpha_attn, ff_scales, att_low, grad_up, grad_gate, down_own = back_joint(
        n_line, seqs, branch_low, down_full, up_rows, gate_rows, rates, up_first, up_last, gate_full,
        mlp_in, inner, grad_first, first, unit_att, att_c, first_c, hidden_fine,
    )
    grad_up_scale, grad_gate_scale = ff_scales[0], ff_scales[1]
    down_own = down_own.reshape(8, attn_each, ff_local)

    dq, dkv, out_own, up_own = attend_back(
        n_line, qz, att_low.reshape(seqs, group_rows, width), out_full, mixed, attended, inverse,
        kv_all, places, grad_up,
    )
    out_own = out_own.reshape(4, attn_each, local_width)
    alpha = jnp.concatenate(
        [grad_alpha_attn.reshape(4, n_blk, attn_each), grad_alpha_mlp.reshape(4, n_blk, attn_each)], axis=2
    )
    ff_sums = jnp.concatenate(
        [grad_up_scale.reshape(n_line, ff_each), grad_gate_scale.reshape(n_line, ff_each)], axis=1
    )
    sides = (jnp.arange(2) == side)[None, :, None]
    ff_sums = jnp.where(sides, ff_sums[:, None], 0.0).reshape(n_blk, 2 * ff_each)
    rest = jnp.concatenate([jnp.zeros((n_blk, 256), F32), row(ff_sums, 384)], axis=1)
    gq, gk, gv, grad_hidden, out_gradient, down_gradient, sums, gate_own = leave(
        n_line, group_hidden, dq, dkv, y_both, c_both, cos, sin, scale_both, wq, wk, wv,
        grad_residual.reshape(seqs, rows_each, width), out_own, down_own,
        row(alpha, 128)[:, :, None], rest[:, None], grad_gate,
    )
    sums = sums[0]
    layer_out, grad_hidden, gq, gk, gv, out_gradient, up_own, gate_own, down_gradient = settle(
        layer_out.reshape(hidden.shape), grad_hidden, gq, gk, gv, out_gradient, up_own, gate_own,
        down_gradient,
    )
    return (
        layer_out,
        grad_hidden,
        gq,
        gk,
        gv,
        out_gradient,
        up_own,
        gate_own,
        down_gradient,
        sums[128 : 128 + attn_each],
        sums[:attn_each],
        sums[attn_each : 2 * attn_each],
        sums[256 : 256 + ff_each],
        sums[256 + ff_each : 256 + 2 * ff_each],
    )


def solution(mesh):
    far = mesh.shape["uly"] // 2
    line = mesh.shape["blk"] // 2
    finer = Mesh(mesh.devices.reshape(far, 2, line, 2), AXES)
    rows, tokens, flat = P(AXES, None), P(None, AXES, None), P(AXES)
    return jax.shard_map(
        local,
        mesh=finer,
        in_specs=(tokens, P(None, AXES)) + (rows,) * 7 + (flat,) * 5 + (tokens,),
        out_specs=(tokens, tokens) + (rows,) * 7 + (flat,) * 5,
        check_vma=False,
    )
```

```python
import functools

import jax
import jax.numpy as jnp
from jax import lax
from jax.experimental import pallas as pl
from jax.experimental.pallas import tpu as pltpu
from jax.sharding import Mesh
from jax.sharding import PartitionSpec as P

D = 1280
HEADS = 20
HEAD_DIM = 64
AXES = ("far", "core", "line", "side")
PLANE = ("far", "core", "side")
VMEM_BYTES = 60 * 1024 * 1024

rotary_base = 10000.0
tiny_eps = 1e-06
BF = jnp.bfloat16
F32 = jnp.float32


def place():
    return tuple(lax.axis_index(name) for name in AXES)


def remote(src, dst, send, recv, device):
    return pltpu.make_async_remote_copy(
        src_ref=src,
        dst_ref=dst,
        send_sem=send,
        recv_sem=recv,
        device_id=device,
        device_id_type=pl.DeviceIdType.MESH,
    )


def signal_to(device):
    pl.semaphore_signal(
        pltpu.get_barrier_semaphore(), inc=1, device_id=device, device_id_type=pl.DeviceIdType.MESH
    )


def greet(devices, maybe=()):
    count = len(devices)
    for device in devices:
        signal_to(device)
    for there, device in maybe:
        pl.when(there)(functools.partial(signal_to, device))
        count = count + jnp.where(there, 1, 0)
    pl.semaphore_wait(pltpu.get_barrier_semaphore(), count)


def params(collective_id, room=VMEM_BYTES):
    return pltpu.CompilerParams(
        collective_id=collective_id, has_side_effects=True, vmem_limit_bytes=room
    )


class UlyGather:
    sems = staticmethod(lambda parts: [pltpu.SemaphoreType.DMA((3, parts))] * 2 + [pltpu.SemaphoreType.DMA((parts,))])

    def __init__(self, x, o, send, recv, local, pick=None):
        pick = pick or (lambda i, u: o.at[i, u])
        y, c, z, s = place()
        u, v = y * 2 + c, (1 - y) * 2 + c
        mate, across = (y, 1 - c, z, s), (1 - y, c, z, s)
        self.parts = x.shape[0]
        parts = range(self.parts)
        self.far = [remote(x.at[i], pick(i, u), send.at[0, i], recv.at[0, i], across) for i in parts]
        self.near = [remote(x.at[i], pick(i, u), send.at[1, i], recv.at[1, i], mate) for i in parts]
        self.on = [remote(pick(i, v), pick(i, v), send.at[2, i], recv.at[2, i], mate) for i in parts]
        self.own = [pltpu.make_async_copy(x.at[i], pick(i, u), local.at[i]) for i in parts]

    def start_part(self, i):
        self.far[i].start()
        self.near[i].start()
        self.own[i].start()

    def start(self):
        for i in range(self.parts):
            self.start_part(i)

    def forward(self):
        for i in range(self.parts):
            self.far[i].wait_recv()
            self.on[i].start()

    def finish(self):
        for i in range(self.parts):
            self.near[i].wait_recv()
            self.on[i].wait_recv()
            self.own[i].wait()
            self.far[i].wait_send()
            self.near[i].wait_send()
            self.on[i].wait_send()


def uly_peers():
    y, c, z, s = place()
    return [(y, 1 - c, z, s), (1 - y, c, z, s)]


def add_low(*terms):
    total = terms[0].astype(F32)
    for term in terms[1:]:
        total = total + term.astype(F32)
    return total


class UlyReduce:
    @staticmethod
    def scratch(x):
        parts, _, rows, width = x.shape
        return [
            pltpu.VMEM((parts, 2, rows, width), x.dtype),
            pltpu.VMEM((parts, rows, width), x.dtype),
            pltpu.VMEM((parts, rows, width), x.dtype),
            pltpu.SemaphoreType.DMA((3, parts)),
            pltpu.SemaphoreType.DMA((3, parts)),
        ]

    def __init__(self, x, near, mid, far_in, send, recv):
        y, c, z, s = place()
        mate, across = uly_peers()
        self.x, self.near_ref, self.mid, self.far_in = x, near, mid, far_in
        self.y, self.c, self.parts = y, c, x.shape[0]
        parts = range(self.parts)
        self.near = [
            [
                remote(x.at[i, f * 2 + 1 - c], near.at[i, k], send.at[k, i], recv.at[k, i], mate)
                for k, f in enumerate((1 - y, y))
            ]
            for i in parts
        ]
        self.far = [remote(mid.at[i], far_in.at[i], send.at[2, i], recv.at[2, i], across) for i in parts]

    def start(self):
        for i in range(self.parts):
            for copy in self.near[i]:
                copy.start()

    def middle(self):
        for i in range(self.parts):
            self.near[i][0].wait_recv()
            self.mid[i] = add_low(self.x[i, (1 - self.y) * 2 + self.c], self.near_ref[i, 0]).astype(BF)
            self.far[i].start()

    def result(self, i):
        self.near[i][1].wait_recv()
        self.far[i].wait_recv()
        return add_low(self.x[i, self.y * 2 + self.c], self.near_ref[i, 1], self.far_in[i])

    def finish(self):
        for i in range(self.parts):
            for copy in self.near[i] + [self.far[i]]:
                copy.wait_send()


def plane_peers():
    y, c, z, s = place()
    return [(y, 1 - c, z, s), (1 - y, c, z, s), (y, c, z, 1 - s)]


def plane_index(y, c, s):
    return (y * 2 + c) * 2 + s


class PlaneGather:
    @staticmethod
    def sems(parts):
        return [pltpu.SemaphoreType.DMA((7, parts))] * 2 + [pltpu.SemaphoreType.DMA((parts,))]

    def __init__(self, x, o, send, recv, local):
        y, c, z, s = place()
        mate, across, cross = plane_peers()
        self.parts = parts = range(x.shape[0])
        me, py, px, pd = (
            plane_index(y, c, s),
            plane_index(1 - y, c, s),
            plane_index(y, c, 1 - s),
            plane_index(1 - y, c, 1 - s),
        )

        def copy(source, p, i, slot, device):
            return remote(source, o.at[p, i], send.at[slot, i], recv.at[slot, i], device)

        def on(p, i, slot, device):
            return copy(o.at[p, i], p, i, slot, device)

        self.by_y = [copy(x.at[i], me, i, 0, across) for i in parts]
        self.by_x = [copy(x.at[i], me, i, 1, cross) for i in parts]
        self.near = [copy(x.at[i], me, i, 2, mate) for i in parts]
        self.corner = [on(px, i, 3, across) if i % 2 else on(py, i, 3, cross) for i in parts]
        self.pass_y = [on(py, i, 4, mate) for i in parts]
        self.pass_x = [on(px, i, 5, mate) for i in parts]
        self.pass_d = [on(pd, i, 6, mate) for i in parts]
        self.own = [pltpu.make_async_copy(x.at[i], o.at[me, i], local.at[i]) for i in parts]

    def start_part(self, i):
        for copy in (self.by_y[i], self.by_x[i], self.near[i], self.own[i]):
            copy.start()

    def forward_part(self, i):
        ways = [(self.by_y[i], self.pass_y[i]), (self.by_x[i], self.pass_x[i])]
        first, then = ways[:: 1 - 2 * (i % 2)]
        first[0].wait_recv()
        self.corner[i].start()
        first[1].start()
        then[0].wait_recv()
        then[1].start()

    def finish(self):
        for i in self.parts:
            self.corner[i].wait_recv()
            self.pass_d[i].start()
        for i in self.parts:
            for copy in (self.near[i], self.pass_y[i], self.pass_x[i], self.pass_d[i]):
                copy.wait()
            for copy in (self.by_y[i], self.by_x[i], self.corner[i]):
                copy.wait_send()
            self.own[i].wait()


class PlaneReduce:
    @staticmethod
    def scratch(x):
        one = pltpu.VMEM(x.shape[1:], x.dtype)
        sems = pltpu.SemaphoreType.DMA((7, x.shape[1]))
        return [pltpu.VMEM((4,) + x.shape[1:], x.dtype)] + [one] * 6 + [sems] * 2

    def __init__(self, x, near, out_x, out_y, out_d, in_x, in_y, in_d, send, recv):
        y, c, z, s = place()
        mate, across, cross = plane_peers()
        self.c = c
        self.parts = parts = range(x.shape[1])
        self.spots = ((1 - y, 1 - s), (y, 1 - s), (1 - y, s), (y, s))
        self.x, self.near_ref = x, near
        self.out_x, self.out_y, self.out_d = out_x, out_y, out_d
        self.in_x, self.in_y, self.in_d = in_x, in_y, in_d

        def copy(source, target, i, slot, device):
            return remote(source, target, send.at[slot, i], recv.at[slot, i], device)

        self.near = [
            [copy(x.at[plane_index(sy, 1 - c, ss), i], near.at[k, i], i, k, mate) for i in parts]
            for k, (sy, ss) in enumerate(self.spots)
        ]
        self.corner = [copy(out_d.at[i], in_d.at[i], i, 4, across if i % 2 else cross) for i in parts]
        self.by_x = [copy(out_x.at[i], in_x.at[i], i, 5, cross) for i in parts]
        self.by_y = [copy(out_y.at[i], in_y.at[i], i, 6, across) for i in parts]

    def pair(self, k, i):
        sy, ss = self.spots[k]
        self.near[k][i].wait_recv()
        return add_low(self.x[plane_index(sy, self.c, ss), i], self.near_ref[k, i])

    def middle(self, far):
        for i in self.parts:
            if far:
                self.out_d[i] = self.pair(0, i).astype(BF)
                self.corner[i].start()
                if i % 2 == 1:
                    self.out_y[i] = self.pair(2, i).astype(BF)
                    self.by_y[i].start()
            elif i % 2 == 0:
                self.out_x[i] = self.pair(1, i).astype(BF)
                self.by_x[i].start()

    def last(self):
        for i in self.parts:
            k, out, by = (1, self.out_x, self.by_x) if i % 2 else (2, self.out_y, self.by_y)
            part = self.pair(k, i)
            self.corner[i].wait_recv()
            out[i] = (part + self.in_d[i].astype(F32)).astype(BF)
            by[i].start()

    def result(self, i):
        own = self.pair(3, i)
        self.by_x[i].wait_recv()
        self.by_y[i].wait_recv()
        return own + add_low(self.in_x[i], self.in_y[i])

    def finish(self):
        for copy in [c for spot in self.near for c in spot] + self.corner + self.by_x + self.by_y:
            copy.wait_send()


def plane_corners():
    y, c, z, s = place()
    return [
        (y, 1 - c, s), (1 - y, c, s), (1 - y, 1 - c, s),
        (y, c, 1 - s), (y, 1 - c, 1 - s), (1 - y, c, 1 - s), (1 - y, 1 - c, 1 - s),
    ]


def line_ends(n_line):
    y, c, z, s = place()
    return (z > 0, (y, c, z - 1, s)), (z < n_line - 1, (y, c, z + 1, s)), (y, c, z, 1 - s)


class BlkGather:
    @staticmethod
    def sems(n_line):
        return [
            pltpu.SemaphoreType.DMA((3,)),
            pltpu.SemaphoreType.DMA((1,)),
            pltpu.SemaphoreType.DMA((4, n_line)),
            pltpu.SemaphoreType.DMA((4, n_line)),
            pltpu.SemaphoreType.DMA((1,)),
        ]

    def __init__(self, n_line, pick_x, pick_o, own_send, own_recv, send, recv, local):
        y, c, z, s = place()
        self.z, self.s, self.n = z, s, n_line
        (self.has_low, self.low), (self.has_high, self.high), self.cross = line_ends(n_line)
        self.pick_x, self.pick_o = pick_x, pick_o
        self.sem = (own_send, own_recv, send, recv, local)

    def block(self, way, k):
        z = self.z - k if way == 0 else self.z + k
        return self.pick_o(z * 2 + self.s)

    def own(self, way):
        own_send, own_recv, send, recv, local = self.sem
        arrival = own_recv.at[0] if way == 2 else recv.at[way, 0]
        target = (self.high, self.low, self.cross)[way]
        return remote(self.pick_x(), self.pick_o(self.z * 2 + self.s), own_send.at[way], arrival, target)

    def keep(self):
        return pltpu.make_async_copy(self.pick_x(), self.pick_o(self.z * 2 + self.s), self.sem[4].at[0])

    def onward(self, way, k):
        send, recv = self.sem[2:4]
        target = self.high if way == 0 else self.low
        return remote(self.block(way, k), self.block(way, k), send.at[way, k], recv.at[way, k], target)

    def over(self, way, k):
        send, recv = self.sem[2:4]
        return remote(self.block(way, k), self.block(way, k), send.at[2 + way, k], recv.at[2 + way, k], self.cross)

    def arrive(self, way, k):
        send, recv = self.sem[2:4]
        return remote(self.block(way, k), self.block(way, k), send.at[way, k], recv.at[way, k - 1], self.cross)

    def there(self, way, k):
        return self.z >= k if way == 0 else self.z + k < self.n

    def start(self):
        pl.when(self.has_high)(lambda: self.own(0).start())
        pl.when(self.has_low)(lambda: self.own(1).start())
        self.own(2).start()
        self.keep().start()

    def take(self, way, k):
        self.arrive(way, k).wait_recv()
        pl.when((self.has_high, self.has_low)[way])(lambda: self.onward(way, k).start())
        self.over(way, k).start()

    def step(self, k):
        for way in (0, 1):
            pl.when(self.there(way, k))(lambda: self.take(way, k))

    def finish_arrivals(self):
        self.own(2).wait_recv()
        for k in range(1, self.n):
            for way in (0, 1):
                pl.when(self.there(way, k))(lambda: self.over(way, k).wait_recv())
        self.keep().wait()

    def finish_sends(self):
        pl.when(self.has_high)(lambda: self.own(0).wait_send())
        pl.when(self.has_low)(lambda: self.own(1).wait_send())
        self.own(2).wait_send()
        for k in range(1, self.n):
            for way in (0, 1):
                @pl.when(self.there(way, k))
                def _():
                    self.over(way, k).wait_send()

                    @pl.when((self.has_high, self.has_low)[way])
                    def _():
                        self.onward(way, k).wait_send()


def blk_greet(n_line):
    low, high, cross = line_ends(n_line)
    greet([cross], [low, high])


class BlkReduce:
    @staticmethod
    def scratch(n_line, a):
        return [
            pltpu.VMEM((n_line,) + a.shape[1:], a.dtype),
            pltpu.VMEM((n_line + 1,) + a.shape[1:], a.dtype),
            pltpu.SemaphoreType.DMA((n_line,)),
            pltpu.SemaphoreType.DMA((n_line,)),
            pltpu.SemaphoreType.DMA((2, n_line)),
            pltpu.SemaphoreType.DMA((2, n_line)),
        ]

    def __init__(self, n_line, x, side_in, line_in, side_send, side_recv, send, recv):
        y, c, self.z, self.s = place()
        self.n = n_line
        (self.has_low, self.low), (self.has_high, self.high), self.cross = line_ends(n_line)
        self.x = x
        self.side_in, self.line_in = side_in, line_in
        self.sem = (side_send, side_recv, send, recv)

    def spot(self, way, k):
        return self.z + k * (1 - 2 * way)

    def exists(self, way, k):
        return (self.spot(way, k) >= 0) & (self.spot(way, k) < self.n)

    def toward(self, way):
        y, c, z, s = place()
        return (y, c, z + 1 - 2 * way, s)

    def side(self, zz):
        side_send, side_recv = self.sem[:2]
        return remote(
            self.x.at[zz * 2 + 1 - self.s], self.side_in.at[zz], side_send.at[zz], side_recv.at[zz], self.cross
        )

    def slot(self, way, k):
        return jnp.where((way == 1) & (k == 0), self.n, self.spot(way, k))

    def move(self, way, k):
        send, recv = self.sem[2:]
        zz = self.spot(way, k)
        there = jnp.where((way == 1) & (k == 1), self.n, zz)
        return remote(
            self.side_in.at[zz], self.line_in.at[there], send.at[way, k], recv.at[way, k - 1], self.toward(way)
        )

    def arrive(self, way, k):
        send, recv = self.sem[2:]
        there = self.line_in.at[self.slot(way, k)]
        return remote(there, there, send.at[way, k], recv.at[way, k], self.toward(1 - way))

    def start(self, k):
        for way in (0, 1) if k > 0 else (0,):
            pl.when(self.exists(way, k))(lambda: self.side(self.spot(way, k)).start())

    def move_on(self, way, k):
        zz = self.spot(way, k)
        self.side(zz).wait_recv()
        passed = jnp.where(way == 0, self.has_low, self.has_high)

        @pl.when(passed)
        def _():
            self.arrive(way, k).wait_recv()
            self.side_in[zz] = add_low(
                self.x[zz * 2 + self.s], self.side_in[zz], self.line_in[zz]
            ).astype(self.side_in.dtype)

        @pl.when(jnp.logical_not(passed))
        def _():
            self.side_in[zz] = add_low(self.x[zz * 2 + self.s], self.side_in[zz]).astype(
                self.side_in.dtype
            )

        self.move(way, k).start()

    def step(self, k):
        def one(way, carry):
            pl.when(self.exists(way, k))(lambda: self.move_on(way, k))
            return carry

        lax.fori_loop(0, 2, one, 0)

    def result(self, o):
        z = self.z
        self.side(z).wait_recv()
        pl.when(self.has_low)(lambda: self.arrive(0, 0).wait_recv())
        pl.when(self.has_high)(lambda: self.arrive(1, 0).wait_recv())
        own = lambda: add_low(self.x[z * 2 + self.s], self.side_in[z])
        both = self.has_low & self.has_high

        @pl.when(both)
        def _():
            o[...] = (own() + add_low(self.line_in[z], self.line_in[self.n])).astype(o.dtype)

        @pl.when(jnp.logical_not(both))
        def _():
            other = self.line_in[jnp.where(self.has_low, z, self.n)].astype(F32)
            o[...] = (own() + other).astype(o.dtype)

    def finish(self):
        for k in range(self.n - 1, -1, -1):
            for way in (0, 1) if k > 0 else (0,):
                @pl.when(self.exists(way, k))
                def _():
                    self.side(self.spot(way, k)).wait_send()
                    if k > 0:
                        self.move(way, k).wait_send()


class LineGather:
    @staticmethod
    def sems(n_line):
        dma = pltpu.SemaphoreType.DMA
        return [dma((2,)), dma((2, n_line)), dma((2, n_line)), dma((1,))]

    def __init__(self, n_line, pick_x, pick_o, own_send, send, recv, local):
        y, c, self.z, s = place()
        self.n = n_line
        (self.has_low, self.low), (self.has_high, self.high), _ = line_ends(n_line)
        self.pick_x, self.pick_o = pick_x, pick_o
        self.own_send, self.send, self.recv, self.local = own_send, send, recv, local

    def goes(self, way):
        return (self.has_high, self.has_low)[way]

    def own(self, way):
        target = (self.high, self.low)[way]
        return remote(self.pick_x(), self.pick_o(self.z), self.own_send.at[way], self.recv.at[way, 0], target)

    def keep(self):
        return pltpu.make_async_copy(self.pick_x(), self.pick_o(self.z), self.local.at[0])

    def onward(self, way, k):
        block = self.pick_o(self.z - k if way == 0 else self.z + k)
        target = (self.high, self.low)[way]
        return remote(block, block, self.send.at[way, k], self.recv.at[way, k], target)

    def arrive(self, way, k):
        block = self.pick_o(self.z - k if way == 0 else self.z + k)
        return remote(block, block, self.send.at[way, k], self.recv.at[way, k - 1], (self.low, self.high)[way])

    def there(self, way, k):
        return self.z >= k if way == 0 else self.z + k < self.n

    def start(self):
        for way in (0, 1):
            pl.when(self.goes(way))(lambda: self.own(way).start())
        self.keep().start()

    def step(self, k):
        for way in (0, 1):
            @pl.when(self.there(way, k))
            def _():
                self.arrive(way, k).wait_recv()
                pl.when(self.goes(way))(lambda: self.onward(way, k).start())

    def finish(self):
        self.keep().wait()
        for way in (0, 1):
            pl.when(self.goes(way))(lambda: self.own(way).wait_send())
            for k in range(1, self.n):
                pl.when(self.there(way, k) & self.goes(way))(lambda: self.onward(way, k).wait_send())


class LineReduce:
    @staticmethod
    def scratch(n_line, a):
        dma = pltpu.SemaphoreType.DMA
        return [
            pltpu.VMEM((n_line,) + a.shape[1:], a.dtype),
            pltpu.VMEM((n_line + 1,) + a.shape[1:], a.dtype),
            dma((2, n_line)), dma((2, n_line)),
        ]

    def __init__(self, n_line, x, sums, line_in, send, recv):
        y, c, self.z, s = place()
        self.n, self.x, self.sums, self.line_in, self.send, self.recv = n_line, x, sums, line_in, send, recv
        (self.has_low, self.low), (self.has_high, self.high), _ = line_ends(n_line)

    def spot(self, way, k):
        return self.z + k * (1 - 2 * way)

    def exists(self, way, k):
        return (self.spot(way, k) >= 0) & (self.spot(way, k) < self.n)

    def passed(self, way):
        return jnp.where(way == 0, self.has_low, self.has_high)

    def slot(self, way, k):
        return jnp.where((way == 1) & (k == 0), self.n, self.spot(way, k))

    def toward(self, way):
        y, c, z, s = place()
        return (y, c, z + 1 - 2 * way, s)

    def move(self, way, k, source):
        zz = self.spot(way, k)
        there = jnp.where((way == 1) & (k == 1), self.n, zz)
        return remote(
            source.at[zz], self.line_in.at[there], self.send.at[way, k], self.recv.at[way, k - 1], self.toward(way)
        )

    def arrive(self, way, k):
        there = self.line_in.at[self.slot(way, k)]
        return remote(there, there, self.send.at[way, k], self.recv.at[way, k], self.toward(1 - way))

    def step(self, k):
        def one(way, carry):
            exists, passed = self.exists(way, k), self.passed(way)

            @pl.when(exists & passed)
            def _():
                zz = self.spot(way, k)
                self.arrive(way, k).wait_recv()
                self.sums[zz] = add_low(self.x[zz], self.line_in[zz]).astype(self.sums.dtype)
                self.move(way, k, self.sums).start()

            pl.when(exists & jnp.logical_not(passed))(lambda: self.move(way, k, self.x).start())
            return carry

        lax.fori_loop(0, 2, one, 0)

    def result(self, o):
        z = self.z
        pl.when(self.has_low)(lambda: self.arrive(0, 0).wait_recv())
        pl.when(self.has_high)(lambda: self.arrive(1, 0).wait_recv())
        both = self.has_low & self.has_high

        @pl.when(both)
        def _():
            o[...] = add_low(self.x[z], self.line_in[z], self.line_in[self.n]).astype(o.dtype)

        @pl.when(jnp.logical_not(both))
        def _():
            o[...] = add_low(self.x[z], self.line_in[jnp.where(self.has_low, z, self.n)]).astype(o.dtype)

    def finish(self):
        for k in range(self.n - 1, 0, -1):
            for way in (0, 1):
                pl.when(self.exists(way, k))(lambda: self.move(way, k, self.sums).wait_send())


def lane_chunks(width):
    cut = width // 256 * 128
    return [slice(0, cut), slice(cut, width)]


LINE_CHUNKS = 2


def line_gathers(n_line, x, pick_o, sems):
    jobs = []
    for i, lanes in enumerate(lane_chunks(x.shape[-1])):
        cut = (slice(None),) * (len(x.shape) - 1) + (lanes,)
        jobs.append(
            LineGather(
                n_line, lambda cut=cut: x.at[cut], lambda z, cut=cut: pick_o(z).at[cut],
                *sems[4 * i : 4 * i + 4],
            )
        )
    return jobs


def line_gather_sems(n_line):
    return LineGather.sems(n_line) * LINE_CHUNKS


def line_reduces(n_line, x, scratch):
    jobs = []
    for i, lanes in enumerate(lane_chunks(x.shape[-1])):
        cut = (slice(None),) * (len(x.shape) - 1) + (lanes,)
        jobs.append((LineReduce(n_line, x.at[cut], *scratch[4 * i : 4 * i + 4]), cut[1:]))
    return jobs


def line_reduce_scratch(n_line, a):
    scratch = []
    for lanes in lane_chunks(a.shape[-1]):
        one = jax.ShapeDtypeStruct(a.shape[:-1] + (lanes.stop - lanes.start,), a.dtype)
        scratch += LineReduce.scratch(n_line, one)
    return scratch


def comm_call(
    kernel, name, collective_id, args, outs, scratch, micros, room=VMEM_BYTES, far_args=(), far_outs=(), late=()
):
    vmem, anyway = pl.BlockSpec(memory_space=pltpu.VMEM), pl.BlockSpec(memory_space=pl.ANY)
    held = [pltpu.VMEM(args[i].shape, args[i].dtype) for i in late]
    held += [pltpu.SemaphoreType.DMA((len(late),))] * (len(late) > 0)

    def whole(*refs):
        refs = list(refs)
        mine, copies = refs[len(refs) - len(held) :], []
        refs = refs[: len(refs) - len(held)]
        for j, i in enumerate(late):
            copies.append(pltpu.make_async_copy(refs[i], mine[j], mine[-1].at[j]))
            copies[-1].start()
            refs[i] = mine[j]

        def ready():
            for copy in copies:
                copy.wait()

        kernel(ready, *refs)

    return pl.pallas_call(
        whole,
        out_shape=[jax.ShapeDtypeStruct(shape, dtype) for shape, dtype in outs],
        in_specs=[anyway if i in far_args or i in late else vmem for i in range(len(args))],
        out_specs=[anyway if i in far_outs else vmem for i in range(len(outs))],
        scratch_shapes=list(scratch) + held,
        compiler_params=params(collective_id, room),
        cost_estimate=pl.CostEstimate(flops=0, bytes_accessed=micros * 3_000_000, transcendentals=0),
        name=name,
    )(*args)


def exit_kernel(
    n_line, ready, x, dq, dkv, yy_ref, cc_ref, cos, sin, scale, wq, wk, wv, res, oc, dc, alpha, rest, gg,
    gq_o, gk_o, gv_o, gh_o, go_o, gd_o, sum_o, gg_o, oc_o, dc_o,
    flat, acc, gq, gk, gv, gh, scale_s,
    alpha_in, line_out, line_all, oc_s, oc_r, dc_s, dc_r, al_s, al_r, su_s, su_r, keep, *scratch,
):
    y, c, z, s = place()
    u, p, b, n_blk = y * 2 + c, plane_index(y, c, s), z * 2 + s, 2 * n_line
    low, high, cross = line_ends(n_line)
    corners = plane_corners()
    others = []
    for i in range(1, n_blk):
        to = lax.rem(b + i, n_blk)
        others.append((y, c, to // 2, lax.rem(to, 2)))
    once = [(to[3] != 1 - s) | (to[2] != z) for to in others]
    greet([(yy, cc, z, ss) for yy, cc, ss in corners], list(zip(once, others)))
    each = 6
    jobs = [BlkReduce(n_line, g, *scratch[each * i : each * (i + 1)]) for i, g in enumerate((gq, gk, gv))]
    split = each * 3 + len(UlyReduce.scratch(gh))
    hid = UlyReduce(gh, *scratch[each * 3 : split])
    gates = line_reduces(n_line, gg, scratch[split:])
    small, cols = [], []
    for k, (yy, cc, ss) in enumerate(corners):
        target = (yy, cc, z, ss)
        cols.append(remote(dc.at[plane_index(yy, cc, ss)], dc_o.at[p], dc_s.at[k], dc_r.at[k], target))
        if k < 3:
            cols.append(remote(oc.at[yy * 2 + cc], oc_o.at[u], oc_s.at[k], oc_r.at[k], target))
            small.append(remote(alpha.at[yy * 2 + cc], alpha_in.at[k], al_s.at[k], al_r.at[k], target))
    for job in small:
        job.start()
    for job, _ in gates:
        job.step(n_line - 1)
    ready()
    rows_all = x[...]
    seqs, group_rows, wide = dq.shape
    heads = wide // 128
    factor = jnp.where(lanes_of((1, 128)) < HEAD_DIM, HEAD_DIM**0.5, 1.0)
    late_steps = [(min(1 + 2 * i, heads - 1), k) for i, k in enumerate(range(n_line - 2, 0, -1))]

    def head(h, carry):
        lanes = pl.ds(pl.multiple_of(h * 128, 128), 128)
        queries = jnp.concatenate([dq[i, :, lanes] for i in range(seqs)], axis=0)
        pairs = jnp.concatenate([dkv[i, :, lanes] for i in range(seqs)], axis=0)
        low_half = lanes_of(queries.shape) < HEAD_DIM
        dy = jnp.where(low_half, queries.astype(F32), pltpu.roll(pairs.astype(F32), HEAD_DIM, 1))
        unit = yy_ref[:, lanes]
        scale_s[h] = jnp.sum(dy * unit, axis=0, keepdims=True) * factor
        dy = dy * scale[pl.ds(h, 1)]
        dr = cc_ref[:, lanes] * (dy - unit * halves(unit * dy))
        raw = (dr * cos[...] - turn(dr) * sin[...]).astype(BF)
        both = jnp.concatenate([raw, jnp.where(low_half, jnp.zeros_like(pairs), pairs)], axis=1)
        grad = dot_tn(both, rows_all).astype(BF)
        at = pl.ds(pl.multiple_of(h * HEAD_DIM, HEAD_DIM), HEAD_DIM)
        for j, lo in enumerate((0, HEAD_DIM, 3 * HEAD_DIM)):
            flat[j, at] = grad[lo : lo + HEAD_DIM]
        w_value = wv[h]
        more = dot_nn(both, jnp.concatenate([wq[h], wk[h], jnp.zeros_like(w_value), w_value], axis=0))

        @pl.when(h == 0)
        def _():
            acc[...] = more

        @pl.when(h > 0)
        def _():
            acc[...] = acc[...] + more

        for when, k in late_steps:
            @pl.when(h == when)
            def _():
                for job, _ in gates:
                    job.step(k)

        return carry

    lax.fori_loop(0, heads, head, 0)
    each_rows = gq.shape[1]
    for i, g in enumerate((gq, gk, gv)):
        for k in range(n_blk):
            g[k] = flat[i, k * each_rows : (k + 1) * each_rows]
    for i in range(seqs):
        gh[i] = acc[i * group_rows : (i + 1) * group_rows].astype(BF).reshape(gh.shape[1:])
    hid.start()
    for k in range(n_line - 1, -1, -1):
        for job in jobs:
            job.start(k)
    mine = [
        pltpu.make_async_copy(dc.at[p], dc_o.at[p], keep.at[0]),
        pltpu.make_async_copy(oc.at[u], oc_o.at[u], keep.at[1]),
    ]
    for job in mine:
        job.start()
    hid.middle()
    for job in cols:
        job.start()
    for job in small:
        job.wait_recv()
    line_out[...] = rest[...]
    line_out[:, :, :128] = alpha[u] + alpha_in[0] + alpha_in[1] + alpha_in[2]
    scales = jnp.concatenate(
        [scale_s[h][:, :HEAD_DIM] + scale_s[h][:, HEAD_DIM:] for h in range(heads)], axis=1
    )
    for k in range(n_blk):
        line_out[k, :, 128 : 128 + each_rows] = scales[:, k * each_rows : (k + 1) * each_rows]
    line_jobs = []
    for i in range(1, n_blk):
        to = lax.rem(b + i, n_blk)
        line_jobs.append(
            remote(line_out.at[to], line_all.at[i - 1], su_s.at[i - 1], su_r.at[i - 1], others[i - 1])
        )
    for job in line_jobs:
        job.start()
    for k in range(n_line - 1, 0, -1):
        for job in jobs:
            job.step(k)
    for i in range(gh.shape[0]):
        gh_o[i] = res[i] + hid.result(i)
    for job in cols:
        job.wait_recv()
    for job in mine:
        job.wait()
    wide, ff_each = oc.shape[-1], dc.shape[-1] // n_line
    for v in range(4):
        go_o[:, v * wide : (v + 1) * wide] = oc_o[v].astype(F32)
        for t in (0, 1):
            for k in range(n_line):
                at = ((v * n_line + k) * 2 + t) * ff_each
                gd_o[:, at : at + ff_each] = dc_o[v * 2 + t, :, k * ff_each : (k + 1) * ff_each].astype(F32)
    total = line_out[b]
    for i, job in enumerate(line_jobs):
        job.wait_recv()
        total = total + line_all[i]
    sum_o[...] = total
    for job, o in zip(jobs, (gq_o, gk_o, gv_o)):
        job.result(o)
    for job, cut in gates:
        job.result(gg_o.at[cut])
        job.finish()
    hid.finish()
    for job in jobs:
        job.finish()
    for job in line_jobs + small:
        job.wait_send()
    for job in cols:
        job.wait_send()


def leave(n_line, x, dq, dkv, y, c, cos, sin, scale, wq, wk, wv, res, oc, dc, alpha, rest, gg):
    n_blk = 2 * n_line
    heads, _, width = wq.shape
    seqs, rows, _ = res.shape
    vmem = pl.BlockSpec(memory_space=pltpu.VMEM)
    dma = pltpu.SemaphoreType.DMA
    grad = jax.ShapeDtypeStruct((n_blk, heads * HEAD_DIM // n_blk, width), BF)
    gh = jax.ShapeDtypeStruct((seqs, 4, rows, width), BF)
    scratch = [
        pltpu.VMEM(oc.shape, oc.dtype),
        pltpu.VMEM(dc.shape, dc.dtype),
        pltpu.VMEM((3, heads * HEAD_DIM, width), BF),
        pltpu.VMEM(x.shape, F32),
        pltpu.VMEM(grad.shape, BF), pltpu.VMEM(grad.shape, BF), pltpu.VMEM(grad.shape, BF),
        pltpu.VMEM(gh.shape, BF),
        pltpu.VMEM((heads, 1, 128), F32),
        pltpu.VMEM((3,) + alpha.shape[1:], F32),
        pltpu.VMEM(rest.shape, F32),
        pltpu.VMEM((n_blk - 1,) + rest.shape[1:], F32),
        dma((3,)), dma((3,)), dma((7,)), dma((7,)), dma((3,)), dma((3,)),
        dma((n_blk - 1,)), dma((n_blk - 1,)), dma((2,)),
    ]
    scratch += BlkReduce.scratch(n_line, grad) * 3
    scratch += UlyReduce.scratch(gh) + line_reduce_scratch(n_line, gg)
    args = (x, dq, dkv, y, c, cos, sin, scale, wq, wk, wv, res, oc, dc, alpha, rest, gg)
    outs = [grad.shape[1:]] * 3 + [
        res.shape, (oc.shape[1], 4 * oc.shape[2]), (dc.shape[1], 8 * dc.shape[2]), rest.shape[1:], gg.shape[1:]
    ]
    return comm_call(
        functools.partial(exit_kernel, n_line), "leave", 8, args, [(shape, F32) for shape in outs], scratch,
        60, late=tuple(range(11)),
    )


def entry_kernel(
    n_line, hid, small, wq, wk, wv, wo, wd, wu,
    hid_o, small_o, wq_o, wk_o, wv_o, oc_o, dc_o, wu_o, oc, dc, *sems
):
    y, c, z, s = place()
    u, p = y * 2 + c, plane_index(y, c, s)
    low, high, cross = line_ends(n_line)
    corners = plane_corners()
    greet([(yy, cc, z, ss) for yy, cc, ss in corners], [low, high])
    hid_job = UlyGather(hid, hid_o, *sems[:3])
    at, jobs = 3, []
    for x, pick in (
        (small, lambda block: small_o.at[u, block]),
        (wq, lambda block: wq_o.at[block]),
        (wk, lambda block: wk_o.at[block]),
        (wv, lambda block: wv_o.at[block]),
    ):
        jobs.append(BlkGather(n_line, lambda x=x: x, pick, *sems[at : at + 5]))
        at += 5
    first = wu_o.shape[-1]
    up_jobs = [
        LineGather(n_line, lambda: wu.at[:, slice(0, first)], lambda z: wu_o.at[z], *sems[at : at + 4])
    ]
    oc_s, oc_r, dc_s, dc_r, sm_s, sm_r, keep = sems[at + 4 :]
    jobs[0].start()
    for job in jobs[1:]:
        job.start()
    hid_job.start()
    for v in range(4):
        wide = oc.shape[-1]
        oc[v] = wo[:, v * wide : (v + 1) * wide]
        ff_each = dc.shape[-1] // n_line
        for t in (0, 1):
            for k in range(n_line):
                at = ((v * n_line + k) * 2 + t) * ff_each
                dc[v * 2 + t, :, k * ff_each : (k + 1) * ff_each] = wd[:, at : at + ff_each]
    col_jobs = []
    for k, (yy, cc, ss) in enumerate(corners):
        target = (yy, cc, z, ss)
        col_jobs.append(
            remote(dc.at[plane_index(yy, cc, ss)], dc_o.at[p], dc_s.at[k], dc_r.at[k], target)
        )
        if k < 3:
            col_jobs.append(remote(oc.at[yy * 2 + cc], oc_o.at[u], oc_s.at[k], oc_r.at[k], target))
    for job in col_jobs:
        job.start()
    for job in up_jobs:
        job.start()
    mine = [
        pltpu.make_async_copy(dc.at[p], dc_o.at[p], keep.at[0]),
        pltpu.make_async_copy(oc.at[u], oc_o.at[u], keep.at[1]),
    ]
    for job in mine:
        job.start()
    for k in range(1, n_line):
        for job in jobs:
            job.step(k)
        if k == 1:
            hid_job.forward()
    jobs[0].finish_arrivals()
    small_jobs = [
        remote(small_o.at[u], small_o.at[u], sm_s.at[k], sm_r.at[k], (yy, cc, z, ss))
        for k, (yy, cc, ss) in enumerate(corners[:3])
    ]
    for job in small_jobs:
        job.start()
    for k in range(1, n_line):
        for job in up_jobs:
            job.step(k)
    for job in jobs[1:]:
        job.finish_arrivals()
    hid_job.finish()
    for job in up_jobs:
        job.finish()
    for job in small_jobs + col_jobs:
        job.wait()
    for job in mine:
        job.wait()
    for job in jobs:
        job.finish_sends()


def entry(n_line, hid, small, wq, wk, wv, wo, wd, wu):
    n_blk = 2 * n_line
    oc = jax.ShapeDtypeStruct((4, wo.shape[0], wo.shape[1] // 4), wo.dtype)
    dc = jax.ShapeDtypeStruct((8, wd.shape[0], wd.shape[1] // 8), wd.dtype)
    parts = hid.shape[0]
    vmem, anyway = pl.BlockSpec(memory_space=pltpu.VMEM), pl.BlockSpec(memory_space=pl.ANY)

    def out(shape, like):
        return jax.ShapeDtypeStruct(shape, like.dtype)

    return pl.pallas_call(
        functools.partial(entry_kernel, n_line),
        out_shape=[
            out((parts, 4) + hid.shape[1:], hid),
            out((4, n_blk) + small.shape, small),
            out((n_blk,) + wq.shape, wq),
            out((n_blk,) + wk.shape, wk),
            out((n_blk,) + wv.shape, wv),
            out(oc.shape, oc),
            out(dc.shape, dc),
            out((n_line, wu.shape[0], lane_chunks(wu.shape[1])[0].stop), wu),
        ],
        in_specs=[vmem] * 8,
        out_specs=[vmem, vmem, anyway, anyway, anyway, vmem, vmem, anyway],
        scratch_shapes=[pltpu.VMEM(oc.shape, oc.dtype), pltpu.VMEM(dc.shape, dc.dtype)]
        + UlyGather.sems(parts)
        + BlkGather.sems(n_line) * 4
        + LineGather.sems(n_line)
        + [pltpu.SemaphoreType.DMA((3,))] * 2
        + [pltpu.SemaphoreType.DMA((7,))] * 2
        + [pltpu.SemaphoreType.DMA((3,))] * 2
        + [pltpu.SemaphoreType.DMA((2,))],
        compiler_params=params(6),
        cost_estimate=pl.CostEstimate(flops=0, bytes_accessed=40 * 3_000_000, transcendentals=0),
        name="entry",
    )(hid, small, wq, wk, wv, wo, wd, wu)
def dot_nt(a, b):
    return lax.dot_general(a, b, (((1,), (1,)), ((), ())), preferred_element_type=F32)


def dot_nn(a, b):
    return lax.dot_general(a, b, (((1,), (0,)), ((), ())), preferred_element_type=F32)


def dot_tn(a, b):
    return lax.dot_general(a, b, (((0,), (0,)), ((), ())), preferred_element_type=F32)


def lanes_of(shape):
    return lax.broadcasted_iota(jnp.int32, shape, len(shape) - 1)


def halves(x):
    row = lax.broadcasted_iota(jnp.int32, (128, 128), 0) // HEAD_DIM
    same = jnp.where(row == lanes_of((128, 128)) // HEAD_DIM, 1.0, 0.0).astype(BF)
    high = x.astype(BF)
    rest = (x - high.astype(F32)).astype(BF)
    return dot_nn(high, same) + dot_nn(rest, same)


def turn(x):
    first = lanes_of(x.shape) % HEAD_DIM < HEAD_DIM // 2
    return jnp.where(first, pltpu.roll(x, 128 - 32, 1), pltpu.roll(x, 32, 1))


def down_columns(row):
    n = row.shape[1]
    one = jnp.transpose(jnp.broadcast_to(row, (128, n)))
    return jnp.concatenate([one] * (n // 128), axis=1)


def arrivals(n_line, body):
    each = 2 * n_line - 1

    def step(t, carry):
        stage, r = t // each, lax.rem(t, each)
        body(stage, (r + 1) // 2, lax.rem(r + 1, 2))
        return carry

    lax.fori_loop(0, 2 * each, step, 0)


def attend_kernel(
    n_line, ready, x_ref, wq_ref, wk_ref, wv_ref, cos_ref, sin_ref, scale_ref, oc_ref, wg_ref, wu_ref, kp_ref,
    q_ref, y_ref, c_ref, kv_o, oc_o, wg_o, wu_o, o_ref, mixed_ref, inv_ref, kv_ref, acc, total, place_q, *sems,
):
    y, c, z, s = place()
    blk_greet(n_line)
    seqs, rows, wide = q_ref.shape
    heads = wide // 128
    chunk = 4 * LINE_CHUNKS
    cut = wu_ref.shape[-1] - wu_o.shape[-1]
    up = LineGather(
        n_line, lambda: wu_ref.at[:, slice(cut, wu_ref.shape[-1])], lambda zz: wu_o.at[zz], *sems[-4:]
    )
    up.start()
    ready()

    each = len(BlkGather.sems(n_line))
    picks = [
        (lambda i=i: kv_ref.at[i], lambda block, i=i: kv_o.at[block, i]) for i in range(seqs)
    ] + [(lambda: oc_ref, lambda block: oc_o.at[:, block])]
    jobs = [
        BlkGather(n_line, *pick, *sems[each * i : each * (i + 1)]) for i, pick in enumerate(picks)
    ]

    def make(t, carry):
        i, h = t // heads, lax.rem(t, heads)
        lanes = pl.ds(pl.multiple_of(h * 128, 128), 128)
        mine = pl.ds(pl.multiple_of(i * rows, rows), rows)
        wv = wv_ref[h]
        got = dot_nt(x_ref[mine], jnp.concatenate([wq_ref[h], wk_ref[h], jnp.zeros_like(wv), wv], axis=0))
        raw, value = got[:, :128], got[:, 128:]
        low = lanes_of(raw.shape) < HEAD_DIM
        turned = raw * cos_ref[mine] + turn(raw) * sin_ref[mine]
        norm = lax.rsqrt(halves(turned * turned) + HEAD_DIM * tiny_eps)
        unit = turned * norm
        both = unit * scale_ref[pl.ds(h, 1)]
        q_ref[i, :, lanes] = jnp.where(low, both, 0.0).astype(BF)
        kv_ref[i, :, lanes] = jnp.where(low, pltpu.roll(both, HEAD_DIM, 1), value).astype(BF)
        y_ref[mine, lanes] = unit
        c_ref[mine, lanes] = norm
        for j in range(seqs):
            pl.when(t == heads * (j + 1) - 1)(jobs[j].start)
        return carry

    lax.fori_loop(0, seqs * heads, make, 0)
    gates = line_gathers(
        n_line, wg_ref, lambda z: wg_o.at[z], sems[each * (seqs + 1) : each * (seqs + 1) + chunk]
    )
    jobs[-1].start()
    for job in gates:
        job.keep().start()
    acc[...] = jnp.zeros_like(acc)
    total[...] = jnp.zeros_like(total)
    for i in range(seqs):
        place_q[i] = down_columns(kp_ref[i, z * 2 + s])

    def attend_to(i, block, keys):
        allowed = kp_ref[i, block] <= place_q[i]
        for h in range(heads):
            lanes = slice(h * 128, (h + 1) * 128)
            kv = keys(lanes)
            p = jnp.where(allowed, jnp.exp(dot_nt(q_ref[i, :, lanes], kv)), 0.0)
            part = p[:, :128]
            for j in range(1, rows // 128):
                part = part + p[:, j * 128 : (j + 1) * 128]
            total[i, h] = total[i, h] + part
            acc[i, h] = acc[i, h] + dot_nn(p.astype(BF), kv)

    def body(stage, k, way):
        ahead = jnp.where(k == 0, 1, k + 1)

        @pl.when((stage == 1) & ((k == 0) | (way == 1)) & (ahead < n_line))
        def _():
            for job in gates + [up]:
                job.step(ahead)

        there = (k == 0) | jnp.where(way == 0, z >= k, z + k < n_line)

        @pl.when(there)
        def _():
            for job in jobs:
                for w in (0, 1):
                    pl.when((stage == 0) & (k > 0) & (way == w))(lambda: job.take(w, k))
                    pl.when((stage == 1) & (k > 0) & (way == w))(lambda: job.over(w, k).wait_recv())
                pl.when((stage == 1) & (k == 0))(lambda: job.own(2).wait_recv())
                pl.when((stage == 0) & (k == 0))(lambda: job.keep().wait())
            for w, last in ((0, z), (1, n_line - 1 - z)):
                @pl.when((stage == 0) & (k == last) & ((k == 0) | (way == w)))
                def _():
                    for job in gates:
                        pl.when(job.goes(w))(lambda: job.own(w).start())
            zz = jnp.where(way == 0, z - k, z + k)
            block = zz * 2 + jnp.where(stage == 0, s, 1 - s)

            def one(i, carry):
                attend_to(i, block, lambda lanes: kv_o[block, i, :, lanes])
                return carry

            lax.fori_loop(0, seqs, one, 0)

    arrivals(n_line, body)
    low = lanes_of((rows, 128)) < HEAD_DIM
    for i in range(seqs):
        outs = []
        for h in range(heads):
            inverse = 1.0 / jnp.broadcast_to(jnp.sum(total[i, h], axis=-1, keepdims=True), (rows, 128))
            out = acc[i, h] * inverse
            o_ref[i, h] = out
            inv_ref[i, h] = jnp.transpose(inverse)[:8]
            outs.append(out)
        for h in range(0, heads - 1, 2):
            mixed_ref[i, :, h * HEAD_DIM : (h + 2) * HEAD_DIM] = jnp.where(
                low, pltpu.roll(outs[h], HEAD_DIM, 1), outs[h + 1]
            ).astype(BF)
        if heads % 2 == 1:
            mixed_ref[i, :, (heads - 1) * HEAD_DIM :] = pltpu.roll(outs[-1], HEAD_DIM, 1)[:, :HEAD_DIM].astype(BF)
    for job in jobs:
        job.finish_sends()
    for job in gates + [up]:
        job.finish()


def attend(n_line, seqs, x, wq, wk, wv, cos, sin, scale, oc, wg, wu, k_places):
    tokens, width = x.shape
    n_blk, heads, rows = 2 * n_line, wq.shape[0], tokens // seqs
    head, wide = (seqs, heads, rows, 128), (seqs, rows, heads * 128)
    flat = ((tokens, heads * 128), F32)
    first = lane_chunks(width)[0].stop
    return comm_call(
        functools.partial(attend_kernel, n_line), "attend", 5,
        (x, wq, wk, wv, cos, sin, scale, oc, wg, wu, k_places),
        [
            (wide, BF), flat, flat, ((n_blk,) + wide, BF), (oc.shape[:1] + (n_blk,) + oc.shape[1:], BF),
            ((n_line,) + wg.shape, BF), ((n_line, wu.shape[0], width - first), BF), (head, F32),
            ((seqs, rows, heads * HEAD_DIM), BF), ((seqs, heads, 8, rows), F32),
        ],
        [pltpu.VMEM(wide, BF), pltpu.VMEM(head, F32), pltpu.VMEM(head, F32), pltpu.VMEM((seqs, rows, rows), F32)]
        + BlkGather.sems(n_line) * (seqs + 1) + line_gather_sems(n_line) + LineGather.sems(n_line),
        90, far_outs=(4, 5, 6), late=(0, 1, 2, 3, 4, 5),
    )


def attend_back_kernel(
    n_line, fits, ready, q_ref, low_ref, w_ref, mixed_ref, o_ref, inv_ref, kv_ref, kp_ref, gu_ref,
    dq_ref, dkv_ref, oc_ref, gu_o, dz, delta, dq, parts, oparts, key_s, key_sem, *scratch,
):
    y, c, z, s = place()
    blk_greet(n_line)
    seqs, rows, wide = q_ref.shape
    heads, width = wide // 128, low_ref.shape[-1]
    each = 6
    ups = line_reduces(n_line, gu_ref, scratch[each * (seqs + 1) :])
    for line_job, _ in ups:
        line_job.step(n_line - 1)
    ready()
    low_rows = low_ref[...].reshape(seqs * rows, width)
    grad = dot_tn(low_rows, mixed_ref[...].reshape(seqs * rows, mixed_ref.shape[-1])).astype(BF)
    n_blk, each_out = 2 * n_line, width // (8 * n_line)
    for b in range(n_blk):
        for v in range(4):
            at = (v * n_blk + b) * each_out
            oparts[b, v * each_out : (v + 1) * each_out] = grad[at : at + each_out]
    each = 6
    jobs = [BlkReduce(n_line, parts.at[:, i], *scratch[each * i : each * (i + 1)]) for i in range(seqs)]
    out_job = BlkReduce(n_line, oparts, *scratch[each * seqs : each * (seqs + 1)])
    for k in range(n_line - 1, -1, -1):
        out_job.start(k)
    low = lanes_of((rows, 128)) < HEAD_DIM
    for i in range(seqs):
        d = dot_nn(low_rows[i * rows : (i + 1) * rows], w_ref[...]).astype(BF).astype(F32)
        for h in range(heads):
            at = h // 2 * 128
            if h == heads - 1 and heads % 2 == 1:
                tile = jnp.concatenate([jnp.zeros((rows, HEAD_DIM), F32), d[:, at:]], axis=1)
            else:
                tile = d[:, at : at + 128]
                if h % 2 == 0:
                    tile = pltpu.roll(tile, HEAD_DIM, 1)
                tile = jnp.where(low, 0.0, tile)
            dz[i, h] = tile.astype(BF)
            row = jnp.sum(tile * o_ref[i, h], axis=-1, keepdims=True)
            delta[i, h] = jnp.transpose(jnp.broadcast_to(row, (rows, 128)))[:8]
    dq[...] = jnp.zeros_like(dq)

    def block_of(block):
        if fits:
            keys = kv_ref.at[block]
        else:
            keys = key_s
            copy = pltpu.make_async_copy(kv_ref.at[block], key_s, key_sem.at[0])
            copy.start()
            copy.wait()
        def one(i, carry):
            allowed = down_columns(kp_ref[i, block]) <= kp_ref[i, z * 2 + s]
            for h in range(heads):
                lanes = slice(h * 128, (h + 1) * 128)
                kv = keys[i, :, lanes]
                pair = jnp.concatenate([q_ref[i, :, lanes], dz[i, h]], axis=0)
                scores = dot_nt(kv, pair)
                p = jnp.where(allowed, jnp.exp(scores[:, :rows]) * inv_ref[i, h][:1], 0.0)
                ds = (p * (scores[:, rows:] - delta[i, h][:1])).astype(BF)
                parts[block, i, :, lanes] = dot_nn(
                    jnp.concatenate([ds, p.astype(BF)], axis=1), pair
                ).astype(BF)
                dq[i, h] = dq[i, h] + dot_tn(ds, kv)
            return carry

        lax.fori_loop(0, seqs, one, 0)

    def step(t, carry):
        k, r = n_line - 1 - t // 4, lax.rem(t, 4)
        way, stays = r // 2, lax.rem(r, 2)

        @pl.when((r == 0) & (k > 0) & (k < n_line - 1))
        def _():
            for line_job, _ in ups:
                line_job.step(k)

        there = jnp.where(k == 0, way == 0, jnp.where(way == 0, z + k < n_line, z >= k))

        @pl.when(there)
        def _():
            zz = jnp.where(way == 0, z + k, z - k)
            block_of(zz * 2 + jnp.where(stays == 0, 1 - s, s))

            @pl.when(stays == 0)
            def _():
                for job in jobs:
                    job.side(zz).start()

        @pl.when((r == 3) & (k + 1 < n_line))
        def _():
            for w in (0, 1):
                @pl.when(jobs[0].exists(w, k + 1))
                def _():
                    for job in jobs + [out_job]:
                        job.move_on(w, k + 1)

        return carry

    lax.fori_loop(0, 4 * n_line, step, 0)
    for i in range(seqs):
        for h in range(heads):
            dq_ref[i, :, h * 128 : (h + 1) * 128] = dq[i, h].astype(BF)
    out_job.result(oc_ref)
    for i, job in enumerate(jobs):
        job.result(dkv_ref.at[i])
    for job, cut in ups:
        job.result(gu_o.at[cut])
    for job in jobs + [out_job] + [job for job, _ in ups]:
        job.finish()


def attend_back(n_line, q, low, w, mixed, o, inv, kv, k_places, gu):
    seqs, rows, wide = q.shape
    n_blk, heads = 2 * n_line, wide // 128
    head = (seqs, heads, rows, 128)
    width, columns = w.shape
    out_shape = (width // n_blk, columns)
    one = jax.ShapeDtypeStruct((n_blk,) + kv.shape[2:], BF)
    out_one = jax.ShapeDtypeStruct((n_blk,) + out_shape, BF)
    fits = kv.size * 2 <= 8_000_000
    return comm_call(
        functools.partial(attend_back_kernel, n_line, fits), "attend_back", 7,
        (q, low, w, mixed, o, inv, kv, k_places, gu),
        [(q.shape, BF), (kv.shape[1:], BF), (out_shape, BF), (gu.shape[1:], F32)],
        [
            pltpu.VMEM(head, BF), pltpu.VMEM((seqs, heads, 8, rows), F32), pltpu.VMEM(head, F32),
            pltpu.VMEM(kv.shape, BF), pltpu.VMEM(out_one.shape, BF),
            pltpu.VMEM((16, 128) if fits else kv.shape[1:], BF), pltpu.SemaphoreType.DMA((1,)),
        ]
        + BlkReduce.scratch(n_line, one) * seqs + BlkReduce.scratch(n_line, out_one)
        + line_reduce_scratch(n_line, gu),
        75, 67_000_000, () if fits else (6,), late=(0, 1, 2, 3, 4) + (6,) * fits,
    )


def unit_of(x):
    c = lax.rsqrt(jnp.sum(x * x, axis=-1, keepdims=True) + x.shape[-1] * tiny_eps)
    return x * c, c


def unit_back(y, c, dy):
    return c * (dy - y * jnp.sum(y * dy, axis=-1, keepdims=True))


class Late:
    @staticmethod
    def scratch(arrays):
        return [pltpu.VMEM(a.shape, a.dtype) for a in arrays] + [pltpu.SemaphoreType.DMA((len(arrays),))]

    def __init__(self, refs, scratch):
        *self.bufs, sem = scratch
        self.copies = [
            pltpu.make_async_copy(ref, buf, sem.at[i]) for i, (ref, buf) in enumerate(zip(refs, self.bufs))
        ]
        for copy in self.copies:
            copy.start()

    def __call__(self, i):
        self.copies[i].wait()
        return self.bufs[i]


def attn_joint_kernel(
    n_line, ready, mixed, w, hid, rate, dc, first_o, ua_o, ca_o, cv_o, all_o, down_o, part, low, *scratch
):
    ends = line_ends(n_line)
    greet(plane_peers(), ends[:2])
    ready()
    split = len(UlyReduce.scratch(part))
    job = UlyReduce(part, *scratch[:split])
    out = PlaneGather(low, all_o, *scratch[split : split + 3])
    downs = line_gathers(n_line, dc, lambda z: down_o.at[:, z], scratch[split + 3 :])
    for line_job in downs:
        line_job.start()
    steps = [(k, line_job) for k in range(1, n_line) for line_job in downs]
    parts, _, rows, width = part.shape
    seqs = mixed.shape[0]
    each = parts // seqs
    for i in range(seqs):
        got = dot_nt(mixed[i], w[...]).astype(BF)
        for k in range(each):
            for u in range(4):
                at = (u * each + k) * rows
                part[i * each + k, u] = got[at : at + rows]
            for copy in job.near[i * each + k]:
                copy.start()
    job.middle()
    k, line_job = steps.pop(0)
    line_job.step(k)
    for i in range(parts):
        ua, ca = unit_of(job.result(i))
        h = hid[i].astype(F32)
        first, cv = unit_of(h + rate[0:1] * (ua - h))
        low[i] = first.astype(BF)
        out.start_part(i)
        first_o[i], ua_o[i] = first, ua
        ca_o[i] = jnp.broadcast_to(ca, (rows, 128))
        cv_o[i] = jnp.broadcast_to(cv, (rows, 128))
        if i > 0:
            out.forward_part(i - 1)
        if len(steps) > 0:
            k, line_job = steps.pop(0)
            line_job.step(k)
    out.forward_part(parts - 1)
    for k, line_job in steps:
        line_job.step(k)
    out.finish()
    job.finish()
    for line_job in downs:
        line_job.finish()


def attn_joint(n_line, mixed, w, hid, rate, dc):
    parts, rows, width = hid.shape
    part = jax.ShapeDtypeStruct((parts, 4, rows, width), BF)
    thin = ((parts, rows, 128), F32)
    return comm_call(
        functools.partial(attn_joint_kernel, n_line), "attn_joint", 1, (mixed, w, hid, rate, dc),
        [
            (hid.shape, F32), (hid.shape, F32), thin, thin, ((8, parts, rows, width), BF),
            (dc.shape[:1] + (n_line,) + dc.shape[1:], BF),
        ],
        [pltpu.VMEM(part.shape, BF), pltpu.VMEM(hid.shape, BF)]
        + UlyReduce.scratch(part) + PlaneGather.sems(parts) + line_gather_sems(n_line),
        25, far_outs=(5,), late=(0, 1, 2, 4),
    )


def plane_products(job, part, y, c, prepare, product):
    _, parts, rows, width = part.shape
    for yy, spots in ((1 - y, (0, 2)), (y, (1, 3))):
        def one(j, carry):
            cc = jnp.where(j == 0, 1 - c, c)
            prepare(yy, cc)
            got = product(yy, cc).astype(BF).reshape(2, parts, rows, width)
            for ss in (0, 1):
                part[plane_index(yy, cc, ss)] = got[ss]

            @pl.when(j == 0)
            def _():
                for k in spots:
                    for copy in job.near[k]:
                        copy.start()

            return carry

        lax.fori_loop(0, 2, one, 0)
        job.middle(spots[0] == 0)


def ff_joint_kernel(
    ready, x, wu, wu2, wg, rate, w, first, cot, out_o, d1_o, sum_o, all_o, inner_h, up_h, gate_h,
    part, low, inner, up_s, gate_s, kept, *scratch,
):
    y, c, z, s = place()
    greet(plane_peers())
    split = len(PlaneReduce.scratch(part))
    job = PlaneReduce(part, *scratch[:split])
    out = PlaneGather(low, all_o, *scratch[split:])
    _, seqs, rows, width = part.shape
    columns, tokens = inner.shape[-1], 2 * seqs * rows
    cut = wu.shape[1]

    def forward(yy, cc):
        block = x[yy, cc].reshape(tokens, width)
        up = dot_nt(block[:, :cut], wu[...]) + dot_nt(block[:, cut:], wu2[...])
        gate = dot_nt(block, wg[...])
        gz = gate * rate[3:4, :columns] * D**0.5
        got = gz / (1.0 + jnp.exp(-gz)) * (up * rate[2:3, :columns])
        inner[yy, cc] = got.astype(BF).reshape(inner.shape[2:])
        up_s[yy, cc] = up.reshape(up_s.shape[2:])
        gate_s[yy, cc] = gate.reshape(gate_s.shape[2:])

    ready()
    plane_products(
        job, part, y, c, forward, lambda yy, cc: dot_nt(inner[yy, cc].reshape(tokens, columns), w[...])
    )
    keeps = [
        pltpu.make_async_copy(a, o, kept.at[i])
        for i, (a, o) in enumerate(((inner, inner_h), (up_s, up_h), (gate_s, gate_h)))
    ]
    for copy in keeps:
        copy.start()
    job.last()
    for i in range(seqs):
        ub, cb = unit_of(job.result(i))
        f, b = first[i], rate[1:2]
        o, cw = unit_of(f + b * (ub - f))
        dw = unit_back(o, cw, cot[i].astype(F32))
        step = b * dw
        low[i] = unit_back(ub, cb, step).astype(BF)
        out.start_part(i)
        out_o[i] = o.astype(BF)
        d1_o[i] = dw - step
        total = jnp.sum(dw * (ub - f), axis=0, keepdims=True)
        sum_o[...] = total if i == 0 else sum_o[...] + total
        if i > 0:
            out.forward_part(i - 1)
    out.forward_part(seqs - 1)
    out.finish()
    job.finish()
    for copy in keeps:
        copy.wait()


def ff_joint(x, wu, wu2, wg, rate, w, first, cot):
    seqs, rows, width = first.shape
    part = jax.ShapeDtypeStruct((8, seqs, rows, width), BF)
    columns = wg.shape[0]
    wide = (2, 2, 2, seqs * rows, columns)
    return comm_call(
        ff_joint_kernel, "ff_joint", 2,
        (x.reshape(wide[:4] + (width,)), wu, wu2, wg, rate, w, first, cot),
        [
            (first.shape, BF), (first.shape, F32), ((1, width), F32), (part.shape, BF),
            (wide, BF), (wide, F32), (wide, F32),
        ],
        [
            pltpu.VMEM(part.shape, BF), pltpu.VMEM(first.shape, BF), pltpu.VMEM(wide, BF),
            pltpu.VMEM(wide, F32), pltpu.VMEM(wide, F32), pltpu.SemaphoreType.DMA((3,)),
        ]
        + PlaneReduce.scratch(part) + PlaneGather.sems(seqs),
        35, far_outs=(4, 5, 6), late=(0, 1, 2, 3, 5),
    )


def back_joint_kernel(
    n_line, ready, d, inner, rate, d1, first, ua, ca, cv, hid, wd_h, up_h, gate_h, wu_h, wu2_h, wg_h, x_h,
    res_o, sum_o, ff_sum_o, all_o, up_o, gate_o, down_o, part, low, down_s, du, dg, *scratch,
):
    y, c, z, s = place()
    late = Late((wd_h, up_h, gate_h, wu_h, wu2_h, wg_h, x_h), scratch[:8])
    scratch = scratch[8:]
    greet(plane_peers(), line_ends(n_line)[:2])
    ready()
    split = len(PlaneReduce.scratch(part))
    job = PlaneReduce(part, *scratch[:split])
    _, parts, rows, width = part.shape
    columns = du.shape[-1]
    tokens = 8 * parts * rows
    each = parts // all_o.shape[0]
    out = UlyGather(
        low, all_o, *scratch[split : split + 3],
        pick=lambda i, u: all_o.at[i // each, u, pl.ds(i % each * rows, rows)],
    )
    downs = line_reduces(n_line, down_s, scratch[split + 3 :])
    flat = lambda ref: ref[...].reshape(tokens, ref.shape[-1])

    deep = width // (4 * n_line)
    inner_all = flat(inner)

    def down_half(i, carry):
        lanes = pl.ds(pl.multiple_of(i * (width // 2), 128), width // 2)
        grad = dot_tn(d[:, :, :, :, lanes].reshape(tokens, width // 2), inner_all).astype(BF)
        for v in (0, 1):
            for k in range(n_line):
                at = (v * n_line + k) * deep
                down_s[k, 2 * i + v] = grad[at : at + deep]
        return carry

    lax.fori_loop(0, 2, down_half, 0)
    for line_job, _ in downs:
        line_job.step(n_line - 1)

    wd, up_ref, gate_ref = late(0), late(1), late(2)
    u_scale, g_scale = rate[2:3, :columns], rate[3:4, :columns] * D**0.5

    ff_sum_o[...] = jnp.zeros_like(ff_sum_o)

    def gated_back(yy, cc):
        got = dot_nn(d[yy, cc].reshape(tokens // 4, width), wd[...])
        up, gate = up_ref[yy, cc].reshape(got.shape), gate_ref[yy, cc].reshape(got.shape)
        gz = gate * g_scale
        sig = 1.0 / (1.0 + jnp.exp(-gz))
        d_up = got * (gz * sig)
        d_gate = got * (up * u_scale) * sig * (1.0 + gz * (1.0 - sig))
        du[yy, cc] = (d_up * u_scale).astype(BF).reshape(du.shape[2:])
        dg[yy, cc] = (d_gate * g_scale).astype(BF).reshape(dg.shape[2:])
        ff_sum_o[0:1] = ff_sum_o[0:1] + jnp.sum(d_up * up, axis=0, keepdims=True)
        ff_sum_o[1:2] = ff_sum_o[1:2] + jnp.sum(d_gate * gate, axis=0, keepdims=True) * D**0.5

    wu, wu2, wg = late(3), late(4), late(5)

    def product(yy, cc):
        u, g = du[yy, cc].reshape(tokens // 4, columns), dg[yy, cc].reshape(tokens // 4, columns)
        got = jnp.concatenate([dot_nn(u, wu[...]), dot_nn(u, wu2[...])], axis=1)
        return got + dot_nn(g, wg[...])

    plane_products(job, part, y, c, gated_back, product)
    steps = [(k, line_job) for k in range(n_line - 2, 0, -1) for line_job, _ in downs]
    job.last()
    x = late(6)

    def by_line(o, ref):
        n, rows_all = columns // n_line, flat(ref)

        def half(i, carry):
            lanes = pl.ds(pl.multiple_of(i * (width // 2), 128), width // 2)
            grad = dot_tn(rows_all, x[:, lanes]).astype(BF)
            for k in range(n_line):
                o[k, :, lanes] = grad[k * n : (k + 1) * n]
            return carry

        lax.fori_loop(0, 2, half, 0)

    by_line(up_o, du)
    for i in range(parts):
        f, h, u, a = first[i], hid[i].astype(F32), ua[i], rate[0:1]
        dv = unit_back(f, cv[i][:, :1], d1[i] + job.result(i))
        step = a * dv
        low[i] = unit_back(u, ca[i][:, :1], step).astype(BF)
        out.start_part(i)
        res_o[i] = dv - step
        total = jnp.sum(dv * (u - h), axis=0, keepdims=True)
        sum_o[...] = total if i == 0 else sum_o[...] + total
        if len(steps) > 0:
            k, line_job = steps.pop(0)
            line_job.step(k)
    for k, line_job in steps:
        line_job.step(k)
    by_line(gate_o, dg)
    out.forward()
    out.finish()
    job.finish()
    for line_job, cut in downs:
        line_job.result(down_o.at[cut])
        line_job.finish()


def back_joint(n_line, seqs, d, wd, up, gate, rate, wu, wu2, wg, x, inner, d1, first, ua, ca, cv, hid):
    parts, rows, width = first.shape
    columns = wd.shape[1]
    part = jax.ShapeDtypeStruct((8, parts, rows, width), BF)
    down = jax.ShapeDtypeStruct((n_line, 4, width // (4 * n_line), columns), BF)
    by_line = ((n_line, columns // n_line, width), BF)
    wide = lambda a: a.reshape(2, 2, 2, parts * rows, a.shape[-1])
    thin = pltpu.VMEM((2, 2, 2, parts * rows, columns), BF)
    late = (wd, wide(up), wide(gate), wu, wu2, wg, x)
    return comm_call(
        functools.partial(back_joint_kernel, n_line), "back_joint", 3,
        (wide(d), wide(inner), rate, d1, first, ua, ca, cv, hid) + late,
        [
            (first.shape, F32), ((1, width), F32), ((2, columns), F32),
            ((seqs, 4, parts * rows // seqs, width), BF), by_line, by_line, (down.shape[1:], BF),
        ],
        [pltpu.VMEM(part.shape, BF), pltpu.VMEM(first.shape, BF), pltpu.VMEM(down.shape, BF), thin, thin]
        + Late.scratch(late) + PlaneReduce.scratch(part) + UlyGather.sems(parts)
        + line_reduce_scratch(n_line, down),
        40, VMEM_BYTES, tuple(range(9, 16)), late=(0, 1),
    )


def settle_kernel(*refs):
    count = len(refs) // 2
    for x, o in zip(refs[:count], refs[count:]):
        o[...] = x[...]


def settle(*arrays):
    vmem = pl.BlockSpec(memory_space=pltpu.VMEM)
    return pl.pallas_call(
        settle_kernel,
        out_shape=[jax.ShapeDtypeStruct(a.shape, a.dtype) for a in arrays],
        in_specs=[vmem] * len(arrays),
        out_specs=[vmem] * len(arrays),
        compiler_params=pltpu.CompilerParams(vmem_limit_bytes=VMEM_BYTES),
        name="settle",
    )(*arrays)
def local(
    hidden, positions, w_query, w_key, w_value, w_out, w_up, w_gate, w_down,
    qk_scale, alpha_attn, alpha_mlp, up_scale, gate_scale, cotangent,
):
    seqs, rows_each, width = hidden.shape
    n_line = lax.axis_size("line")
    n_blk = 2 * n_line
    heads = HEADS // 4
    local_width = heads * HEAD_DIM
    group_rows = 4 * rows_each
    tokens = seqs * rows_each
    group_tokens = 4 * tokens
    plane_tokens = 8 * tokens
    attn_each, ff_each = w_query.shape[0], w_up.shape[0]
    ff_local = ff_each * n_line
    far, core, line, side = place()
    uly = far * 2 + core

    def row(x, wide):
        return jnp.pad(x, ((0, 0),) * (x.ndim - 1) + ((0, wide - x.shape[-1]),))

    pieces = [v.astype(F32) for v in (qk_scale, alpha_attn, alpha_mlp, up_scale, gate_scale)]
    pieces.append(positions.reshape(-1).astype(F32))
    used = sum(v.shape[0] for v in pieces)
    room, at, small = used + -used % 1024, 0, 0.0
    for v in pieces:
        small = small + jnp.pad(v, (at, room - at - v.shape[0]))
        at += v.shape[0]
    small = small.reshape(-1, 128)

    hid_all, small_all, wq_all, wk_all, wv_all, out_cols, down_cols, up_first = entry(
        n_line, hidden, small, w_query, w_key, w_value, w_out, w_down, w_up
    )
    up_first = up_first.reshape(ff_local, -1)

    flat = small_all.reshape(4, n_blk, -1)
    cut = [0, attn_each, 2 * attn_each, 3 * attn_each, 3 * attn_each + ff_each, 3 * attn_each + 2 * ff_each, used]
    own = lax.dynamic_slice_in_dim(flat, uly, 1, 0)[0]
    scale_wide = own[:, : cut[1]].reshape(heads, HEAD_DIM)
    attn_rate = flat[:, :, cut[1] : cut[2]].reshape(-1)
    mlp_rate = flat[:, :, cut[2] : cut[3]].reshape(-1)
    mine = lax.dynamic_slice_in_dim(own.reshape(n_line, 2, -1), side, 1, 1)[:, 0]
    up_wide = mine[:, cut[3] : cut[4]].reshape(-1)
    gate_wide = mine[:, cut[4] : cut[5]].reshape(-1)
    assert ff_local <= width
    rates = jnp.pad(
        jnp.stack([attn_rate, mlp_rate, row(up_wide, width), row(gate_wide, width)]), ((0, 4), (0, 0))
    )
    places = jnp.transpose(
        flat[:, :, cut[5] : cut[6]].reshape(4, n_blk, seqs, rows_each), (2, 1, 0, 3)
    ).reshape(seqs, n_blk, 1, group_rows)
    q_places = lax.dynamic_slice_in_dim(places, line * 2 + side, 1, 1)[:, 0]

    lane = jnp.arange(128) % HEAD_DIM
    freqs = rotary_base ** (-((lane % 32).astype(F32) * (2.0 / HEAD_DIM)))
    angles = q_places.reshape(group_tokens, 1) * freqs
    cos = jnp.cos(angles)
    sin = jnp.where(lane < 32, -1.0, 1.0) * jnp.sin(angles)
    scale_both = jnp.concatenate([scale_wide * HEAD_DIM**0.5, scale_wide], axis=1)

    group_hidden = hid_all.reshape(group_tokens, width)
    wq = wq_all.reshape(heads, HEAD_DIM, width)
    wk = wk_all.reshape(heads, HEAD_DIM, width)
    wv = wv_all.reshape(heads, HEAD_DIM, width)
    qz, y_both, c_both, kv_all, out_all, gate_full, up_last, attended, mixed, inverse = attend(
        n_line, seqs, group_hidden, wq, wk, wv, cos, sin, scale_both, out_cols, w_gate, w_up,
        places,
    )
    up_last = up_last.reshape(ff_local, -1)
    gate_full = gate_full.reshape(ff_local, width)
    out_full = out_all.reshape(width, local_width)

    fine = (2 * seqs, rows_each // 2, width)
    hidden_fine = hidden.reshape(fine)
    first, unit_att, att_c, first_c, mlp_in, down_full = attn_joint(
        n_line, mixed, out_full, hidden_fine, rates,
        down_cols.reshape(4, 2 * attn_each, ff_local),
    )
    down_full = down_full.reshape(width, ff_local)
    mlp_in = mlp_in.reshape(plane_tokens, width)
    layer_out, grad_first, grad_alpha_mlp, branch_low, inner, up_rows, gate_rows = ff_joint(
        mlp_in, up_first, up_last, gate_full, rates, down_full, first, cotangent.reshape(fine)
    )
    branch_low = branch_low.reshape(plane_tokens, width)
    grad_residual, grad_alpha_attn, ff_scales, att_low, grad_up, grad_gate, down_own = back_joint(
        n_line, seqs, branch_low, down_full, up_rows, gate_rows, rates, up_first, up_last, gate_full,
        mlp_in, inner, grad_first, first, unit_att, att_c, first_c, hidden_fine,
    )
    grad_up_scale, grad_gate_scale = ff_scales[0], ff_scales[1]
    down_own = down_own.reshape(8, attn_each, ff_local)

    dq, dkv, out_own, up_own = attend_back(
        n_line, qz, att_low.reshape(seqs, group_rows, width), out_full, mixed, attended, inverse,
        kv_all, places, grad_up,
    )
    out_own = out_own.reshape(4, attn_each, local_width)
    alpha = jnp.concatenate(
        [grad_alpha_attn.reshape(4, n_blk, attn_each), grad_alpha_mlp.reshape(4, n_blk, attn_each)], axis=2
    )
    ff_sums = jnp.concatenate(
        [grad_up_scale.reshape(n_line, ff_each), grad_gate_scale.reshape(n_line, ff_each)], axis=1
    )
    sides = (jnp.arange(2) == side)[None, :, None]
    ff_sums = jnp.where(sides, ff_sums[:, None], 0.0).reshape(n_blk, 2 * ff_each)
    rest = jnp.concatenate([jnp.zeros((n_blk, 256), F32), row(ff_sums, 384)], axis=1)
    gq, gk, gv, grad_hidden, out_gradient, down_gradient, sums, gate_own = leave(
        n_line, group_hidden, dq, dkv, y_both, c_both, cos, sin, scale_both, wq, wk, wv,
        grad_residual.reshape(seqs, rows_each, width), out_own, down_own,
        row(alpha, 128)[:, :, None], rest[:, None], grad_gate,
    )
    sums = sums[0]
    layer_out, grad_hidden, gq, gk, gv, out_gradient, up_own, gate_own, down_gradient = settle(
        layer_out.reshape(hidden.shape), grad_hidden, gq, gk, gv, out_gradient, up_own, gate_own,
        down_gradient,
    )
    return (
        layer_out,
        grad_hidden,
        gq,
        gk,
        gv,
        out_gradient,
        up_own,
        gate_own,
        down_gradient,
        sums[128 : 128 + attn_each],
        sums[:attn_each],
        sums[attn_each : 2 * attn_each],
        sums[256 : 256 + ff_each],
        sums[256 + ff_each : 256 + 2 * ff_each],
    )


def solution(mesh):
    far = mesh.shape["uly"] // 2
    line = mesh.shape["blk"] // 2
    finer = Mesh(mesh.devices.reshape(far, 2, line, 2), AXES)
    rows, tokens, flat = P(AXES, None), P(None, AXES, None), P(AXES)
    return jax.shard_map(
        local,
        mesh=finer,
        in_specs=(tokens, P(None, AXES)) + (rows,) * 7 + (flat,) * 5 + (tokens,),
        out_specs=(tokens, tokens) + (rows,) * 7 + (flat,) * 5,
        check_vma=False,
    )
```

```python
import functools

import jax
import jax.numpy as jnp
from jax import lax
from jax.experimental import pallas as pl
from jax.experimental.pallas import tpu as pltpu
from jax.sharding import Mesh
from jax.sharding import PartitionSpec as P

D = 1280
HEADS = 20
HEAD_DIM = 64
AXES = ("far", "core", "line", "side")
PLANE = ("far", "core", "side")
VMEM_BYTES = 60 * 1024 * 1024

rotary_base = 10000.0
tiny_eps = 1e-06
BF = jnp.bfloat16
F32 = jnp.float32


def place():
    return tuple(lax.axis_index(name) for name in AXES)


def remote(src, dst, send, recv, device):
    return pltpu.make_async_remote_copy(
        src_ref=src,
        dst_ref=dst,
        send_sem=send,
        recv_sem=recv,
        device_id=device,
        device_id_type=pl.DeviceIdType.MESH,
    )


def signal_to(device):
    pl.semaphore_signal(
        pltpu.get_barrier_semaphore(), inc=1, device_id=device, device_id_type=pl.DeviceIdType.MESH
    )


def greet(devices, maybe=()):
    count = len(devices)
    for device in devices:
        signal_to(device)
    for there, device in maybe:
        pl.when(there)(functools.partial(signal_to, device))
        count = count + jnp.where(there, 1, 0)
    pl.semaphore_wait(pltpu.get_barrier_semaphore(), count)


def params(collective_id, room=VMEM_BYTES):
    return pltpu.CompilerParams(
        collective_id=collective_id, has_side_effects=True, vmem_limit_bytes=room
    )


class UlyGather:
    sems = staticmethod(lambda parts: [pltpu.SemaphoreType.DMA((3, parts))] * 2 + [pltpu.SemaphoreType.DMA((parts,))])

    def __init__(self, x, o, send, recv, local, pick=None):
        pick = pick or (lambda i, u: o.at[i, u])
        y, c, z, s = place()
        u, v = y * 2 + c, (1 - y) * 2 + c
        mate, across = (y, 1 - c, z, s), (1 - y, c, z, s)
        self.parts = x.shape[0]
        parts = range(self.parts)
        self.far = [remote(x.at[i], pick(i, u), send.at[0, i], recv.at[0, i], across) for i in parts]
        self.near = [remote(x.at[i], pick(i, u), send.at[1, i], recv.at[1, i], mate) for i in parts]
        self.on = [remote(pick(i, v), pick(i, v), send.at[2, i], recv.at[2, i], mate) for i in parts]
        self.own = [pltpu.make_async_copy(x.at[i], pick(i, u), local.at[i]) for i in parts]

    def start_part(self, i):
        self.far[i].start()
        self.near[i].start()
        self.own[i].start()

    def start(self):
        for i in range(self.parts):
            self.start_part(i)

    def forward(self):
        for i in range(self.parts):
            self.far[i].wait_recv()
            self.on[i].start()

    def finish(self):
        for i in range(self.parts):
            self.near[i].wait_recv()
            self.on[i].wait_recv()
            self.own[i].wait()
            self.far[i].wait_send()
            self.near[i].wait_send()
            self.on[i].wait_send()


def uly_peers():
    y, c, z, s = place()
    return [(y, 1 - c, z, s), (1 - y, c, z, s)]


def add_low(*terms):
    total = terms[0].astype(F32)
    for term in terms[1:]:
        total = total + term.astype(F32)
    return total


class UlyReduce:
    @staticmethod
    def scratch(x):
        parts, _, rows, width = x.shape
        return [
            pltpu.VMEM((parts, 2, rows, width), x.dtype),
            pltpu.VMEM((parts, rows, width), x.dtype),
            pltpu.VMEM((parts, rows, width), x.dtype),
            pltpu.SemaphoreType.DMA((3, parts)),
            pltpu.SemaphoreType.DMA((3, parts)),
        ]

    def __init__(self, x, near, mid, far_in, send, recv):
        y, c, z, s = place()
        mate, across = uly_peers()
        self.x, self.near_ref, self.mid, self.far_in = x, near, mid, far_in
        self.y, self.c, self.parts = y, c, x.shape[0]
        parts = range(self.parts)
        self.near = [
            [
                remote(x.at[i, f * 2 + 1 - c], near.at[i, k], send.at[k, i], recv.at[k, i], mate)
                for k, f in enumerate((1 - y, y))
            ]
            for i in parts
        ]
        self.far = [remote(mid.at[i], far_in.at[i], send.at[2, i], recv.at[2, i], across) for i in parts]

    def start(self):
        for i in range(self.parts):
            for copy in self.near[i]:
                copy.start()

    def middle(self):
        for i in range(self.parts):
            self.near[i][0].wait_recv()
            self.mid[i] = add_low(self.x[i, (1 - self.y) * 2 + self.c], self.near_ref[i, 0]).astype(BF)
            self.far[i].start()

    def result(self, i):
        self.near[i][1].wait_recv()
        self.far[i].wait_recv()
        return add_low(self.x[i, self.y * 2 + self.c], self.near_ref[i, 1], self.far_in[i])

    def finish(self):
        for i in range(self.parts):
            for copy in self.near[i] + [self.far[i]]:
                copy.wait_send()


def plane_peers():
    y, c, z, s = place()
    return [(y, 1 - c, z, s), (1 - y, c, z, s), (y, c, z, 1 - s)]


def plane_index(y, c, s):
    return (y * 2 + c) * 2 + s


class PlaneGather:
    @staticmethod
    def sems(parts):
        return [pltpu.SemaphoreType.DMA((7, parts))] * 2 + [pltpu.SemaphoreType.DMA((parts,))]

    def __init__(self, x, o, send, recv, local):
        y, c, z, s = place()
        mate, across, cross = plane_peers()
        self.parts = parts = range(x.shape[0])
        me, py, px, pd = (
            plane_index(y, c, s),
            plane_index(1 - y, c, s),
            plane_index(y, c, 1 - s),
            plane_index(1 - y, c, 1 - s),
        )

        def copy(source, p, i, slot, device):
            return remote(source, o.at[p, i], send.at[slot, i], recv.at[slot, i], device)

        def on(p, i, slot, device):
            return copy(o.at[p, i], p, i, slot, device)

        self.by_y = [copy(x.at[i], me, i, 0, across) for i in parts]
        self.by_x = [copy(x.at[i], me, i, 1, cross) for i in parts]
        self.near = [copy(x.at[i], me, i, 2, mate) for i in parts]
        self.corner = [on(px, i, 3, across) if i % 2 else on(py, i, 3, cross) for i in parts]
        self.pass_y = [on(py, i, 4, mate) for i in parts]
        self.pass_x = [on(px, i, 5, mate) for i in parts]
        self.pass_d = [on(pd, i, 6, mate) for i in parts]
        self.own = [pltpu.make_async_copy(x.at[i], o.at[me, i], local.at[i]) for i in parts]

    def start_part(self, i):
        for copy in (self.by_y[i], self.by_x[i], self.near[i], self.own[i]):
            copy.start()

    def forward_part(self, i):
        ways = [(self.by_y[i], self.pass_y[i]), (self.by_x[i], self.pass_x[i])]
        first, then = ways[:: 1 - 2 * (i % 2)]
        first[0].wait_recv()
        self.corner[i].start()
        first[1].start()
        then[0].wait_recv()
        then[1].start()

    def finish(self):
        for i in self.parts:
            self.corner[i].wait_recv()
            self.pass_d[i].start()
        for i in self.parts:
            for copy in (self.near[i], self.pass_y[i], self.pass_x[i], self.pass_d[i]):
                copy.wait()
            for copy in (self.by_y[i], self.by_x[i], self.corner[i]):
                copy.wait_send()
            self.own[i].wait()


class PlaneReduce:
    @staticmethod
    def scratch(x):
        one = pltpu.VMEM(x.shape[1:], x.dtype)
        sems = pltpu.SemaphoreType.DMA((7, x.shape[1]))
        return [pltpu.VMEM((4,) + x.shape[1:], x.dtype)] + [one] * 6 + [sems] * 2

    def __init__(self, x, near, out_x, out_y, out_d, in_x, in_y, in_d, send, recv):
        y, c, z, s = place()
        mate, across, cross = plane_peers()
        self.c = c
        self.parts = parts = range(x.shape[1])
        self.spots = ((1 - y, 1 - s), (y, 1 - s), (1 - y, s), (y, s))
        self.x, self.near_ref = x, near
        self.out_x, self.out_y, self.out_d = out_x, out_y, out_d
        self.in_x, self.in_y, self.in_d = in_x, in_y, in_d

        def copy(source, target, i, slot, device):
            return remote(source, target, send.at[slot, i], recv.at[slot, i], device)

        self.near = [
            [copy(x.at[plane_index(sy, 1 - c, ss), i], near.at[k, i], i, k, mate) for i in parts]
            for k, (sy, ss) in enumerate(self.spots)
        ]
        self.corner = [copy(out_d.at[i], in_d.at[i], i, 4, across if i % 2 else cross) for i in parts]
        self.by_x = [copy(out_x.at[i], in_x.at[i], i, 5, cross) for i in parts]
        self.by_y = [copy(out_y.at[i], in_y.at[i], i, 6, across) for i in parts]

    def pair(self, k, i):
        sy, ss = self.spots[k]
        self.near[k][i].wait_recv()
        return add_low(self.x[plane_index(sy, self.c, ss), i], self.near_ref[k, i])

    def middle(self, far):
        for i in self.parts:
            if far:
                self.out_d[i] = self.pair(0, i).astype(BF)
                self.corner[i].start()
                if i % 2 == 1:
                    self.out_y[i] = self.pair(2, i).astype(BF)
                    self.by_y[i].start()
            elif i % 2 == 0:
                self.out_x[i] = self.pair(1, i).astype(BF)
                self.by_x[i].start()

    def last(self):
        for i in self.parts:
            k, out, by = (1, self.out_x, self.by_x) if i % 2 else (2, self.out_y, self.by_y)
            part = self.pair(k, i)
            self.corner[i].wait_recv()
            out[i] = (part + self.in_d[i].astype(F32)).astype(BF)
            by[i].start()

    def result(self, i):
        own = self.pair(3, i)
        self.by_x[i].wait_recv()
        self.by_y[i].wait_recv()
        return own + add_low(self.in_x[i], self.in_y[i])

    def finish(self):
        for copy in [c for spot in self.near for c in spot] + self.corner + self.by_x + self.by_y:
            copy.wait_send()


def plane_corners():
    y, c, z, s = place()
    return [
        (y, 1 - c, s), (1 - y, c, s), (1 - y, 1 - c, s),
        (y, c, 1 - s), (y, 1 - c, 1 - s), (1 - y, c, 1 - s), (1 - y, 1 - c, 1 - s),
    ]


def line_ends(n_line):
    y, c, z, s = place()
    return (z > 0, (y, c, z - 1, s)), (z < n_line - 1, (y, c, z + 1, s)), (y, c, z, 1 - s)


class BlkGather:
    @staticmethod
    def sems(n_line):
        return [
            pltpu.SemaphoreType.DMA((3,)),
            pltpu.SemaphoreType.DMA((1,)),
            pltpu.SemaphoreType.DMA((4, n_line)),
            pltpu.SemaphoreType.DMA((4, n_line)),
            pltpu.SemaphoreType.DMA((1,)),
        ]

    def __init__(self, n_line, pick_x, pick_o, own_send, own_recv, send, recv, local):
        y, c, z, s = place()
        self.z, self.s, self.n = z, s, n_line
        (self.has_low, self.low), (self.has_high, self.high), self.cross = line_ends(n_line)
        self.pick_x, self.pick_o = pick_x, pick_o
        self.sem = (own_send, own_recv, send, recv, local)

    def block(self, way, k):
        z = self.z - k if way == 0 else self.z + k
        return self.pick_o(z * 2 + self.s)

    def own(self, way):
        own_send, own_recv, send, recv, local = self.sem
        arrival = own_recv.at[0] if way == 2 else recv.at[way, 0]
        target = (self.high, self.low, self.cross)[way]
        return remote(self.pick_x(), self.pick_o(self.z * 2 + self.s), own_send.at[way], arrival, target)

    def keep(self):
        return pltpu.make_async_copy(self.pick_x(), self.pick_o(self.z * 2 + self.s), self.sem[4].at[0])

    def onward(self, way, k):
        send, recv = self.sem[2:4]
        target = self.high if way == 0 else self.low
        return remote(self.block(way, k), self.block(way, k), send.at[way, k], recv.at[way, k], target)

    def over(self, way, k):
        send, recv = self.sem[2:4]
        return remote(self.block(way, k), self.block(way, k), send.at[2 + way, k], recv.at[2 + way, k], self.cross)

    def arrive(self, way, k):
        send, recv = self.sem[2:4]
        return remote(self.block(way, k), self.block(way, k), send.at[way, k], recv.at[way, k - 1], self.cross)

    def there(self, way, k):
        return self.z >= k if way == 0 else self.z + k < self.n

    def start(self):
        pl.when(self.has_high)(lambda: self.own(0).start())
        pl.when(self.has_low)(lambda: self.own(1).start())
        self.own(2).start()
        self.keep().start()

    def take(self, way, k):
        self.arrive(way, k).wait_recv()
        pl.when((self.has_high, self.has_low)[way])(lambda: self.onward(way, k).start())
        self.over(way, k).start()

    def step(self, k):
        for way in (0, 1):
            pl.when(self.there(way, k))(lambda: self.take(way, k))

    def finish_arrivals(self):
        self.own(2).wait_recv()
        for k in range(1, self.n):
            for way in (0, 1):
                pl.when(self.there(way, k))(lambda: self.over(way, k).wait_recv())
        self.keep().wait()

    def finish_sends(self):
        pl.when(self.has_high)(lambda: self.own(0).wait_send())
        pl.when(self.has_low)(lambda: self.own(1).wait_send())
        self.own(2).wait_send()
        for k in range(1, self.n):
            for way in (0, 1):
                @pl.when(self.there(way, k))
                def _():
                    self.over(way, k).wait_send()

                    @pl.when((self.has_high, self.has_low)[way])
                    def _():
                        self.onward(way, k).wait_send()


def blk_greet(n_line):
    low, high, cross = line_ends(n_line)
    greet([cross], [low, high])


class BlkReduce:
    @staticmethod
    def scratch(n_line, a):
        return [
            pltpu.VMEM((n_line,) + a.shape[1:], a.dtype),
            pltpu.VMEM((n_line + 1,) + a.shape[1:], a.dtype),
            pltpu.SemaphoreType.DMA((n_line,)),
            pltpu.SemaphoreType.DMA((n_line,)),
            pltpu.SemaphoreType.DMA((2, n_line)),
            pltpu.SemaphoreType.DMA((2, n_line)),
        ]

    def __init__(self, n_line, x, side_in, line_in, side_send, side_recv, send, recv):
        y, c, self.z, self.s = place()
        self.n = n_line
        (self.has_low, self.low), (self.has_high, self.high), self.cross = line_ends(n_line)
        self.x = x
        self.side_in, self.line_in = side_in, line_in
        self.sem = (side_send, side_recv, send, recv)

    def spot(self, way, k):
        return self.z + k * (1 - 2 * way)

    def exists(self, way, k):
        return (self.spot(way, k) >= 0) & (self.spot(way, k) < self.n)

    def toward(self, way):
        y, c, z, s = place()
        return (y, c, z + 1 - 2 * way, s)

    def side(self, zz):
        side_send, side_recv = self.sem[:2]
        return remote(
            self.x.at[zz * 2 + 1 - self.s], self.side_in.at[zz], side_send.at[zz], side_recv.at[zz], self.cross
        )

    def slot(self, way, k):
        return jnp.where((way == 1) & (k == 0), self.n, self.spot(way, k))

    def move(self, way, k):
        send, recv = self.sem[2:]
        zz = self.spot(way, k)
        there = jnp.where((way == 1) & (k == 1), self.n, zz)
        return remote(
            self.side_in.at[zz], self.line_in.at[there], send.at[way, k], recv.at[way, k - 1], self.toward(way)
        )

    def arrive(self, way, k):
        send, recv = self.sem[2:]
        there = self.line_in.at[self.slot(way, k)]
        return remote(there, there, send.at[way, k], recv.at[way, k], self.toward(1 - way))

    def start(self, k):
        for way in (0, 1) if k > 0 else (0,):
            pl.when(self.exists(way, k))(lambda: self.side(self.spot(way, k)).start())

    def move_on(self, way, k):
        zz = self.spot(way, k)
        self.side(zz).wait_recv()
        passed = jnp.where(way == 0, self.has_low, self.has_high)

        @pl.when(passed)
        def _():
            self.arrive(way, k).wait_recv()
            self.side_in[zz] = add_low(
                self.x[zz * 2 + self.s], self.side_in[zz], self.line_in[zz]
            ).astype(self.side_in.dtype)

        @pl.when(jnp.logical_not(passed))
        def _():
            self.side_in[zz] = add_low(self.x[zz * 2 + self.s], self.side_in[zz]).astype(
                self.side_in.dtype
            )

        self.move(way, k).start()

    def step(self, k):
        def one(way, carry):
            pl.when(self.exists(way, k))(lambda: self.move_on(way, k))
            return carry

        lax.fori_loop(0, 2, one, 0)

    def result(self, o):
        z = self.z
        self.side(z).wait_recv()
        pl.when(self.has_low)(lambda: self.arrive(0, 0).wait_recv())
        pl.when(self.has_high)(lambda: self.arrive(1, 0).wait_recv())
        own = lambda: add_low(self.x[z * 2 + self.s], self.side_in[z])
        both = self.has_low & self.has_high

        @pl.when(both)
        def _():
            o[...] = (own() + add_low(self.line_in[z], self.line_in[self.n])).astype(o.dtype)

        @pl.when(jnp.logical_not(both))
        def _():
            other = self.line_in[jnp.where(self.has_low, z, self.n)].astype(F32)
            o[...] = (own() + other).astype(o.dtype)

    def finish(self):
        for k in range(self.n - 1, -1, -1):
            for way in (0, 1) if k > 0 else (0,):
                @pl.when(self.exists(way, k))
                def _():
                    self.side(self.spot(way, k)).wait_send()
                    if k > 0:
                        self.move(way, k).wait_send()


class LineGather:
    @staticmethod
    def sems(n_line):
        dma = pltpu.SemaphoreType.DMA
        return [dma((2,)), dma((2, n_line)), dma((2, n_line)), dma((1,))]

    def __init__(self, n_line, pick_x, pick_o, own_send, send, recv, local):
        y, c, self.z, s = place()
        self.n = n_line
        (self.has_low, self.low), (self.has_high, self.high), _ = line_ends(n_line)
        self.pick_x, self.pick_o = pick_x, pick_o
        self.own_send, self.send, self.recv, self.local = own_send, send, recv, local

    def goes(self, way):
        return (self.has_high, self.has_low)[way]

    def own(self, way):
        target = (self.high, self.low)[way]
        return remote(self.pick_x(), self.pick_o(self.z), self.own_send.at[way], self.recv.at[way, 0], target)

    def keep(self):
        return pltpu.make_async_copy(self.pick_x(), self.pick_o(self.z), self.local.at[0])

    def onward(self, way, k):
        block = self.pick_o(self.z - k if way == 0 else self.z + k)
        target = (self.high, self.low)[way]
        return remote(block, block, self.send.at[way, k], self.recv.at[way, k], target)

    def arrive(self, way, k):
        block = self.pick_o(self.z - k if way == 0 else self.z + k)
        return remote(block, block, self.send.at[way, k], self.recv.at[way, k - 1], (self.low, self.high)[way])

    def there(self, way, k):
        return self.z >= k if way == 0 else self.z + k < self.n

    def start(self):
        for way in (0, 1):
            pl.when(self.goes(way))(lambda: self.own(way).start())
        self.keep().start()

    def step(self, k):
        for way in (0, 1):
            @pl.when(self.there(way, k))
            def _():
                self.arrive(way, k).wait_recv()
                pl.when(self.goes(way))(lambda: self.onward(way, k).start())

    def finish(self):
        self.keep().wait()
        for way in (0, 1):
            pl.when(self.goes(way))(lambda: self.own(way).wait_send())
            for k in range(1, self.n):
                pl.when(self.there(way, k) & self.goes(way))(lambda: self.onward(way, k).wait_send())


class LineReduce:
    @staticmethod
    def scratch(n_line, a):
        dma = pltpu.SemaphoreType.DMA
        return [
            pltpu.VMEM((n_line,) + a.shape[1:], a.dtype),
            pltpu.VMEM((n_line + 1,) + a.shape[1:], a.dtype),
            dma((2, n_line)), dma((2, n_line)),
        ]

    def __init__(self, n_line, x, sums, line_in, send, recv):
        y, c, self.z, s = place()
        self.n, self.x, self.sums, self.line_in, self.send, self.recv = n_line, x, sums, line_in, send, recv
        (self.has_low, self.low), (self.has_high, self.high), _ = line_ends(n_line)

    def spot(self, way, k):
        return self.z + k * (1 - 2 * way)

    def exists(self, way, k):
        return (self.spot(way, k) >= 0) & (self.spot(way, k) < self.n)

    def passed(self, way):
        return jnp.where(way == 0, self.has_low, self.has_high)

    def slot(self, way, k):
        return jnp.where((way == 1) & (k == 0), self.n, self.spot(way, k))

    def toward(self, way):
        y, c, z, s = place()
        return (y, c, z + 1 - 2 * way, s)

    def move(self, way, k, source):
        zz = self.spot(way, k)
        there = jnp.where((way == 1) & (k == 1), self.n, zz)
        return remote(
            source.at[zz], self.line_in.at[there], self.send.at[way, k], self.recv.at[way, k - 1], self.toward(way)
        )

    def arrive(self, way, k):
        there = self.line_in.at[self.slot(way, k)]
        return remote(there, there, self.send.at[way, k], self.recv.at[way, k], self.toward(1 - way))

    def step(self, k):
        def one(way, carry):
            exists, passed = self.exists(way, k), self.passed(way)

            @pl.when(exists & passed)
            def _():
                zz = self.spot(way, k)
                self.arrive(way, k).wait_recv()
                self.sums[zz] = add_low(self.x[zz], self.line_in[zz]).astype(self.sums.dtype)
                self.move(way, k, self.sums).start()

            pl.when(exists & jnp.logical_not(passed))(lambda: self.move(way, k, self.x).start())
            return carry

        lax.fori_loop(0, 2, one, 0)

    def result(self, o):
        z = self.z
        pl.when(self.has_low)(lambda: self.arrive(0, 0).wait_recv())
        pl.when(self.has_high)(lambda: self.arrive(1, 0).wait_recv())
        both = self.has_low & self.has_high

        @pl.when(both)
        def _():
            o[...] = add_low(self.x[z], self.line_in[z], self.line_in[self.n]).astype(o.dtype)

        @pl.when(jnp.logical_not(both))
        def _():
            o[...] = add_low(self.x[z], self.line_in[jnp.where(self.has_low, z, self.n)]).astype(o.dtype)

    def finish(self):
        for k in range(self.n - 1, 0, -1):
            for way in (0, 1):
                pl.when(self.exists(way, k))(lambda: self.move(way, k, self.sums).wait_send())


def lane_chunks(width):
    cut = width // 256 * 128
    return [slice(0, cut), slice(cut, width)]


LINE_CHUNKS = 2


def line_gathers(n_line, x, pick_o, sems):
    jobs = []
    for i, lanes in enumerate(lane_chunks(x.shape[-1])):
        cut = (slice(None),) * (len(x.shape) - 1) + (lanes,)
        jobs.append(
            LineGather(
                n_line, lambda cut=cut: x.at[cut], lambda z, cut=cut: pick_o(z).at[cut],
                *sems[4 * i : 4 * i + 4],
            )
        )
    return jobs


def line_gather_sems(n_line):
    return LineGather.sems(n_line) * LINE_CHUNKS


def line_reduces(n_line, x, scratch):
    jobs = []
    for i, lanes in enumerate(lane_chunks(x.shape[-1])):
        cut = (slice(None),) * (len(x.shape) - 1) + (lanes,)
        jobs.append((LineReduce(n_line, x.at[cut], *scratch[4 * i : 4 * i + 4]), cut[1:]))
    return jobs


def line_reduce_scratch(n_line, a):
    scratch = []
    for lanes in lane_chunks(a.shape[-1]):
        one = jax.ShapeDtypeStruct(a.shape[:-1] + (lanes.stop - lanes.start,), a.dtype)
        scratch += LineReduce.scratch(n_line, one)
    return scratch


def comm_call(
    kernel, name, collective_id, args, outs, scratch, micros, room=VMEM_BYTES, far_args=(), far_outs=(), late=()
):
    vmem, anyway = pl.BlockSpec(memory_space=pltpu.VMEM), pl.BlockSpec(memory_space=pl.ANY)
    held = [pltpu.VMEM(args[i].shape, args[i].dtype) for i in late]
    held += [pltpu.SemaphoreType.DMA((len(late),))] * (len(late) > 0)

    def whole(*refs):
        refs = list(refs)
        mine, copies = refs[len(refs) - len(held) :], []
        refs = refs[: len(refs) - len(held)]
        for j, i in enumerate(late):
            copies.append(pltpu.make_async_copy(refs[i], mine[j], mine[-1].at[j]))
            copies[-1].start()
            refs[i] = mine[j]

        def ready():
            for copy in copies:
                copy.wait()

        kernel(ready, *refs)

    return pl.pallas_call(
        whole,
        out_shape=[jax.ShapeDtypeStruct(shape, dtype) for shape, dtype in outs],
        in_specs=[anyway if i in far_args or i in late else vmem for i in range(len(args))],
        out_specs=[anyway if i in far_outs else vmem for i in range(len(outs))],
        scratch_shapes=list(scratch) + held,
        compiler_params=params(collective_id, room),
        cost_estimate=pl.CostEstimate(flops=0, bytes_accessed=micros * 3_000_000, transcendentals=0),
        name=name,
    )(*args)


def exit_kernel(
    n_line, ready, x, dq, dkv, yy_ref, cc_ref, cos, sin, scale, wq, wk, wv, res, oc, dc, a_sum, m_sum, ff_sum, gg,
    gq_o, gk_o, gv_o, gh_o, go_o, gd_o, sum_o, gg_o, oc_o, dc_o,
    flat, acc, gq, gk, gv, gh, scale_s, alpha,
    alpha_in, line_out, line_all, oc_s, oc_r, dc_s, dc_r, al_s, al_r, su_s, su_r, keep, *scratch,
):
    y, c, z, s = place()
    u, p, b, n_blk = y * 2 + c, plane_index(y, c, s), z * 2 + s, 2 * n_line
    low, high, cross = line_ends(n_line)
    corners = plane_corners()
    others = []
    for i in range(1, n_blk):
        to = lax.rem(b + i, n_blk)
        others.append((y, c, to // 2, lax.rem(to, 2)))
    once = [(to[3] != 1 - s) | (to[2] != z) for to in others]
    greet([(yy, cc, z, ss) for yy, cc, ss in corners], list(zip(once, others)))
    each = 6
    jobs = [BlkReduce(n_line, g, *scratch[each * i : each * (i + 1)]) for i, g in enumerate((gq, gk, gv))]
    split = each * 3 + len(UlyReduce.scratch(gh))
    hid = UlyReduce(gh, *scratch[each * 3 : split])
    gates = line_reduces(n_line, gg, scratch[split:])
    small, cols = [], []
    for k, (yy, cc, ss) in enumerate(corners):
        target = (yy, cc, z, ss)
        cols.append(remote(dc.at[plane_index(yy, cc, ss)], dc_o.at[p], dc_s.at[k], dc_r.at[k], target))
        if k < 3:
            cols.append(remote(oc.at[yy * 2 + cc], oc_o.at[u], oc_s.at[k], oc_r.at[k], target))
            small.append(remote(alpha.at[yy * 2 + cc], alpha_in.at[k], al_s.at[k], al_r.at[k], target))
    for job, _ in gates:
        job.step(n_line - 1)
    for job in cols:
        job.start()
    each_rows = gq.shape[1]
    for v in range(4):
        for k in range(n_blk):
            at = (v * n_blk + k) * each_rows
            alpha[v, k, :, :each_rows] = a_sum[:, at : at + each_rows]
            alpha[v, k, :, each_rows : 2 * each_rows] = m_sum[:, at : at + each_rows]
    for job in small:
        job.start()
    ready()
    rows_all = x[...]
    seqs, group_rows, wide = dq.shape
    heads = wide // 128
    factor = jnp.where(lanes_of((1, 128)) < HEAD_DIM, HEAD_DIM**0.5, 1.0)
    late_steps = [(min(1 + 2 * i, heads - 1), k) for i, k in enumerate(range(n_line - 2, 0, -1))]

    def head(h, carry):
        lanes = pl.ds(pl.multiple_of(h * 128, 128), 128)
        queries = jnp.concatenate([dq[i, :, lanes] for i in range(seqs)], axis=0)
        pairs = jnp.concatenate([dkv[i, :, lanes] for i in range(seqs)], axis=0)
        low_half = lanes_of(queries.shape) < HEAD_DIM
        dy = jnp.where(low_half, queries.astype(F32), pltpu.roll(pairs.astype(F32), HEAD_DIM, 1))
        unit = yy_ref[:, lanes]
        scale_s[h] = jnp.sum(dy * unit, axis=0, keepdims=True) * factor
        dy = dy * scale[pl.ds(h, 1)]
        dr = cc_ref[:, lanes] * (dy - unit * halves(unit * dy))
        raw = (dr * cos[...] - turn(dr) * sin[...]).astype(BF)
        both = jnp.concatenate([raw, jnp.where(low_half, jnp.zeros_like(pairs), pairs)], axis=1)
        grad = dot_tn(both, rows_all).astype(BF)
        at = pl.ds(pl.multiple_of(h * HEAD_DIM, HEAD_DIM), HEAD_DIM)
        for j, lo in enumerate((0, HEAD_DIM, 3 * HEAD_DIM)):
            flat[j, at] = grad[lo : lo + HEAD_DIM]
        w_value = wv[h]
        more = dot_nn(both, jnp.concatenate([wq[h], wk[h], jnp.zeros_like(w_value), w_value], axis=0))

        @pl.when(h == 0)
        def _():
            acc[...] = more

        @pl.when(h > 0)
        def _():
            acc[...] = acc[...] + more

        for when, k in late_steps:
            @pl.when(h == when)
            def _():
                for job, _ in gates:
                    job.step(k)

        return carry

    lax.fori_loop(0, heads, head, 0)
    for i, g in enumerate((gq, gk, gv)):
        for k in range(n_blk):
            g[k] = flat[i, k * each_rows : (k + 1) * each_rows]
    for i in range(seqs):
        gh[i] = acc[i * group_rows : (i + 1) * group_rows].astype(BF).reshape(gh.shape[1:])
    hid.start()
    for k in range(n_line - 1, -1, -1):
        for job in jobs:
            job.start(k)
    mine = [
        pltpu.make_async_copy(dc.at[p], dc_o.at[p], keep.at[0]),
        pltpu.make_async_copy(oc.at[u], oc_o.at[u], keep.at[1]),
    ]
    for job in mine:
        job.start()
    hid.middle()
    for job in small:
        job.wait_recv()
    line_out[...] = jnp.zeros_like(line_out)
    ff_each = ff_sum.shape[1] // n_line
    for k in range(n_line):
        for j in (0, 1):
            line_out[k * 2 + s, :, 256 + j * ff_each : 256 + (j + 1) * ff_each] = ff_sum[
                j : j + 1, k * ff_each : (k + 1) * ff_each
            ]
    line_out[:, :, :128] = alpha[u] + alpha_in[0] + alpha_in[1] + alpha_in[2]
    scales = jnp.concatenate(
        [scale_s[h][:, :HEAD_DIM] + scale_s[h][:, HEAD_DIM:] for h in range(heads)], axis=1
    )
    for k in range(n_blk):
        line_out[k, :, 128 : 128 + each_rows] = scales[:, k * each_rows : (k + 1) * each_rows]
    line_jobs = []
    for i in range(1, n_blk):
        to = lax.rem(b + i, n_blk)
        line_jobs.append(
            remote(line_out.at[to], line_all.at[i - 1], su_s.at[i - 1], su_r.at[i - 1], others[i - 1])
        )
    for job in line_jobs:
        job.start()
    for k in range(n_line - 1, 0, -1):
        for job in jobs:
            job.step(k)
    for i in range(gh.shape[0]):
        gh_o[i] = res[i] + hid.result(i)
    for job in cols:
        job.wait_recv()
    for job in mine:
        job.wait()
    wide, ff_each = oc.shape[-1], dc.shape[-1] // n_line
    for v in range(4):
        go_o[:, v * wide : (v + 1) * wide] = oc_o[v].astype(F32)
        for t in (0, 1):
            for k in range(n_line):
                at = ((v * n_line + k) * 2 + t) * ff_each
                gd_o[:, at : at + ff_each] = dc_o[v * 2 + t, :, k * ff_each : (k + 1) * ff_each].astype(F32)
    total = line_out[b]
    for i, job in enumerate(line_jobs):
        job.wait_recv()
        total = total + line_all[i]
    sum_o[...] = total
    for job, o in zip(jobs, (gq_o, gk_o, gv_o)):
        job.result(o)
    for job, cut in gates:
        job.result(gg_o.at[cut])
        job.finish()
    hid.finish()
    for job in jobs:
        job.finish()
    for job in line_jobs + small:
        job.wait_send()
    for job in cols:
        job.wait_send()


def leave(n_line, x, dq, dkv, y, c, cos, sin, scale, wq, wk, wv, res, oc, dc, a_sum, m_sum, ff_sum, gg):
    n_blk = 2 * n_line
    heads, _, width = wq.shape
    seqs, rows, _ = res.shape
    vmem = pl.BlockSpec(memory_space=pltpu.VMEM)
    dma = pltpu.SemaphoreType.DMA
    grad = jax.ShapeDtypeStruct((n_blk, heads * HEAD_DIM // n_blk, width), BF)
    gh = jax.ShapeDtypeStruct((seqs, 4, rows, width), BF)
    scratch = [
        pltpu.VMEM(oc.shape, oc.dtype),
        pltpu.VMEM(dc.shape, dc.dtype),
        pltpu.VMEM((3, heads * HEAD_DIM, width), BF),
        pltpu.VMEM(x.shape, F32),
        pltpu.VMEM(grad.shape, BF), pltpu.VMEM(grad.shape, BF), pltpu.VMEM(grad.shape, BF),
        pltpu.VMEM(gh.shape, BF),
        pltpu.VMEM((heads, 1, 128), F32),
        pltpu.VMEM((4, n_blk, 1, 128), F32),
        pltpu.VMEM((3, n_blk, 1, 128), F32),
        pltpu.VMEM((n_blk, 1, 640), F32),
        pltpu.VMEM((n_blk - 1, 1, 640), F32),
        dma((3,)), dma((3,)), dma((7,)), dma((7,)), dma((3,)), dma((3,)),
        dma((n_blk - 1,)), dma((n_blk - 1,)), dma((2,)),
    ]
    scratch += BlkReduce.scratch(n_line, grad) * 3
    scratch += UlyReduce.scratch(gh) + line_reduce_scratch(n_line, gg)
    args = (x, dq, dkv, y, c, cos, sin, scale, wq, wk, wv, res, oc, dc, a_sum, m_sum, ff_sum, gg)
    outs = [grad.shape[1:]] * 3 + [
        res.shape, (oc.shape[1], 4 * oc.shape[2]), (dc.shape[1], 8 * dc.shape[2]), (1, 640), gg.shape[1:]
    ]
    return comm_call(
        functools.partial(exit_kernel, n_line), "leave", 8, args, [(shape, F32) for shape in outs], scratch,
        60, late=tuple(range(11)),
    )


def entry_kernel(
    n_line, hid, small, wq, wk, wv, wo, wd, wu,
    hid_o, small_o, wq_o, wk_o, wv_o, oc_o, dc_o, wu_o, oc, dc, *sems
):
    y, c, z, s = place()
    u, p = y * 2 + c, plane_index(y, c, s)
    low, high, cross = line_ends(n_line)
    corners = plane_corners()
    greet([(yy, cc, z, ss) for yy, cc, ss in corners], [low, high])
    hid_job = UlyGather(hid, hid_o, *sems[:3])
    at, jobs = 3, []
    for x, pick in (
        (small, lambda block: small_o.at[u, block]),
        (wq, lambda block: wq_o.at[block]),
        (wk, lambda block: wk_o.at[block]),
        (wv, lambda block: wv_o.at[block]),
    ):
        jobs.append(BlkGather(n_line, lambda x=x: x, pick, *sems[at : at + 5]))
        at += 5
    first = wu_o.shape[-1]
    up_jobs = [
        LineGather(n_line, lambda: wu.at[:, slice(0, first)], lambda z: wu_o.at[z], *sems[at : at + 4])
    ]
    oc_s, oc_r, dc_s, dc_r, sm_s, sm_r, keep = sems[at + 4 :]
    jobs[0].start()
    for job in jobs[1:]:
        job.start()
    hid_job.start()
    for v in range(4):
        wide = oc.shape[-1]
        oc[v] = wo[:, v * wide : (v + 1) * wide]
        ff_each = dc.shape[-1] // n_line
        for t in (0, 1):
            for k in range(n_line):
                at = ((v * n_line + k) * 2 + t) * ff_each
                dc[v * 2 + t, :, k * ff_each : (k + 1) * ff_each] = wd[:, at : at + ff_each]
    col_jobs = []
    for k, (yy, cc, ss) in enumerate(corners):
        target = (yy, cc, z, ss)
        col_jobs.append(
            remote(dc.at[plane_index(yy, cc, ss)], dc_o.at[p], dc_s.at[k], dc_r.at[k], target)
        )
        if k < 3:
            col_jobs.append(remote(oc.at[yy * 2 + cc], oc_o.at[u], oc_s.at[k], oc_r.at[k], target))
    for job in col_jobs:
        job.start()
    for job in up_jobs:
        job.start()
    mine = [
        pltpu.make_async_copy(dc.at[p], dc_o.at[p], keep.at[0]),
        pltpu.make_async_copy(oc.at[u], oc_o.at[u], keep.at[1]),
    ]
    for job in mine:
        job.start()
    for k in range(1, n_line):
        for job in jobs:
            job.step(k)
        if k == 1:
            hid_job.forward()
    jobs[0].finish_arrivals()
    small_jobs = [
        remote(small_o.at[u], small_o.at[u], sm_s.at[k], sm_r.at[k], (yy, cc, z, ss))
        for k, (yy, cc, ss) in enumerate(corners[:3])
    ]
    for job in small_jobs:
        job.start()
    for k in range(1, n_line):
        for job in up_jobs:
            job.step(k)
    for job in jobs[1:]:
        job.finish_arrivals()
    hid_job.finish()
    for job in up_jobs:
        job.finish()
    for job in small_jobs + col_jobs:
        job.wait()
    for job in mine:
        job.wait()
    for job in jobs:
        job.finish_sends()


def entry(n_line, hid, small, wq, wk, wv, wo, wd, wu):
    n_blk = 2 * n_line
    oc = jax.ShapeDtypeStruct((4, wo.shape[0], wo.shape[1] // 4), wo.dtype)
    dc = jax.ShapeDtypeStruct((8, wd.shape[0], wd.shape[1] // 8), wd.dtype)
    parts = hid.shape[0]
    vmem, anyway = pl.BlockSpec(memory_space=pltpu.VMEM), pl.BlockSpec(memory_space=pl.ANY)

    def out(shape, like):
        return jax.ShapeDtypeStruct(shape, like.dtype)

    return pl.pallas_call(
        functools.partial(entry_kernel, n_line),
        out_shape=[
            out((parts, 4) + hid.shape[1:], hid),
            out((4, n_blk) + small.shape, small),
            out((n_blk,) + wq.shape, wq),
            out((n_blk,) + wk.shape, wk),
            out((n_blk,) + wv.shape, wv),
            out(oc.shape, oc),
            out(dc.shape, dc),
            out((n_line, wu.shape[0], lane_chunks(wu.shape[1])[0].stop), wu),
        ],
        in_specs=[vmem] * 8,
        out_specs=[vmem, vmem, anyway, anyway, anyway, vmem, vmem, anyway],
        scratch_shapes=[pltpu.VMEM(oc.shape, oc.dtype), pltpu.VMEM(dc.shape, dc.dtype)]
        + UlyGather.sems(parts)
        + BlkGather.sems(n_line) * 4
        + LineGather.sems(n_line)
        + [pltpu.SemaphoreType.DMA((3,))] * 2
        + [pltpu.SemaphoreType.DMA((7,))] * 2
        + [pltpu.SemaphoreType.DMA((3,))] * 2
        + [pltpu.SemaphoreType.DMA((2,))],
        compiler_params=params(6),
        cost_estimate=pl.CostEstimate(flops=0, bytes_accessed=40 * 3_000_000, transcendentals=0),
        name="entry",
    )(hid, small, wq, wk, wv, wo, wd, wu)
def dot_nt(a, b):
    return lax.dot_general(a, b, (((1,), (1,)), ((), ())), preferred_element_type=F32)


def dot_nn(a, b):
    return lax.dot_general(a, b, (((1,), (0,)), ((), ())), preferred_element_type=F32)


def dot_tn(a, b):
    return lax.dot_general(a, b, (((0,), (0,)), ((), ())), preferred_element_type=F32)


def lanes_of(shape):
    return lax.broadcasted_iota(jnp.int32, shape, len(shape) - 1)


def halves(x):
    row = lax.broadcasted_iota(jnp.int32, (128, 128), 0) // HEAD_DIM
    same = jnp.where(row == lanes_of((128, 128)) // HEAD_DIM, 1.0, 0.0).astype(BF)
    high = x.astype(BF)
    rest = (x - high.astype(F32)).astype(BF)
    return dot_nn(high, same) + dot_nn(rest, same)


def turn(x):
    first = lanes_of(x.shape) % HEAD_DIM < HEAD_DIM // 2
    return jnp.where(first, pltpu.roll(x, 128 - 32, 1), pltpu.roll(x, 32, 1))


def down_columns(row):
    n = row.shape[1]
    one = jnp.transpose(jnp.broadcast_to(row, (128, n)))
    return jnp.concatenate([one] * (n // 128), axis=1)


def arrivals(n_line, body):
    each = 2 * n_line - 1

    def step(t, carry):
        stage, r = t // each, lax.rem(t, each)
        body(stage, (r + 1) // 2, lax.rem(r + 1, 2))
        return carry

    lax.fori_loop(0, 2 * each, step, 0)


def attend_kernel(
    n_line, ready, x_ref, wq_ref, wk_ref, wv_ref, cos_ref, sin_ref, scale_ref, oc_ref, wg_ref, wu_ref, kp_ref,
    q_h, y_h, c_h, kv_h, oc_o, wg_o, wu_o, o_ref, mixed_ref, inv_ref,
    kv_ref, acc, total, place_q, q_ref, y_ref, c_ref, kv_o, kept, *sems,
):
    y, c, z, s = place()
    blk_greet(n_line)
    seqs, rows, wide = q_ref.shape
    heads = wide // 128
    chunk = 4 * LINE_CHUNKS
    cut = wu_ref.shape[-1] - wu_o.shape[-1]
    up = LineGather(
        n_line, lambda: wu_ref.at[:, slice(cut, wu_ref.shape[-1])], lambda zz: wu_o.at[zz], *sems[-4:]
    )
    up.start()
    ready()

    each = len(BlkGather.sems(n_line))
    picks = [
        (lambda i=i: kv_ref.at[i], lambda block, i=i: kv_o.at[block, i]) for i in range(seqs)
    ] + [(lambda: oc_ref, lambda block: oc_o.at[:, block])]
    jobs = [
        BlkGather(n_line, *pick, *sems[each * i : each * (i + 1)]) for i, pick in enumerate(picks)
    ]

    def make(t, carry):
        i, h = t // heads, lax.rem(t, heads)
        lanes = pl.ds(pl.multiple_of(h * 128, 128), 128)
        mine = pl.ds(pl.multiple_of(i * rows, rows), rows)
        wv = wv_ref[h]
        got = dot_nt(x_ref[mine], jnp.concatenate([wq_ref[h], wk_ref[h], jnp.zeros_like(wv), wv], axis=0))
        raw, value = got[:, :128], got[:, 128:]
        low = lanes_of(raw.shape) < HEAD_DIM
        turned = raw * cos_ref[mine] + turn(raw) * sin_ref[mine]
        norm = lax.rsqrt(halves(turned * turned) + HEAD_DIM * tiny_eps)
        unit = turned * norm
        both = unit * scale_ref[pl.ds(h, 1)]
        q_ref[i, :, lanes] = jnp.where(low, both, 0.0).astype(BF)
        kv_ref[i, :, lanes] = jnp.where(low, pltpu.roll(both, HEAD_DIM, 1), value).astype(BF)
        y_ref[mine, lanes] = unit
        c_ref[mine, lanes] = norm
        for j in range(seqs):
            pl.when(t == heads * (j + 1) - 1)(jobs[j].start)
        return carry

    lax.fori_loop(0, seqs * heads, make, 0)
    gates = line_gathers(
        n_line, wg_ref, lambda z: wg_o.at[z], sems[each * (seqs + 1) : each * (seqs + 1) + chunk]
    )
    jobs[-1].start()
    for job in gates:
        job.keep().start()
    n_blk = 2 * n_line
    keeps = [
        pltpu.make_async_copy(a, o, kept.at[n_blk + i])
        for i, (a, o) in enumerate(((q_ref, q_h), (y_ref, y_h), (c_ref, c_h)))
    ]
    for copy in keeps:
        copy.start()

    def keep_keys(block):
        return pltpu.make_async_copy(kv_o.at[block], kv_h.at[block], kept.at[block])

    acc[...] = jnp.zeros_like(acc)
    total[...] = jnp.zeros_like(total)
    for i in range(seqs):
        place_q[i] = down_columns(kp_ref[i, z * 2 + s])

    def attend_to(i, block, keys):
        allowed = kp_ref[i, block] <= place_q[i]
        for h in range(heads):
            lanes = slice(h * 128, (h + 1) * 128)
            kv = keys(lanes)
            p = jnp.where(allowed, jnp.exp(dot_nt(q_ref[i, :, lanes], kv)), 0.0)
            part = p[:, :128]
            for j in range(1, rows // 128):
                part = part + p[:, j * 128 : (j + 1) * 128]
            total[i, h] = total[i, h] + part
            acc[i, h] = acc[i, h] + dot_nn(p.astype(BF), kv)

    def body(stage, k, way):
        ahead = jnp.where(k == 0, 1, k + 1)

        @pl.when((stage == 1) & ((k == 0) | (way == 1)) & (ahead < n_line))
        def _():
            for job in gates + [up]:
                job.step(ahead)

        @pl.when((stage == 0) & (k > 0) & (way == 0))
        def _():
            for job in jobs:
                job.step(k)

        for w, last in ((0, z), (1, n_line - 1 - z)):
            @pl.when((stage == 0) & (k == last) & ((k == 0) | (way == 0)))
            def _():
                for job in gates:
                    pl.when(job.goes(w))(lambda: job.own(w).start())

        there = (k == 0) | jnp.where(way == 0, z >= k, z + k < n_line)

        @pl.when(there)
        def _():
            for job in jobs:
                for w in (0, 1):
                    pl.when((stage == 1) & (k > 0) & (way == w))(lambda: job.over(w, k).wait_recv())
                pl.when((stage == 1) & (k == 0))(lambda: job.own(2).wait_recv())
                pl.when((stage == 0) & (k == 0))(lambda: job.keep().wait())
            zz = jnp.where(way == 0, z - k, z + k)
            block = zz * 2 + jnp.where(stage == 0, s, 1 - s)
            keep_keys(block).start()

            def one(i, carry):
                attend_to(i, block, lambda lanes: kv_o[block, i, :, lanes])
                return carry

            lax.fori_loop(0, seqs, one, 0)

    arrivals(n_line, body)
    low = lanes_of((rows, 128)) < HEAD_DIM
    for i in range(seqs):
        outs = []
        for h in range(heads):
            inverse = 1.0 / jnp.broadcast_to(jnp.sum(total[i, h], axis=-1, keepdims=True), (rows, 128))
            out = acc[i, h] * inverse
            o_ref[i, h] = out
            inv_ref[i, h] = jnp.transpose(inverse)[:8]
            outs.append(out)
        for h in range(0, heads - 1, 2):
            mixed_ref[i, :, h * HEAD_DIM : (h + 2) * HEAD_DIM] = jnp.where(
                low, pltpu.roll(outs[h], HEAD_DIM, 1), outs[h + 1]
            ).astype(BF)
        if heads % 2 == 1:
            mixed_ref[i, :, (heads - 1) * HEAD_DIM :] = pltpu.roll(outs[-1], HEAD_DIM, 1)[:, :HEAD_DIM].astype(BF)
    for job in jobs:
        job.finish_sends()
    for job in gates + [up]:
        job.finish()
    for copy in keeps + [keep_keys(block) for block in range(n_blk)]:
        copy.wait()


def attend(n_line, seqs, x, wq, wk, wv, cos, sin, scale, oc, wg, wu, k_places):
    tokens, width = x.shape
    n_blk, heads, rows = 2 * n_line, wq.shape[0], tokens // seqs
    head, wide = (seqs, heads, rows, 128), (seqs, rows, heads * 128)
    flat = ((tokens, heads * 128), F32)
    first = lane_chunks(width)[0].stop
    return comm_call(
        functools.partial(attend_kernel, n_line), "attend", 5,
        (x, wq, wk, wv, cos, sin, scale, oc, wg, wu, k_places),
        [
            (wide, BF), flat, flat, ((n_blk,) + wide, BF), (oc.shape[:1] + (n_blk,) + oc.shape[1:], BF),
            ((n_line,) + wg.shape, BF), ((n_line, wu.shape[0], width - first), BF), (head, F32),
            ((seqs, rows, heads * HEAD_DIM), BF), ((seqs, heads, 8, rows), F32),
        ],
        [
            pltpu.VMEM(wide, BF), pltpu.VMEM(head, F32), pltpu.VMEM(head, F32), pltpu.VMEM((seqs, rows, rows), F32),
            pltpu.VMEM(wide, BF), pltpu.VMEM(*flat), pltpu.VMEM(*flat), pltpu.VMEM((n_blk,) + wide, BF),
            pltpu.SemaphoreType.DMA((n_blk + 3,)),
        ]
        + BlkGather.sems(n_line) * (seqs + 1) + line_gather_sems(n_line) + LineGather.sems(n_line),
        90, far_outs=(0, 1, 2, 3, 4, 5, 6), late=(0, 1, 2, 3, 4, 5),
    )


def attend_back_kernel(
    n_line, fits, ready, q_ref, low_ref, w_ref, mixed_ref, o_ref, inv_ref, kv_ref, kp_ref, gu_ref,
    dq_ref, dkv_ref, oc_ref, gu_o, dz, delta, dq, parts, oparts, key_s, key_sem, *scratch,
):
    y, c, z, s = place()
    blk_greet(n_line)
    seqs, rows, wide = q_ref.shape
    heads, width = wide // 128, low_ref.shape[-1]
    each = 6
    ups = line_reduces(n_line, gu_ref, scratch[each * (seqs + 1) :])
    for line_job, _ in ups:
        line_job.step(n_line - 1)
    ready()
    low_rows = low_ref[...].reshape(seqs * rows, width)
    grad = dot_tn(low_rows, mixed_ref[...].reshape(seqs * rows, mixed_ref.shape[-1])).astype(BF)
    n_blk, each_out = 2 * n_line, width // (8 * n_line)
    for b in range(n_blk):
        for v in range(4):
            at = (v * n_blk + b) * each_out
            oparts[b, v * each_out : (v + 1) * each_out] = grad[at : at + each_out]
    each = 6
    jobs = [BlkReduce(n_line, parts.at[:, i], *scratch[each * i : each * (i + 1)]) for i in range(seqs)]
    out_job = BlkReduce(n_line, oparts, *scratch[each * seqs : each * (seqs + 1)])
    for k in range(n_line - 1, -1, -1):
        out_job.start(k)
    low = lanes_of((rows, 128)) < HEAD_DIM
    for i in range(seqs):
        d = dot_nn(low_rows[i * rows : (i + 1) * rows], w_ref[...]).astype(BF).astype(F32)
        for h in range(heads):
            at = h // 2 * 128
            if h == heads - 1 and heads % 2 == 1:
                tile = jnp.concatenate([jnp.zeros((rows, HEAD_DIM), F32), d[:, at:]], axis=1)
            else:
                tile = d[:, at : at + 128]
                if h % 2 == 0:
                    tile = pltpu.roll(tile, HEAD_DIM, 1)
                tile = jnp.where(low, 0.0, tile)
            dz[i, h] = tile.astype(BF)
            row = jnp.sum(tile * o_ref[i, h], axis=-1, keepdims=True)
            delta[i, h] = jnp.transpose(jnp.broadcast_to(row, (rows, 128)))[:8]
    dq[...] = jnp.zeros_like(dq)

    def block_of(block):
        if fits:
            keys = kv_ref.at[block]
        else:
            keys = key_s
            copy = pltpu.make_async_copy(kv_ref.at[block], key_s, key_sem.at[0])
            copy.start()
            copy.wait()
        def one(i, carry):
            allowed = down_columns(kp_ref[i, block]) <= kp_ref[i, z * 2 + s]
            for h in range(heads):
                lanes = slice(h * 128, (h + 1) * 128)
                kv = keys[i, :, lanes]
                pair = jnp.concatenate([q_ref[i, :, lanes], dz[i, h]], axis=0)
                scores = dot_nt(kv, pair)
                p = jnp.where(allowed, jnp.exp(scores[:, :rows]) * inv_ref[i, h][:1], 0.0)
                ds = (p * (scores[:, rows:] - delta[i, h][:1])).astype(BF)
                parts[block, i, :, lanes] = dot_nn(
                    jnp.concatenate([ds, p.astype(BF)], axis=1), pair
                ).astype(BF)
                dq[i, h] = dq[i, h] + dot_tn(ds, kv)
            return carry

        lax.fori_loop(0, seqs, one, 0)

    def step(t, carry):
        k, r = n_line - 1 - t // 4, lax.rem(t, 4)
        way, stays = r // 2, lax.rem(r, 2)

        @pl.when((r == 0) & (k > 0) & (k < n_line - 1))
        def _():
            for line_job, _ in ups:
                line_job.step(k)

        there = jnp.where(k == 0, way == 0, jnp.where(way == 0, z + k < n_line, z >= k))

        @pl.when(there)
        def _():
            zz = jnp.where(way == 0, z + k, z - k)
            block_of(zz * 2 + jnp.where(stays == 0, 1 - s, s))

            @pl.when(stays == 0)
            def _():
                for job in jobs:
                    job.side(zz).start()

        @pl.when((r == 3) & (k + 1 < n_line))
        def _():
            for w in (0, 1):
                @pl.when(jobs[0].exists(w, k + 1))
                def _():
                    for job in jobs + [out_job]:
                        job.move_on(w, k + 1)

        return carry

    lax.fori_loop(0, 4 * n_line, step, 0)
    for i in range(seqs):
        for h in range(heads):
            dq_ref[i, :, h * 128 : (h + 1) * 128] = dq[i, h].astype(BF)
    out_job.result(oc_ref)
    for i, job in enumerate(jobs):
        job.result(dkv_ref.at[i])
    for job, cut in ups:
        job.result(gu_o.at[cut])
    for job in jobs + [out_job] + [job for job, _ in ups]:
        job.finish()


def attend_back(n_line, q, low, w, mixed, o, inv, kv, k_places, gu):
    seqs, rows, wide = q.shape
    n_blk, heads = 2 * n_line, wide // 128
    head = (seqs, heads, rows, 128)
    width, columns = w.shape
    out_shape = (width // n_blk, columns)
    one = jax.ShapeDtypeStruct((n_blk,) + kv.shape[2:], BF)
    out_one = jax.ShapeDtypeStruct((n_blk,) + out_shape, BF)
    fits = kv.size * 2 <= 8_000_000
    return comm_call(
        functools.partial(attend_back_kernel, n_line, fits), "attend_back", 7,
        (q, low, w, mixed, o, inv, kv, k_places, gu),
        [(q.shape, BF), (kv.shape[1:], BF), (out_shape, BF), (gu.shape[1:], F32)],
        [
            pltpu.VMEM(head, BF), pltpu.VMEM((seqs, heads, 8, rows), F32), pltpu.VMEM(head, F32),
            pltpu.VMEM(kv.shape, BF), pltpu.VMEM(out_one.shape, BF),
            pltpu.VMEM((16, 128) if fits else kv.shape[1:], BF), pltpu.SemaphoreType.DMA((1,)),
        ]
        + BlkReduce.scratch(n_line, one) * seqs + BlkReduce.scratch(n_line, out_one)
        + line_reduce_scratch(n_line, gu),
        75, 67_000_000, () if fits else (6,), late=(0, 1, 2, 3, 4) + (6,) * fits,
    )


def unit_of(x):
    c = lax.rsqrt(jnp.sum(x * x, axis=-1, keepdims=True) + x.shape[-1] * tiny_eps)
    return x * c, c


def unit_back(y, c, dy):
    return c * (dy - y * jnp.sum(y * dy, axis=-1, keepdims=True))


class Late:
    @staticmethod
    def scratch(arrays):
        return [pltpu.VMEM(a.shape, a.dtype) for a in arrays] + [pltpu.SemaphoreType.DMA((len(arrays),))]

    def __init__(self, refs, scratch):
        *self.bufs, sem = scratch
        self.copies = [
            pltpu.make_async_copy(ref, buf, sem.at[i]) for i, (ref, buf) in enumerate(zip(refs, self.bufs))
        ]
        for copy in self.copies:
            copy.start()

    def __call__(self, i):
        self.copies[i].wait()
        return self.bufs[i]


def attn_joint_kernel(
    n_line, ready, mixed, w, hid, rate, dc, first_o, ua_o, ca_o, cv_o, all_o, down_o, part, low, *scratch
):
    ends = line_ends(n_line)
    greet(plane_peers(), ends[:2])
    ready()
    split = len(UlyReduce.scratch(part))
    job = UlyReduce(part, *scratch[:split])
    out = PlaneGather(low, all_o, *scratch[split : split + 3])
    downs = line_gathers(n_line, dc, lambda z: down_o.at[:, z], scratch[split + 3 :])
    for line_job in downs:
        line_job.start()
    steps = [(k, line_job) for k in range(1, n_line) for line_job in downs]
    parts, _, rows, width = part.shape
    seqs = mixed.shape[0]
    each = parts // seqs
    for i in range(seqs):
        got = dot_nt(mixed[i], w[...]).astype(BF)
        for k in range(each):
            for u in range(4):
                at = (u * each + k) * rows
                part[i * each + k, u] = got[at : at + rows]
            for copy in job.near[i * each + k]:
                copy.start()
    job.middle()
    k, line_job = steps.pop(0)
    line_job.step(k)
    for i in range(parts):
        ua, ca = unit_of(job.result(i))
        h = hid[i].astype(F32)
        first, cv = unit_of(h + rate[0:1] * (ua - h))
        low[i] = first.astype(BF)
        out.start_part(i)
        first_o[i], ua_o[i] = first, ua
        ca_o[i] = jnp.broadcast_to(ca, (rows, 128))
        cv_o[i] = jnp.broadcast_to(cv, (rows, 128))
        if i > 0:
            out.forward_part(i - 1)
        if len(steps) > 0:
            k, line_job = steps.pop(0)
            line_job.step(k)
    out.forward_part(parts - 1)
    for k, line_job in steps:
        line_job.step(k)
    out.finish()
    job.finish()
    for line_job in downs:
        line_job.finish()


def attn_joint(n_line, mixed, w, hid, rate, dc):
    parts, rows, width = hid.shape
    part = jax.ShapeDtypeStruct((parts, 4, rows, width), BF)
    thin = ((parts, rows, 128), F32)
    return comm_call(
        functools.partial(attn_joint_kernel, n_line), "attn_joint", 1, (mixed, w, hid, rate, dc),
        [
            (hid.shape, F32), (hid.shape, F32), thin, thin, ((8, parts, rows, width), BF),
            (dc.shape[:1] + (n_line,) + dc.shape[1:], BF),
        ],
        [pltpu.VMEM(part.shape, BF), pltpu.VMEM(hid.shape, BF)]
        + UlyReduce.scratch(part) + PlaneGather.sems(parts) + line_gather_sems(n_line),
        25, far_outs=(4, 5), late=(0, 1, 2, 4),
    )


def plane_products(job, part, y, c, prepare, product):
    _, parts, rows, width = part.shape
    for yy, spots in ((1 - y, (0, 2)), (y, (1, 3))):
        def one(j, carry):
            cc = jnp.where(j == 0, 1 - c, c)
            prepare(yy, cc)
            got = product(yy, cc).astype(BF).reshape(2, parts, rows, width)
            for ss in (0, 1):
                part[plane_index(yy, cc, ss)] = got[ss]

            @pl.when(j == 0)
            def _():
                for k in spots:
                    for copy in job.near[k]:
                        copy.start()

            return carry

        lax.fori_loop(0, 2, one, 0)
        job.middle(spots[0] == 0)


def ff_joint_kernel(
    ready, x, wu, wu2, wg, rate, w, first, cot, out_o, d1_o, sum_o, all_o, inner_h, up_h, gate_h,
    part, low, inner, up_s, gate_s, kept, *scratch,
):
    y, c, z, s = place()
    greet(plane_peers())
    split = len(PlaneReduce.scratch(part))
    job = PlaneReduce(part, *scratch[:split])
    out = PlaneGather(low, all_o, *scratch[split:])
    _, seqs, rows, width = part.shape
    columns, tokens = inner.shape[-1], 2 * seqs * rows
    cut = wu.shape[1]

    def forward(yy, cc):
        block = x[yy, cc].reshape(tokens, width)
        up = dot_nt(block[:, :cut], wu[...]) + dot_nt(block[:, cut:], wu2[...])
        gate = dot_nt(block, wg[...])
        gz = gate * rate[3:4, :columns] * D**0.5
        got = gz / (1.0 + jnp.exp(-gz)) * (up * rate[2:3, :columns])
        inner[yy, cc] = got.astype(BF).reshape(inner.shape[2:])
        up_s[yy, cc] = up.reshape(up_s.shape[2:])
        gate_s[yy, cc] = gate.reshape(gate_s.shape[2:])

    ready()
    plane_products(
        job, part, y, c, forward, lambda yy, cc: dot_nt(inner[yy, cc].reshape(tokens, columns), w[...])
    )
    keeps = [
        pltpu.make_async_copy(a, o, kept.at[i])
        for i, (a, o) in enumerate(((inner, inner_h), (up_s, up_h), (gate_s, gate_h)))
    ]
    for copy in keeps:
        copy.start()
    job.last()
    for i in range(seqs):
        ub, cb = unit_of(job.result(i))
        f, b = first[i], rate[1:2]
        o, cw = unit_of(f + b * (ub - f))
        dw = unit_back(o, cw, cot[i].astype(F32))
        step = b * dw
        low[i] = unit_back(ub, cb, step).astype(BF)
        out.start_part(i)
        out_o[i] = o.astype(BF)
        d1_o[i] = dw - step
        total = jnp.sum(dw * (ub - f), axis=0, keepdims=True)
        sum_o[...] = total if i == 0 else sum_o[...] + total
        if i > 0:
            out.forward_part(i - 1)
    out.forward_part(seqs - 1)
    out.finish()
    job.finish()
    for copy in keeps:
        copy.wait()


def ff_joint(x, wu, wu2, wg, rate, w, first, cot):
    seqs, rows, width = first.shape
    part = jax.ShapeDtypeStruct((8, seqs, rows, width), BF)
    columns = wg.shape[0]
    wide = (2, 2, 2, seqs * rows, columns)
    return comm_call(
        ff_joint_kernel, "ff_joint", 2,
        (x.reshape(wide[:4] + (width,)), wu, wu2, wg, rate, w, first, cot),
        [
            (first.shape, BF), (first.shape, F32), ((1, width), F32), (part.shape, BF),
            (wide, BF), (wide, F32), (wide, F32),
        ],
        [
            pltpu.VMEM(part.shape, BF), pltpu.VMEM(first.shape, BF), pltpu.VMEM(wide, BF),
            pltpu.VMEM(wide, F32), pltpu.VMEM(wide, F32), pltpu.SemaphoreType.DMA((3,)),
        ]
        + PlaneReduce.scratch(part) + PlaneGather.sems(seqs),
        35, far_outs=(3, 4, 5, 6), late=(0, 1, 2, 3, 5),
    )


def back_joint_kernel(
    n_line, ready, d, inner, rate, d1, first, ua, ca, cv, hid, wd_h, up_h, gate_h, wu_h, wu2_h, wg_h, x_h,
    res_o, sum_o, ff_sum_o, all_o, up_o, gate_o, down_o, part, low, down_s, du, dg, *scratch,
):
    y, c, z, s = place()
    late = Late((wd_h, up_h, gate_h, wu_h, wu2_h, wg_h, x_h), scratch[:8])
    scratch = scratch[8:]
    greet(plane_peers(), line_ends(n_line)[:2])
    ready()
    split = len(PlaneReduce.scratch(part))
    job = PlaneReduce(part, *scratch[:split])
    _, parts, rows, width = part.shape
    columns = du.shape[-1]
    tokens = 8 * parts * rows
    each = parts // all_o.shape[0]
    out = UlyGather(
        low, all_o, *scratch[split : split + 3],
        pick=lambda i, u: all_o.at[i // each, u, pl.ds(i % each * rows, rows)],
    )
    downs = line_reduces(n_line, down_s, scratch[split + 3 :])
    flat = lambda ref: ref[...].reshape(tokens, ref.shape[-1])

    deep = width // (4 * n_line)
    inner_all = flat(inner)

    def down_half(i, carry):
        lanes = pl.ds(pl.multiple_of(i * (width // 2), 128), width // 2)
        grad = dot_tn(d[:, :, :, :, lanes].reshape(tokens, width // 2), inner_all).astype(BF)
        for v in (0, 1):
            for k in range(n_line):
                at = (v * n_line + k) * deep
                down_s[k, 2 * i + v] = grad[at : at + deep]
        return carry

    lax.fori_loop(0, 2, down_half, 0)
    for line_job, _ in downs:
        line_job.step(n_line - 1)

    wd, up_ref, gate_ref = late(0), late(1), late(2)
    u_scale, g_scale = rate[2:3, :columns], rate[3:4, :columns] * D**0.5

    ff_sum_o[...] = jnp.zeros_like(ff_sum_o)

    def gated_back(yy, cc):
        got = dot_nn(d[yy, cc].reshape(tokens // 4, width), wd[...])
        up, gate = up_ref[yy, cc].reshape(got.shape), gate_ref[yy, cc].reshape(got.shape)
        gz = gate * g_scale
        sig = 1.0 / (1.0 + jnp.exp(-gz))
        d_up = got * (gz * sig)
        d_gate = got * (up * u_scale) * sig * (1.0 + gz * (1.0 - sig))
        du[yy, cc] = (d_up * u_scale).astype(BF).reshape(du.shape[2:])
        dg[yy, cc] = (d_gate * g_scale).astype(BF).reshape(dg.shape[2:])
        ff_sum_o[0:1] = ff_sum_o[0:1] + jnp.sum(d_up * up, axis=0, keepdims=True)
        ff_sum_o[1:2] = ff_sum_o[1:2] + jnp.sum(d_gate * gate, axis=0, keepdims=True) * D**0.5

    wu, wu2, wg = late(3), late(4), late(5)

    def product(yy, cc):
        u, g = du[yy, cc].reshape(tokens // 4, columns), dg[yy, cc].reshape(tokens // 4, columns)
        got = jnp.concatenate([dot_nn(u, wu[...]), dot_nn(u, wu2[...])], axis=1)
        return got + dot_nn(g, wg[...])

    plane_products(job, part, y, c, gated_back, product)
    steps = [(k, line_job) for k in range(n_line - 2, 0, -1) for line_job, _ in downs]
    job.last()
    x = late(6)

    def by_line(o, ref):
        n, rows_all = columns // n_line, flat(ref)

        def half(i, carry):
            lanes = pl.ds(pl.multiple_of(i * (width // 2), 128), width // 2)
            grad = dot_tn(rows_all, x[:, lanes]).astype(BF)
            for k in range(n_line):
                o[k, :, lanes] = grad[k * n : (k + 1) * n]
            return carry

        lax.fori_loop(0, 2, half, 0)

    by_line(up_o, du)
    for i in range(parts):
        f, h, u, a = first[i], hid[i].astype(F32), ua[i], rate[0:1]
        dv = unit_back(f, cv[i][:, :1], d1[i] + job.result(i))
        step = a * dv
        low[i] = unit_back(u, ca[i][:, :1], step).astype(BF)
        out.start_part(i)
        res_o[i] = dv - step
        total = jnp.sum(dv * (u - h), axis=0, keepdims=True)
        sum_o[...] = total if i == 0 else sum_o[...] + total
        if len(steps) > 0:
            k, line_job = steps.pop(0)
            line_job.step(k)
    for k, line_job in steps:
        line_job.step(k)
    by_line(gate_o, dg)
    out.forward()
    out.finish()
    job.finish()
    for line_job, cut in downs:
        line_job.result(down_o.at[cut])
        line_job.finish()


def back_joint(n_line, seqs, d, wd, up, gate, rate, wu, wu2, wg, x, inner, d1, first, ua, ca, cv, hid):
    parts, rows, width = first.shape
    columns = wd.shape[1]
    part = jax.ShapeDtypeStruct((8, parts, rows, width), BF)
    down = jax.ShapeDtypeStruct((n_line, 4, width // (4 * n_line), columns), BF)
    by_line = ((n_line, columns // n_line, width), BF)
    wide = lambda a: a.reshape(2, 2, 2, parts * rows, a.shape[-1])
    thin = pltpu.VMEM((2, 2, 2, parts * rows, columns), BF)
    late = (wd, wide(up), wide(gate), wu, wu2, wg, x)
    return comm_call(
        functools.partial(back_joint_kernel, n_line), "back_joint", 3,
        (wide(d), wide(inner), rate, d1, first, ua, ca, cv, hid) + late,
        [
            (first.shape, F32), ((1, width), F32), ((2, columns), F32),
            ((seqs, 4, parts * rows // seqs, width), BF), by_line, by_line, (down.shape[1:], BF),
        ],
        [pltpu.VMEM(part.shape, BF), pltpu.VMEM(first.shape, BF), pltpu.VMEM(down.shape, BF), thin, thin]
        + Late.scratch(late) + PlaneReduce.scratch(part) + UlyGather.sems(parts)
        + line_reduce_scratch(n_line, down),
        40, VMEM_BYTES, tuple(range(9, 16)), far_outs=(3,), late=(0, 1),
    )


def settle_kernel(count, *refs):
    ins, outs, bufs = refs[:count], refs[count : 2 * count], refs[2 * count : 3 * count]
    come, go = refs[3 * count :]
    into = [pltpu.make_async_copy(x, b, come.at[i]) for i, (x, b) in enumerate(zip(ins, bufs))]
    out = [pltpu.make_async_copy(b, o, go.at[i]) for i, (b, o) in enumerate(zip(bufs, outs))]
    for copy in into:
        copy.start()
    for a, b in zip(into, out):
        a.wait()
        b.start()
    for copy in out:
        copy.wait()


def settle(*arrays):
    count = len(arrays)
    anyway = pl.BlockSpec(memory_space=pl.ANY)
    return pl.pallas_call(
        functools.partial(settle_kernel, count),
        out_shape=[jax.ShapeDtypeStruct(a.shape, a.dtype) for a in arrays],
        in_specs=[anyway] * count,
        out_specs=[anyway] * count,
        scratch_shapes=[pltpu.VMEM(a.shape, a.dtype) for a in arrays]
        + [pltpu.SemaphoreType.DMA((count,))] * 2,
        compiler_params=pltpu.CompilerParams(vmem_limit_bytes=VMEM_BYTES),
        name="settle",
    )(*arrays)


def local(
    hidden, positions, w_query, w_key, w_value, w_out, w_up, w_gate, w_down,
    qk_scale, alpha_attn, alpha_mlp, up_scale, gate_scale, cotangent,
):
    seqs, rows_each, width = hidden.shape
    n_line = lax.axis_size("line")
    n_blk = 2 * n_line
    heads = HEADS // 4
    local_width = heads * HEAD_DIM
    group_rows = 4 * rows_each
    tokens = seqs * rows_each
    group_tokens = 4 * tokens
    plane_tokens = 8 * tokens
    attn_each, ff_each = w_query.shape[0], w_up.shape[0]
    ff_local = ff_each * n_line
    far, core, line, side = place()
    uly = far * 2 + core

    def row(x, wide):
        return jnp.pad(x, ((0, 0),) * (x.ndim - 1) + ((0, wide - x.shape[-1]),))

    pieces = [v.astype(F32) for v in (qk_scale, alpha_attn, alpha_mlp, up_scale, gate_scale)]
    pieces.append(positions.reshape(-1).astype(F32))
    rows_of = [-(-v.shape[0] // 128) for v in pieces]
    starts = [sum(rows_of[:i]) for i in range(len(pieces) + 1)]
    tall = starts[-1] + -starts[-1] % 8
    small = 0.0
    for v, start in zip(pieces, starts):
        small = small + jnp.pad(v, (start * 128, (tall - start) * 128 - v.shape[0]))
    small = small.reshape(tall, 128)

    hid_all, small_all, wq_all, wk_all, wv_all, out_cols, down_cols, up_first = entry(
        n_line, hidden, small, w_query, w_key, w_value, w_out, w_down, w_up
    )
    up_first = up_first.reshape(ff_local, -1)

    flat = small_all.reshape(4, n_blk, tall * 128)

    def piece(rows, i):
        return rows[..., starts[i] * 128 : starts[i] * 128 + pieces[i].shape[0]]

    own = lax.dynamic_slice_in_dim(flat, uly, 1, 0)[0]
    scale_wide = piece(own, 0).reshape(heads, HEAD_DIM)
    attn_rate = piece(flat, 1).reshape(-1)
    mlp_rate = piece(flat, 2).reshape(-1)
    mine = lax.dynamic_slice_in_dim(own.reshape(n_line, 2, -1), side, 1, 1)[:, 0]
    up_wide = piece(mine, 3).reshape(-1)
    gate_wide = piece(mine, 4).reshape(-1)
    assert ff_local <= width
    rates = jnp.pad(
        jnp.stack([attn_rate, mlp_rate, row(up_wide, width), row(gate_wide, width)]), ((0, 4), (0, 0))
    )
    places = jnp.transpose(
        piece(flat, 5).reshape(4, n_blk, seqs, rows_each), (2, 1, 0, 3)
    ).reshape(seqs, n_blk, 1, group_rows)
    q_places = lax.dynamic_slice_in_dim(places, line * 2 + side, 1, 1)[:, 0]

    lane = jnp.arange(128) % HEAD_DIM
    freqs = rotary_base ** (-((lane % 32).astype(F32) * (2.0 / HEAD_DIM)))
    angles = q_places.reshape(group_tokens, 1) * freqs
    cos = jnp.cos(angles)
    sin = jnp.where(lane < 32, -1.0, 1.0) * jnp.sin(angles)
    scale_both = jnp.concatenate([scale_wide * HEAD_DIM**0.5, scale_wide], axis=1)

    group_hidden = hid_all.reshape(group_tokens, width)
    wq = wq_all.reshape(heads, HEAD_DIM, width)
    wk = wk_all.reshape(heads, HEAD_DIM, width)
    wv = wv_all.reshape(heads, HEAD_DIM, width)
    qz, y_both, c_both, kv_all, out_all, gate_full, up_last, attended, mixed, inverse = attend(
        n_line, seqs, group_hidden, wq, wk, wv, cos, sin, scale_both, out_cols, w_gate, w_up,
        places,
    )
    up_last = up_last.reshape(ff_local, -1)
    gate_full = gate_full.reshape(ff_local, width)
    out_full = out_all.reshape(width, local_width)

    fine = (2 * seqs, rows_each // 2, width)
    hidden_fine = hidden.reshape(fine)
    first, unit_att, att_c, first_c, mlp_in, down_full = attn_joint(
        n_line, mixed, out_full, hidden_fine, rates,
        down_cols.reshape(4, 2 * attn_each, ff_local),
    )
    down_full = down_full.reshape(width, ff_local)
    mlp_in = mlp_in.reshape(plane_tokens, width)
    layer_out, grad_first, grad_alpha_mlp, branch_low, inner, up_rows, gate_rows = ff_joint(
        mlp_in, up_first, up_last, gate_full, rates, down_full, first, cotangent.reshape(fine)
    )
    branch_low = branch_low.reshape(plane_tokens, width)
    grad_residual, grad_alpha_attn, ff_scales, att_low, grad_up, grad_gate, down_own = back_joint(
        n_line, seqs, branch_low, down_full, up_rows, gate_rows, rates, up_first, up_last, gate_full,
        mlp_in, inner, grad_first, first, unit_att, att_c, first_c, hidden_fine,
    )
    down_own = down_own.reshape(8, attn_each, ff_local)

    dq, dkv, out_own, up_own = attend_back(
        n_line, qz, att_low.reshape(seqs, group_rows, width), out_full, mixed, attended, inverse,
        kv_all, places, grad_up,
    )
    out_own = out_own.reshape(4, attn_each, local_width)
    gq, gk, gv, grad_hidden, out_gradient, down_gradient, sums, gate_own = leave(
        n_line, group_hidden, dq, dkv, y_both, c_both, cos, sin, scale_both, wq, wk, wv,
        grad_residual.reshape(seqs, rows_each, width), out_own, down_own,
        grad_alpha_attn, grad_alpha_mlp, ff_scales, grad_gate,
    )
    sums = sums[0]
    layer_out, grad_hidden, gq, gk, gv, out_gradient, up_own, gate_own, down_gradient = settle(
        layer_out.reshape(hidden.shape), grad_hidden, gq, gk, gv, out_gradient, up_own, gate_own,
        down_gradient,
    )
    return (
        layer_out,
        grad_hidden,
        gq,
        gk,
        gv,
        out_gradient,
        up_own,
        gate_own,
        down_gradient,
        sums[128 : 128 + attn_each],
        sums[:attn_each],
        sums[attn_each : 2 * attn_each],
        sums[256 : 256 + ff_each],
        sums[256 + ff_each : 256 + 2 * ff_each],
    )


def solution(mesh):
    far = mesh.shape["uly"] // 2
    line = mesh.shape["blk"] // 2
    finer = Mesh(mesh.devices.reshape(far, 2, line, 2), AXES)
    rows, tokens, flat = P(AXES, None), P(None, AXES, None), P(AXES)
    return jax.shard_map(
        local,
        mesh=finer,
        in_specs=(tokens, P(None, AXES)) + (rows,) * 7 + (flat,) * 5 + (tokens,),
        out_specs=(tokens, tokens) + (rows,) * 7 + (flat,) * 5,
        check_vma=False,
    )
```

```python
import functools
import math

import jax
import jax.numpy as jnp
from jax import lax
from jax.experimental import pallas as pl
from jax.experimental.pallas import tpu as pltpu
from jax.sharding import Mesh
from jax.sharding import PartitionSpec as P

D = 1280
HEADS = 20
HEAD_DIM = 64
AXES = ("far", "core", "line", "side")
PLANE = ("far", "core", "side")
VMEM_BYTES = 60 * 1024 * 1024

rotary_base = 10000.0
tiny_eps = 1e-06
BF = jnp.bfloat16
F32 = jnp.float32


def place():
    return tuple(lax.axis_index(name) for name in AXES)


def remote(src, dst, send, recv, device):
    return pltpu.make_async_remote_copy(
        src_ref=src,
        dst_ref=dst,
        send_sem=send,
        recv_sem=recv,
        device_id=device,
        device_id_type=pl.DeviceIdType.MESH,
    )


def signal_to(device):
    pl.semaphore_signal(
        pltpu.get_barrier_semaphore(), inc=1, device_id=device, device_id_type=pl.DeviceIdType.MESH
    )


def greet(devices, maybe=()):
    count = len(devices)
    for device in devices:
        signal_to(device)
    for there, device in maybe:
        pl.when(there)(functools.partial(signal_to, device))
        count = count + jnp.where(there, 1, 0)
    pl.semaphore_wait(pltpu.get_barrier_semaphore(), count)


def params(collective_id, room=VMEM_BYTES):
    return pltpu.CompilerParams(
        collective_id=collective_id, has_side_effects=True, vmem_limit_bytes=room
    )


class UlyGather:
    sems = staticmethod(lambda parts: [pltpu.SemaphoreType.DMA((3, parts))] * 2 + [pltpu.SemaphoreType.DMA((parts,))])

    def __init__(self, x, o, send, recv, local, pick=None):
        pick = pick or (lambda i, u: o.at[i, u])
        y, c, z, s = place()
        u, v = y * 2 + c, (1 - y) * 2 + c
        mate, across = (y, 1 - c, z, s), (1 - y, c, z, s)
        self.parts = x.shape[0]
        parts = range(self.parts)
        self.far = [remote(x.at[i], pick(i, u), send.at[0, i], recv.at[0, i], across) for i in parts]
        self.near = [remote(x.at[i], pick(i, u), send.at[1, i], recv.at[1, i], mate) for i in parts]
        self.on = [remote(pick(i, v), pick(i, v), send.at[2, i], recv.at[2, i], mate) for i in parts]
        self.own = [pltpu.make_async_copy(x.at[i], pick(i, u), local.at[i]) for i in parts]

    def start_part(self, i):
        self.far[i].start()
        self.near[i].start()
        self.own[i].start()

    def start(self):
        for i in range(self.parts):
            self.start_part(i)

    def forward(self):
        for i in range(self.parts):
            self.far[i].wait_recv()
            self.on[i].start()

    def finish(self):
        for i in range(self.parts):
            self.near[i].wait_recv()
            self.on[i].wait_recv()
            self.own[i].wait()
            self.far[i].wait_send()
            self.near[i].wait_send()
            self.on[i].wait_send()


def uly_peers():
    y, c, z, s = place()
    return [(y, 1 - c, z, s), (1 - y, c, z, s)]


def add_low(*terms):
    total = terms[0].astype(F32)
    for term in terms[1:]:
        total = total + term.astype(F32)
    return total


class UlyReduce:
    @staticmethod
    def scratch(x):
        parts, _, rows, width = x.shape
        return [
            pltpu.VMEM((parts, 2, rows, width), x.dtype),
            pltpu.VMEM((parts, rows, width), x.dtype),
            pltpu.VMEM((parts, rows, width), x.dtype),
            pltpu.SemaphoreType.DMA((3, parts)),
            pltpu.SemaphoreType.DMA((3, parts)),
        ]

    def __init__(self, x, near, mid, far_in, send, recv):
        y, c, z, s = place()
        mate, across = uly_peers()
        self.x, self.near_ref, self.mid, self.far_in = x, near, mid, far_in
        self.y, self.c, self.parts = y, c, x.shape[0]
        parts = range(self.parts)
        self.near = [
            [
                remote(x.at[i, f * 2 + 1 - c], near.at[i, k], send.at[k, i], recv.at[k, i], mate)
                for k, f in enumerate((1 - y, y))
            ]
            for i in parts
        ]
        self.far = [remote(mid.at[i], far_in.at[i], send.at[2, i], recv.at[2, i], across) for i in parts]

    def start(self):
        for i in range(self.parts):
            for copy in self.near[i]:
                copy.start()

    def middle(self):
        for i in range(self.parts):
            self.near[i][0].wait_recv()
            self.mid[i] = add_low(self.x[i, (1 - self.y) * 2 + self.c], self.near_ref[i, 0]).astype(BF)
            self.far[i].start()

    def result(self, i):
        self.near[i][1].wait_recv()
        self.far[i].wait_recv()
        return add_low(self.x[i, self.y * 2 + self.c], self.near_ref[i, 1], self.far_in[i])

    def finish(self):
        for i in range(self.parts):
            for copy in self.near[i] + [self.far[i]]:
                copy.wait_send()


def plane_peers():
    y, c, z, s = place()
    return [(y, 1 - c, z, s), (1 - y, c, z, s), (y, c, z, 1 - s)]


def plane_index(y, c, s):
    return (y * 2 + c) * 2 + s


class PlaneGather:
    @staticmethod
    def sems(parts):
        return [pltpu.SemaphoreType.DMA((7, parts))] * 2 + [pltpu.SemaphoreType.DMA((parts,))]

    def __init__(self, x, o, send, recv, local):
        y, c, z, s = place()
        mate, across, cross = plane_peers()
        self.parts = parts = range(x.shape[0])
        me, py, px, pd = (
            plane_index(y, c, s),
            plane_index(1 - y, c, s),
            plane_index(y, c, 1 - s),
            plane_index(1 - y, c, 1 - s),
        )

        def copy(source, p, i, slot, device):
            return remote(source, o.at[p, i], send.at[slot, i], recv.at[slot, i], device)

        def on(p, i, slot, device):
            return copy(o.at[p, i], p, i, slot, device)

        self.by_y = [copy(x.at[i], me, i, 0, across) for i in parts]
        self.by_x = [copy(x.at[i], me, i, 1, cross) for i in parts]
        self.near = [copy(x.at[i], me, i, 2, mate) for i in parts]
        self.corner = [on(px, i, 3, across) if i % 2 else on(py, i, 3, cross) for i in parts]
        self.pass_y = [on(py, i, 4, mate) for i in parts]
        self.pass_x = [on(px, i, 5, mate) for i in parts]
        self.pass_d = [on(pd, i, 6, mate) for i in parts]
        self.own = [pltpu.make_async_copy(x.at[i], o.at[me, i], local.at[i]) for i in parts]

    def start_part(self, i):
        for copy in (self.by_y[i], self.by_x[i], self.near[i], self.own[i]):
            copy.start()

    def forward_part(self, i):
        ways = [(self.by_y[i], self.pass_y[i]), (self.by_x[i], self.pass_x[i])]
        first, then = ways[:: 1 - 2 * (i % 2)]
        first[0].wait_recv()
        self.corner[i].start()
        first[1].start()
        then[0].wait_recv()
        then[1].start()

    def finish(self):
        for i in self.parts:
            self.corner[i].wait_recv()
            self.pass_d[i].start()
        for i in self.parts:
            for copy in (self.near[i], self.pass_y[i], self.pass_x[i], self.pass_d[i]):
                copy.wait()
            for copy in (self.by_y[i], self.by_x[i], self.corner[i]):
                copy.wait_send()
            self.own[i].wait()


class PlaneReduce:
    @staticmethod
    def scratch(x):
        one = pltpu.VMEM(x.shape[1:], x.dtype)
        sems = pltpu.SemaphoreType.DMA((7, x.shape[1]))
        return [pltpu.VMEM((4,) + x.shape[1:], x.dtype)] + [one] * 6 + [sems] * 2

    def __init__(self, x, near, out_x, out_y, out_d, in_x, in_y, in_d, send, recv):
        y, c, z, s = place()
        mate, across, cross = plane_peers()
        self.c = c
        self.parts = parts = range(x.shape[1])
        self.spots = ((1 - y, 1 - s), (y, 1 - s), (1 - y, s), (y, s))
        self.x, self.near_ref = x, near
        self.out_x, self.out_y, self.out_d = out_x, out_y, out_d
        self.in_x, self.in_y, self.in_d = in_x, in_y, in_d

        def copy(source, target, i, slot, device):
            return remote(source, target, send.at[slot, i], recv.at[slot, i], device)

        self.near = [
            [copy(x.at[plane_index(sy, 1 - c, ss), i], near.at[k, i], i, k, mate) for i in parts]
            for k, (sy, ss) in enumerate(self.spots)
        ]
        self.corner = [copy(out_d.at[i], in_d.at[i], i, 4, across if i % 2 else cross) for i in parts]
        self.by_x = [copy(out_x.at[i], in_x.at[i], i, 5, cross) for i in parts]
        self.by_y = [copy(out_y.at[i], in_y.at[i], i, 6, across) for i in parts]

    def pair(self, k, i):
        sy, ss = self.spots[k]
        self.near[k][i].wait_recv()
        return add_low(self.x[plane_index(sy, self.c, ss), i], self.near_ref[k, i])

    def middle(self, far):
        for i in self.parts:
            if far:
                self.out_d[i] = self.pair(0, i).astype(BF)
                self.corner[i].start()
                if i % 2 == 1:
                    self.out_y[i] = self.pair(2, i).astype(BF)
                    self.by_y[i].start()
            elif i % 2 == 0:
                self.out_x[i] = self.pair(1, i).astype(BF)
                self.by_x[i].start()

    def last(self):
        for i in self.parts:
            k, out, by = (1, self.out_x, self.by_x) if i % 2 else (2, self.out_y, self.by_y)
            part = self.pair(k, i)
            self.corner[i].wait_recv()
            out[i] = (part + self.in_d[i].astype(F32)).astype(BF)
            by[i].start()

    def result(self, i):
        own = self.pair(3, i)
        self.by_x[i].wait_recv()
        self.by_y[i].wait_recv()
        return own + add_low(self.in_x[i], self.in_y[i])

    def finish(self):
        for copy in [c for spot in self.near for c in spot] + self.corner + self.by_x + self.by_y:
            copy.wait_send()


def plane_corners():
    y, c, z, s = place()
    return [
        (y, 1 - c, s), (1 - y, c, s), (1 - y, 1 - c, s),
        (y, c, 1 - s), (y, 1 - c, 1 - s), (1 - y, c, 1 - s), (1 - y, 1 - c, 1 - s),
    ]


def line_ends(n_line):
    y, c, z, s = place()
    return (z > 0, (y, c, z - 1, s)), (z < n_line - 1, (y, c, z + 1, s)), (y, c, z, 1 - s)


class BlkGather:
    @staticmethod
    def sems(n_line):
        return [
            pltpu.SemaphoreType.DMA((3,)),
            pltpu.SemaphoreType.DMA((1,)),
            pltpu.SemaphoreType.DMA((4, n_line)),
            pltpu.SemaphoreType.DMA((4, n_line)),
            pltpu.SemaphoreType.DMA((1,)),
        ]

    def __init__(self, n_line, pick_x, pick_o, own_send, own_recv, send, recv, local):
        y, c, z, s = place()
        self.z, self.s, self.n = z, s, n_line
        (self.has_low, self.low), (self.has_high, self.high), self.cross = line_ends(n_line)
        self.pick_x, self.pick_o = pick_x, pick_o
        self.sem = (own_send, own_recv, send, recv, local)

    def block(self, way, k):
        z = self.z - k if way == 0 else self.z + k
        return self.pick_o(z * 2 + self.s)

    def own(self, way):
        own_send, own_recv, send, recv, local = self.sem
        arrival = own_recv.at[0] if way == 2 else recv.at[way, 0]
        target = (self.high, self.low, self.cross)[way]
        return remote(self.pick_x(), self.pick_o(self.z * 2 + self.s), own_send.at[way], arrival, target)

    def keep(self):
        return pltpu.make_async_copy(self.pick_x(), self.pick_o(self.z * 2 + self.s), self.sem[4].at[0])

    def onward(self, way, k):
        send, recv = self.sem[2:4]
        target = self.high if way == 0 else self.low
        return remote(self.block(way, k), self.block(way, k), send.at[way, k], recv.at[way, k], target)

    def over(self, way, k):
        send, recv = self.sem[2:4]
        return remote(self.block(way, k), self.block(way, k), send.at[2 + way, k], recv.at[2 + way, k], self.cross)

    def arrive(self, way, k):
        send, recv = self.sem[2:4]
        return remote(self.block(way, k), self.block(way, k), send.at[way, k], recv.at[way, k - 1], self.cross)

    def there(self, way, k):
        return self.z >= k if way == 0 else self.z + k < self.n

    def start(self):
        pl.when(self.has_high)(lambda: self.own(0).start())
        pl.when(self.has_low)(lambda: self.own(1).start())
        self.own(2).start()
        self.keep().start()

    def take(self, way, k):
        self.arrive(way, k).wait_recv()
        pl.when((self.has_high, self.has_low)[way])(lambda: self.onward(way, k).start())
        self.over(way, k).start()

    def step(self, k):
        for way in (0, 1):
            pl.when(self.there(way, k))(lambda: self.take(way, k))

    def finish_arrivals(self):
        self.own(2).wait_recv()
        for k in range(1, self.n):
            for way in (0, 1):
                pl.when(self.there(way, k))(lambda: self.over(way, k).wait_recv())
        self.keep().wait()

    def finish_sends(self):
        pl.when(self.has_high)(lambda: self.own(0).wait_send())
        pl.when(self.has_low)(lambda: self.own(1).wait_send())
        self.own(2).wait_send()
        for k in range(1, self.n):
            for way in (0, 1):
                @pl.when(self.there(way, k))
                def _():
                    self.over(way, k).wait_send()

                    @pl.when((self.has_high, self.has_low)[way])
                    def _():
                        self.onward(way, k).wait_send()


def blk_greet(n_line):
    low, high, cross = line_ends(n_line)
    greet([cross], [low, high])


class BlkReduce:
    @staticmethod
    def scratch(n_line, a):
        return [
            pltpu.VMEM((n_line,) + a.shape[1:], a.dtype),
            pltpu.VMEM((n_line + 1,) + a.shape[1:], a.dtype),
            pltpu.SemaphoreType.DMA((n_line,)),
            pltpu.SemaphoreType.DMA((n_line,)),
            pltpu.SemaphoreType.DMA((2, n_line)),
            pltpu.SemaphoreType.DMA((2, n_line)),
        ]

    def __init__(self, n_line, x, side_in, line_in, side_send, side_recv, send, recv):
        y, c, self.z, self.s = place()
        self.n = n_line
        (self.has_low, self.low), (self.has_high, self.high), self.cross = line_ends(n_line)
        self.x = x
        self.side_in, self.line_in = side_in, line_in
        self.sem = (side_send, side_recv, send, recv)

    def spot(self, way, k):
        return self.z + k * (1 - 2 * way)

    def exists(self, way, k):
        return (self.spot(way, k) >= 0) & (self.spot(way, k) < self.n)

    def toward(self, way):
        y, c, z, s = place()
        return (y, c, z + 1 - 2 * way, s)

    def side(self, zz):
        side_send, side_recv = self.sem[:2]
        return remote(
            self.x.at[zz * 2 + 1 - self.s], self.side_in.at[zz], side_send.at[zz], side_recv.at[zz], self.cross
        )

    def slot(self, way, k):
        return jnp.where((way == 1) & (k == 0), self.n, self.spot(way, k))

    def move(self, way, k):
        send, recv = self.sem[2:]
        zz = self.spot(way, k)
        there = jnp.where((way == 1) & (k == 1), self.n, zz)
        return remote(
            self.side_in.at[zz], self.line_in.at[there], send.at[way, k], recv.at[way, k - 1], self.toward(way)
        )

    def arrive(self, way, k):
        send, recv = self.sem[2:]
        there = self.line_in.at[self.slot(way, k)]
        return remote(there, there, send.at[way, k], recv.at[way, k], self.toward(1 - way))

    def start(self, k):
        for way in (0, 1) if k > 0 else (0,):
            pl.when(self.exists(way, k))(lambda: self.side(self.spot(way, k)).start())

    def move_on(self, way, k):
        zz = self.spot(way, k)
        self.side(zz).wait_recv()
        passed = jnp.where(way == 0, self.has_low, self.has_high)

        @pl.when(passed)
        def _():
            self.arrive(way, k).wait_recv()
            self.side_in[zz] = add_low(
                self.x[zz * 2 + self.s], self.side_in[zz], self.line_in[zz]
            ).astype(self.side_in.dtype)

        @pl.when(jnp.logical_not(passed))
        def _():
            self.side_in[zz] = add_low(self.x[zz * 2 + self.s], self.side_in[zz]).astype(
                self.side_in.dtype
            )

        self.move(way, k).start()

    def step(self, k):
        def one(way, carry):
            pl.when(self.exists(way, k))(lambda: self.move_on(way, k))
            return carry

        lax.fori_loop(0, 2, one, 0)

    def result(self, o):
        z = self.z
        self.side(z).wait_recv()
        pl.when(self.has_low)(lambda: self.arrive(0, 0).wait_recv())
        pl.when(self.has_high)(lambda: self.arrive(1, 0).wait_recv())
        own = lambda: add_low(self.x[z * 2 + self.s], self.side_in[z])
        both = self.has_low & self.has_high

        @pl.when(both)
        def _():
            o[...] = (own() + add_low(self.line_in[z], self.line_in[self.n])).astype(o.dtype)

        @pl.when(jnp.logical_not(both))
        def _():
            other = self.line_in[jnp.where(self.has_low, z, self.n)].astype(F32)
            o[...] = (own() + other).astype(o.dtype)

    def finish(self):
        for k in range(self.n - 1, -1, -1):
            for way in (0, 1) if k > 0 else (0,):
                @pl.when(self.exists(way, k))
                def _():
                    self.side(self.spot(way, k)).wait_send()
                    if k > 0:
                        self.move(way, k).wait_send()


class LineGather:
    @staticmethod
    def sems(n_line):
        dma = pltpu.SemaphoreType.DMA
        return [dma((2,)), dma((2, n_line)), dma((2, n_line)), dma((1,))]

    def __init__(self, n_line, pick_x, pick_o, own_send, send, recv, local):
        y, c, self.z, s = place()
        self.n = n_line
        (self.has_low, self.low), (self.has_high, self.high), _ = line_ends(n_line)
        self.pick_x, self.pick_o = pick_x, pick_o
        self.own_send, self.send, self.recv, self.local = own_send, send, recv, local

    def goes(self, way):
        return (self.has_high, self.has_low)[way]

    def own(self, way):
        target = (self.high, self.low)[way]
        return remote(self.pick_x(), self.pick_o(self.z), self.own_send.at[way], self.recv.at[way, 0], target)

    def keep(self):
        return pltpu.make_async_copy(self.pick_x(), self.pick_o(self.z), self.local.at[0])

    def onward(self, way, k):
        block = self.pick_o(self.z - k if way == 0 else self.z + k)
        target = (self.high, self.low)[way]
        return remote(block, block, self.send.at[way, k], self.recv.at[way, k], target)

    def arrive(self, way, k):
        block = self.pick_o(self.z - k if way == 0 else self.z + k)
        return remote(block, block, self.send.at[way, k], self.recv.at[way, k - 1], (self.low, self.high)[way])

    def there(self, way, k):
        return self.z >= k if way == 0 else self.z + k < self.n

    def start(self):
        for way in (0, 1):
            pl.when(self.goes(way))(lambda: self.own(way).start())
        self.keep().start()

    def step(self, k):
        for way in (0, 1):
            @pl.when(self.there(way, k))
            def _():
                self.arrive(way, k).wait_recv()
                pl.when(self.goes(way))(lambda: self.onward(way, k).start())

    def finish(self):
        self.keep().wait()
        for way in (0, 1):
            pl.when(self.goes(way))(lambda: self.own(way).wait_send())
            for k in range(1, self.n):
                pl.when(self.there(way, k) & self.goes(way))(lambda: self.onward(way, k).wait_send())


class LineReduce:
    @staticmethod
    def scratch(n_line, a):
        dma = pltpu.SemaphoreType.DMA
        return [
            pltpu.VMEM((n_line,) + a.shape[1:], a.dtype),
            pltpu.VMEM((n_line + 1,) + a.shape[1:], a.dtype),
            dma((2, n_line)), dma((2, n_line)),
        ]

    def __init__(self, n_line, x, sums, line_in, send, recv):
        y, c, self.z, s = place()
        self.n, self.x, self.sums, self.line_in, self.send, self.recv = n_line, x, sums, line_in, send, recv
        (self.has_low, self.low), (self.has_high, self.high), _ = line_ends(n_line)

    def spot(self, way, k):
        return self.z + k * (1 - 2 * way)

    def exists(self, way, k):
        return (self.spot(way, k) >= 0) & (self.spot(way, k) < self.n)

    def passed(self, way):
        return jnp.where(way == 0, self.has_low, self.has_high)

    def slot(self, way, k):
        return jnp.where((way == 1) & (k == 0), self.n, self.spot(way, k))

    def toward(self, way):
        y, c, z, s = place()
        return (y, c, z + 1 - 2 * way, s)

    def move(self, way, k, source):
        zz = self.spot(way, k)
        there = jnp.where((way == 1) & (k == 1), self.n, zz)
        return remote(
            source.at[zz], self.line_in.at[there], self.send.at[way, k], self.recv.at[way, k - 1], self.toward(way)
        )

    def arrive(self, way, k):
        there = self.line_in.at[self.slot(way, k)]
        return remote(there, there, self.send.at[way, k], self.recv.at[way, k], self.toward(1 - way))

    def step(self, k):
        def one(way, carry):
            exists, passed = self.exists(way, k), self.passed(way)

            @pl.when(exists & passed)
            def _():
                zz = self.spot(way, k)
                self.arrive(way, k).wait_recv()
                self.sums[zz] = add_low(self.x[zz], self.line_in[zz]).astype(self.sums.dtype)
                self.move(way, k, self.sums).start()

            pl.when(exists & jnp.logical_not(passed))(lambda: self.move(way, k, self.x).start())
            return carry

        lax.fori_loop(0, 2, one, 0)

    def result(self, o):
        z = self.z
        pl.when(self.has_low)(lambda: self.arrive(0, 0).wait_recv())
        pl.when(self.has_high)(lambda: self.arrive(1, 0).wait_recv())
        both = self.has_low & self.has_high

        @pl.when(both)
        def _():
            o[...] = add_low(self.x[z], self.line_in[z], self.line_in[self.n]).astype(o.dtype)

        @pl.when(jnp.logical_not(both))
        def _():
            o[...] = add_low(self.x[z], self.line_in[jnp.where(self.has_low, z, self.n)]).astype(o.dtype)

    def finish(self):
        for k in range(self.n - 1, 0, -1):
            for way in (0, 1):
                pl.when(self.exists(way, k))(lambda: self.move(way, k, self.sums).wait_send())


def lane_chunks(width):
    cut = width // 256 * 128
    return [slice(0, cut), slice(cut, width)]


LINE_CHUNKS = 2


def line_gathers(n_line, x, pick_o, sems):
    jobs = []
    for i, lanes in enumerate(lane_chunks(x.shape[-1])):
        cut = (slice(None),) * (len(x.shape) - 1) + (lanes,)
        jobs.append(
            LineGather(
                n_line, lambda cut=cut: x.at[cut], lambda z, cut=cut: pick_o(z).at[cut],
                *sems[4 * i : 4 * i + 4],
            )
        )
    return jobs


def line_gather_sems(n_line):
    return LineGather.sems(n_line) * LINE_CHUNKS


def line_reduces(n_line, x, scratch):
    jobs = []
    for i, lanes in enumerate(lane_chunks(x.shape[-1])):
        cut = (slice(None),) * (len(x.shape) - 1) + (lanes,)
        jobs.append((LineReduce(n_line, x.at[cut], *scratch[4 * i : 4 * i + 4]), cut[1:]))
    return jobs


def line_reduce_scratch(n_line, a):
    scratch = []
    for lanes in lane_chunks(a.shape[-1]):
        one = jax.ShapeDtypeStruct(a.shape[:-1] + (lanes.stop - lanes.start,), a.dtype)
        scratch += LineReduce.scratch(n_line, one)
    return scratch


def comm_call(
    kernel, name, collective_id, args, outs, scratch, micros, room=VMEM_BYTES, far_args=(), far_outs=(), late=()
):
    vmem, anyway = pl.BlockSpec(memory_space=pltpu.VMEM), pl.BlockSpec(memory_space=pl.ANY)
    held = [pltpu.VMEM(args[i].shape, args[i].dtype) for i in late]
    held += [pltpu.SemaphoreType.DMA((len(late),))] * (len(late) > 0)

    def whole(*refs):
        refs = list(refs)
        mine, copies = refs[len(refs) - len(held) :], []
        refs = refs[: len(refs) - len(held)]
        for j, i in enumerate(late):
            copies.append(pltpu.make_async_copy(refs[i], mine[j], mine[-1].at[j]))
            copies[-1].start()
            refs[i] = mine[j]

        def ready():
            for copy in copies:
                copy.wait()

        kernel(ready, *refs)

    return pl.pallas_call(
        whole,
        out_shape=[jax.ShapeDtypeStruct(shape, dtype) for shape, dtype in outs],
        in_specs=[anyway if i in far_args or i in late else vmem for i in range(len(args))],
        out_specs=[anyway if i in far_outs else vmem for i in range(len(outs))],
        scratch_shapes=list(scratch) + held,
        compiler_params=params(collective_id, room),
        cost_estimate=pl.CostEstimate(flops=0, bytes_accessed=micros * 3_000_000, transcendentals=0),
        name=name,
    )(*args)


def exit_kernel(
    n_line, ready, x, dq, dkv, yy_ref, cc_ref, cos, sin, scale, wq, wk, wv, res, oc, dc, a_sum, m_sum, ff_sum, gg,
    gq_o, gk_o, gv_o, gh_o, go_o, gd_o, sum_o, gg_o, oc_o, dc_o,
    flat, acc, gq, gk, gv, gh, scale_s, alpha,
    alpha_in, line_out, line_all, oc_s, oc_r, dc_s, dc_r, al_s, al_r, su_s, su_r, keep, *scratch,
):
    y, c, z, s = place()
    u, p, b, n_blk = y * 2 + c, plane_index(y, c, s), z * 2 + s, 2 * n_line
    low, high, cross = line_ends(n_line)
    corners = plane_corners()
    others = []
    for i in range(1, n_blk):
        to = lax.rem(b + i, n_blk)
        others.append((y, c, to // 2, lax.rem(to, 2)))
    once = [(to[3] != 1 - s) | (to[2] != z) for to in others]
    greet([(yy, cc, z, ss) for yy, cc, ss in corners], list(zip(once, others)))
    each = 6
    jobs = [BlkReduce(n_line, g, *scratch[each * i : each * (i + 1)]) for i, g in enumerate((gq, gk, gv))]
    split = each * 3 + len(UlyReduce.scratch(gh))
    hid = UlyReduce(gh, *scratch[each * 3 : split])
    gates = line_reduces(n_line, gg, scratch[split:])
    small, cols = [], []
    for k, (yy, cc, ss) in enumerate(corners):
        target = (yy, cc, z, ss)
        cols.append(remote(dc.at[plane_index(yy, cc, ss)], dc_o.at[p], dc_s.at[k], dc_r.at[k], target))
        if k < 3:
            cols.append(remote(oc.at[yy * 2 + cc], oc_o.at[u], oc_s.at[k], oc_r.at[k], target))
            small.append(remote(alpha.at[yy * 2 + cc], alpha_in.at[k], al_s.at[k], al_r.at[k], target))
    for job, _ in gates:
        job.step(n_line - 1)
    for job in cols:
        job.start()
    each_rows = gq.shape[1]
    for v in range(4):
        for k in range(n_blk):
            at = (v * n_blk + k) * each_rows
            alpha[v, k, :, :each_rows] = a_sum[:, at : at + each_rows]
            alpha[v, k, :, each_rows : 2 * each_rows] = m_sum[:, at : at + each_rows]
    for job in small:
        job.start()
    ready()
    rows_all = x[...]
    seqs, group_rows, wide = dq.shape
    heads = wide // 128
    factor = jnp.where(lanes_of((1, 128)) < HEAD_DIM, HEAD_DIM**0.5, 1.0)
    late_steps = [(min(1 + 2 * i, heads - 1), k) for i, k in enumerate(range(n_line - 2, 0, -1))]

    def head(h, carry):
        lanes = pl.ds(pl.multiple_of(h * 128, 128), 128)
        queries = jnp.concatenate([dq[i, :, lanes] for i in range(seqs)], axis=0)
        pairs = jnp.concatenate([dkv[i, :, lanes] for i in range(seqs)], axis=0)
        low_half = lanes_of(queries.shape) < HEAD_DIM
        dy = jnp.where(low_half, queries.astype(F32), pltpu.roll(pairs.astype(F32), HEAD_DIM, 1))
        unit = yy_ref[:, lanes]
        scale_s[h] = jnp.sum(dy * unit, axis=0, keepdims=True) * factor
        dy = dy * scale[pl.ds(h, 1)]
        dr = cc_ref[:, lanes] * (dy - unit * halves(unit * dy))
        raw = (dr * cos[...] - turn(dr) * sin[...]).astype(BF)
        both = jnp.concatenate([raw, jnp.where(low_half, jnp.zeros_like(pairs), pairs)], axis=1)
        grad = dot_tn(both, rows_all).astype(BF)
        at = pl.ds(pl.multiple_of(h * HEAD_DIM, HEAD_DIM), HEAD_DIM)
        for j, lo in enumerate((0, HEAD_DIM, 3 * HEAD_DIM)):
            flat[j, at] = grad[lo : lo + HEAD_DIM]
        w_value = wv[h]
        more = dot_nn(both, jnp.concatenate([wq[h], wk[h], jnp.zeros_like(w_value), w_value], axis=0))

        @pl.when(h == 0)
        def _():
            acc[...] = more

        @pl.when(h > 0)
        def _():
            acc[...] = acc[...] + more

        for when, k in late_steps:
            @pl.when(h == when)
            def _():
                for job, _ in gates:
                    job.step(k)

        return carry

    lax.fori_loop(0, heads, head, 0)
    for i, g in enumerate((gq, gk, gv)):
        for k in range(n_blk):
            g[k] = flat[i, k * each_rows : (k + 1) * each_rows]
    for i in range(seqs):
        gh[i] = acc[i * group_rows : (i + 1) * group_rows].astype(BF).reshape(gh.shape[1:])
    hid.start()
    for k in range(n_line - 1, -1, -1):
        for job in jobs:
            job.start(k)
    mine = [
        pltpu.make_async_copy(dc.at[p], dc_o.at[p], keep.at[0]),
        pltpu.make_async_copy(oc.at[u], oc_o.at[u], keep.at[1]),
    ]
    for job in mine:
        job.start()
    hid.middle()
    for job in small:
        job.wait_recv()
    line_out[...] = jnp.zeros_like(line_out)
    ff_each = ff_sum.shape[1] // n_line
    for k in range(n_line):
        for j in (0, 1):
            line_out[k * 2 + s, :, 256 + j * ff_each : 256 + (j + 1) * ff_each] = ff_sum[
                j : j + 1, k * ff_each : (k + 1) * ff_each
            ]
    line_out[:, :, :128] = alpha[u] + alpha_in[0] + alpha_in[1] + alpha_in[2]
    scales = jnp.concatenate(
        [scale_s[h][:, :HEAD_DIM] + scale_s[h][:, HEAD_DIM:] for h in range(heads)], axis=1
    )
    for k in range(n_blk):
        line_out[k, :, 128 : 128 + each_rows] = scales[:, k * each_rows : (k + 1) * each_rows]
    line_jobs = []
    for i in range(1, n_blk):
        to = lax.rem(b + i, n_blk)
        line_jobs.append(
            remote(line_out.at[to], line_all.at[i - 1], su_s.at[i - 1], su_r.at[i - 1], others[i - 1])
        )
    for job in line_jobs:
        job.start()
    for k in range(n_line - 1, 0, -1):
        for job in jobs:
            job.step(k)
    for i in range(gh.shape[0]):
        gh_o[i] = res[i] + hid.result(i)
    for job in cols:
        job.wait_recv()
    for job in mine:
        job.wait()
    wide, ff_each = oc.shape[-1], dc.shape[-1] // n_line
    for v in range(4):
        go_o[:, v * wide : (v + 1) * wide] = oc_o[v].astype(F32)
        for t in (0, 1):
            for k in range(n_line):
                at = ((v * n_line + k) * 2 + t) * ff_each
                gd_o[:, at : at + ff_each] = dc_o[v * 2 + t, :, k * ff_each : (k + 1) * ff_each].astype(F32)
    total = line_out[b]
    for i, job in enumerate(line_jobs):
        job.wait_recv()
        total = total + line_all[i]
    sum_o[...] = total
    for job, o in zip(jobs, (gq_o, gk_o, gv_o)):
        job.result(o)
    for job, cut in gates:
        job.result(gg_o.at[cut])
        job.finish()
    hid.finish()
    for job in jobs:
        job.finish()
    for job in line_jobs + small:
        job.wait_send()
    for job in cols:
        job.wait_send()


def leave(n_line, x, dq, dkv, y, c, cos, sin, scale, wq, wk, wv, res, oc, dc, a_sum, m_sum, ff_sum, gg):
    n_blk = 2 * n_line
    heads, _, width = wq.shape
    seqs, rows, _ = res.shape
    vmem = pl.BlockSpec(memory_space=pltpu.VMEM)
    dma = pltpu.SemaphoreType.DMA
    grad = jax.ShapeDtypeStruct((n_blk, heads * HEAD_DIM // n_blk, width), BF)
    gh = jax.ShapeDtypeStruct((seqs, 4, rows, width), BF)
    scratch = [
        pltpu.VMEM(oc.shape, oc.dtype),
        pltpu.VMEM(dc.shape, dc.dtype),
        pltpu.VMEM((3, heads * HEAD_DIM, width), BF),
        pltpu.VMEM(x.shape, F32),
        pltpu.VMEM(grad.shape, BF), pltpu.VMEM(grad.shape, BF), pltpu.VMEM(grad.shape, BF),
        pltpu.VMEM(gh.shape, BF),
        pltpu.VMEM((heads, 1, 128), F32),
        pltpu.VMEM((4, n_blk, 1, 128), F32),
        pltpu.VMEM((3, n_blk, 1, 128), F32),
        pltpu.VMEM((n_blk, 1, 640), F32),
        pltpu.VMEM((n_blk - 1, 1, 640), F32),
        dma((3,)), dma((3,)), dma((7,)), dma((7,)), dma((3,)), dma((3,)),
        dma((n_blk - 1,)), dma((n_blk - 1,)), dma((2,)),
    ]
    scratch += BlkReduce.scratch(n_line, grad) * 3
    scratch += UlyReduce.scratch(gh) + line_reduce_scratch(n_line, gg)
    args = (x, dq, dkv, y, c, cos, sin, scale, wq, wk, wv, res, oc, dc, a_sum, m_sum, ff_sum, gg)
    outs = [grad.shape[1:]] * 3 + [
        res.shape, (oc.shape[1], 4 * oc.shape[2]), (dc.shape[1], 8 * dc.shape[2]), (1, 640), gg.shape[1:]
    ]
    return comm_call(
        functools.partial(exit_kernel, n_line), "leave", 8, args, [(shape, F32) for shape in outs], scratch,
        60, late=tuple(range(11)),
    )


def tables(n_line, starts, sizes, small, places, cos, sin, scale, rates):
    y, c, z, s = place()
    u, b, n_blk = y * 2 + c, z * 2 + s, 2 * n_line
    seqs, rows_each = places.shape[0], places.shape[-1] // 4
    for v in range(4):
        for k in range(n_blk):
            row = small[v, k, starts[5] : starts[5] + 1]
            for i in range(seqs):
                places[i, k, :, v * rows_each : (v + 1) * rows_each] = row[:, i * rows_each : (i + 1) * rows_each]
    lane = lanes_of((1, 128)) % HEAD_DIM
    freqs = jnp.exp((lane % 32).astype(F32) * (-math.log(rotary_base) * 2.0 / HEAD_DIM))
    turns = jnp.where(lane < 32, -1.0, 1.0)
    for i in range(seqs):
        spot = places[i, b]
        group = spot.shape[1]
        angles = jnp.transpose(jnp.broadcast_to(spot, (128, group))) * freqs
        cos[i * group : (i + 1) * group] = jnp.cos(angles)
        sin[i * group : (i + 1) * group] = jnp.sin(angles) * turns
    each = sizes[0]
    flat = jnp.concatenate([small[u, k, 0:1, :each] for k in range(n_blk)], axis=1)
    scale[...] = jnp.zeros_like(scale)
    for h in range(flat.shape[1] // HEAD_DIM):
        piece = flat[:, h * HEAD_DIM : (h + 1) * HEAD_DIM]
        scale[h : h + 1] = jnp.concatenate([piece * HEAD_DIM**0.5, piece], axis=1)
    rates[...] = jnp.zeros_like(rates)
    for j in (1, 2):
        for v in range(4):
            for k in range(n_blk):
                at = (v * n_blk + k) * each
                rates[j - 1 : j, at : at + each] = small[v, k, starts[j] : starts[j] + 1, :each]
    for j in (3, 4):
        for k in range(n_line):
            for r in range(starts[j + 1] - starts[j]):
                wide = min(128, sizes[j] - 128 * r)
                at = k * sizes[j] + 128 * r
                rates[j - 1 : j, at : at + wide] = small[u, k * 2 + s, starts[j] + r : starts[j] + r + 1, :wide]


def entry_kernel(
    n_line, starts, sizes, hid, small, wq, wk, wv, wo, wd, wu,
    hid_o, places_o, cos_o, sin_o, scale_o, rates_o, wq_o, wk_o, wv_o, oc_o, dc_o, wu_o, small_o, oc, dc, *sems
):
    y, c, z, s = place()
    u, p = y * 2 + c, plane_index(y, c, s)
    low, high, cross = line_ends(n_line)
    corners = plane_corners()
    greet([(yy, cc, z, ss) for yy, cc, ss in corners], [low, high])
    hid_job = UlyGather(hid, hid_o, *sems[:3])
    at, jobs = 3, []
    for x, pick in (
        (small, lambda block: small_o.at[u, block]),
        (wq, lambda block: wq_o.at[block]),
        (wk, lambda block: wk_o.at[block]),
        (wv, lambda block: wv_o.at[block]),
    ):
        jobs.append(BlkGather(n_line, lambda x=x: x, pick, *sems[at : at + 5]))
        at += 5
    first = wu_o.shape[-1]
    up_jobs = [
        LineGather(n_line, lambda: wu.at[:, slice(0, first)], lambda z: wu_o.at[z], *sems[at : at + 4])
    ]
    oc_s, oc_r, dc_s, dc_r, sm_s, sm_r, keep = sems[at + 4 :]
    jobs[0].start()
    for job in jobs[1:]:
        job.start()
    hid_job.start()
    for v in range(4):
        wide = oc.shape[-1]
        oc[v] = wo[:, v * wide : (v + 1) * wide]
        ff_each = dc.shape[-1] // n_line
        for t in (0, 1):
            for k in range(n_line):
                at = ((v * n_line + k) * 2 + t) * ff_each
                dc[v * 2 + t, :, k * ff_each : (k + 1) * ff_each] = wd[:, at : at + ff_each]
    col_jobs = []
    for k, (yy, cc, ss) in enumerate(corners):
        target = (yy, cc, z, ss)
        col_jobs.append(
            remote(dc.at[plane_index(yy, cc, ss)], dc_o.at[p], dc_s.at[k], dc_r.at[k], target)
        )
        if k < 3:
            col_jobs.append(remote(oc.at[yy * 2 + cc], oc_o.at[u], oc_s.at[k], oc_r.at[k], target))
    for job in col_jobs:
        job.start()
    for job in up_jobs:
        job.start()
    mine = [
        pltpu.make_async_copy(dc.at[p], dc_o.at[p], keep.at[0]),
        pltpu.make_async_copy(oc.at[u], oc_o.at[u], keep.at[1]),
    ]
    for job in mine:
        job.start()
    for k in range(1, n_line):
        for job in jobs:
            job.step(k)
        if k == 1:
            hid_job.forward()
    jobs[0].finish_arrivals()
    small_jobs = [
        remote(small_o.at[u], small_o.at[u], sm_s.at[k], sm_r.at[k], (yy, cc, z, ss))
        for k, (yy, cc, ss) in enumerate(corners[:3])
    ]
    for job in small_jobs:
        job.start()
    for k in range(1, n_line):
        for job in up_jobs:
            job.step(k)
    for job in small_jobs:
        job.wait_recv()
    tables(n_line, starts, sizes, small_o, places_o, cos_o, sin_o, scale_o, rates_o)
    for job in jobs[1:]:
        job.finish_arrivals()
    hid_job.finish()
    for job in up_jobs:
        job.finish()
    for job in small_jobs:
        job.wait_send()
    for job in col_jobs:
        job.wait()
    for job in mine:
        job.wait()
    for job in jobs:
        job.finish_sends()


def entry(n_line, starts, sizes, hid, small, wq, wk, wv, wo, wd, wu):
    n_blk = 2 * n_line
    oc = jax.ShapeDtypeStruct((4, wo.shape[0], wo.shape[1] // 4), wo.dtype)
    dc = jax.ShapeDtypeStruct((8, wd.shape[0], wd.shape[1] // 8), wd.dtype)
    parts = hid.shape[0]
    vmem, anyway = pl.BlockSpec(memory_space=pltpu.VMEM), pl.BlockSpec(memory_space=pl.ANY)

    def out(shape, like):
        return jax.ShapeDtypeStruct(shape, like.dtype)

    return pl.pallas_call(
        functools.partial(entry_kernel, n_line, starts, sizes),
        out_shape=[
            out((parts, 4) + hid.shape[1:], hid),
            out((parts, n_blk, 1, 4 * hid.shape[1]), small),
            out((parts * 4 * hid.shape[1], 128), small),
            out((parts * 4 * hid.shape[1], 128), small),
            out((8, 128), small),
            out((8, hid.shape[2]), small),
            out((n_blk,) + wq.shape, wq),
            out((n_blk,) + wk.shape, wk),
            out((n_blk,) + wv.shape, wv),
            out(oc.shape, oc),
            out(dc.shape, dc),
            out((n_line, wu.shape[0], lane_chunks(wu.shape[1])[0].stop), wu),
        ],
        in_specs=[vmem] * 8,
        out_specs=[vmem] * 6 + [anyway, anyway, anyway, vmem, vmem, anyway],
        scratch_shapes=[
            pltpu.VMEM((4, n_blk) + small.shape, small.dtype),
            pltpu.VMEM(oc.shape, oc.dtype),
            pltpu.VMEM(dc.shape, dc.dtype),
        ]
        + UlyGather.sems(parts)
        + BlkGather.sems(n_line) * 4
        + LineGather.sems(n_line)
        + [pltpu.SemaphoreType.DMA((3,))] * 2
        + [pltpu.SemaphoreType.DMA((7,))] * 2
        + [pltpu.SemaphoreType.DMA((3,))] * 2
        + [pltpu.SemaphoreType.DMA((2,))],
        compiler_params=params(6),
        cost_estimate=pl.CostEstimate(flops=0, bytes_accessed=40 * 3_000_000, transcendentals=0),
        name="entry",
    )(hid, small, wq, wk, wv, wo, wd, wu)
def dot_nt(a, b):
    return lax.dot_general(a, b, (((1,), (1,)), ((), ())), preferred_element_type=F32)


def dot_nn(a, b):
    return lax.dot_general(a, b, (((1,), (0,)), ((), ())), preferred_element_type=F32)


def dot_tn(a, b):
    return lax.dot_general(a, b, (((0,), (0,)), ((), ())), preferred_element_type=F32)


def lanes_of(shape):
    return lax.broadcasted_iota(jnp.int32, shape, len(shape) - 1)


def halves(x):
    row = lax.broadcasted_iota(jnp.int32, (128, 128), 0) // HEAD_DIM
    same = jnp.where(row == lanes_of((128, 128)) // HEAD_DIM, 1.0, 0.0).astype(BF)
    high = x.astype(BF)
    rest = (x - high.astype(F32)).astype(BF)
    return dot_nn(high, same) + dot_nn(rest, same)


def turn(x):
    first = lanes_of(x.shape) % HEAD_DIM < HEAD_DIM // 2
    return jnp.where(first, pltpu.roll(x, 128 - 32, 1), pltpu.roll(x, 32, 1))


def down_columns(row):
    n = row.shape[1]
    one = jnp.transpose(jnp.broadcast_to(row, (128, n)))
    return jnp.concatenate([one] * (n // 128), axis=1)


def arrivals(n_line, body):
    each = 2 * n_line - 1

    def step(t, carry):
        stage, r = t // each, lax.rem(t, each)
        body(stage, (r + 1) // 2, lax.rem(r + 1, 2))
        return carry

    lax.fori_loop(0, 2 * each, step, 0)


def attend_kernel(
    n_line, ready, x_ref, wq_ref, wk_ref, wv_ref, cos_ref, sin_ref, scale_ref, oc_ref, wg_ref, wu_ref, kp_ref,
    q_h, y_h, c_h, kv_h, oc_o, wg_o, wu_o, o_ref, mixed_ref, inv_ref,
    kv_ref, acc, total, place_q, q_ref, y_ref, c_ref, kv_o, kept, *sems,
):
    y, c, z, s = place()
    blk_greet(n_line)
    seqs, rows, wide = q_ref.shape
    heads = wide // 128
    chunk = 4 * LINE_CHUNKS
    cut = wu_ref.shape[-1] - wu_o.shape[-1]
    up = LineGather(
        n_line, lambda: wu_ref.at[:, slice(cut, wu_ref.shape[-1])], lambda zz: wu_o.at[zz], *sems[-4:]
    )
    up.start()
    ready()

    each = len(BlkGather.sems(n_line))
    picks = [
        (lambda i=i: kv_ref.at[i], lambda block, i=i: kv_o.at[block, i]) for i in range(seqs)
    ] + [(lambda: oc_ref, lambda block: oc_o.at[:, block])]
    jobs = [
        BlkGather(n_line, *pick, *sems[each * i : each * (i + 1)]) for i, pick in enumerate(picks)
    ]

    def make(t, carry):
        i, h = t // heads, lax.rem(t, heads)
        lanes = pl.ds(pl.multiple_of(h * 128, 128), 128)
        mine = pl.ds(pl.multiple_of(i * rows, rows), rows)
        wv = wv_ref[h]
        got = dot_nt(x_ref[mine], jnp.concatenate([wq_ref[h], wk_ref[h], jnp.zeros_like(wv), wv], axis=0))
        raw, value = got[:, :128], got[:, 128:]
        low = lanes_of(raw.shape) < HEAD_DIM
        turned = raw * cos_ref[mine] + turn(raw) * sin_ref[mine]
        norm = lax.rsqrt(halves(turned * turned) + HEAD_DIM * tiny_eps)
        unit = turned * norm
        both = unit * scale_ref[pl.ds(h, 1)]
        q_ref[i, :, lanes] = jnp.where(low, both, 0.0).astype(BF)
        kv_ref[i, :, lanes] = jnp.where(low, pltpu.roll(both, HEAD_DIM, 1), value).astype(BF)
        y_ref[mine, lanes] = unit
        c_ref[mine, lanes] = norm
        for j in range(seqs):
            pl.when(t == heads * (j + 1) - 1)(jobs[j].start)
        return carry

    lax.fori_loop(0, seqs * heads, make, 0)
    gates = line_gathers(
        n_line, wg_ref, lambda z: wg_o.at[z], sems[each * (seqs + 1) : each * (seqs + 1) + chunk]
    )
    jobs[-1].start()
    for job in gates:
        job.keep().start()
    n_blk = 2 * n_line
    keeps = [
        pltpu.make_async_copy(a, o, kept.at[n_blk + i])
        for i, (a, o) in enumerate(((q_ref, q_h), (y_ref, y_h), (c_ref, c_h)))
    ]
    for copy in keeps:
        copy.start()

    def keep_keys(block):
        return pltpu.make_async_copy(kv_o.at[block], kv_h.at[block], kept.at[block])

    acc[...] = jnp.zeros_like(acc)
    total[...] = jnp.zeros_like(total)
    for i in range(seqs):
        place_q[i] = down_columns(kp_ref[i, z * 2 + s])

    def attend_to(i, block, keys):
        allowed = kp_ref[i, block] <= place_q[i]
        for h in range(heads):
            lanes = slice(h * 128, (h + 1) * 128)
            kv = keys(lanes)
            p = jnp.where(allowed, jnp.exp(dot_nt(q_ref[i, :, lanes], kv)), 0.0)
            part = p[:, :128]
            for j in range(1, rows // 128):
                part = part + p[:, j * 128 : (j + 1) * 128]
            total[i, h] = total[i, h] + part
            acc[i, h] = acc[i, h] + dot_nn(p.astype(BF), kv)

    def body(stage, k, way):
        ahead = jnp.where(k == 0, 1, k + 1)

        @pl.when((stage == 1) & ((k == 0) | (way == 1)) & (ahead < n_line))
        def _():
            for job in gates + [up]:
                job.step(ahead)

        @pl.when((stage == 0) & (k > 0) & (way == 0))
        def _():
            for job in jobs:
                job.step(k)

        for w, last in ((0, z), (1, n_line - 1 - z)):
            @pl.when((stage == 0) & (k == last) & ((k == 0) | (way == 0)))
            def _():
                for job in gates:
                    pl.when(job.goes(w))(lambda: job.own(w).start())

        there = (k == 0) | jnp.where(way == 0, z >= k, z + k < n_line)

        @pl.when(there)
        def _():
            for job in jobs:
                for w in (0, 1):
                    pl.when((stage == 1) & (k > 0) & (way == w))(lambda: job.over(w, k).wait_recv())
                pl.when((stage == 1) & (k == 0))(lambda: job.own(2).wait_recv())
                pl.when((stage == 0) & (k == 0))(lambda: job.keep().wait())
            zz = jnp.where(way == 0, z - k, z + k)
            block = zz * 2 + jnp.where(stage == 0, s, 1 - s)
            keep_keys(block).start()

            def one(i, carry):
                attend_to(i, block, lambda lanes: kv_o[block, i, :, lanes])
                return carry

            lax.fori_loop(0, seqs, one, 0)

    arrivals(n_line, body)
    low = lanes_of((rows, 128)) < HEAD_DIM
    for i in range(seqs):
        outs = []
        for h in range(heads):
            inverse = 1.0 / jnp.broadcast_to(jnp.sum(total[i, h], axis=-1, keepdims=True), (rows, 128))
            out = acc[i, h] * inverse
            o_ref[i, h] = out
            inv_ref[i, h] = jnp.transpose(inverse)[:8]
            outs.append(out)
        for h in range(0, heads - 1, 2):
            mixed_ref[i, :, h * HEAD_DIM : (h + 2) * HEAD_DIM] = jnp.where(
                low, pltpu.roll(outs[h], HEAD_DIM, 1), outs[h + 1]
            ).astype(BF)
        if heads % 2 == 1:
            mixed_ref[i, :, (heads - 1) * HEAD_DIM :] = pltpu.roll(outs[-1], HEAD_DIM, 1)[:, :HEAD_DIM].astype(BF)
    for job in jobs:
        job.finish_sends()
    for job in gates + [up]:
        job.finish()
    for copy in keeps + [keep_keys(block) for block in range(n_blk)]:
        copy.wait()


def attend(n_line, seqs, x, wq, wk, wv, cos, sin, scale, oc, wg, wu, k_places):
    tokens, width = x.shape
    n_blk, heads, rows = 2 * n_line, wq.shape[0], tokens // seqs
    head, wide = (seqs, heads, rows, 128), (seqs, rows, heads * 128)
    flat = ((tokens, heads * 128), F32)
    first = lane_chunks(width)[0].stop
    return comm_call(
        functools.partial(attend_kernel, n_line), "attend", 5,
        (x, wq, wk, wv, cos, sin, scale, oc, wg, wu, k_places),
        [
            (wide, BF), flat, flat, ((n_blk,) + wide, BF), (oc.shape[:1] + (n_blk,) + oc.shape[1:], BF),
            ((n_line,) + wg.shape, BF), ((n_line, wu.shape[0], width - first), BF), (head, F32),
            ((seqs, rows, heads * HEAD_DIM), BF), ((seqs, heads, 8, rows), F32),
        ],
        [
            pltpu.VMEM(wide, BF), pltpu.VMEM(head, F32), pltpu.VMEM(head, F32), pltpu.VMEM((seqs, rows, rows), F32),
            pltpu.VMEM(wide, BF), pltpu.VMEM(*flat), pltpu.VMEM(*flat), pltpu.VMEM((n_blk,) + wide, BF),
            pltpu.SemaphoreType.DMA((n_blk + 3,)),
        ]
        + BlkGather.sems(n_line) * (seqs + 1) + line_gather_sems(n_line) + LineGather.sems(n_line),
        90, far_outs=(0, 1, 2, 3, 4, 5, 6), late=(0, 1, 2, 3, 4, 5),
    )


def attend_back_kernel(
    n_line, fits, ready, q_ref, low_ref, w_ref, mixed_ref, o_ref, inv_ref, kv_ref, kp_ref, gu_ref,
    dq_ref, dkv_ref, oc_ref, gu_o, dz, delta, dq, parts, oparts, key_s, key_sem, *scratch,
):
    y, c, z, s = place()
    blk_greet(n_line)
    seqs, rows, wide = q_ref.shape
    heads, width = wide // 128, low_ref.shape[-1]
    each = 6
    ups = line_reduces(n_line, gu_ref, scratch[each * (seqs + 1) :])
    for line_job, _ in ups:
        line_job.step(n_line - 1)
    ready()
    low_rows = low_ref[...].reshape(seqs * rows, width)
    grad = dot_tn(low_rows, mixed_ref[...].reshape(seqs * rows, mixed_ref.shape[-1])).astype(BF)
    n_blk, each_out = 2 * n_line, width // (8 * n_line)
    for b in range(n_blk):
        for v in range(4):
            at = (v * n_blk + b) * each_out
            oparts[b, v * each_out : (v + 1) * each_out] = grad[at : at + each_out]
    each = 6
    jobs = [BlkReduce(n_line, parts.at[:, i], *scratch[each * i : each * (i + 1)]) for i in range(seqs)]
    out_job = BlkReduce(n_line, oparts, *scratch[each * seqs : each * (seqs + 1)])
    for k in range(n_line - 1, -1, -1):
        out_job.start(k)
    low = lanes_of((rows, 128)) < HEAD_DIM
    for i in range(seqs):
        d = dot_nn(low_rows[i * rows : (i + 1) * rows], w_ref[...]).astype(BF).astype(F32)
        for h in range(heads):
            at = h // 2 * 128
            if h == heads - 1 and heads % 2 == 1:
                tile = jnp.concatenate([jnp.zeros((rows, HEAD_DIM), F32), d[:, at:]], axis=1)
            else:
                tile = d[:, at : at + 128]
                if h % 2 == 0:
                    tile = pltpu.roll(tile, HEAD_DIM, 1)
                tile = jnp.where(low, 0.0, tile)
            dz[i, h] = tile.astype(BF)
            row = jnp.sum(tile * o_ref[i, h], axis=-1, keepdims=True)
            delta[i, h] = jnp.transpose(jnp.broadcast_to(row, (rows, 128)))[:8]
    dq[...] = jnp.zeros_like(dq)

    def block_of(block):
        if fits:
            keys = kv_ref.at[block]
        else:
            keys = key_s
            copy = pltpu.make_async_copy(kv_ref.at[block], key_s, key_sem.at[0])
            copy.start()
            copy.wait()
        def one(i, carry):
            allowed = down_columns(kp_ref[i, block]) <= kp_ref[i, z * 2 + s]
            for h in range(heads):
                lanes = slice(h * 128, (h + 1) * 128)
                kv = keys[i, :, lanes]
                pair = jnp.concatenate([q_ref[i, :, lanes], dz[i, h]], axis=0)
                scores = dot_nt(kv, pair)
                p = jnp.where(allowed, jnp.exp(scores[:, :rows]) * inv_ref[i, h][:1], 0.0)
                ds = (p * (scores[:, rows:] - delta[i, h][:1])).astype(BF)
                parts[block, i, :, lanes] = dot_nn(
                    jnp.concatenate([ds, p.astype(BF)], axis=1), pair
                ).astype(BF)
                dq[i, h] = dq[i, h] + dot_tn(ds, kv)
            return carry

        lax.fori_loop(0, seqs, one, 0)

    def step(t, carry):
        k, r = n_line - 1 - t // 4, lax.rem(t, 4)
        way, stays = r // 2, lax.rem(r, 2)

        @pl.when((r == 0) & (k > 0) & (k < n_line - 1))
        def _():
            for line_job, _ in ups:
                line_job.step(k)

        there = jnp.where(k == 0, way == 0, jnp.where(way == 0, z + k < n_line, z >= k))

        @pl.when(there)
        def _():
            zz = jnp.where(way == 0, z + k, z - k)
            block_of(zz * 2 + jnp.where(stays == 0, 1 - s, s))

            @pl.when(stays == 0)
            def _():
                for job in jobs:
                    job.side(zz).start()

        @pl.when((r == 3) & (k + 1 < n_line))
        def _():
            for w in (0, 1):
                @pl.when(jobs[0].exists(w, k + 1))
                def _():
                    for job in jobs + [out_job]:
                        job.move_on(w, k + 1)

        return carry

    lax.fori_loop(0, 4 * n_line, step, 0)
    for i in range(seqs):
        for h in range(heads):
            dq_ref[i, :, h * 128 : (h + 1) * 128] = dq[i, h].astype(BF)
    out_job.result(oc_ref)
    for i, job in enumerate(jobs):
        job.result(dkv_ref.at[i])
    for job, cut in ups:
        job.result(gu_o.at[cut])
    for job in jobs + [out_job] + [job for job, _ in ups]:
        job.finish()


def attend_back(n_line, q, low, w, mixed, o, inv, kv, k_places, gu):
    seqs, rows, wide = q.shape
    n_blk, heads = 2 * n_line, wide // 128
    head = (seqs, heads, rows, 128)
    width, columns = w.shape
    out_shape = (width // n_blk, columns)
    one = jax.ShapeDtypeStruct((n_blk,) + kv.shape[2:], BF)
    out_one = jax.ShapeDtypeStruct((n_blk,) + out_shape, BF)
    fits = kv.size * 2 <= 8_000_000
    return comm_call(
        functools.partial(attend_back_kernel, n_line, fits), "attend_back", 7,
        (q, low, w, mixed, o, inv, kv, k_places, gu),
        [(q.shape, BF), (kv.shape[1:], BF), (out_shape, BF), (gu.shape[1:], F32)],
        [
            pltpu.VMEM(head, BF), pltpu.VMEM((seqs, heads, 8, rows), F32), pltpu.VMEM(head, F32),
            pltpu.VMEM(kv.shape, BF), pltpu.VMEM(out_one.shape, BF),
            pltpu.VMEM((16, 128) if fits else kv.shape[1:], BF), pltpu.SemaphoreType.DMA((1,)),
        ]
        + BlkReduce.scratch(n_line, one) * seqs + BlkReduce.scratch(n_line, out_one)
        + line_reduce_scratch(n_line, gu),
        75, 67_000_000, () if fits else (6,), late=(0, 1, 2, 3, 4) + (6,) * fits,
    )


def unit_of(x):
    c = lax.rsqrt(jnp.sum(x * x, axis=-1, keepdims=True) + x.shape[-1] * tiny_eps)
    return x * c, c


def unit_back(y, c, dy):
    return c * (dy - y * jnp.sum(y * dy, axis=-1, keepdims=True))


class Late:
    @staticmethod
    def scratch(arrays):
        return [pltpu.VMEM(a.shape, a.dtype) for a in arrays] + [pltpu.SemaphoreType.DMA((len(arrays),))]

    def __init__(self, refs, scratch):
        *self.bufs, sem = scratch
        self.copies = [
            pltpu.make_async_copy(ref, buf, sem.at[i]) for i, (ref, buf) in enumerate(zip(refs, self.bufs))
        ]
        for copy in self.copies:
            copy.start()

    def __call__(self, i):
        self.copies[i].wait()
        return self.bufs[i]


def attn_joint_kernel(
    n_line, ready, mixed, w, hid, rate, dc, first_o, ua_o, ca_o, cv_o, all_o, down_o, part, low, *scratch
):
    ends = line_ends(n_line)
    greet(plane_peers(), ends[:2])
    ready()
    split = len(UlyReduce.scratch(part))
    job = UlyReduce(part, *scratch[:split])
    out = PlaneGather(low, all_o, *scratch[split : split + 3])
    downs = line_gathers(n_line, dc, lambda z: down_o.at[:, z], scratch[split + 3 :])
    for line_job in downs:
        line_job.start()
    steps = [(k, line_job) for k in range(1, n_line) for line_job in downs]
    parts, _, rows, width = part.shape
    seqs = mixed.shape[0]
    each = parts // seqs
    for i in range(seqs):
        got = dot_nt(mixed[i], w[...]).astype(BF)
        for k in range(each):
            for u in range(4):
                at = (u * each + k) * rows
                part[i * each + k, u] = got[at : at + rows]
            for copy in job.near[i * each + k]:
                copy.start()
    job.middle()
    k, line_job = steps.pop(0)
    line_job.step(k)
    for i in range(parts):
        ua, ca = unit_of(job.result(i))
        h = hid[i].astype(F32)
        first, cv = unit_of(h + rate[0:1] * (ua - h))
        low[i] = first.astype(BF)
        out.start_part(i)
        first_o[i], ua_o[i] = first, ua
        ca_o[i] = jnp.broadcast_to(ca, (rows, 128))
        cv_o[i] = jnp.broadcast_to(cv, (rows, 128))
        if i > 0:
            out.forward_part(i - 1)
        if len(steps) > 0:
            k, line_job = steps.pop(0)
            line_job.step(k)
    out.forward_part(parts - 1)
    for k, line_job in steps:
        line_job.step(k)
    out.finish()
    job.finish()
    for line_job in downs:
        line_job.finish()


def attn_joint(n_line, mixed, w, hid, rate, dc):
    parts, rows, width = hid.shape
    part = jax.ShapeDtypeStruct((parts, 4, rows, width), BF)
    thin = ((parts, rows, 128), F32)
    return comm_call(
        functools.partial(attn_joint_kernel, n_line), "attn_joint", 1, (mixed, w, hid, rate, dc),
        [
            (hid.shape, F32), (hid.shape, F32), thin, thin, ((8, parts, rows, width), BF),
            (dc.shape[:1] + (n_line,) + dc.shape[1:], BF),
        ],
        [pltpu.VMEM(part.shape, BF), pltpu.VMEM(hid.shape, BF)]
        + UlyReduce.scratch(part) + PlaneGather.sems(parts) + line_gather_sems(n_line),
        25, far_outs=(4, 5), late=(0, 1, 2, 4),
    )


def plane_products(job, part, y, c, prepare, product):
    _, parts, rows, width = part.shape
    for yy, spots in ((1 - y, (0, 2)), (y, (1, 3))):
        def one(j, carry):
            cc = jnp.where(j == 0, 1 - c, c)
            prepare(yy, cc)
            got = product(yy, cc).astype(BF).reshape(2, parts, rows, width)
            for ss in (0, 1):
                part[plane_index(yy, cc, ss)] = got[ss]

            @pl.when(j == 0)
            def _():
                for k in spots:
                    for copy in job.near[k]:
                        copy.start()

            return carry

        lax.fori_loop(0, 2, one, 0)
        job.middle(spots[0] == 0)


def ff_joint_kernel(
    ready, x, wu, wu2, wg, rate, w, first, cot, out_o, d1_o, sum_o, all_o, inner_h, up_h, gate_h,
    part, low, inner, up_s, gate_s, kept, *scratch,
):
    y, c, z, s = place()
    greet(plane_peers())
    split = len(PlaneReduce.scratch(part))
    job = PlaneReduce(part, *scratch[:split])
    out = PlaneGather(low, all_o, *scratch[split:])
    _, seqs, rows, width = part.shape
    columns, tokens = inner.shape[-1], 2 * seqs * rows
    cut = wu.shape[1]

    def forward(yy, cc):
        block = x[yy, cc].reshape(tokens, width)
        up = dot_nt(block[:, :cut], wu[...]) + dot_nt(block[:, cut:], wu2[...])
        gate = dot_nt(block, wg[...])
        gz = gate * rate[3:4, :columns] * D**0.5
        got = gz / (1.0 + jnp.exp(-gz)) * (up * rate[2:3, :columns])
        inner[yy, cc] = got.astype(BF).reshape(inner.shape[2:])
        up_s[yy, cc] = up.reshape(up_s.shape[2:])
        gate_s[yy, cc] = gate.reshape(gate_s.shape[2:])

    ready()
    plane_products(
        job, part, y, c, forward, lambda yy, cc: dot_nt(inner[yy, cc].reshape(tokens, columns), w[...])
    )
    keeps = [
        pltpu.make_async_copy(a, o, kept.at[i])
        for i, (a, o) in enumerate(((inner, inner_h), (up_s, up_h), (gate_s, gate_h)))
    ]
    for copy in keeps:
        copy.start()
    job.last()
    for i in range(seqs):
        ub, cb = unit_of(job.result(i))
        f, b = first[i], rate[1:2]
        o, cw = unit_of(f + b * (ub - f))
        dw = unit_back(o, cw, cot[i].astype(F32))
        step = b * dw
        low[i] = unit_back(ub, cb, step).astype(BF)
        out.start_part(i)
        out_o[i] = o.astype(BF)
        d1_o[i] = dw - step
        total = jnp.sum(dw * (ub - f), axis=0, keepdims=True)
        sum_o[...] = total if i == 0 else sum_o[...] + total
        if i > 0:
            out.forward_part(i - 1)
    out.forward_part(seqs - 1)
    out.finish()
    job.finish()
    for copy in keeps:
        copy.wait()


def ff_joint(x, wu, wu2, wg, rate, w, first, cot):
    seqs, rows, width = first.shape
    part = jax.ShapeDtypeStruct((8, seqs, rows, width), BF)
    columns = wg.shape[0]
    wide = (2, 2, 2, seqs * rows, columns)
    return comm_call(
        ff_joint_kernel, "ff_joint", 2,
        (x.reshape(wide[:4] + (width,)), wu, wu2, wg, rate, w, first, cot),
        [
            (first.shape, BF), (first.shape, F32), ((1, width), F32), (part.shape, BF),
            (wide, BF), (wide, F32), (wide, F32),
        ],
        [
            pltpu.VMEM(part.shape, BF), pltpu.VMEM(first.shape, BF), pltpu.VMEM(wide, BF),
            pltpu.VMEM(wide, F32), pltpu.VMEM(wide, F32), pltpu.SemaphoreType.DMA((3,)),
        ]
        + PlaneReduce.scratch(part) + PlaneGather.sems(seqs),
        35, far_outs=(3, 4, 5, 6), late=(0, 1, 2, 3, 5),
    )


def back_joint_kernel(
    n_line, ready, d, inner, rate, d1, first, ua, ca, cv, hid, wd_h, up_h, gate_h, wu_h, wu2_h, wg_h, x_h,
    res_o, sum_o, ff_sum_o, all_o, up_o, gate_o, down_o, part, low, down_s, du, dg, *scratch,
):
    y, c, z, s = place()
    late = Late((wd_h, up_h, gate_h, wu_h, wu2_h, wg_h, x_h), scratch[:8])
    scratch = scratch[8:]
    greet(plane_peers(), line_ends(n_line)[:2])
    ready()
    split = len(PlaneReduce.scratch(part))
    job = PlaneReduce(part, *scratch[:split])
    _, parts, rows, width = part.shape
    columns = du.shape[-1]
    tokens = 8 * parts * rows
    each = parts // all_o.shape[0]
    out = UlyGather(
        low, all_o, *scratch[split : split + 3],
        pick=lambda i, u: all_o.at[i // each, u, pl.ds(i % each * rows, rows)],
    )
    downs = line_reduces(n_line, down_s, scratch[split + 3 :])
    flat = lambda ref: ref[...].reshape(tokens, ref.shape[-1])

    deep = width // (4 * n_line)
    inner_all = flat(inner)

    def down_half(i, carry):
        lanes = pl.ds(pl.multiple_of(i * (width // 2), 128), width // 2)
        grad = dot_tn(d[:, :, :, :, lanes].reshape(tokens, width // 2), inner_all).astype(BF)
        for v in (0, 1):
            for k in range(n_line):
                at = (v * n_line + k) * deep
                down_s[k, 2 * i + v] = grad[at : at + deep]
        return carry

    lax.fori_loop(0, 2, down_half, 0)
    for line_job, _ in downs:
        line_job.step(n_line - 1)

    wd, up_ref, gate_ref = late(0), late(1), late(2)
    u_scale, g_scale = rate[2:3, :columns], rate[3:4, :columns] * D**0.5

    ff_sum_o[...] = jnp.zeros_like(ff_sum_o)

    def gated_back(yy, cc):
        got = dot_nn(d[yy, cc].reshape(tokens // 4, width), wd[...])
        up, gate = up_ref[yy, cc].reshape(got.shape), gate_ref[yy, cc].reshape(got.shape)
        gz = gate * g_scale
        sig = 1.0 / (1.0 + jnp.exp(-gz))
        d_up = got * (gz * sig)
        d_gate = got * (up * u_scale) * sig * (1.0 + gz * (1.0 - sig))
        du[yy, cc] = (d_up * u_scale).astype(BF).reshape(du.shape[2:])
        dg[yy, cc] = (d_gate * g_scale).astype(BF).reshape(dg.shape[2:])
        ff_sum_o[0:1] = ff_sum_o[0:1] + jnp.sum(d_up * up, axis=0, keepdims=True)
        ff_sum_o[1:2] = ff_sum_o[1:2] + jnp.sum(d_gate * gate, axis=0, keepdims=True) * D**0.5

    wu, wu2, wg = late(3), late(4), late(5)

    def product(yy, cc):
        u, g = du[yy, cc].reshape(tokens // 4, columns), dg[yy, cc].reshape(tokens // 4, columns)
        got = jnp.concatenate([dot_nn(u, wu[...]), dot_nn(u, wu2[...])], axis=1)
        return got + dot_nn(g, wg[...])

    plane_products(job, part, y, c, gated_back, product)
    steps = [(k, line_job) for k in range(n_line - 2, 0, -1) for line_job, _ in downs]
    job.last()
    x = late(6)

    def by_line(o, ref):
        n, rows_all = columns // n_line, flat(ref)

        def half(i, carry):
            lanes = pl.ds(pl.multiple_of(i * (width // 2), 128), width // 2)
            grad = dot_tn(rows_all, x[:, lanes]).astype(BF)
            for k in range(n_line):
                o[k, :, lanes] = grad[k * n : (k + 1) * n]
            return carry

        lax.fori_loop(0, 2, half, 0)

    by_line(up_o, du)
    for i in range(parts):
        f, h, u, a = first[i], hid[i].astype(F32), ua[i], rate[0:1]
        dv = unit_back(f, cv[i][:, :1], d1[i] + job.result(i))
        step = a * dv
        low[i] = unit_back(u, ca[i][:, :1], step).astype(BF)
        out.start_part(i)
        res_o[i] = dv - step
        total = jnp.sum(dv * (u - h), axis=0, keepdims=True)
        sum_o[...] = total if i == 0 else sum_o[...] + total
        if len(steps) > 0:
            k, line_job = steps.pop(0)
            line_job.step(k)
    for k, line_job in steps:
        line_job.step(k)
    by_line(gate_o, dg)
    out.forward()
    out.finish()
    job.finish()
    for line_job, cut in downs:
        line_job.result(down_o.at[cut])
        line_job.finish()


def back_joint(n_line, seqs, d, wd, up, gate, rate, wu, wu2, wg, x, inner, d1, first, ua, ca, cv, hid):
    parts, rows, width = first.shape
    columns = wd.shape[1]
    part = jax.ShapeDtypeStruct((8, parts, rows, width), BF)
    down = jax.ShapeDtypeStruct((n_line, 4, width // (4 * n_line), columns), BF)
    by_line = ((n_line, columns // n_line, width), BF)
    wide = lambda a: a.reshape(2, 2, 2, parts * rows, a.shape[-1])
    thin = pltpu.VMEM((2, 2, 2, parts * rows, columns), BF)
    late = (wd, wide(up), wide(gate), wu, wu2, wg, x)
    return comm_call(
        functools.partial(back_joint_kernel, n_line), "back_joint", 3,
        (wide(d), wide(inner), rate, d1, first, ua, ca, cv, hid) + late,
        [
            (first.shape, F32), ((1, width), F32), ((2, columns), F32),
            ((seqs, 4, parts * rows // seqs, width), BF), by_line, by_line, (down.shape[1:], BF),
        ],
        [pltpu.VMEM(part.shape, BF), pltpu.VMEM(first.shape, BF), pltpu.VMEM(down.shape, BF), thin, thin]
        + Late.scratch(late) + PlaneReduce.scratch(part) + UlyGather.sems(parts)
        + line_reduce_scratch(n_line, down),
        40, VMEM_BYTES, tuple(range(9, 16)), far_outs=(3,), late=(0, 1),
    )


def settle_kernel(count, *refs):
    ins, outs, bufs = refs[:count], refs[count : 2 * count], refs[2 * count : 3 * count]
    come, go = refs[3 * count :]
    into = [pltpu.make_async_copy(x, b, come.at[i]) for i, (x, b) in enumerate(zip(ins, bufs))]
    out = [pltpu.make_async_copy(b, o, go.at[i]) for i, (b, o) in enumerate(zip(bufs, outs))]
    for copy in into:
        copy.start()
    for a, b in zip(into, out):
        a.wait()
        b.start()
    for copy in out:
        copy.wait()


def settle(*arrays):
    count = len(arrays)
    anyway = pl.BlockSpec(memory_space=pl.ANY)
    return pl.pallas_call(
        functools.partial(settle_kernel, count),
        out_shape=[jax.ShapeDtypeStruct(a.shape, a.dtype) for a in arrays],
        in_specs=[anyway] * count,
        out_specs=[anyway] * count,
        scratch_shapes=[pltpu.VMEM(a.shape, a.dtype) for a in arrays]
        + [pltpu.SemaphoreType.DMA((count,))] * 2,
        compiler_params=pltpu.CompilerParams(vmem_limit_bytes=VMEM_BYTES),
        name="settle",
    )(*arrays)


def local(
    hidden, positions, w_query, w_key, w_value, w_out, w_up, w_gate, w_down,
    qk_scale, alpha_attn, alpha_mlp, up_scale, gate_scale, cotangent,
):
    seqs, rows_each, width = hidden.shape
    n_line = lax.axis_size("line")
    n_blk = 2 * n_line
    heads = HEADS // 4
    local_width = heads * HEAD_DIM
    group_rows = 4 * rows_each
    tokens = seqs * rows_each
    group_tokens = 4 * tokens
    plane_tokens = 8 * tokens
    attn_each, ff_each = w_query.shape[0], w_up.shape[0]
    ff_local = ff_each * n_line
    far, core, line, side = place()
    uly = far * 2 + core

    def row(x, wide):
        return jnp.pad(x, ((0, 0),) * (x.ndim - 1) + ((0, wide - x.shape[-1]),))

    pieces = [v.astype(F32) for v in (qk_scale, alpha_attn, alpha_mlp, up_scale, gate_scale)]
    pieces.append(positions.reshape(-1).astype(F32))
    rows_of = [-(-v.shape[0] // 128) for v in pieces]
    starts = [sum(rows_of[:i]) for i in range(len(pieces) + 1)]
    tall = starts[-1] + -starts[-1] % 8
    small = 0.0
    for v, start in zip(pieces, starts):
        small = small + jnp.pad(v, (start * 128, (tall - start) * 128 - v.shape[0]))
    small = small.reshape(tall, 128)

    sizes = tuple(v.shape[0] for v in pieces)
    assert ff_local <= width and tokens <= 128 and attn_each <= 64
    (
        hid_all, places, cos, sin, scale_both, rates, wq_all, wk_all, wv_all, out_cols, down_cols, up_first
    ) = entry(
        n_line, tuple(starts), sizes, hidden, small, w_query, w_key, w_value, w_out, w_down, w_up
    )
    up_first = up_first.reshape(ff_local, -1)

    group_hidden = hid_all.reshape(group_tokens, width)
    wq = wq_all.reshape(heads, HEAD_DIM, width)
    wk = wk_all.reshape(heads, HEAD_DIM, width)
    wv = wv_all.reshape(heads, HEAD_DIM, width)
    qz, y_both, c_both, kv_all, out_all, gate_full, up_last, attended, mixed, inverse = attend(
        n_line, seqs, group_hidden, wq, wk, wv, cos, sin, scale_both, out_cols, w_gate, w_up,
        places,
    )
    up_last = up_last.reshape(ff_local, -1)
    gate_full = gate_full.reshape(ff_local, width)
    out_full = out_all.reshape(width, local_width)

    fine = (2 * seqs, rows_each // 2, width)
    hidden_fine = hidden.reshape(fine)
    first, unit_att, att_c, first_c, mlp_in, down_full = attn_joint(
        n_line, mixed, out_full, hidden_fine, rates,
        down_cols.reshape(4, 2 * attn_each, ff_local),
    )
    down_full = down_full.reshape(width, ff_local)
    mlp_in = mlp_in.reshape(plane_tokens, width)
    layer_out, grad_first, grad_alpha_mlp, branch_low, inner, up_rows, gate_rows = ff_joint(
        mlp_in, up_first, up_last, gate_full, rates, down_full, first, cotangent.reshape(fine)
    )
    branch_low = branch_low.reshape(plane_tokens, width)
    grad_residual, grad_alpha_attn, ff_scales, att_low, grad_up, grad_gate, down_own = back_joint(
        n_line, seqs, branch_low, down_full, up_rows, gate_rows, rates, up_first, up_last, gate_full,
        mlp_in, inner, grad_first, first, unit_att, att_c, first_c, hidden_fine,
    )
    down_own = down_own.reshape(8, attn_each, ff_local)

    dq, dkv, out_own, up_own = attend_back(
        n_line, qz, att_low.reshape(seqs, group_rows, width), out_full, mixed, attended, inverse,
        kv_all, places, grad_up,
    )
    out_own = out_own.reshape(4, attn_each, local_width)
    gq, gk, gv, grad_hidden, out_gradient, down_gradient, sums, gate_own = leave(
        n_line, group_hidden, dq, dkv, y_both, c_both, cos, sin, scale_both, wq, wk, wv,
        grad_residual.reshape(seqs, rows_each, width), out_own, down_own,
        grad_alpha_attn, grad_alpha_mlp, ff_scales, grad_gate,
    )
    sums = sums[0]
    layer_out, grad_hidden, gq, gk, gv, out_gradient, up_own, gate_own, down_gradient = settle(
        layer_out.reshape(hidden.shape), grad_hidden, gq, gk, gv, out_gradient, up_own, gate_own,
        down_gradient,
    )
    return (
        layer_out,
        grad_hidden,
        gq,
        gk,
        gv,
        out_gradient,
        up_own,
        gate_own,
        down_gradient,
        sums[128 : 128 + attn_each],
        sums[:attn_each],
        sums[attn_each : 2 * attn_each],
        sums[256 : 256 + ff_each],
        sums[256 + ff_each : 256 + 2 * ff_each],
    )


def solution(mesh):
    far = mesh.shape["uly"] // 2
    line = mesh.shape["blk"] // 2
    finer = Mesh(mesh.devices.reshape(far, 2, line, 2), AXES)
    rows, tokens, flat = P(AXES, None), P(None, AXES, None), P(AXES)
    return jax.shard_map(
        local,
        mesh=finer,
        in_specs=(tokens, P(None, AXES)) + (rows,) * 7 + (flat,) * 5 + (tokens,),
        out_specs=(tokens, tokens) + (rows,) * 7 + (flat,) * 5,
        check_vma=False,
    )
```

```python
import functools
import math

import jax
import jax.numpy as jnp
from jax import lax
from jax.experimental import pallas as pl
from jax.experimental.pallas import tpu as pltpu
from jax.sharding import Mesh
from jax.sharding import PartitionSpec as P

D = 1280
HEADS = 20
HEAD_DIM = 64
AXES = ("far", "core", "line", "side")
PLANE = ("far", "core", "side")
VMEM_BYTES = 60 * 1024 * 1024

rotary_base = 10000.0
tiny_eps = 1e-06
BF = jnp.bfloat16
F32 = jnp.float32


def place():
    return tuple(lax.axis_index(name) for name in AXES)


def remote(src, dst, send, recv, device):
    return pltpu.make_async_remote_copy(
        src_ref=src,
        dst_ref=dst,
        send_sem=send,
        recv_sem=recv,
        device_id=device,
        device_id_type=pl.DeviceIdType.MESH,
    )


def signal_to(device):
    pl.semaphore_signal(
        pltpu.get_barrier_semaphore(), inc=1, device_id=device, device_id_type=pl.DeviceIdType.MESH
    )


def greet(devices, maybe=()):
    count = len(devices)
    for device in devices:
        signal_to(device)
    for there, device in maybe:
        pl.when(there)(functools.partial(signal_to, device))
        count = count + jnp.where(there, 1, 0)
    pl.semaphore_wait(pltpu.get_barrier_semaphore(), count)


def params(collective_id, room=VMEM_BYTES):
    return pltpu.CompilerParams(
        collective_id=collective_id, has_side_effects=True, vmem_limit_bytes=room
    )


class UlyGather:
    sems = staticmethod(lambda parts: [pltpu.SemaphoreType.DMA((3, parts))] * 2 + [pltpu.SemaphoreType.DMA((parts,))])

    def __init__(self, x, o, send, recv, local, pick=None):
        pick = pick or (lambda i, u: o.at[i, u])
        y, c, z, s = place()
        u, v = y * 2 + c, (1 - y) * 2 + c
        mate, across = (y, 1 - c, z, s), (1 - y, c, z, s)
        self.parts = x.shape[0]
        parts = range(self.parts)
        self.far = [remote(x.at[i], pick(i, u), send.at[0, i], recv.at[0, i], across) for i in parts]
        self.near = [remote(x.at[i], pick(i, u), send.at[1, i], recv.at[1, i], mate) for i in parts]
        self.on = [remote(pick(i, v), pick(i, v), send.at[2, i], recv.at[2, i], mate) for i in parts]
        self.own = [pltpu.make_async_copy(x.at[i], pick(i, u), local.at[i]) for i in parts]

    def start_part(self, i):
        self.far[i].start()
        self.near[i].start()
        self.own[i].start()

    def start(self):
        for i in range(self.parts):
            self.start_part(i)

    def forward(self):
        for i in range(self.parts):
            self.far[i].wait_recv()
            self.on[i].start()

    def finish(self):
        for i in range(self.parts):
            self.near[i].wait_recv()
            self.on[i].wait_recv()
            self.own[i].wait()
            self.far[i].wait_send()
            self.near[i].wait_send()
            self.on[i].wait_send()


def uly_peers():
    y, c, z, s = place()
    return [(y, 1 - c, z, s), (1 - y, c, z, s)]


def add_low(*terms):
    total = terms[0].astype(F32)
    for term in terms[1:]:
        total = total + term.astype(F32)
    return total


class UlyReduce:
    @staticmethod
    def scratch(x):
        parts, _, rows, width = x.shape
        return [
            pltpu.VMEM((parts, 2, rows, width), x.dtype),
            pltpu.VMEM((parts, rows, width), x.dtype),
            pltpu.VMEM((parts, rows, width), x.dtype),
            pltpu.SemaphoreType.DMA((3, parts)),
            pltpu.SemaphoreType.DMA((3, parts)),
        ]

    def __init__(self, x, near, mid, far_in, send, recv):
        y, c, z, s = place()
        mate, across = uly_peers()
        self.x, self.near_ref, self.mid, self.far_in = x, near, mid, far_in
        self.y, self.c, self.parts = y, c, x.shape[0]
        parts = range(self.parts)
        self.near = [
            [
                remote(x.at[i, f * 2 + 1 - c], near.at[i, k], send.at[k, i], recv.at[k, i], mate)
                for k, f in enumerate((1 - y, y))
            ]
            for i in parts
        ]
        self.far = [remote(mid.at[i], far_in.at[i], send.at[2, i], recv.at[2, i], across) for i in parts]

    def start(self):
        for i in range(self.parts):
            for copy in self.near[i]:
                copy.start()

    def middle(self):
        for i in range(self.parts):
            self.near[i][0].wait_recv()
            self.mid[i] = add_low(self.x[i, (1 - self.y) * 2 + self.c], self.near_ref[i, 0]).astype(BF)
            self.far[i].start()

    def result(self, i):
        self.near[i][1].wait_recv()
        self.far[i].wait_recv()
        return add_low(self.x[i, self.y * 2 + self.c], self.near_ref[i, 1], self.far_in[i])

    def finish(self):
        for i in range(self.parts):
            for copy in self.near[i] + [self.far[i]]:
                copy.wait_send()


def plane_peers():
    y, c, z, s = place()
    return [(y, 1 - c, z, s), (1 - y, c, z, s), (y, c, z, 1 - s)]


def plane_index(y, c, s):
    return (y * 2 + c) * 2 + s


class PlaneGather:
    @staticmethod
    def sems(parts):
        return [pltpu.SemaphoreType.DMA((7, parts))] * 2 + [pltpu.SemaphoreType.DMA((parts,))]

    def __init__(self, x, o, send, recv, local):
        y, c, z, s = place()
        mate, across, cross = plane_peers()
        self.parts = parts = range(x.shape[0])
        me, py, px, pd = (
            plane_index(y, c, s),
            plane_index(1 - y, c, s),
            plane_index(y, c, 1 - s),
            plane_index(1 - y, c, 1 - s),
        )

        def copy(source, p, i, slot, device):
            return remote(source, o.at[p, i], send.at[slot, i], recv.at[slot, i], device)

        def on(p, i, slot, device):
            return copy(o.at[p, i], p, i, slot, device)

        self.by_y = [copy(x.at[i], me, i, 0, across) for i in parts]
        self.by_x = [copy(x.at[i], me, i, 1, cross) for i in parts]
        self.near = [copy(x.at[i], me, i, 2, mate) for i in parts]
        self.corner = [on(px, i, 3, across) if i % 2 else on(py, i, 3, cross) for i in parts]
        self.pass_y = [on(py, i, 4, mate) for i in parts]
        self.pass_x = [on(px, i, 5, mate) for i in parts]
        self.pass_d = [on(pd, i, 6, mate) for i in parts]
        self.own = [pltpu.make_async_copy(x.at[i], o.at[me, i], local.at[i]) for i in parts]

    def start_part(self, i):
        for copy in (self.by_y[i], self.by_x[i], self.near[i], self.own[i]):
            copy.start()

    def forward_part(self, i):
        ways = [(self.by_y[i], self.pass_y[i]), (self.by_x[i], self.pass_x[i])]
        first, then = ways[:: 1 - 2 * (i % 2)]
        first[0].wait_recv()
        self.corner[i].start()
        first[1].start()
        then[0].wait_recv()
        then[1].start()

    def finish(self):
        for i in self.parts:
            self.corner[i].wait_recv()
            self.pass_d[i].start()
        for i in self.parts:
            for copy in (self.near[i], self.pass_y[i], self.pass_x[i], self.pass_d[i]):
                copy.wait()
            for copy in (self.by_y[i], self.by_x[i], self.corner[i]):
                copy.wait_send()
            self.own[i].wait()


class PlaneReduce:
    @staticmethod
    def scratch(x):
        one = pltpu.VMEM(x.shape[1:], x.dtype)
        sems = pltpu.SemaphoreType.DMA((7, x.shape[1]))
        return [pltpu.VMEM((4,) + x.shape[1:], x.dtype)] + [one] * 6 + [sems] * 2

    def __init__(self, x, near, out_x, out_y, out_d, in_x, in_y, in_d, send, recv):
        y, c, z, s = place()
        mate, across, cross = plane_peers()
        self.c = c
        self.parts = parts = range(x.shape[1])
        self.spots = ((1 - y, 1 - s), (y, 1 - s), (1 - y, s), (y, s))
        self.x, self.near_ref = x, near
        self.out_x, self.out_y, self.out_d = out_x, out_y, out_d
        self.in_x, self.in_y, self.in_d = in_x, in_y, in_d

        def copy(source, target, i, slot, device):
            return remote(source, target, send.at[slot, i], recv.at[slot, i], device)

        self.near = [
            [copy(x.at[plane_index(sy, 1 - c, ss), i], near.at[k, i], i, k, mate) for i in parts]
            for k, (sy, ss) in enumerate(self.spots)
        ]
        self.corner = [copy(out_d.at[i], in_d.at[i], i, 4, across if i % 2 else cross) for i in parts]
        self.by_x = [copy(out_x.at[i], in_x.at[i], i, 5, cross) for i in parts]
        self.by_y = [copy(out_y.at[i], in_y.at[i], i, 6, across) for i in parts]

    def pair(self, k, i):
        sy, ss = self.spots[k]
        self.near[k][i].wait_recv()
        return add_low(self.x[plane_index(sy, self.c, ss), i], self.near_ref[k, i])

    def middle(self, far):
        for i in self.parts:
            if far:
                self.out_d[i] = self.pair(0, i).astype(BF)
                self.corner[i].start()
                if i % 2 == 1:
                    self.out_y[i] = self.pair(2, i).astype(BF)
                    self.by_y[i].start()
            elif i % 2 == 0:
                self.out_x[i] = self.pair(1, i).astype(BF)
                self.by_x[i].start()

    def last(self):
        for i in self.parts:
            k, out, by = (1, self.out_x, self.by_x) if i % 2 else (2, self.out_y, self.by_y)
            part = self.pair(k, i)
            self.corner[i].wait_recv()
            out[i] = (part + self.in_d[i].astype(F32)).astype(BF)
            by[i].start()

    def result(self, i):
        own = self.pair(3, i)
        self.by_x[i].wait_recv()
        self.by_y[i].wait_recv()
        return own + add_low(self.in_x[i], self.in_y[i])

    def finish(self):
        for copy in [c for spot in self.near for c in spot] + self.corner + self.by_x + self.by_y:
            copy.wait_send()


def plane_corners():
    y, c, z, s = place()
    return [
        (y, 1 - c, s), (1 - y, c, s), (1 - y, 1 - c, s),
        (y, c, 1 - s), (y, 1 - c, 1 - s), (1 - y, c, 1 - s), (1 - y, 1 - c, 1 - s),
    ]


def line_ends(n_line):
    y, c, z, s = place()
    return (z > 0, (y, c, z - 1, s)), (z < n_line - 1, (y, c, z + 1, s)), (y, c, z, 1 - s)


class BlkGather:
    @staticmethod
    def sems(n_line):
        return [
            pltpu.SemaphoreType.DMA((3,)),
            pltpu.SemaphoreType.DMA((1,)),
            pltpu.SemaphoreType.DMA((4, n_line)),
            pltpu.SemaphoreType.DMA((4, n_line)),
            pltpu.SemaphoreType.DMA((1,)),
        ]

    def __init__(self, n_line, pick_x, pick_o, own_send, own_recv, send, recv, local):
        y, c, z, s = place()
        self.z, self.s, self.n = z, s, n_line
        (self.has_low, self.low), (self.has_high, self.high), self.cross = line_ends(n_line)
        self.pick_x, self.pick_o = pick_x, pick_o
        self.sem = (own_send, own_recv, send, recv, local)

    def block(self, way, k):
        z = self.z - k if way == 0 else self.z + k
        return self.pick_o(z * 2 + self.s)

    def own(self, way):
        own_send, own_recv, send, recv, local = self.sem
        arrival = own_recv.at[0] if way == 2 else recv.at[way, 0]
        target = (self.high, self.low, self.cross)[way]
        return remote(self.pick_x(), self.pick_o(self.z * 2 + self.s), own_send.at[way], arrival, target)

    def keep(self):
        return pltpu.make_async_copy(self.pick_x(), self.pick_o(self.z * 2 + self.s), self.sem[4].at[0])

    def onward(self, way, k):
        send, recv = self.sem[2:4]
        target = self.high if way == 0 else self.low
        return remote(self.block(way, k), self.block(way, k), send.at[way, k], recv.at[way, k], target)

    def over(self, way, k):
        send, recv = self.sem[2:4]
        return remote(self.block(way, k), self.block(way, k), send.at[2 + way, k], recv.at[2 + way, k], self.cross)

    def arrive(self, way, k):
        send, recv = self.sem[2:4]
        return remote(self.block(way, k), self.block(way, k), send.at[way, k], recv.at[way, k - 1], self.cross)

    def there(self, way, k):
        return self.z >= k if way == 0 else self.z + k < self.n

    def start(self):
        pl.when(self.has_high)(lambda: self.own(0).start())
        pl.when(self.has_low)(lambda: self.own(1).start())
        self.own(2).start()
        self.keep().start()

    def take(self, way, k):
        self.arrive(way, k).wait_recv()
        pl.when((self.has_high, self.has_low)[way])(lambda: self.onward(way, k).start())
        self.over(way, k).start()

    def step(self, k):
        for way in (0, 1):
            pl.when(self.there(way, k))(lambda: self.take(way, k))

    def finish_arrivals(self):
        self.own(2).wait_recv()
        for k in range(1, self.n):
            for way in (0, 1):
                pl.when(self.there(way, k))(lambda: self.over(way, k).wait_recv())
        self.keep().wait()

    def finish_sends(self):
        pl.when(self.has_high)(lambda: self.own(0).wait_send())
        pl.when(self.has_low)(lambda: self.own(1).wait_send())
        self.own(2).wait_send()
        for k in range(1, self.n):
            for way in (0, 1):
                @pl.when(self.there(way, k))
                def _():
                    self.over(way, k).wait_send()

                    @pl.when((self.has_high, self.has_low)[way])
                    def _():
                        self.onward(way, k).wait_send()


def blk_greet(n_line):
    low, high, cross = line_ends(n_line)
    greet([cross], [low, high])


class BlkReduce:
    @staticmethod
    def scratch(n_line, a):
        return [
            pltpu.VMEM((n_line,) + a.shape[1:], a.dtype),
            pltpu.VMEM((n_line + 1,) + a.shape[1:], a.dtype),
            pltpu.SemaphoreType.DMA((n_line,)),
            pltpu.SemaphoreType.DMA((n_line,)),
            pltpu.SemaphoreType.DMA((2, n_line)),
            pltpu.SemaphoreType.DMA((2, n_line)),
        ]

    def __init__(self, n_line, x, side_in, line_in, side_send, side_recv, send, recv):
        y, c, self.z, self.s = place()
        self.n = n_line
        (self.has_low, self.low), (self.has_high, self.high), self.cross = line_ends(n_line)
        self.x = x
        self.side_in, self.line_in = side_in, line_in
        self.sem = (side_send, side_recv, send, recv)

    def spot(self, way, k):
        return self.z + k * (1 - 2 * way)

    def exists(self, way, k):
        return (self.spot(way, k) >= 0) & (self.spot(way, k) < self.n)

    def toward(self, way):
        y, c, z, s = place()
        return (y, c, z + 1 - 2 * way, s)

    def side(self, zz):
        side_send, side_recv = self.sem[:2]
        return remote(
            self.x.at[zz * 2 + 1 - self.s], self.side_in.at[zz], side_send.at[zz], side_recv.at[zz], self.cross
        )

    def slot(self, way, k):
        return jnp.where((way == 1) & (k == 0), self.n, self.spot(way, k))

    def move(self, way, k):
        send, recv = self.sem[2:]
        zz = self.spot(way, k)
        there = jnp.where((way == 1) & (k == 1), self.n, zz)
        return remote(
            self.side_in.at[zz], self.line_in.at[there], send.at[way, k], recv.at[way, k - 1], self.toward(way)
        )

    def arrive(self, way, k):
        send, recv = self.sem[2:]
        there = self.line_in.at[self.slot(way, k)]
        return remote(there, there, send.at[way, k], recv.at[way, k], self.toward(1 - way))

    def start(self, k):
        for way in (0, 1) if k > 0 else (0,):
            pl.when(self.exists(way, k))(lambda: self.side(self.spot(way, k)).start())

    def move_on(self, way, k):
        zz = self.spot(way, k)
        self.side(zz).wait_recv()
        passed = jnp.where(way == 0, self.has_low, self.has_high)

        @pl.when(passed)
        def _():
            self.arrive(way, k).wait_recv()
            self.side_in[zz] = add_low(
                self.x[zz * 2 + self.s], self.side_in[zz], self.line_in[zz]
            ).astype(self.side_in.dtype)

        @pl.when(jnp.logical_not(passed))
        def _():
            self.side_in[zz] = add_low(self.x[zz * 2 + self.s], self.side_in[zz]).astype(
                self.side_in.dtype
            )

        self.move(way, k).start()

    def step(self, k):
        def one(way, carry):
            pl.when(self.exists(way, k))(lambda: self.move_on(way, k))
            return carry

        lax.fori_loop(0, 2, one, 0)

    def result(self, o):
        z = self.z
        self.side(z).wait_recv()
        pl.when(self.has_low)(lambda: self.arrive(0, 0).wait_recv())
        pl.when(self.has_high)(lambda: self.arrive(1, 0).wait_recv())
        own = lambda: add_low(self.x[z * 2 + self.s], self.side_in[z])
        both = self.has_low & self.has_high

        @pl.when(both)
        def _():
            o[...] = (own() + add_low(self.line_in[z], self.line_in[self.n])).astype(o.dtype)

        @pl.when(jnp.logical_not(both))
        def _():
            other = self.line_in[jnp.where(self.has_low, z, self.n)].astype(F32)
            o[...] = (own() + other).astype(o.dtype)

    def finish(self):
        for k in range(self.n - 1, -1, -1):
            for way in (0, 1) if k > 0 else (0,):
                @pl.when(self.exists(way, k))
                def _():
                    self.side(self.spot(way, k)).wait_send()
                    if k > 0:
                        self.move(way, k).wait_send()


class LineGather:
    @staticmethod
    def sems(n_line):
        dma = pltpu.SemaphoreType.DMA
        return [dma((2,)), dma((2, n_line)), dma((2, n_line)), dma((1,))]

    def __init__(self, n_line, pick_x, pick_o, own_send, send, recv, local):
        y, c, self.z, s = place()
        self.n = n_line
        (self.has_low, self.low), (self.has_high, self.high), _ = line_ends(n_line)
        self.pick_x, self.pick_o = pick_x, pick_o
        self.own_send, self.send, self.recv, self.local = own_send, send, recv, local

    def goes(self, way):
        return (self.has_high, self.has_low)[way]

    def own(self, way):
        target = (self.high, self.low)[way]
        return remote(self.pick_x(), self.pick_o(self.z), self.own_send.at[way], self.recv.at[way, 0], target)

    def keep(self):
        return pltpu.make_async_copy(self.pick_x(), self.pick_o(self.z), self.local.at[0])

    def onward(self, way, k):
        block = self.pick_o(self.z - k if way == 0 else self.z + k)
        target = (self.high, self.low)[way]
        return remote(block, block, self.send.at[way, k], self.recv.at[way, k], target)

    def arrive(self, way, k):
        block = self.pick_o(self.z - k if way == 0 else self.z + k)
        return remote(block, block, self.send.at[way, k], self.recv.at[way, k - 1], (self.low, self.high)[way])

    def there(self, way, k):
        return self.z >= k if way == 0 else self.z + k < self.n

    def start(self):
        for way in (0, 1):
            pl.when(self.goes(way))(lambda: self.own(way).start())
        self.keep().start()

    def step(self, k):
        for way in (0, 1):
            @pl.when(self.there(way, k))
            def _():
                self.arrive(way, k).wait_recv()
                pl.when(self.goes(way))(lambda: self.onward(way, k).start())

    def finish(self):
        self.keep().wait()
        for way in (0, 1):
            pl.when(self.goes(way))(lambda: self.own(way).wait_send())
            for k in range(1, self.n):
                pl.when(self.there(way, k) & self.goes(way))(lambda: self.onward(way, k).wait_send())


class LineReduce:
    @staticmethod
    def scratch(n_line, a):
        dma = pltpu.SemaphoreType.DMA
        return [
            pltpu.VMEM((n_line,) + a.shape[1:], a.dtype),
            pltpu.VMEM((n_line + 1,) + a.shape[1:], a.dtype),
            dma((2, n_line)), dma((2, n_line)),
        ]

    def __init__(self, n_line, x, sums, line_in, send, recv):
        y, c, self.z, s = place()
        self.n, self.x, self.sums, self.line_in, self.send, self.recv = n_line, x, sums, line_in, send, recv
        (self.has_low, self.low), (self.has_high, self.high), _ = line_ends(n_line)

    def spot(self, way, k):
        return self.z + k * (1 - 2 * way)

    def exists(self, way, k):
        return (self.spot(way, k) >= 0) & (self.spot(way, k) < self.n)

    def passed(self, way):
        return jnp.where(way == 0, self.has_low, self.has_high)

    def slot(self, way, k):
        return jnp.where((way == 1) & (k == 0), self.n, self.spot(way, k))

    def toward(self, way):
        y, c, z, s = place()
        return (y, c, z + 1 - 2 * way, s)

    def move(self, way, k, source):
        zz = self.spot(way, k)
        there = jnp.where((way == 1) & (k == 1), self.n, zz)
        return remote(
            source.at[zz], self.line_in.at[there], self.send.at[way, k], self.recv.at[way, k - 1], self.toward(way)
        )

    def arrive(self, way, k):
        there = self.line_in.at[self.slot(way, k)]
        return remote(there, there, self.send.at[way, k], self.recv.at[way, k], self.toward(1 - way))

    def step(self, k):
        def one(way, carry):
            exists, passed = self.exists(way, k), self.passed(way)

            @pl.when(exists & passed)
            def _():
                zz = self.spot(way, k)
                self.arrive(way, k).wait_recv()
                self.sums[zz] = add_low(self.x[zz], self.line_in[zz]).astype(self.sums.dtype)
                self.move(way, k, self.sums).start()

            pl.when(exists & jnp.logical_not(passed))(lambda: self.move(way, k, self.x).start())
            return carry

        lax.fori_loop(0, 2, one, 0)

    def result(self, o):
        z = self.z
        pl.when(self.has_low)(lambda: self.arrive(0, 0).wait_recv())
        pl.when(self.has_high)(lambda: self.arrive(1, 0).wait_recv())
        both = self.has_low & self.has_high

        @pl.when(both)
        def _():
            o[...] = add_low(self.x[z], self.line_in[z], self.line_in[self.n]).astype(o.dtype)

        @pl.when(jnp.logical_not(both))
        def _():
            o[...] = add_low(self.x[z], self.line_in[jnp.where(self.has_low, z, self.n)]).astype(o.dtype)

    def finish(self):
        for k in range(self.n - 1, 0, -1):
            for way in (0, 1):
                pl.when(self.exists(way, k))(lambda: self.move(way, k, self.sums).wait_send())


def lane_chunks(width):
    cut = width // 256 * 128
    return [slice(0, cut), slice(cut, width)]


LINE_CHUNKS = 2


def line_gathers(n_line, x, pick_o, sems):
    jobs = []
    for i, lanes in enumerate(lane_chunks(x.shape[-1])):
        cut = (slice(None),) * (len(x.shape) - 1) + (lanes,)
        jobs.append(
            LineGather(
                n_line, lambda cut=cut: x.at[cut], lambda z, cut=cut: pick_o(z).at[cut],
                *sems[4 * i : 4 * i + 4],
            )
        )
    return jobs


def line_gather_sems(n_line):
    return LineGather.sems(n_line) * LINE_CHUNKS


def line_reduces(n_line, x, scratch):
    jobs = []
    for i, lanes in enumerate(lane_chunks(x.shape[-1])):
        cut = (slice(None),) * (len(x.shape) - 1) + (lanes,)
        jobs.append((LineReduce(n_line, x.at[cut], *scratch[4 * i : 4 * i + 4]), cut[1:]))
    return jobs


def line_reduce_scratch(n_line, a):
    scratch = []
    for lanes in lane_chunks(a.shape[-1]):
        one = jax.ShapeDtypeStruct(a.shape[:-1] + (lanes.stop - lanes.start,), a.dtype)
        scratch += LineReduce.scratch(n_line, one)
    return scratch


def comm_call(
    kernel, name, collective_id, args, outs, scratch, micros, room=VMEM_BYTES, far_args=(), far_outs=(), late=()
):
    vmem, anyway = pl.BlockSpec(memory_space=pltpu.VMEM), pl.BlockSpec(memory_space=pl.ANY)
    held = [pltpu.VMEM(args[i].shape, args[i].dtype) for i in late]
    held += [pltpu.SemaphoreType.DMA((len(late),))] * (len(late) > 0)

    def whole(*refs):
        refs = list(refs)
        mine, copies = refs[len(refs) - len(held) :], []
        refs = refs[: len(refs) - len(held)]
        for j, i in enumerate(late):
            copies.append(pltpu.make_async_copy(refs[i], mine[j], mine[-1].at[j]))
            copies[-1].start()
            refs[i] = mine[j]

        def ready():
            for copy in copies:
                copy.wait()

        kernel(ready, *refs)

    return pl.pallas_call(
        whole,
        out_shape=[jax.ShapeDtypeStruct(shape, dtype) for shape, dtype in outs],
        in_specs=[anyway if i in far_args or i in late else vmem for i in range(len(args))],
        out_specs=[anyway if i in far_outs else vmem for i in range(len(outs))],
        scratch_shapes=list(scratch) + held,
        compiler_params=params(collective_id, room),
        cost_estimate=pl.CostEstimate(flops=0, bytes_accessed=micros * 3_000_000, transcendentals=0),
        name=name,
    )(*args)


def exit_kernel(
    n_line, ready, x, dq, dkv, yy_ref, cc_ref, cos, sin, scale, wq, wk, wv, res, oc, dc, a_sum, m_sum, ff_sum, gg,
    gq_o, gk_o, gv_o, gh_o, go_o, gd_o, sum_o, gg_o, oc_o, dc_o,
    flat, acc, gq, gk, gv, gh, scale_s, alpha,
    alpha_in, line_out, line_all, oc_s, oc_r, dc_s, dc_r, al_s, al_r, su_s, su_r, keep, *scratch,
):
    y, c, z, s = place()
    u, p, b, n_blk = y * 2 + c, plane_index(y, c, s), z * 2 + s, 2 * n_line
    low, high, cross = line_ends(n_line)
    corners = plane_corners()
    others = []
    for i in range(1, n_blk):
        to = lax.rem(b + i, n_blk)
        others.append((y, c, to // 2, lax.rem(to, 2)))
    once = [(to[3] != 1 - s) | (to[2] != z) for to in others]
    greet([(yy, cc, z, ss) for yy, cc, ss in corners], list(zip(once, others)))
    each = 6
    jobs = [BlkReduce(n_line, g, *scratch[each * i : each * (i + 1)]) for i, g in enumerate((gq, gk, gv))]
    split = each * 3 + len(UlyReduce.scratch(gh))
    hid = UlyReduce(gh, *scratch[each * 3 : split])
    gates = line_reduces(n_line, gg, scratch[split:])
    small, cols = [], []
    for k, (yy, cc, ss) in enumerate(corners):
        target = (yy, cc, z, ss)
        cols.append(remote(dc.at[plane_index(yy, cc, ss)], dc_o.at[p], dc_s.at[k], dc_r.at[k], target))
        if k < 3:
            cols.append(remote(oc.at[yy * 2 + cc], oc_o.at[u], oc_s.at[k], oc_r.at[k], target))
            small.append(remote(alpha.at[yy * 2 + cc], alpha_in.at[k], al_s.at[k], al_r.at[k], target))
    for job, _ in gates:
        job.step(n_line - 1)
    for job in cols:
        job.start()
    each_rows = gq.shape[1]
    for v in range(4):
        for k in range(n_blk):
            at = (v * n_blk + k) * each_rows
            alpha[v, k, :, :each_rows] = a_sum[:, at : at + each_rows]
            alpha[v, k, :, each_rows : 2 * each_rows] = m_sum[:, at : at + each_rows]
    for job in small:
        job.start()
    ready()
    rows_all = x[...]
    seqs, group_rows, wide = dq.shape
    heads = wide // 128
    factor = jnp.where(lanes_of((1, 128)) < HEAD_DIM, HEAD_DIM**0.5, 1.0)
    late_steps = [(min(1 + 2 * i, heads - 1), k) for i, k in enumerate(range(n_line - 2, 0, -1))]

    def head(h, carry):
        lanes = pl.ds(pl.multiple_of(h * 128, 128), 128)
        queries = jnp.concatenate([dq[i, :, lanes] for i in range(seqs)], axis=0)
        pairs = jnp.concatenate([dkv[i, :, lanes] for i in range(seqs)], axis=0)
        low_half = lanes_of(queries.shape) < HEAD_DIM
        dy = jnp.where(low_half, queries.astype(F32), pltpu.roll(pairs.astype(F32), HEAD_DIM, 1))
        unit = yy_ref[:, lanes]
        scale_s[h] = jnp.sum(dy * unit, axis=0, keepdims=True) * factor
        dy = dy * scale[pl.ds(h, 1)]
        dr = cc_ref[:, lanes] * (dy - unit * halves(unit * dy))
        raw = (dr * cos[...] - turn(dr) * sin[...]).astype(BF)
        both = jnp.concatenate([raw, jnp.where(low_half, jnp.zeros_like(pairs), pairs)], axis=1)
        grad = dot_tn(both, rows_all).astype(BF)
        at = pl.ds(pl.multiple_of(h * HEAD_DIM, HEAD_DIM), HEAD_DIM)
        for j, lo in enumerate((0, HEAD_DIM, 3 * HEAD_DIM)):
            flat[j, at] = grad[lo : lo + HEAD_DIM]
        w_value = wv[h]
        more = dot_nn(both, jnp.concatenate([wq[h], wk[h], jnp.zeros_like(w_value), w_value], axis=0))

        @pl.when(h == 0)
        def _():
            acc[...] = more

        @pl.when(h > 0)
        def _():
            acc[...] = acc[...] + more

        for when, k in late_steps:
            @pl.when(h == when)
            def _():
                for job, _ in gates:
                    job.step(k)

        return carry

    lax.fori_loop(0, heads, head, 0)
    for i, g in enumerate((gq, gk, gv)):
        for k in range(n_blk):
            g[k] = flat[i, k * each_rows : (k + 1) * each_rows]
    for i in range(seqs):
        gh[i] = acc[i * group_rows : (i + 1) * group_rows].astype(BF).reshape(gh.shape[1:])
    hid.start()
    for k in range(n_line - 1, -1, -1):
        for job in jobs:
            job.start(k)
    mine = [
        pltpu.make_async_copy(dc.at[p], dc_o.at[p], keep.at[0]),
        pltpu.make_async_copy(oc.at[u], oc_o.at[u], keep.at[1]),
    ]
    for job in mine:
        job.start()
    hid.middle()
    for job in small:
        job.wait_recv()
    line_out[...] = jnp.zeros_like(line_out)
    ff_each = ff_sum.shape[1] // n_line
    for k in range(n_line):
        for j in (0, 1):
            line_out[k * 2 + s, :, 256 + j * ff_each : 256 + (j + 1) * ff_each] = ff_sum[
                j : j + 1, k * ff_each : (k + 1) * ff_each
            ]
    line_out[:, :, :128] = alpha[u] + alpha_in[0] + alpha_in[1] + alpha_in[2]
    scales = jnp.concatenate(
        [scale_s[h][:, :HEAD_DIM] + scale_s[h][:, HEAD_DIM:] for h in range(heads)], axis=1
    )
    for k in range(n_blk):
        line_out[k, :, 128 : 128 + each_rows] = scales[:, k * each_rows : (k + 1) * each_rows]
    line_jobs = []
    for i in range(1, n_blk):
        to = lax.rem(b + i, n_blk)
        line_jobs.append(
            remote(line_out.at[to], line_all.at[i - 1], su_s.at[i - 1], su_r.at[i - 1], others[i - 1])
        )
    for job in line_jobs:
        job.start()
    for k in range(n_line - 1, 0, -1):
        for job in jobs:
            job.step(k)
    for i in range(gh.shape[0]):
        gh_o[i] = res[i] + hid.result(i)
    for job in cols:
        job.wait_recv()
    for job in mine:
        job.wait()
    wide, ff_each = oc.shape[-1], dc.shape[-1] // n_line
    for v in range(4):
        go_o[:, v * wide : (v + 1) * wide] = oc_o[v].astype(F32)
        for t in (0, 1):
            for k in range(n_line):
                at = ((v * n_line + k) * 2 + t) * ff_each
                gd_o[:, at : at + ff_each] = dc_o[v * 2 + t, :, k * ff_each : (k + 1) * ff_each].astype(F32)
    total = line_out[b]
    for i, job in enumerate(line_jobs):
        job.wait_recv()
        total = total + line_all[i]
    sum_o[...] = total
    for job, o in zip(jobs, (gq_o, gk_o, gv_o)):
        job.result(o)
    for job, cut in gates:
        job.result(gg_o.at[cut])
        job.finish()
    hid.finish()
    for job in jobs:
        job.finish()
    for job in line_jobs + small:
        job.wait_send()
    for job in cols:
        job.wait_send()


def leave(n_line, x, dq, dkv, y, c, cos, sin, scale, wq, wk, wv, res, oc, dc, a_sum, m_sum, ff_sum, gg):
    n_blk = 2 * n_line
    heads, _, width = wq.shape
    seqs, rows, _ = res.shape
    vmem = pl.BlockSpec(memory_space=pltpu.VMEM)
    dma = pltpu.SemaphoreType.DMA
    grad = jax.ShapeDtypeStruct((n_blk, heads * HEAD_DIM // n_blk, width), BF)
    gh = jax.ShapeDtypeStruct((seqs, 4, rows, width), BF)
    scratch = [
        pltpu.VMEM(oc.shape, oc.dtype),
        pltpu.VMEM(dc.shape, dc.dtype),
        pltpu.VMEM((3, heads * HEAD_DIM, width), BF),
        pltpu.VMEM(x.shape, F32),
        pltpu.VMEM(grad.shape, BF), pltpu.VMEM(grad.shape, BF), pltpu.VMEM(grad.shape, BF),
        pltpu.VMEM(gh.shape, BF),
        pltpu.VMEM((heads, 1, 128), F32),
        pltpu.VMEM((4, n_blk, 1, 128), F32),
        pltpu.VMEM((3, n_blk, 1, 128), F32),
        pltpu.VMEM((n_blk, 1, 640), F32),
        pltpu.VMEM((n_blk - 1, 1, 640), F32),
        dma((3,)), dma((3,)), dma((7,)), dma((7,)), dma((3,)), dma((3,)),
        dma((n_blk - 1,)), dma((n_blk - 1,)), dma((2,)),
    ]
    scratch += BlkReduce.scratch(n_line, grad) * 3
    scratch += UlyReduce.scratch(gh) + line_reduce_scratch(n_line, gg)
    args = (x, dq, dkv, y, c, cos, sin, scale, wq, wk, wv, res, oc, dc, a_sum, m_sum, ff_sum, gg)
    outs = [grad.shape[1:]] * 3 + [
        res.shape, (oc.shape[1], 4 * oc.shape[2]), (dc.shape[1], 8 * dc.shape[2]), (1, 640), gg.shape[1:]
    ]
    return comm_call(
        functools.partial(exit_kernel, n_line), "leave", 8, args, [(shape, F32) for shape in outs], scratch,
        60, late=tuple(range(11)),
    )


def tables(n_line, starts, sizes, small, places, cos, sin, scale, rates):
    y, c, z, s = place()
    u, b, n_blk = y * 2 + c, z * 2 + s, 2 * n_line
    seqs, rows_each = places.shape[0], places.shape[-1] // 4
    for v in range(4):
        for k in range(n_blk):
            row = small[v, k, starts[5] : starts[5] + 1]
            for i in range(seqs):
                places[i, k, :, v * rows_each : (v + 1) * rows_each] = row[:, i * rows_each : (i + 1) * rows_each]
    lane = lanes_of((1, 128)) % HEAD_DIM
    freqs = jnp.exp((lane % 32).astype(F32) * (-math.log(rotary_base) * 2.0 / HEAD_DIM))
    turns = jnp.where(lane < 32, -1.0, 1.0)
    for i in range(seqs):
        spot = places[i, b]
        group = spot.shape[1]
        angles = jnp.transpose(jnp.broadcast_to(spot, (128, group))) * freqs
        cos[i * group : (i + 1) * group] = jnp.cos(angles)
        sin[i * group : (i + 1) * group] = jnp.sin(angles) * turns
    each = sizes[0]
    flat = jnp.concatenate([small[u, k, 0:1, :each] for k in range(n_blk)], axis=1)
    scale[...] = jnp.zeros_like(scale)
    for h in range(flat.shape[1] // HEAD_DIM):
        piece = flat[:, h * HEAD_DIM : (h + 1) * HEAD_DIM]
        scale[h : h + 1] = jnp.concatenate([piece * HEAD_DIM**0.5, piece], axis=1)
    rates[...] = jnp.zeros_like(rates)
    for j in (1, 2):
        for v in range(4):
            for k in range(n_blk):
                at = (v * n_blk + k) * each
                rates[j - 1 : j, at : at + each] = small[v, k, starts[j] : starts[j] + 1, :each]
    for j in (3, 4):
        for k in range(n_line):
            for r in range(starts[j + 1] - starts[j]):
                wide = min(128, sizes[j] - 128 * r)
                at = k * sizes[j] + 128 * r
                rates[j - 1 : j, at : at + wide] = small[u, k * 2 + s, starts[j] + r : starts[j] + r + 1, :wide]


def entry_kernel(
    n_line, starts, sizes, hid, small, wq, wk, wv, wo, wd, wu,
    hid_o, places_o, cos_o, sin_o, scale_o, rates_o, wq_o, wk_o, wv_o, oc_o, dc_o, wu_o, small_o, oc, dc, *sems
):
    y, c, z, s = place()
    u, p = y * 2 + c, plane_index(y, c, s)
    low, high, cross = line_ends(n_line)
    corners = plane_corners()
    greet([(yy, cc, z, ss) for yy, cc, ss in corners], [low, high])
    hid_job = UlyGather(hid, hid_o, *sems[:3])
    at, jobs = 3, []
    for x, pick in (
        (small, lambda block: small_o.at[u, block]),
        (wq, lambda block: wq_o.at[block]),
        (wk, lambda block: wk_o.at[block]),
        (wv, lambda block: wv_o.at[block]),
    ):
        jobs.append(BlkGather(n_line, lambda x=x: x, pick, *sems[at : at + 5]))
        at += 5
    first = wu_o.shape[-1]
    up_jobs = [
        LineGather(n_line, lambda: wu.at[:, slice(0, first)], lambda z: wu_o.at[z], *sems[at : at + 4])
    ]
    oc_s, oc_r, dc_s, dc_r, sm_s, sm_r, keep = sems[at + 4 :]
    jobs[0].start()
    for job in jobs[1:]:
        job.start()
    hid_job.start()
    for v in range(4):
        wide = oc.shape[-1]
        oc[v] = wo[:, v * wide : (v + 1) * wide]
        ff_each = dc.shape[-1] // n_line
        for t in (0, 1):
            for k in range(n_line):
                at = ((v * n_line + k) * 2 + t) * ff_each
                dc[v * 2 + t, :, k * ff_each : (k + 1) * ff_each] = wd[:, at : at + ff_each]
    col_jobs = []
    for k, (yy, cc, ss) in enumerate(corners):
        target = (yy, cc, z, ss)
        col_jobs.append(
            remote(dc.at[plane_index(yy, cc, ss)], dc_o.at[p], dc_s.at[k], dc_r.at[k], target)
        )
        if k < 3:
            col_jobs.append(remote(oc.at[yy * 2 + cc], oc_o.at[u], oc_s.at[k], oc_r.at[k], target))
    for job in col_jobs:
        job.start()
    for job in up_jobs:
        job.start()
    mine = [
        pltpu.make_async_copy(dc.at[p], dc_o.at[p], keep.at[0]),
        pltpu.make_async_copy(oc.at[u], oc_o.at[u], keep.at[1]),
    ]
    for job in mine:
        job.start()
    for k in range(1, n_line):
        for job in jobs:
            job.step(k)
        if k == 1:
            hid_job.forward()
    jobs[0].finish_arrivals()
    small_jobs = [
        remote(small_o.at[u], small_o.at[u], sm_s.at[k], sm_r.at[k], (yy, cc, z, ss))
        for k, (yy, cc, ss) in enumerate(corners[:3])
    ]
    for job in small_jobs:
        job.start()
    for k in range(1, n_line):
        for job in up_jobs:
            job.step(k)
        if k == 1:
            for job in small_jobs:
                job.wait_recv()
            tables(n_line, starts, sizes, small_o, places_o, cos_o, sin_o, scale_o, rates_o)
    for job in jobs[1:]:
        job.finish_arrivals()
    hid_job.finish()
    for job in up_jobs:
        job.finish()
    for job in small_jobs:
        job.wait_send()
    for job in col_jobs:
        job.wait()
    for job in mine:
        job.wait()
    for job in jobs:
        job.finish_sends()


def entry(n_line, starts, sizes, hid, small, wq, wk, wv, wo, wd, wu):
    n_blk = 2 * n_line
    oc = jax.ShapeDtypeStruct((4, wo.shape[0], wo.shape[1] // 4), wo.dtype)
    dc = jax.ShapeDtypeStruct((8, wd.shape[0], wd.shape[1] // 8), wd.dtype)
    parts = hid.shape[0]
    vmem, anyway = pl.BlockSpec(memory_space=pltpu.VMEM), pl.BlockSpec(memory_space=pl.ANY)

    def out(shape, like):
        return jax.ShapeDtypeStruct(shape, like.dtype)

    return pl.pallas_call(
        functools.partial(entry_kernel, n_line, starts, sizes),
        out_shape=[
            out((parts, 4) + hid.shape[1:], hid),
            out((parts, n_blk, 1, 4 * hid.shape[1]), small),
            out((parts * 4 * hid.shape[1], 128), small),
            out((parts * 4 * hid.shape[1], 128), small),
            out((8, 128), small),
            out((8, hid.shape[2]), small),
            out((n_blk,) + wq.shape, wq),
            out((n_blk,) + wk.shape, wk),
            out((n_blk,) + wv.shape, wv),
            out(oc.shape, oc),
            out(dc.shape, dc),
            out((n_line, wu.shape[0], lane_chunks(wu.shape[1])[0].stop), wu),
        ],
        in_specs=[vmem] * 8,
        out_specs=[vmem] * 6 + [anyway, anyway, anyway, vmem, vmem, anyway],
        scratch_shapes=[
            pltpu.VMEM((4, n_blk) + small.shape, small.dtype),
            pltpu.VMEM(oc.shape, oc.dtype),
            pltpu.VMEM(dc.shape, dc.dtype),
        ]
        + UlyGather.sems(parts)
        + BlkGather.sems(n_line) * 4
        + LineGather.sems(n_line)
        + [pltpu.SemaphoreType.DMA((3,))] * 2
        + [pltpu.SemaphoreType.DMA((7,))] * 2
        + [pltpu.SemaphoreType.DMA((3,))] * 2
        + [pltpu.SemaphoreType.DMA((2,))],
        compiler_params=params(6),
        cost_estimate=pl.CostEstimate(flops=0, bytes_accessed=40 * 3_000_000, transcendentals=0),
        name="entry",
    )(hid, small, wq, wk, wv, wo, wd, wu)
def dot_nt(a, b):
    return lax.dot_general(a, b, (((1,), (1,)), ((), ())), preferred_element_type=F32)


def dot_nn(a, b):
    return lax.dot_general(a, b, (((1,), (0,)), ((), ())), preferred_element_type=F32)


def dot_tn(a, b):
    return lax.dot_general(a, b, (((0,), (0,)), ((), ())), preferred_element_type=F32)


def lanes_of(shape):
    return lax.broadcasted_iota(jnp.int32, shape, len(shape) - 1)


def halves(x):
    row = lax.broadcasted_iota(jnp.int32, (128, 128), 0) // HEAD_DIM
    same = jnp.where(row == lanes_of((128, 128)) // HEAD_DIM, 1.0, 0.0).astype(BF)
    high = x.astype(BF)
    rest = (x - high.astype(F32)).astype(BF)
    return dot_nn(high, same) + dot_nn(rest, same)


def turn(x):
    first = lanes_of(x.shape) % HEAD_DIM < HEAD_DIM // 2
    return jnp.where(first, pltpu.roll(x, 128 - 32, 1), pltpu.roll(x, 32, 1))


def down_columns(row):
    n = row.shape[1]
    one = jnp.transpose(jnp.broadcast_to(row, (128, n)))
    return jnp.concatenate([one] * (n // 128), axis=1)


def arrivals(n_line, body):
    each = 2 * n_line - 1

    def step(t, carry):
        stage, r = t // each, lax.rem(t, each)
        body(stage, (r + 1) // 2, lax.rem(r + 1, 2))
        return carry

    lax.fori_loop(0, 2 * each, step, 0)


def attend_kernel(
    n_line, ready, x_ref, wq_ref, wk_ref, wv_ref, cos_ref, sin_ref, scale_ref, oc_ref, wg_ref, wu_ref, kp_ref,
    q_h, y_h, c_h, kv_h, oc_o, wg_o, wu_o, o_ref, mixed_ref, inv_ref,
    kv_ref, acc, total, place_q, q_ref, y_ref, c_ref, kv_o, kept, *sems,
):
    y, c, z, s = place()
    blk_greet(n_line)
    seqs, rows, wide = q_ref.shape
    heads = wide // 128
    chunk = 4 * LINE_CHUNKS
    cut = wu_ref.shape[-1] - wu_o.shape[-1]
    up = LineGather(
        n_line, lambda: wu_ref.at[:, slice(cut, wu_ref.shape[-1])], lambda zz: wu_o.at[zz], *sems[-4:]
    )
    up.start()
    ready()

    each = len(BlkGather.sems(n_line))
    picks = [
        (lambda i=i: kv_ref.at[i], lambda block, i=i: kv_o.at[block, i]) for i in range(seqs)
    ] + [(lambda: oc_ref, lambda block: oc_o.at[:, block])]
    jobs = [
        BlkGather(n_line, *pick, *sems[each * i : each * (i + 1)]) for i, pick in enumerate(picks)
    ]

    def make(t, carry):
        i, h = t // heads, lax.rem(t, heads)
        lanes = pl.ds(pl.multiple_of(h * 128, 128), 128)
        mine = pl.ds(pl.multiple_of(i * rows, rows), rows)
        wv = wv_ref[h]
        got = dot_nt(x_ref[mine], jnp.concatenate([wq_ref[h], wk_ref[h], jnp.zeros_like(wv), wv], axis=0))
        raw, value = got[:, :128], got[:, 128:]
        low = lanes_of(raw.shape) < HEAD_DIM
        turned = raw * cos_ref[mine] + turn(raw) * sin_ref[mine]
        norm = lax.rsqrt(halves(turned * turned) + HEAD_DIM * tiny_eps)
        unit = turned * norm
        both = unit * scale_ref[pl.ds(h, 1)]
        q_ref[i, :, lanes] = jnp.where(low, both, 0.0).astype(BF)
        kv_ref[i, :, lanes] = jnp.where(low, pltpu.roll(both, HEAD_DIM, 1), value).astype(BF)
        y_ref[mine, lanes] = unit
        c_ref[mine, lanes] = norm
        for j in range(seqs):
            pl.when(t == heads * (j + 1) - 1)(jobs[j].start)
        return carry

    lax.fori_loop(0, seqs * heads, make, 0)
    gates = line_gathers(
        n_line, wg_ref, lambda z: wg_o.at[z], sems[each * (seqs + 1) : each * (seqs + 1) + chunk]
    )
    jobs[-1].start()
    for job in gates:
        job.keep().start()
    n_blk = 2 * n_line
    keeps = [
        pltpu.make_async_copy(a, o, kept.at[n_blk + i])
        for i, (a, o) in enumerate(((q_ref, q_h), (y_ref, y_h), (c_ref, c_h)))
    ]
    for copy in keeps:
        copy.start()

    def keep_keys(block):
        return pltpu.make_async_copy(kv_o.at[block], kv_h.at[block], kept.at[block])

    acc[...] = jnp.zeros_like(acc)
    total[...] = jnp.zeros_like(total)
    for i in range(seqs):
        place_q[i] = down_columns(kp_ref[i, z * 2 + s])

    def attend_to(i, block, keys):
        allowed = kp_ref[i, block] <= place_q[i]
        for h in range(heads):
            lanes = slice(h * 128, (h + 1) * 128)
            kv = keys(lanes)
            p = jnp.where(allowed, jnp.exp(dot_nt(q_ref[i, :, lanes], kv)), 0.0)
            part = p[:, :128]
            for j in range(1, rows // 128):
                part = part + p[:, j * 128 : (j + 1) * 128]
            total[i, h] = total[i, h] + part
            acc[i, h] = acc[i, h] + dot_nn(p.astype(BF), kv)

    def body(stage, k, way):
        ahead = jnp.where(k == 0, 1, k + 1)

        @pl.when((stage == 1) & ((k == 0) | (way == 1)) & (ahead < n_line))
        def _():
            for job in gates + [up]:
                job.step(ahead)

        @pl.when((stage == 0) & (k > 0) & (way == 0))
        def _():
            for job in jobs:
                job.step(k)

        for w, last in ((0, z), (1, n_line - 1 - z)):
            @pl.when((stage == 0) & (k == last) & ((k == 0) | (way == 0)))
            def _():
                for job in gates:
                    pl.when(job.goes(w))(lambda: job.own(w).start())

        there = (k == 0) | jnp.where(way == 0, z >= k, z + k < n_line)

        @pl.when(there)
        def _():
            for job in jobs:
                for w in (0, 1):
                    pl.when((stage == 1) & (k > 0) & (way == w))(lambda: job.over(w, k).wait_recv())
                pl.when((stage == 1) & (k == 0))(lambda: job.own(2).wait_recv())
                pl.when((stage == 0) & (k == 0))(lambda: job.keep().wait())
            zz = jnp.where(way == 0, z - k, z + k)
            block = zz * 2 + jnp.where(stage == 0, s, 1 - s)
            keep_keys(block).start()

            def one(i, carry):
                attend_to(i, block, lambda lanes: kv_o[block, i, :, lanes])
                return carry

            lax.fori_loop(0, seqs, one, 0)

    arrivals(n_line, body)
    low = lanes_of((rows, 128)) < HEAD_DIM
    for i in range(seqs):
        outs = []
        for h in range(heads):
            inverse = 1.0 / jnp.broadcast_to(jnp.sum(total[i, h], axis=-1, keepdims=True), (rows, 128))
            out = acc[i, h] * inverse
            o_ref[i, h] = out
            inv_ref[i, h] = jnp.transpose(inverse)[:8]
            outs.append(out)
        for h in range(0, heads - 1, 2):
            mixed_ref[i, :, h * HEAD_DIM : (h + 2) * HEAD_DIM] = jnp.where(
                low, pltpu.roll(outs[h], HEAD_DIM, 1), outs[h + 1]
            ).astype(BF)
        if heads % 2 == 1:
            mixed_ref[i, :, (heads - 1) * HEAD_DIM :] = pltpu.roll(outs[-1], HEAD_DIM, 1)[:, :HEAD_DIM].astype(BF)
    for job in jobs:
        job.finish_sends()
    for job in gates + [up]:
        job.finish()
    for copy in keeps + [keep_keys(block) for block in range(n_blk)]:
        copy.wait()


def attend(n_line, seqs, x, wq, wk, wv, cos, sin, scale, oc, wg, wu, k_places):
    tokens, width = x.shape
    n_blk, heads, rows = 2 * n_line, wq.shape[0], tokens // seqs
    head, wide = (seqs, heads, rows, 128), (seqs, rows, heads * 128)
    flat = ((tokens, heads * 128), F32)
    first = lane_chunks(width)[0].stop
    return comm_call(
        functools.partial(attend_kernel, n_line), "attend", 5,
        (x, wq, wk, wv, cos, sin, scale, oc, wg, wu, k_places),
        [
            (wide, BF), flat, flat, ((n_blk,) + wide, BF), (oc.shape[:1] + (n_blk,) + oc.shape[1:], BF),
            ((n_line,) + wg.shape, BF), ((n_line, wu.shape[0], width - first), BF), (head, F32),
            ((seqs, rows, heads * HEAD_DIM), BF), ((seqs, heads, 8, rows), F32),
        ],
        [
            pltpu.VMEM(wide, BF), pltpu.VMEM(head, F32), pltpu.VMEM(head, F32), pltpu.VMEM((seqs, rows, rows), F32),
            pltpu.VMEM(wide, BF), pltpu.VMEM(*flat), pltpu.VMEM(*flat), pltpu.VMEM((n_blk,) + wide, BF),
            pltpu.SemaphoreType.DMA((n_blk + 3,)),
        ]
        + BlkGather.sems(n_line) * (seqs + 1) + line_gather_sems(n_line) + LineGather.sems(n_line),
        90, far_outs=(0, 1, 2, 3, 4, 5, 6), late=(0, 1, 2, 3, 4, 5),
    )


def attend_back_kernel(
    n_line, fits, ready, q_ref, low_ref, w_ref, mixed_ref, o_ref, inv_ref, kv_ref, kp_ref, gu_ref,
    dq_ref, dkv_ref, oc_ref, gu_o, dz, delta, dq, parts, oparts, key_s, key_sem, *scratch,
):
    y, c, z, s = place()
    blk_greet(n_line)
    seqs, rows, wide = q_ref.shape
    heads, width = wide // 128, low_ref.shape[-1]
    each = 6
    ups = line_reduces(n_line, gu_ref, scratch[each * (seqs + 1) :])
    for line_job, _ in ups:
        line_job.step(n_line - 1)
    ready()
    low_rows = low_ref[...].reshape(seqs * rows, width)
    grad = dot_tn(low_rows, mixed_ref[...].reshape(seqs * rows, mixed_ref.shape[-1])).astype(BF)
    n_blk, each_out = 2 * n_line, width // (8 * n_line)
    for b in range(n_blk):
        for v in range(4):
            at = (v * n_blk + b) * each_out
            oparts[b, v * each_out : (v + 1) * each_out] = grad[at : at + each_out]
    each = 6
    jobs = [BlkReduce(n_line, parts.at[:, i], *scratch[each * i : each * (i + 1)]) for i in range(seqs)]
    out_job = BlkReduce(n_line, oparts, *scratch[each * seqs : each * (seqs + 1)])
    for k in range(n_line - 1, -1, -1):
        out_job.start(k)
    low = lanes_of((rows, 128)) < HEAD_DIM
    for i in range(seqs):
        d = dot_nn(low_rows[i * rows : (i + 1) * rows], w_ref[...]).astype(BF).astype(F32)
        for h in range(heads):
            at = h // 2 * 128
            if h == heads - 1 and heads % 2 == 1:
                tile = jnp.concatenate([jnp.zeros((rows, HEAD_DIM), F32), d[:, at:]], axis=1)
            else:
                tile = d[:, at : at + 128]
                if h % 2 == 0:
                    tile = pltpu.roll(tile, HEAD_DIM, 1)
                tile = jnp.where(low, 0.0, tile)
            dz[i, h] = tile.astype(BF)
            row = jnp.sum(tile * o_ref[i, h], axis=-1, keepdims=True)
            delta[i, h] = jnp.transpose(jnp.broadcast_to(row, (rows, 128)))[:8]
    dq[...] = jnp.zeros_like(dq)

    def block_of(block):
        if fits:
            keys = kv_ref.at[block]
        else:
            keys = key_s
            copy = pltpu.make_async_copy(kv_ref.at[block], key_s, key_sem.at[0])
            copy.start()
            copy.wait()
        def one(i, carry):
            allowed = down_columns(kp_ref[i, block]) <= kp_ref[i, z * 2 + s]
            for h in range(heads):
                lanes = slice(h * 128, (h + 1) * 128)
                kv = keys[i, :, lanes]
                pair = jnp.concatenate([q_ref[i, :, lanes], dz[i, h]], axis=0)
                scores = dot_nt(kv, pair)
                p = jnp.where(allowed, jnp.exp(scores[:, :rows]) * inv_ref[i, h][:1], 0.0)
                ds = (p * (scores[:, rows:] - delta[i, h][:1])).astype(BF)
                parts[block, i, :, lanes] = dot_nn(
                    jnp.concatenate([ds, p.astype(BF)], axis=1), pair
                ).astype(BF)
                dq[i, h] = dq[i, h] + dot_tn(ds, kv)
            return carry

        lax.fori_loop(0, seqs, one, 0)

    def step(t, carry):
        k, r = n_line - 1 - t // 4, lax.rem(t, 4)
        way, stays = r // 2, lax.rem(r, 2)

        @pl.when((r == 0) & (k > 0) & (k < n_line - 1))
        def _():
            for line_job, _ in ups:
                line_job.step(k)

        there = jnp.where(k == 0, way == 0, jnp.where(way == 0, z + k < n_line, z >= k))

        @pl.when(there)
        def _():
            zz = jnp.where(way == 0, z + k, z - k)
            block_of(zz * 2 + jnp.where(stays == 0, 1 - s, s))

            @pl.when(stays == 0)
            def _():
                for job in jobs:
                    job.side(zz).start()

        @pl.when((r == 3) & (k + 1 < n_line))
        def _():
            for w in (0, 1):
                @pl.when(jobs[0].exists(w, k + 1))
                def _():
                    for job in jobs + [out_job]:
                        job.move_on(w, k + 1)

        return carry

    lax.fori_loop(0, 4 * n_line, step, 0)
    for i in range(seqs):
        for h in range(heads):
            dq_ref[i, :, h * 128 : (h + 1) * 128] = dq[i, h].astype(BF)
    out_job.result(oc_ref)
    for i, job in enumerate(jobs):
        job.result(dkv_ref.at[i])
    for job, cut in ups:
        job.result(gu_o.at[cut])
    for job in jobs + [out_job] + [job for job, _ in ups]:
        job.finish()


def attend_back(n_line, q, low, w, mixed, o, inv, kv, k_places, gu):
    seqs, rows, wide = q.shape
    n_blk, heads = 2 * n_line, wide // 128
    head = (seqs, heads, rows, 128)
    width, columns = w.shape
    out_shape = (width // n_blk, columns)
    one = jax.ShapeDtypeStruct((n_blk,) + kv.shape[2:], BF)
    out_one = jax.ShapeDtypeStruct((n_blk,) + out_shape, BF)
    fits = kv.size * 2 <= 8_000_000
    return comm_call(
        functools.partial(attend_back_kernel, n_line, fits), "attend_back", 7,
        (q, low, w, mixed, o, inv, kv, k_places, gu),
        [(q.shape, BF), (kv.shape[1:], BF), (out_shape, BF), (gu.shape[1:], F32)],
        [
            pltpu.VMEM(head, BF), pltpu.VMEM((seqs, heads, 8, rows), F32), pltpu.VMEM(head, F32),
            pltpu.VMEM(kv.shape, BF), pltpu.VMEM(out_one.shape, BF),
            pltpu.VMEM((16, 128) if fits else kv.shape[1:], BF), pltpu.SemaphoreType.DMA((1,)),
        ]
        + BlkReduce.scratch(n_line, one) * seqs + BlkReduce.scratch(n_line, out_one)
        + line_reduce_scratch(n_line, gu),
        75, 67_000_000, () if fits else (6,), late=(0, 1, 2, 3, 4) + (6,) * fits,
    )


def unit_of(x):
    c = lax.rsqrt(jnp.sum(x * x, axis=-1, keepdims=True) + x.shape[-1] * tiny_eps)
    return x * c, c


def unit_back(y, c, dy):
    return c * (dy - y * jnp.sum(y * dy, axis=-1, keepdims=True))


class Late:
    @staticmethod
    def scratch(arrays):
        return [pltpu.VMEM(a.shape, a.dtype) for a in arrays] + [pltpu.SemaphoreType.DMA((len(arrays),))]

    def __init__(self, refs, scratch):
        *self.bufs, sem = scratch
        self.copies = [
            pltpu.make_async_copy(ref, buf, sem.at[i]) for i, (ref, buf) in enumerate(zip(refs, self.bufs))
        ]
        for copy in self.copies:
            copy.start()

    def __call__(self, i):
        self.copies[i].wait()
        return self.bufs[i]


def attn_joint_kernel(
    n_line, ready, mixed, w, hid, rate, dc, first_o, ua_o, ca_o, cv_o, all_o, down_o, part, low, *scratch
):
    ends = line_ends(n_line)
    greet(plane_peers(), ends[:2])
    ready()
    split = len(UlyReduce.scratch(part))
    job = UlyReduce(part, *scratch[:split])
    out = PlaneGather(low, all_o, *scratch[split : split + 3])
    downs = line_gathers(n_line, dc, lambda z: down_o.at[:, z], scratch[split + 3 :])
    for line_job in downs:
        line_job.start()
    steps = [(k, line_job) for k in range(1, n_line) for line_job in downs]
    parts, _, rows, width = part.shape
    seqs = mixed.shape[0]
    each = parts // seqs
    for i in range(seqs):
        got = dot_nt(mixed[i], w[...]).astype(BF)
        for k in range(each):
            for u in range(4):
                at = (u * each + k) * rows
                part[i * each + k, u] = got[at : at + rows]
            for copy in job.near[i * each + k]:
                copy.start()
    job.middle()
    k, line_job = steps.pop(0)
    line_job.step(k)
    for i in range(parts):
        ua, ca = unit_of(job.result(i))
        h = hid[i].astype(F32)
        first, cv = unit_of(h + rate[0:1] * (ua - h))
        low[i] = first.astype(BF)
        out.start_part(i)
        first_o[i], ua_o[i] = first, ua
        ca_o[i] = jnp.broadcast_to(ca, (rows, 128))
        cv_o[i] = jnp.broadcast_to(cv, (rows, 128))
        if i > 0:
            out.forward_part(i - 1)
        if len(steps) > 0:
            k, line_job = steps.pop(0)
            line_job.step(k)
    out.forward_part(parts - 1)
    for k, line_job in steps:
        line_job.step(k)
    out.finish()
    job.finish()
    for line_job in downs:
        line_job.finish()


def attn_joint(n_line, mixed, w, hid, rate, dc):
    parts, rows, width = hid.shape
    part = jax.ShapeDtypeStruct((parts, 4, rows, width), BF)
    thin = ((parts, rows, 128), F32)
    return comm_call(
        functools.partial(attn_joint_kernel, n_line), "attn_joint", 1, (mixed, w, hid, rate, dc),
        [
            (hid.shape, F32), (hid.shape, F32), thin, thin, ((8, parts, rows, width), BF),
            (dc.shape[:1] + (n_line,) + dc.shape[1:], BF),
        ],
        [pltpu.VMEM(part.shape, BF), pltpu.VMEM(hid.shape, BF)]
        + UlyReduce.scratch(part) + PlaneGather.sems(parts) + line_gather_sems(n_line),
        25, far_outs=(4, 5), late=(0, 1, 2, 4),
    )


def plane_products(job, part, y, c, prepare, product):
    _, parts, rows, width = part.shape
    for yy, spots in ((1 - y, (0, 2)), (y, (1, 3))):
        def one(j, carry):
            cc = jnp.where(j == 0, 1 - c, c)
            prepare(yy, cc)
            got = product(yy, cc).astype(BF).reshape(2, parts, rows, width)
            for ss in (0, 1):
                part[plane_index(yy, cc, ss)] = got[ss]

            @pl.when(j == 0)
            def _():
                for k in spots:
                    for copy in job.near[k]:
                        copy.start()

            return carry

        lax.fori_loop(0, 2, one, 0)
        job.middle(spots[0] == 0)


def ff_joint_kernel(
    ready, x, wu, wu2, wg, rate, w, first, cot, out_o, d1_o, sum_o, all_o, inner_h, up_h, gate_h,
    part, low, inner, up_s, gate_s, kept, *scratch,
):
    y, c, z, s = place()
    greet(plane_peers())
    split = len(PlaneReduce.scratch(part))
    job = PlaneReduce(part, *scratch[:split])
    out = PlaneGather(low, all_o, *scratch[split:])
    _, seqs, rows, width = part.shape
    columns, tokens = inner.shape[-1], 2 * seqs * rows
    cut = wu.shape[1]

    def forward(yy, cc):
        block = x[yy, cc].reshape(tokens, width)
        up = dot_nt(block[:, :cut], wu[...]) + dot_nt(block[:, cut:], wu2[...])
        gate = dot_nt(block, wg[...])
        gz = gate * rate[3:4, :columns] * D**0.5
        got = gz / (1.0 + jnp.exp(-gz)) * (up * rate[2:3, :columns])
        inner[yy, cc] = got.astype(BF).reshape(inner.shape[2:])
        up_s[yy, cc] = up.reshape(up_s.shape[2:])
        gate_s[yy, cc] = gate.reshape(gate_s.shape[2:])

    ready()
    plane_products(
        job, part, y, c, forward, lambda yy, cc: dot_nt(inner[yy, cc].reshape(tokens, columns), w[...])
    )
    keeps = [
        pltpu.make_async_copy(a, o, kept.at[i])
        for i, (a, o) in enumerate(((inner, inner_h), (up_s, up_h), (gate_s, gate_h)))
    ]
    for copy in keeps:
        copy.start()
    job.last()
    for i in range(seqs):
        ub, cb = unit_of(job.result(i))
        f, b = first[i], rate[1:2]
        o, cw = unit_of(f + b * (ub - f))
        dw = unit_back(o, cw, cot[i].astype(F32))
        step = b * dw
        low[i] = unit_back(ub, cb, step).astype(BF)
        out.start_part(i)
        out_o[i] = o.astype(BF)
        d1_o[i] = dw - step
        total = jnp.sum(dw * (ub - f), axis=0, keepdims=True)
        sum_o[...] = total if i == 0 else sum_o[...] + total
        if i > 0:
            out.forward_part(i - 1)
    out.forward_part(seqs - 1)
    out.finish()
    job.finish()
    for copy in keeps:
        copy.wait()


def ff_joint(x, wu, wu2, wg, rate, w, first, cot):
    seqs, rows, width = first.shape
    part = jax.ShapeDtypeStruct((8, seqs, rows, width), BF)
    columns = wg.shape[0]
    wide = (2, 2, 2, seqs * rows, columns)
    return comm_call(
        ff_joint_kernel, "ff_joint", 2,
        (x.reshape(wide[:4] + (width,)), wu, wu2, wg, rate, w, first, cot),
        [
            (first.shape, BF), (first.shape, F32), ((1, width), F32), (part.shape, BF),
            (wide, BF), (wide, F32), (wide, F32),
        ],
        [
            pltpu.VMEM(part.shape, BF), pltpu.VMEM(first.shape, BF), pltpu.VMEM(wide, BF),
            pltpu.VMEM(wide, F32), pltpu.VMEM(wide, F32), pltpu.SemaphoreType.DMA((3,)),
        ]
        + PlaneReduce.scratch(part) + PlaneGather.sems(seqs),
        35, far_outs=(3, 4, 5, 6), late=(0, 1, 2, 3, 5),
    )


def back_joint_kernel(
    n_line, ready, d, inner, rate, d1, first, ua, ca, cv, hid, wd_h, up_h, gate_h, wu_h, wu2_h, wg_h, x_h,
    res_o, sum_o, ff_sum_o, all_o, up_o, gate_o, down_o, part, low, down_s, du, dg, *scratch,
):
    y, c, z, s = place()
    late = Late((wd_h, up_h, gate_h, wu_h, wu2_h, wg_h, x_h), scratch[:8])
    scratch = scratch[8:]
    greet(plane_peers(), line_ends(n_line)[:2])
    ready()
    split = len(PlaneReduce.scratch(part))
    job = PlaneReduce(part, *scratch[:split])
    _, parts, rows, width = part.shape
    columns = du.shape[-1]
    tokens = 8 * parts * rows
    each = parts // all_o.shape[0]
    out = UlyGather(
        low, all_o, *scratch[split : split + 3],
        pick=lambda i, u: all_o.at[i // each, u, pl.ds(i % each * rows, rows)],
    )
    downs = line_reduces(n_line, down_s, scratch[split + 3 :])
    flat = lambda ref: ref[...].reshape(tokens, ref.shape[-1])

    deep = width // (4 * n_line)
    inner_all = flat(inner)

    def down_half(i, carry):
        lanes = pl.ds(pl.multiple_of(i * (width // 2), 128), width // 2)
        grad = dot_tn(d[:, :, :, :, lanes].reshape(tokens, width // 2), inner_all).astype(BF)
        for v in (0, 1):
            for k in range(n_line):
                at = (v * n_line + k) * deep
                down_s[k, 2 * i + v] = grad[at : at + deep]
        return carry

    lax.fori_loop(0, 2, down_half, 0)
    for line_job, _ in downs:
        line_job.step(n_line - 1)

    wd, up_ref, gate_ref = late(0), late(1), late(2)
    u_scale, g_scale = rate[2:3, :columns], rate[3:4, :columns] * D**0.5

    ff_sum_o[...] = jnp.zeros_like(ff_sum_o)

    def gated_back(yy, cc):
        got = dot_nn(d[yy, cc].reshape(tokens // 4, width), wd[...])
        up, gate = up_ref[yy, cc].reshape(got.shape), gate_ref[yy, cc].reshape(got.shape)
        gz = gate * g_scale
        sig = 1.0 / (1.0 + jnp.exp(-gz))
        d_up = got * (gz * sig)
        d_gate = got * (up * u_scale) * sig * (1.0 + gz * (1.0 - sig))
        du[yy, cc] = (d_up * u_scale).astype(BF).reshape(du.shape[2:])
        dg[yy, cc] = (d_gate * g_scale).astype(BF).reshape(dg.shape[2:])
        ff_sum_o[0:1] = ff_sum_o[0:1] + jnp.sum(d_up * up, axis=0, keepdims=True)
        ff_sum_o[1:2] = ff_sum_o[1:2] + jnp.sum(d_gate * gate, axis=0, keepdims=True) * D**0.5

    wu, wu2, wg = late(3), late(4), late(5)

    def product(yy, cc):
        u, g = du[yy, cc].reshape(tokens // 4, columns), dg[yy, cc].reshape(tokens // 4, columns)
        got = jnp.concatenate([dot_nn(u, wu[...]), dot_nn(u, wu2[...])], axis=1)
        return got + dot_nn(g, wg[...])

    plane_products(job, part, y, c, gated_back, product)
    steps = [(k, line_job) for k in range(n_line - 2, 0, -1) for line_job, _ in downs]
    job.last()
    x = late(6)

    def by_line(o, ref):
        n, rows_all = columns // n_line, flat(ref)

        def half(i, carry):
            lanes = pl.ds(pl.multiple_of(i * (width // 2), 128), width // 2)
            grad = dot_tn(rows_all, x[:, lanes]).astype(BF)
            for k in range(n_line):
                o[k, :, lanes] = grad[k * n : (k + 1) * n]
            return carry

        lax.fori_loop(0, 2, half, 0)

    by_line(up_o, du)
    for i in range(parts):
        f, h, u, a = first[i], hid[i].astype(F32), ua[i], rate[0:1]
        dv = unit_back(f, cv[i][:, :1], d1[i] + job.result(i))
        step = a * dv
        low[i] = unit_back(u, ca[i][:, :1], step).astype(BF)
        out.start_part(i)
        res_o[i] = dv - step
        total = jnp.sum(dv * (u - h), axis=0, keepdims=True)
        sum_o[...] = total if i == 0 else sum_o[...] + total
        if len(steps) > 0:
            k, line_job = steps.pop(0)
            line_job.step(k)
    for k, line_job in steps:
        line_job.step(k)
    by_line(gate_o, dg)
    out.forward()
    out.finish()
    job.finish()
    for line_job, cut in downs:
        line_job.result(down_o.at[cut])
        line_job.finish()


def back_joint(n_line, seqs, d, wd, up, gate, rate, wu, wu2, wg, x, inner, d1, first, ua, ca, cv, hid):
    parts, rows, width = first.shape
    columns = wd.shape[1]
    part = jax.ShapeDtypeStruct((8, parts, rows, width), BF)
    down = jax.ShapeDtypeStruct((n_line, 4, width // (4 * n_line), columns), BF)
    by_line = ((n_line, columns // n_line, width), BF)
    wide = lambda a: a.reshape(2, 2, 2, parts * rows, a.shape[-1])
    thin = pltpu.VMEM((2, 2, 2, parts * rows, columns), BF)
    late = (wd, wide(up), wide(gate), wu, wu2, wg, x)
    return comm_call(
        functools.partial(back_joint_kernel, n_line), "back_joint", 3,
        (wide(d), wide(inner), rate, d1, first, ua, ca, cv, hid) + late,
        [
            (first.shape, F32), ((1, width), F32), ((2, columns), F32),
            ((seqs, 4, parts * rows // seqs, width), BF), by_line, by_line, (down.shape[1:], BF),
        ],
        [pltpu.VMEM(part.shape, BF), pltpu.VMEM(first.shape, BF), pltpu.VMEM(down.shape, BF), thin, thin]
        + Late.scratch(late) + PlaneReduce.scratch(part) + UlyGather.sems(parts)
        + line_reduce_scratch(n_line, down),
        40, VMEM_BYTES, tuple(range(9, 16)), far_outs=(3,), late=(0, 1),
    )


def settle_kernel(count, cuts, *refs):
    ins, sums = refs[:count], refs[count]
    outs, pieces = refs[count + 1 : 2 * count + 1], refs[2 * count + 1 : 2 * count + 1 + len(cuts)]
    *bufs, come, go = refs[2 * count + 1 + len(cuts) :]
    into = [pltpu.make_async_copy(x, b, come.at[i]) for i, (x, b) in enumerate(zip(ins, bufs))]
    out = [pltpu.make_async_copy(b, o, go.at[i]) for i, (b, o) in enumerate(zip(bufs, outs))]
    for copy in into:
        copy.start()
    for piece, (at, wide) in zip(pieces, cuts):
        piece[...] = sums[:, at : at + wide]
    for a, b in zip(into, out):
        a.wait()
        b.start()
    for copy in out:
        copy.wait()


def settle(sums, cuts, *arrays):
    count = len(arrays)
    anyway, vmem = pl.BlockSpec(memory_space=pl.ANY), pl.BlockSpec(memory_space=pltpu.VMEM)
    return pl.pallas_call(
        functools.partial(settle_kernel, count, cuts),
        out_shape=[jax.ShapeDtypeStruct(a.shape, a.dtype) for a in arrays]
        + [jax.ShapeDtypeStruct((1, wide), F32) for _, wide in cuts],
        in_specs=[anyway] * count + [vmem],
        out_specs=[anyway] * count + [vmem] * len(cuts),
        scratch_shapes=[pltpu.VMEM(a.shape, a.dtype) for a in arrays]
        + [pltpu.SemaphoreType.DMA((count,))] * 2,
        compiler_params=pltpu.CompilerParams(vmem_limit_bytes=VMEM_BYTES),
        name="settle",
    )(*arrays, sums)


def local(
    hidden, positions, w_query, w_key, w_value, w_out, w_up, w_gate, w_down,
    qk_scale, alpha_attn, alpha_mlp, up_scale, gate_scale, cotangent,
):
    seqs, rows_each, width = hidden.shape
    n_line = lax.axis_size("line")
    n_blk = 2 * n_line
    heads = HEADS // 4
    local_width = heads * HEAD_DIM
    group_rows = 4 * rows_each
    tokens = seqs * rows_each
    group_tokens = 4 * tokens
    plane_tokens = 8 * tokens
    attn_each, ff_each = w_query.shape[0], w_up.shape[0]
    ff_local = ff_each * n_line
    far, core, line, side = place()
    uly = far * 2 + core

    def row(x, wide):
        return jnp.pad(x, ((0, 0),) * (x.ndim - 1) + ((0, wide - x.shape[-1]),))

    pieces = [v.astype(F32) for v in (qk_scale, alpha_attn, alpha_mlp, up_scale, gate_scale)]
    pieces.append(positions.reshape(-1).astype(F32))
    rows_of = [-(-v.shape[0] // 128) for v in pieces]
    starts = [sum(rows_of[:i]) for i in range(len(pieces) + 1)]
    tall = starts[-1] + -starts[-1] % 8
    small = 0.0
    for v, start in zip(pieces, starts):
        small = small + jnp.pad(v, (start * 128, (tall - start) * 128 - v.shape[0]))
    small = small.reshape(tall, 128)

    sizes = tuple(v.shape[0] for v in pieces)
    assert ff_local <= width and tokens <= 128 and attn_each <= 64
    (
        hid_all, places, cos, sin, scale_both, rates, wq_all, wk_all, wv_all, out_cols, down_cols, up_first
    ) = entry(
        n_line, tuple(starts), sizes, hidden, small, w_query, w_key, w_value, w_out, w_down, w_up
    )
    up_first = up_first.reshape(ff_local, -1)

    group_hidden = hid_all.reshape(group_tokens, width)
    wq = wq_all.reshape(heads, HEAD_DIM, width)
    wk = wk_all.reshape(heads, HEAD_DIM, width)
    wv = wv_all.reshape(heads, HEAD_DIM, width)
    qz, y_both, c_both, kv_all, out_all, gate_full, up_last, attended, mixed, inverse = attend(
        n_line, seqs, group_hidden, wq, wk, wv, cos, sin, scale_both, out_cols, w_gate, w_up,
        places,
    )
    up_last = up_last.reshape(ff_local, -1)
    gate_full = gate_full.reshape(ff_local, width)
    out_full = out_all.reshape(width, local_width)

    fine = (2 * seqs, rows_each // 2, width)
    hidden_fine = hidden.reshape(fine)
    first, unit_att, att_c, first_c, mlp_in, down_full = attn_joint(
        n_line, mixed, out_full, hidden_fine, rates,
        down_cols.reshape(4, 2 * attn_each, ff_local),
    )
    down_full = down_full.reshape(width, ff_local)
    mlp_in = mlp_in.reshape(plane_tokens, width)
    layer_out, grad_first, grad_alpha_mlp, branch_low, inner, up_rows, gate_rows = ff_joint(
        mlp_in, up_first, up_last, gate_full, rates, down_full, first, cotangent.reshape(fine)
    )
    branch_low = branch_low.reshape(plane_tokens, width)
    grad_residual, grad_alpha_attn, ff_scales, att_low, grad_up, grad_gate, down_own = back_joint(
        n_line, seqs, branch_low, down_full, up_rows, gate_rows, rates, up_first, up_last, gate_full,
        mlp_in, inner, grad_first, first, unit_att, att_c, first_c, hidden_fine,
    )
    down_own = down_own.reshape(8, attn_each, ff_local)

    dq, dkv, out_own, up_own = attend_back(
        n_line, qz, att_low.reshape(seqs, group_rows, width), out_full, mixed, attended, inverse,
        kv_all, places, grad_up,
    )
    out_own = out_own.reshape(4, attn_each, local_width)
    gq, gk, gv, grad_hidden, out_gradient, down_gradient, sums, gate_own = leave(
        n_line, group_hidden, dq, dkv, y_both, c_both, cos, sin, scale_both, wq, wk, wv,
        grad_residual.reshape(seqs, rows_each, width), out_own, down_own,
        grad_alpha_attn, grad_alpha_mlp, ff_scales, grad_gate,
    )
    cuts = (
        (128, attn_each), (0, attn_each), (attn_each, attn_each), (256, ff_each), (256 + ff_each, ff_each)
    )
    settled = settle(
        sums, cuts,
        layer_out.reshape(hidden.shape), grad_hidden, gq, gk, gv, out_gradient, up_own, gate_own,
        down_gradient,
    )
    return tuple(settled[:9]) + tuple(piece.reshape(-1) for piece in settled[9:])


def solution(mesh):
    far = mesh.shape["uly"] // 2
    line = mesh.shape["blk"] // 2
    finer = Mesh(mesh.devices.reshape(far, 2, line, 2), AXES)
    rows, tokens, flat = P(AXES, None), P(None, AXES, None), P(AXES)
    return jax.shard_map(
        local,
        mesh=finer,
        in_specs=(tokens, P(None, AXES)) + (rows,) * 7 + (flat,) * 5 + (tokens,),
        out_specs=(tokens, tokens) + (rows,) * 7 + (flat,) * 5,
        check_vma=False,
    )
```

```python
import functools
import math

import jax
import jax.numpy as jnp
from jax import lax
from jax.experimental import pallas as pl
from jax.experimental.pallas import tpu as pltpu
from jax.sharding import Mesh
from jax.sharding import PartitionSpec as P

D = 1280
HEADS = 20
HEAD_DIM = 64
AXES = ("far", "core", "line", "side")
PLANE = ("far", "core", "side")
VMEM_BYTES = 60 * 1024 * 1024

rotary_base = 10000.0
tiny_eps = 1e-06
BF = jnp.bfloat16
F32 = jnp.float32


def place():
    return tuple(lax.axis_index(name) for name in AXES)


def remote(src, dst, send, recv, device):
    return pltpu.make_async_remote_copy(
        src_ref=src,
        dst_ref=dst,
        send_sem=send,
        recv_sem=recv,
        device_id=device,
        device_id_type=pl.DeviceIdType.MESH,
    )


def signal_to(device):
    pl.semaphore_signal(
        pltpu.get_barrier_semaphore(), inc=1, device_id=device, device_id_type=pl.DeviceIdType.MESH
    )


def greet(devices, maybe=()):
    count = len(devices)
    for device in devices:
        signal_to(device)
    for there, device in maybe:
        pl.when(there)(functools.partial(signal_to, device))
        count = count + jnp.where(there, 1, 0)
    pl.semaphore_wait(pltpu.get_barrier_semaphore(), count)


def params(collective_id, room=VMEM_BYTES):
    return pltpu.CompilerParams(
        collective_id=collective_id, has_side_effects=True, vmem_limit_bytes=room
    )


class UlyGather:
    sems = staticmethod(lambda parts: [pltpu.SemaphoreType.DMA((3, parts))] * 2 + [pltpu.SemaphoreType.DMA((parts,))])

    def __init__(self, x, o, send, recv, local, pick=None):
        pick = pick or (lambda i, u: o.at[i, u])
        y, c, z, s = place()
        u, v = y * 2 + c, (1 - y) * 2 + c
        mate, across = (y, 1 - c, z, s), (1 - y, c, z, s)
        self.parts = x.shape[0]
        parts = range(self.parts)
        self.far = [remote(x.at[i], pick(i, u), send.at[0, i], recv.at[0, i], across) for i in parts]
        self.near = [remote(x.at[i], pick(i, u), send.at[1, i], recv.at[1, i], mate) for i in parts]
        self.on = [remote(pick(i, v), pick(i, v), send.at[2, i], recv.at[2, i], mate) for i in parts]
        self.own = [pltpu.make_async_copy(x.at[i], pick(i, u), local.at[i]) for i in parts]

    def start_part(self, i):
        self.far[i].start()
        self.near[i].start()
        self.own[i].start()

    def start(self):
        for i in range(self.parts):
            self.start_part(i)

    def forward(self):
        for i in range(self.parts):
            self.far[i].wait_recv()
            self.on[i].start()

    def finish(self):
        for i in range(self.parts):
            self.near[i].wait_recv()
            self.on[i].wait_recv()
            self.own[i].wait()
            self.far[i].wait_send()
            self.near[i].wait_send()
            self.on[i].wait_send()


def uly_peers():
    y, c, z, s = place()
    return [(y, 1 - c, z, s), (1 - y, c, z, s)]


def add_low(*terms):
    total = terms[0].astype(F32)
    for term in terms[1:]:
        total = total + term.astype(F32)
    return total


class UlyReduce:
    @staticmethod
    def scratch(x):
        parts, _, rows, width = x.shape
        return [
            pltpu.VMEM((parts, 2, rows, width), x.dtype),
            pltpu.VMEM((parts, rows, width), x.dtype),
            pltpu.VMEM((parts, rows, width), x.dtype),
            pltpu.SemaphoreType.DMA((3, parts)),
            pltpu.SemaphoreType.DMA((3, parts)),
        ]

    def __init__(self, x, near, mid, far_in, send, recv):
        y, c, z, s = place()
        mate, across = uly_peers()
        self.x, self.near_ref, self.mid, self.far_in = x, near, mid, far_in
        self.y, self.c, self.parts = y, c, x.shape[0]
        parts = range(self.parts)
        self.near = [
            [
                remote(x.at[i, f * 2 + 1 - c], near.at[i, k], send.at[k, i], recv.at[k, i], mate)
                for k, f in enumerate((1 - y, y))
            ]
            for i in parts
        ]
        self.far = [remote(mid.at[i], far_in.at[i], send.at[2, i], recv.at[2, i], across) for i in parts]

    def start(self):
        for i in range(self.parts):
            for copy in self.near[i]:
                copy.start()

    def middle(self):
        for i in range(self.parts):
            self.near[i][0].wait_recv()
            self.mid[i] = add_low(self.x[i, (1 - self.y) * 2 + self.c], self.near_ref[i, 0]).astype(BF)
            self.far[i].start()

    def result(self, i):
        self.near[i][1].wait_recv()
        self.far[i].wait_recv()
        return add_low(self.x[i, self.y * 2 + self.c], self.near_ref[i, 1], self.far_in[i])

    def finish(self):
        for i in range(self.parts):
            for copy in self.near[i] + [self.far[i]]:
                copy.wait_send()


def plane_peers():
    y, c, z, s = place()
    return [(y, 1 - c, z, s), (1 - y, c, z, s), (y, c, z, 1 - s)]


def plane_index(y, c, s):
    return (y * 2 + c) * 2 + s


class PlaneGather:
    @staticmethod
    def sems(parts):
        return [pltpu.SemaphoreType.DMA((7, parts))] * 2 + [pltpu.SemaphoreType.DMA((parts,))]

    def __init__(self, x, o, send, recv, local):
        y, c, z, s = place()
        mate, across, cross = plane_peers()
        self.parts = parts = range(x.shape[0])
        me, py, px, pd = (
            plane_index(y, c, s),
            plane_index(1 - y, c, s),
            plane_index(y, c, 1 - s),
            plane_index(1 - y, c, 1 - s),
        )

        def copy(source, p, i, slot, device):
            return remote(source, o.at[p, i], send.at[slot, i], recv.at[slot, i], device)

        def on(p, i, slot, device):
            return copy(o.at[p, i], p, i, slot, device)

        self.by_y = [copy(x.at[i], me, i, 0, across) for i in parts]
        self.by_x = [copy(x.at[i], me, i, 1, cross) for i in parts]
        self.near = [copy(x.at[i], me, i, 2, mate) for i in parts]
        self.corner = [on(px, i, 3, across) if i % 2 else on(py, i, 3, cross) for i in parts]
        self.pass_y = [on(py, i, 4, mate) for i in parts]
        self.pass_x = [on(px, i, 5, mate) for i in parts]
        self.pass_d = [on(pd, i, 6, mate) for i in parts]
        self.own = [pltpu.make_async_copy(x.at[i], o.at[me, i], local.at[i]) for i in parts]

    def start_part(self, i):
        for copy in (self.by_y[i], self.by_x[i], self.near[i], self.own[i]):
            copy.start()

    def forward_part(self, i):
        ways = [(self.by_y[i], self.pass_y[i]), (self.by_x[i], self.pass_x[i])]
        first, then = ways[:: 1 - 2 * (i % 2)]
        first[0].wait_recv()
        self.corner[i].start()
        first[1].start()
        then[0].wait_recv()
        then[1].start()

    def finish(self):
        for i in self.parts:
            self.corner[i].wait_recv()
            self.pass_d[i].start()
        for i in self.parts:
            for copy in (self.near[i], self.pass_y[i], self.pass_x[i], self.pass_d[i]):
                copy.wait()
            for copy in (self.by_y[i], self.by_x[i], self.corner[i]):
                copy.wait_send()
            self.own[i].wait()


class PlaneReduce:
    @staticmethod
    def scratch(x):
        one = pltpu.VMEM(x.shape[1:], x.dtype)
        sems = pltpu.SemaphoreType.DMA((7, x.shape[1]))
        return [pltpu.VMEM((4,) + x.shape[1:], x.dtype)] + [one] * 6 + [sems] * 2

    def __init__(self, x, near, out_x, out_y, out_d, in_x, in_y, in_d, send, recv):
        y, c, z, s = place()
        mate, across, cross = plane_peers()
        self.c = c
        self.parts = parts = range(x.shape[1])
        self.spots = ((1 - y, 1 - s), (y, 1 - s), (1 - y, s), (y, s))
        self.x, self.near_ref = x, near
        self.out_x, self.out_y, self.out_d = out_x, out_y, out_d
        self.in_x, self.in_y, self.in_d = in_x, in_y, in_d

        def copy(source, target, i, slot, device):
            return remote(source, target, send.at[slot, i], recv.at[slot, i], device)

        self.near = [
            [copy(x.at[plane_index(sy, 1 - c, ss), i], near.at[k, i], i, k, mate) for i in parts]
            for k, (sy, ss) in enumerate(self.spots)
        ]
        self.corner = [copy(out_d.at[i], in_d.at[i], i, 4, across if i % 2 else cross) for i in parts]
        self.by_x = [copy(out_x.at[i], in_x.at[i], i, 5, cross) for i in parts]
        self.by_y = [copy(out_y.at[i], in_y.at[i], i, 6, across) for i in parts]

    def pair(self, k, i):
        sy, ss = self.spots[k]
        self.near[k][i].wait_recv()
        return add_low(self.x[plane_index(sy, self.c, ss), i], self.near_ref[k, i])

    def middle(self, far):
        for i in self.parts:
            if far:
                self.out_d[i] = self.pair(0, i).astype(BF)
                self.corner[i].start()
                if i % 2 == 1:
                    self.out_y[i] = self.pair(2, i).astype(BF)
                    self.by_y[i].start()
            elif i % 2 == 0:
                self.out_x[i] = self.pair(1, i).astype(BF)
                self.by_x[i].start()

    def last(self):
        for i in self.parts:
            k, out, by = (1, self.out_x, self.by_x) if i % 2 else (2, self.out_y, self.by_y)
            part = self.pair(k, i)
            self.corner[i].wait_recv()
            out[i] = (part + self.in_d[i].astype(F32)).astype(BF)
            by[i].start()

    def result(self, i):
        own = self.pair(3, i)
        self.by_x[i].wait_recv()
        self.by_y[i].wait_recv()
        return own + add_low(self.in_x[i], self.in_y[i])

    def finish(self):
        for copy in [c for spot in self.near for c in spot] + self.corner + self.by_x + self.by_y:
            copy.wait_send()


def plane_corners():
    y, c, z, s = place()
    return [
        (y, 1 - c, s), (1 - y, c, s), (1 - y, 1 - c, s),
        (y, c, 1 - s), (y, 1 - c, 1 - s), (1 - y, c, 1 - s), (1 - y, 1 - c, 1 - s),
    ]


def line_ends(n_line):
    y, c, z, s = place()
    return (z > 0, (y, c, z - 1, s)), (z < n_line - 1, (y, c, z + 1, s)), (y, c, z, 1 - s)


class BlkGather:
    @staticmethod
    def sems(n_line):
        return [
            pltpu.SemaphoreType.DMA((3,)),
            pltpu.SemaphoreType.DMA((1,)),
            pltpu.SemaphoreType.DMA((4, n_line)),
            pltpu.SemaphoreType.DMA((4, n_line)),
            pltpu.SemaphoreType.DMA((1,)),
        ]

    def __init__(self, n_line, pick_x, pick_o, own_send, own_recv, send, recv, local):
        y, c, z, s = place()
        self.z, self.s, self.n = z, s, n_line
        (self.has_low, self.low), (self.has_high, self.high), self.cross = line_ends(n_line)
        self.pick_x, self.pick_o = pick_x, pick_o
        self.sem = (own_send, own_recv, send, recv, local)

    def block(self, way, k):
        z = self.z - k if way == 0 else self.z + k
        return self.pick_o(z * 2 + self.s)

    def own(self, way):
        own_send, own_recv, send, recv, local = self.sem
        arrival = own_recv.at[0] if way == 2 else recv.at[way, 0]
        target = (self.high, self.low, self.cross)[way]
        return remote(self.pick_x(), self.pick_o(self.z * 2 + self.s), own_send.at[way], arrival, target)

    def keep(self):
        return pltpu.make_async_copy(self.pick_x(), self.pick_o(self.z * 2 + self.s), self.sem[4].at[0])

    def onward(self, way, k):
        send, recv = self.sem[2:4]
        target = self.high if way == 0 else self.low
        return remote(self.block(way, k), self.block(way, k), send.at[way, k], recv.at[way, k], target)

    def over(self, way, k):
        send, recv = self.sem[2:4]
        return remote(self.block(way, k), self.block(way, k), send.at[2 + way, k], recv.at[2 + way, k], self.cross)

    def arrive(self, way, k):
        send, recv = self.sem[2:4]
        return remote(self.block(way, k), self.block(way, k), send.at[way, k], recv.at[way, k - 1], self.cross)

    def there(self, way, k):
        return self.z >= k if way == 0 else self.z + k < self.n

    def start(self):
        pl.when(self.has_high)(lambda: self.own(0).start())
        pl.when(self.has_low)(lambda: self.own(1).start())
        self.own(2).start()
        self.keep().start()

    def take(self, way, k):
        self.arrive(way, k).wait_recv()
        pl.when((self.has_high, self.has_low)[way])(lambda: self.onward(way, k).start())
        self.over(way, k).start()

    def step(self, k):
        for way in (0, 1):
            pl.when(self.there(way, k))(lambda: self.take(way, k))

    def finish_arrivals(self):
        self.own(2).wait_recv()
        for k in range(1, self.n):
            for way in (0, 1):
                pl.when(self.there(way, k))(lambda: self.over(way, k).wait_recv())
        self.keep().wait()

    def finish_sends(self):
        pl.when(self.has_high)(lambda: self.own(0).wait_send())
        pl.when(self.has_low)(lambda: self.own(1).wait_send())
        self.own(2).wait_send()
        for k in range(1, self.n):
            for way in (0, 1):
                @pl.when(self.there(way, k))
                def _():
                    self.over(way, k).wait_send()

                    @pl.when((self.has_high, self.has_low)[way])
                    def _():
                        self.onward(way, k).wait_send()


def blk_greet(n_line):
    low, high, cross = line_ends(n_line)
    greet([cross], [low, high])


class BlkReduce:
    @staticmethod
    def scratch(n_line, a):
        return [
            pltpu.VMEM((n_line,) + a.shape[1:], a.dtype),
            pltpu.VMEM((n_line + 1,) + a.shape[1:], a.dtype),
            pltpu.SemaphoreType.DMA((n_line,)),
            pltpu.SemaphoreType.DMA((n_line,)),
            pltpu.SemaphoreType.DMA((2, n_line)),
            pltpu.SemaphoreType.DMA((2, n_line)),
        ]

    def __init__(self, n_line, x, side_in, line_in, side_send, side_recv, send, recv):
        y, c, self.z, self.s = place()
        self.n = n_line
        (self.has_low, self.low), (self.has_high, self.high), self.cross = line_ends(n_line)
        self.x = x
        self.side_in, self.line_in = side_in, line_in
        self.sem = (side_send, side_recv, send, recv)

    def spot(self, way, k):
        return self.z + k * (1 - 2 * way)

    def exists(self, way, k):
        return (self.spot(way, k) >= 0) & (self.spot(way, k) < self.n)

    def toward(self, way):
        y, c, z, s = place()
        return (y, c, z + 1 - 2 * way, s)

    def side(self, zz):
        side_send, side_recv = self.sem[:2]
        return remote(
            self.x.at[zz * 2 + 1 - self.s], self.side_in.at[zz], side_send.at[zz], side_recv.at[zz], self.cross
        )

    def slot(self, way, k):
        return jnp.where((way == 1) & (k == 0), self.n, self.spot(way, k))

    def move(self, way, k):
        send, recv = self.sem[2:]
        zz = self.spot(way, k)
        there = jnp.where((way == 1) & (k == 1), self.n, zz)
        return remote(
            self.side_in.at[zz], self.line_in.at[there], send.at[way, k], recv.at[way, k - 1], self.toward(way)
        )

    def arrive(self, way, k):
        send, recv = self.sem[2:]
        there = self.line_in.at[self.slot(way, k)]
        return remote(there, there, send.at[way, k], recv.at[way, k], self.toward(1 - way))

    def start(self, k):
        for way in (0, 1) if k > 0 else (0,):
            pl.when(self.exists(way, k))(lambda: self.side(self.spot(way, k)).start())

    def move_on(self, way, k):
        zz = self.spot(way, k)
        self.side(zz).wait_recv()
        passed = jnp.where(way == 0, self.has_low, self.has_high)

        @pl.when(passed)
        def _():
            self.arrive(way, k).wait_recv()
            self.side_in[zz] = add_low(
                self.x[zz * 2 + self.s], self.side_in[zz], self.line_in[zz]
            ).astype(self.side_in.dtype)

        @pl.when(jnp.logical_not(passed))
        def _():
            self.side_in[zz] = add_low(self.x[zz * 2 + self.s], self.side_in[zz]).astype(
                self.side_in.dtype
            )

        self.move(way, k).start()

    def step(self, k):
        def one(way, carry):
            pl.when(self.exists(way, k))(lambda: self.move_on(way, k))
            return carry

        lax.fori_loop(0, 2, one, 0)

    def result(self, o):
        z = self.z
        self.side(z).wait_recv()
        pl.when(self.has_low)(lambda: self.arrive(0, 0).wait_recv())
        pl.when(self.has_high)(lambda: self.arrive(1, 0).wait_recv())
        own = lambda: add_low(self.x[z * 2 + self.s], self.side_in[z])
        both = self.has_low & self.has_high

        @pl.when(both)
        def _():
            o[...] = (own() + add_low(self.line_in[z], self.line_in[self.n])).astype(o.dtype)

        @pl.when(jnp.logical_not(both))
        def _():
            other = self.line_in[jnp.where(self.has_low, z, self.n)].astype(F32)
            o[...] = (own() + other).astype(o.dtype)

    def finish(self):
        for k in range(self.n - 1, -1, -1):
            for way in (0, 1) if k > 0 else (0,):
                @pl.when(self.exists(way, k))
                def _():
                    self.side(self.spot(way, k)).wait_send()
                    if k > 0:
                        self.move(way, k).wait_send()


class LineGather:
    @staticmethod
    def sems(n_line):
        dma = pltpu.SemaphoreType.DMA
        return [dma((2,)), dma((2, n_line)), dma((2, n_line)), dma((1,))]

    def __init__(self, n_line, pick_x, pick_o, own_send, send, recv, local):
        y, c, self.z, s = place()
        self.n = n_line
        (self.has_low, self.low), (self.has_high, self.high), _ = line_ends(n_line)
        self.pick_x, self.pick_o = pick_x, pick_o
        self.own_send, self.send, self.recv, self.local = own_send, send, recv, local

    def goes(self, way):
        return (self.has_high, self.has_low)[way]

    def own(self, way):
        target = (self.high, self.low)[way]
        return remote(self.pick_x(), self.pick_o(self.z), self.own_send.at[way], self.recv.at[way, 0], target)

    def keep(self):
        return pltpu.make_async_copy(self.pick_x(), self.pick_o(self.z), self.local.at[0])

    def onward(self, way, k):
        block = self.pick_o(self.z - k if way == 0 else self.z + k)
        target = (self.high, self.low)[way]
        return remote(block, block, self.send.at[way, k], self.recv.at[way, k], target)

    def arrive(self, way, k):
        block = self.pick_o(self.z - k if way == 0 else self.z + k)
        return remote(block, block, self.send.at[way, k], self.recv.at[way, k - 1], (self.low, self.high)[way])

    def there(self, way, k):
        return self.z >= k if way == 0 else self.z + k < self.n

    def start(self):
        for way in (0, 1):
            pl.when(self.goes(way))(lambda: self.own(way).start())
        self.keep().start()

    def step(self, k):
        for way in (0, 1):
            @pl.when(self.there(way, k))
            def _():
                self.arrive(way, k).wait_recv()
                pl.when(self.goes(way))(lambda: self.onward(way, k).start())

    def finish(self):
        self.keep().wait()
        for way in (0, 1):
            pl.when(self.goes(way))(lambda: self.own(way).wait_send())
            for k in range(1, self.n):
                pl.when(self.there(way, k) & self.goes(way))(lambda: self.onward(way, k).wait_send())


class LineReduce:
    @staticmethod
    def scratch(n_line, a):
        dma = pltpu.SemaphoreType.DMA
        return [
            pltpu.VMEM((n_line,) + a.shape[1:], a.dtype),
            pltpu.VMEM((n_line + 1,) + a.shape[1:], a.dtype),
            dma((2, n_line)), dma((2, n_line)),
        ]

    def __init__(self, n_line, x, sums, line_in, send, recv):
        y, c, self.z, s = place()
        self.n, self.x, self.sums, self.line_in, self.send, self.recv = n_line, x, sums, line_in, send, recv
        (self.has_low, self.low), (self.has_high, self.high), _ = line_ends(n_line)

    def spot(self, way, k):
        return self.z + k * (1 - 2 * way)

    def exists(self, way, k):
        return (self.spot(way, k) >= 0) & (self.spot(way, k) < self.n)

    def passed(self, way):
        return jnp.where(way == 0, self.has_low, self.has_high)

    def slot(self, way, k):
        return jnp.where((way == 1) & (k == 0), self.n, self.spot(way, k))

    def toward(self, way):
        y, c, z, s = place()
        return (y, c, z + 1 - 2 * way, s)

    def move(self, way, k, source):
        zz = self.spot(way, k)
        there = jnp.where((way == 1) & (k == 1), self.n, zz)
        return remote(
            source.at[zz], self.line_in.at[there], self.send.at[way, k], self.recv.at[way, k - 1], self.toward(way)
        )

    def arrive(self, way, k):
        there = self.line_in.at[self.slot(way, k)]
        return remote(there, there, self.send.at[way, k], self.recv.at[way, k], self.toward(1 - way))

    def step(self, k):
        def one(way, carry):
            exists, passed = self.exists(way, k), self.passed(way)

            @pl.when(exists & passed)
            def _():
                zz = self.spot(way, k)
                self.arrive(way, k).wait_recv()
                self.sums[zz] = add_low(self.x[zz], self.line_in[zz]).astype(self.sums.dtype)
                self.move(way, k, self.sums).start()

            pl.when(exists & jnp.logical_not(passed))(lambda: self.move(way, k, self.x).start())
            return carry

        lax.fori_loop(0, 2, one, 0)

    def result(self, o):
        z = self.z
        pl.when(self.has_low)(lambda: self.arrive(0, 0).wait_recv())
        pl.when(self.has_high)(lambda: self.arrive(1, 0).wait_recv())
        both = self.has_low & self.has_high

        @pl.when(both)
        def _():
            o[...] = add_low(self.x[z], self.line_in[z], self.line_in[self.n]).astype(o.dtype)

        @pl.when(jnp.logical_not(both))
        def _():
            o[...] = add_low(self.x[z], self.line_in[jnp.where(self.has_low, z, self.n)]).astype(o.dtype)

    def finish(self):
        for k in range(self.n - 1, 0, -1):
            for way in (0, 1):
                pl.when(self.exists(way, k))(lambda: self.move(way, k, self.sums).wait_send())


def lane_chunks(width):
    cut = width // 256 * 128
    return [slice(0, cut), slice(cut, width)]


LINE_CHUNKS = 2


def line_gathers(n_line, x, pick_o, sems):
    jobs = []
    for i, lanes in enumerate(lane_chunks(x.shape[-1])):
        cut = (slice(None),) * (len(x.shape) - 1) + (lanes,)
        jobs.append(
            LineGather(
                n_line, lambda cut=cut: x.at[cut], lambda z, cut=cut: pick_o(z).at[cut],
                *sems[4 * i : 4 * i + 4],
            )
        )
    return jobs


def line_gather_sems(n_line):
    return LineGather.sems(n_line) * LINE_CHUNKS


def line_reduces(n_line, x, scratch):
    jobs = []
    for i, lanes in enumerate(lane_chunks(x.shape[-1])):
        cut = (slice(None),) * (len(x.shape) - 1) + (lanes,)
        jobs.append((LineReduce(n_line, x.at[cut], *scratch[4 * i : 4 * i + 4]), cut[1:]))
    return jobs


def line_reduce_scratch(n_line, a):
    scratch = []
    for lanes in lane_chunks(a.shape[-1]):
        one = jax.ShapeDtypeStruct(a.shape[:-1] + (lanes.stop - lanes.start,), a.dtype)
        scratch += LineReduce.scratch(n_line, one)
    return scratch


def comm_call(
    kernel, name, collective_id, args, outs, scratch, micros, room=VMEM_BYTES, far_args=(), far_outs=(), late=()
):
    vmem, anyway = pl.BlockSpec(memory_space=pltpu.VMEM), pl.BlockSpec(memory_space=pl.ANY)
    held = [pltpu.VMEM(args[i].shape, args[i].dtype) for i in late]
    held += [pltpu.SemaphoreType.DMA((len(late),))] * (len(late) > 0)

    def whole(*refs):
        refs = list(refs)
        mine, copies = refs[len(refs) - len(held) :], []
        refs = refs[: len(refs) - len(held)]
        for j, i in enumerate(late):
            copies.append(pltpu.make_async_copy(refs[i], mine[j], mine[-1].at[j]))
            copies[-1].start()
            refs[i] = mine[j]

        def ready():
            for copy in copies:
                copy.wait()

        kernel(ready, *refs)

    return pl.pallas_call(
        whole,
        out_shape=[jax.ShapeDtypeStruct(shape, dtype) for shape, dtype in outs],
        in_specs=[anyway if i in far_args or i in late else vmem for i in range(len(args))],
        out_specs=[anyway if i in far_outs else vmem for i in range(len(outs))],
        scratch_shapes=list(scratch) + held,
        compiler_params=params(collective_id, room),
        cost_estimate=pl.CostEstimate(flops=0, bytes_accessed=micros * 3_000_000, transcendentals=0),
        name=name,
    )(*args)


def exit_kernel(
    n_line, ready, x, dq, dkv, yy_ref, cc_ref, cos, sin, scale, wq, wk, wv, res, oc, dc, a_sum, m_sum, ff_sum, gg,
    gq_o, gk_o, gv_o, gh_o, go_o, gd_o, sum_o, gg_o, oc_o, dc_o,
    flat, acc, gq, gk, gv, gh, scale_s, alpha,
    alpha_in, line_out, line_all, oc_s, oc_r, dc_s, dc_r, al_s, al_r, su_s, su_r, keep, *scratch,
):
    y, c, z, s = place()
    u, p, b, n_blk = y * 2 + c, plane_index(y, c, s), z * 2 + s, 2 * n_line
    low, high, cross = line_ends(n_line)
    corners = plane_corners()
    others = []
    for i in range(1, n_blk):
        to = lax.rem(b + i, n_blk)
        others.append((y, c, to // 2, lax.rem(to, 2)))
    once = [(to[3] != 1 - s) | (to[2] != z) for to in others]
    greet([(yy, cc, z, ss) for yy, cc, ss in corners], list(zip(once, others)))
    each = 6
    jobs = [BlkReduce(n_line, g, *scratch[each * i : each * (i + 1)]) for i, g in enumerate((gq, gk, gv))]
    split = each * 3 + len(UlyReduce.scratch(gh))
    hid = UlyReduce(gh, *scratch[each * 3 : split])
    gates = line_reduces(n_line, gg, scratch[split:])
    small, cols = [], []
    for k, (yy, cc, ss) in enumerate(corners):
        target = (yy, cc, z, ss)
        cols.append(remote(dc.at[plane_index(yy, cc, ss)], dc_o.at[p], dc_s.at[k], dc_r.at[k], target))
        if k < 3:
            cols.append(remote(oc.at[yy * 2 + cc], oc_o.at[u], oc_s.at[k], oc_r.at[k], target))
            small.append(remote(alpha.at[yy * 2 + cc], alpha_in.at[k], al_s.at[k], al_r.at[k], target))
    for job, _ in gates:
        job.step(n_line - 1)
    for job in cols:
        job.start()
    each_rows = gq.shape[1]
    for v in range(4):
        for k in range(n_blk):
            at = (v * n_blk + k) * each_rows
            alpha[v, k, :, :each_rows] = a_sum[:, at : at + each_rows]
            alpha[v, k, :, each_rows : 2 * each_rows] = m_sum[:, at : at + each_rows]
    for job in small:
        job.start()
    ready()
    rows_all = x[...]
    seqs, group_rows, wide = dq.shape
    heads = wide // 128
    factor = jnp.where(lanes_of((1, 128)) < HEAD_DIM, HEAD_DIM**0.5, 1.0)
    late_steps = [(min(1 + 2 * i, heads - 1), k) for i, k in enumerate(range(n_line - 2, 0, -1))]

    def head(h, carry):
        lanes = pl.ds(pl.multiple_of(h * 128, 128), 128)
        queries = jnp.concatenate([dq[i, :, lanes] for i in range(seqs)], axis=0)
        pairs = jnp.concatenate([dkv[i, :, lanes] for i in range(seqs)], axis=0)
        low_half = lanes_of(queries.shape) < HEAD_DIM
        dy = jnp.where(low_half, queries.astype(F32), pltpu.roll(pairs.astype(F32), HEAD_DIM, 1))
        unit = yy_ref[:, lanes]
        scale_s[h] = jnp.sum(dy * unit, axis=0, keepdims=True) * factor
        dy = dy * scale[pl.ds(h, 1)]
        dr = cc_ref[:, lanes] * (dy - unit * halves(unit * dy))
        raw = (dr * cos[...] - turn(dr) * sin[...]).astype(BF)
        both = jnp.concatenate([raw, jnp.where(low_half, jnp.zeros_like(pairs), pairs)], axis=1)
        grad = dot_tn(both, rows_all).astype(BF)
        at = pl.ds(pl.multiple_of(h * HEAD_DIM, HEAD_DIM), HEAD_DIM)
        for j, lo in enumerate((0, HEAD_DIM, 3 * HEAD_DIM)):
            flat[j, at] = grad[lo : lo + HEAD_DIM]
        w_value = wv[h]
        more = dot_nn(both, jnp.concatenate([wq[h], wk[h], jnp.zeros_like(w_value), w_value], axis=0))

        @pl.when(h == 0)
        def _():
            acc[...] = more

        @pl.when(h > 0)
        def _():
            acc[...] = acc[...] + more

        for when, k in late_steps:
            @pl.when(h == when)
            def _():
                for job, _ in gates:
                    job.step(k)

        return carry

    lax.fori_loop(0, heads, head, 0)
    for i, g in enumerate((gq, gk, gv)):
        for k in range(n_blk):
            g[k] = flat[i, k * each_rows : (k + 1) * each_rows]
    for i in range(seqs):
        gh[i] = acc[i * group_rows : (i + 1) * group_rows].astype(BF).reshape(gh.shape[1:])
    hid.start()
    for k in range(n_line - 1, -1, -1):
        for job in jobs:
            job.start(k)
    mine = [
        pltpu.make_async_copy(dc.at[p], dc_o.at[p], keep.at[0]),
        pltpu.make_async_copy(oc.at[u], oc_o.at[u], keep.at[1]),
    ]
    for job in mine:
        job.start()
    hid.middle()
    for job in small:
        job.wait_recv()
    line_out[...] = jnp.zeros_like(line_out)
    ff_each = ff_sum.shape[1] // n_line
    for k in range(n_line):
        for j in (0, 1):
            line_out[k * 2 + s, :, 256 + j * ff_each : 256 + (j + 1) * ff_each] = ff_sum[
                j : j + 1, k * ff_each : (k + 1) * ff_each
            ]
    line_out[:, :, :128] = alpha[u] + alpha_in[0] + alpha_in[1] + alpha_in[2]
    scales = jnp.concatenate(
        [scale_s[h][:, :HEAD_DIM] + scale_s[h][:, HEAD_DIM:] for h in range(heads)], axis=1
    )
    for k in range(n_blk):
        line_out[k, :, 128 : 128 + each_rows] = scales[:, k * each_rows : (k + 1) * each_rows]
    line_jobs = []
    for i in range(1, n_blk):
        to = lax.rem(b + i, n_blk)
        line_jobs.append(
            remote(line_out.at[to], line_all.at[i - 1], su_s.at[i - 1], su_r.at[i - 1], others[i - 1])
        )
    for job in line_jobs:
        job.start()
    for k in range(n_line - 1, 0, -1):
        for job in jobs:
            job.step(k)
    for i in range(gh.shape[0]):
        gh_o[i] = res[i] + hid.result(i)
    for job in cols:
        job.wait_recv()
    for job in mine:
        job.wait()
    wide, ff_each = oc.shape[-1], dc.shape[-1] // n_line
    for v in range(4):
        go_o[:, v * wide : (v + 1) * wide] = oc_o[v].astype(F32)
        for t in (0, 1):
            for k in range(n_line):
                at = ((v * n_line + k) * 2 + t) * ff_each
                gd_o[:, at : at + ff_each] = dc_o[v * 2 + t, :, k * ff_each : (k + 1) * ff_each].astype(F32)
    total = line_out[b]
    for i, job in enumerate(line_jobs):
        job.wait_recv()
        total = total + line_all[i]
    sum_o[...] = total
    for job, o in zip(jobs, (gq_o, gk_o, gv_o)):
        job.result(o)
    for job, cut in gates:
        job.result(gg_o.at[cut])
        job.finish()
    hid.finish()
    for job in jobs:
        job.finish()
    for job in line_jobs + small:
        job.wait_send()
    for job in cols:
        job.wait_send()


def leave(n_line, x, dq, dkv, y, c, cos, sin, scale, wq, wk, wv, res, oc, dc, a_sum, m_sum, ff_sum, gg):
    n_blk = 2 * n_line
    heads, _, width = wq.shape
    seqs, rows, _ = res.shape
    vmem = pl.BlockSpec(memory_space=pltpu.VMEM)
    dma = pltpu.SemaphoreType.DMA
    grad = jax.ShapeDtypeStruct((n_blk, heads * HEAD_DIM // n_blk, width), BF)
    gh = jax.ShapeDtypeStruct((seqs, 4, rows, width), BF)
    scratch = [
        pltpu.VMEM(oc.shape, oc.dtype),
        pltpu.VMEM(dc.shape, dc.dtype),
        pltpu.VMEM((3, heads * HEAD_DIM, width), BF),
        pltpu.VMEM(x.shape, F32),
        pltpu.VMEM(grad.shape, BF), pltpu.VMEM(grad.shape, BF), pltpu.VMEM(grad.shape, BF),
        pltpu.VMEM(gh.shape, BF),
        pltpu.VMEM((heads, 1, 128), F32),
        pltpu.VMEM((4, n_blk, 1, 128), F32),
        pltpu.VMEM((3, n_blk, 1, 128), F32),
        pltpu.VMEM((n_blk, 1, 640), F32),
        pltpu.VMEM((n_blk - 1, 1, 640), F32),
        dma((3,)), dma((3,)), dma((7,)), dma((7,)), dma((3,)), dma((3,)),
        dma((n_blk - 1,)), dma((n_blk - 1,)), dma((2,)),
    ]
    scratch += BlkReduce.scratch(n_line, grad) * 3
    scratch += UlyReduce.scratch(gh) + line_reduce_scratch(n_line, gg)
    args = (x, dq, dkv, y, c, cos, sin, scale, wq, wk, wv, res, oc, dc, a_sum, m_sum, ff_sum, gg)
    outs = [grad.shape[1:]] * 3 + [
        res.shape, (oc.shape[1], 4 * oc.shape[2]), (dc.shape[1], 8 * dc.shape[2]), (1, 640), gg.shape[1:]
    ]
    return comm_call(
        functools.partial(exit_kernel, n_line), "leave", 8, args, [(shape, F32) for shape in outs], scratch,
        60, late=tuple(range(11)),
    )


def tables(n_line, starts, sizes, small, places, cos, sin, scale, rates):
    y, c, z, s = place()
    u, b, n_blk = y * 2 + c, z * 2 + s, 2 * n_line
    seqs, rows_each = places.shape[0], places.shape[-1] // 4
    for v in range(4):
        for k in range(n_blk):
            row = small[v, k, starts[5] : starts[5] + 1]
            for i in range(seqs):
                places[i, k, :, v * rows_each : (v + 1) * rows_each] = row[:, i * rows_each : (i + 1) * rows_each]
    lane = lanes_of((1, 128)) % HEAD_DIM
    freqs = jnp.exp((lane % 32).astype(F32) * (-math.log(rotary_base) * 2.0 / HEAD_DIM))
    turns = jnp.where(lane < 32, -1.0, 1.0)
    for i in range(seqs):
        spot = places[i, b]
        group = spot.shape[1]
        angles = jnp.transpose(jnp.broadcast_to(spot, (128, group))) * freqs
        cos[i * group : (i + 1) * group] = jnp.cos(angles)
        sin[i * group : (i + 1) * group] = jnp.sin(angles) * turns
    each = sizes[0]
    flat = jnp.concatenate([small[u, k, 0:1, :each] for k in range(n_blk)], axis=1)
    scale[...] = jnp.zeros_like(scale)
    for h in range(flat.shape[1] // HEAD_DIM):
        piece = flat[:, h * HEAD_DIM : (h + 1) * HEAD_DIM]
        scale[h : h + 1] = jnp.concatenate([piece * HEAD_DIM**0.5, piece], axis=1)
    rates[...] = jnp.zeros_like(rates)
    for j in (1, 2):
        for v in range(4):
            for k in range(n_blk):
                at = (v * n_blk + k) * each
                rates[j - 1 : j, at : at + each] = small[v, k, starts[j] : starts[j] + 1, :each]
    for j in (3, 4):
        for k in range(n_line):
            for r in range(starts[j + 1] - starts[j]):
                wide = min(128, sizes[j] - 128 * r)
                at = k * sizes[j] + 128 * r
                rates[j - 1 : j, at : at + wide] = small[u, k * 2 + s, starts[j] + r : starts[j] + r + 1, :wide]


def entry_kernel(
    n_line, starts, sizes, hid, small, wq, wk, wv, wo, wd, wu,
    hid_o, places_o, cos_o, sin_o, scale_o, rates_o, wq_o, wk_o, wv_o, oc_o, dc_o, wu_o, small_o, oc, dc, *sems
):
    y, c, z, s = place()
    u, p = y * 2 + c, plane_index(y, c, s)
    low, high, cross = line_ends(n_line)
    corners = plane_corners()
    greet([(yy, cc, z, ss) for yy, cc, ss in corners], [low, high])
    hid_job = UlyGather(hid, hid_o, *sems[:3])
    at, jobs = 3, []
    for x, pick in (
        (small, lambda block: small_o.at[u, block]),
        (wq, lambda block: wq_o.at[block]),
        (wk, lambda block: wk_o.at[block]),
        (wv, lambda block: wv_o.at[block]),
    ):
        jobs.append(BlkGather(n_line, lambda x=x: x, pick, *sems[at : at + 5]))
        at += 5
    first = wu_o.shape[-1]
    up_jobs = [
        LineGather(n_line, lambda: wu.at[:, slice(0, first)], lambda z: wu_o.at[z], *sems[at : at + 4])
    ]
    oc_s, oc_r, dc_s, dc_r, sm_s, sm_r, keep = sems[at + 4 :]
    jobs[0].start()
    for job in jobs[1:]:
        job.start()
    hid_job.start()
    for v in range(4):
        wide = oc.shape[-1]
        oc[v] = wo[:, v * wide : (v + 1) * wide]
        ff_each = dc.shape[-1] // n_line
        for t in (0, 1):
            for k in range(n_line):
                at = ((v * n_line + k) * 2 + t) * ff_each
                dc[v * 2 + t, :, k * ff_each : (k + 1) * ff_each] = wd[:, at : at + ff_each]
    col_jobs = []
    for k, (yy, cc, ss) in enumerate(corners):
        target = (yy, cc, z, ss)
        col_jobs.append(
            remote(dc.at[plane_index(yy, cc, ss)], dc_o.at[p], dc_s.at[k], dc_r.at[k], target)
        )
        if k < 3:
            col_jobs.append(remote(oc.at[yy * 2 + cc], oc_o.at[u], oc_s.at[k], oc_r.at[k], target))
    for job in col_jobs:
        job.start()
    for job in up_jobs:
        job.start()
    mine = [
        pltpu.make_async_copy(dc.at[p], dc_o.at[p], keep.at[0]),
        pltpu.make_async_copy(oc.at[u], oc_o.at[u], keep.at[1]),
    ]
    for job in mine:
        job.start()
    for k in range(1, n_line):
        for job in jobs:
            job.step(k)
        if k == 1:
            hid_job.forward()
    jobs[0].finish_arrivals()
    small_jobs = [
        remote(small_o.at[u], small_o.at[u], sm_s.at[k], sm_r.at[k], (yy, cc, z, ss))
        for k, (yy, cc, ss) in enumerate(corners[:3])
    ]
    for job in small_jobs:
        job.start()
    for k in range(1, n_line):
        for job in up_jobs:
            job.step(k)
        if k == 1:
            for job in small_jobs:
                job.wait_recv()
            tables(n_line, starts, sizes, small_o, places_o, cos_o, sin_o, scale_o, rates_o)
    for job in jobs[1:]:
        job.finish_arrivals()
    hid_job.finish()
    for job in up_jobs:
        job.finish()
    for job in small_jobs:
        job.wait_send()
    for job in col_jobs:
        job.wait()
    for job in mine:
        job.wait()
    for job in jobs:
        job.finish_sends()


def entry(n_line, starts, sizes, hid, small, wq, wk, wv, wo, wd, wu):
    n_blk = 2 * n_line
    oc = jax.ShapeDtypeStruct((4, wo.shape[0], wo.shape[1] // 4), wo.dtype)
    dc = jax.ShapeDtypeStruct((8, wd.shape[0], wd.shape[1] // 8), wd.dtype)
    parts = hid.shape[0]
    vmem, anyway = pl.BlockSpec(memory_space=pltpu.VMEM), pl.BlockSpec(memory_space=pl.ANY)

    def out(shape, like):
        return jax.ShapeDtypeStruct(shape, like.dtype)

    return pl.pallas_call(
        functools.partial(entry_kernel, n_line, starts, sizes),
        out_shape=[
            out((parts, 4) + hid.shape[1:], hid),
            out((parts, n_blk, 1, 4 * hid.shape[1]), small),
            out((parts * 4 * hid.shape[1], 128), small),
            out((parts * 4 * hid.shape[1], 128), small),
            out((8, 128), small),
            out((8, hid.shape[2]), small),
            out((n_blk,) + wq.shape, wq),
            out((n_blk,) + wk.shape, wk),
            out((n_blk,) + wv.shape, wv),
            out(oc.shape, oc),
            out(dc.shape, dc),
            out((n_line, wu.shape[0], lane_chunks(wu.shape[1])[0].stop), wu),
        ],
        in_specs=[vmem] * 8,
        out_specs=[vmem] * 6 + [anyway, anyway, anyway, vmem, vmem, anyway],
        scratch_shapes=[
            pltpu.VMEM((4, n_blk) + small.shape, small.dtype),
            pltpu.VMEM(oc.shape, oc.dtype),
            pltpu.VMEM(dc.shape, dc.dtype),
        ]
        + UlyGather.sems(parts)
        + BlkGather.sems(n_line) * 4
        + LineGather.sems(n_line)
        + [pltpu.SemaphoreType.DMA((3,))] * 2
        + [pltpu.SemaphoreType.DMA((7,))] * 2
        + [pltpu.SemaphoreType.DMA((3,))] * 2
        + [pltpu.SemaphoreType.DMA((2,))],
        compiler_params=params(6),
        cost_estimate=pl.CostEstimate(flops=0, bytes_accessed=40 * 3_000_000, transcendentals=0),
        name="entry",
    )(hid, small, wq, wk, wv, wo, wd, wu)
def dot_nt(a, b):
    return lax.dot_general(a, b, (((1,), (1,)), ((), ())), preferred_element_type=F32)


def dot_nn(a, b):
    return lax.dot_general(a, b, (((1,), (0,)), ((), ())), preferred_element_type=F32)


def dot_tn(a, b):
    return lax.dot_general(a, b, (((0,), (0,)), ((), ())), preferred_element_type=F32)


def lanes_of(shape):
    return lax.broadcasted_iota(jnp.int32, shape, len(shape) - 1)


def halves(x):
    row = lax.broadcasted_iota(jnp.int32, (128, 128), 0) // HEAD_DIM
    same = jnp.where(row == lanes_of((128, 128)) // HEAD_DIM, 1.0, 0.0).astype(BF)
    high = x.astype(BF)
    rest = (x - high.astype(F32)).astype(BF)
    return dot_nn(high, same) + dot_nn(rest, same)


def turn(x):
    first = lanes_of(x.shape) % HEAD_DIM < HEAD_DIM // 2
    return jnp.where(first, pltpu.roll(x, 128 - 32, 1), pltpu.roll(x, 32, 1))


def down_columns(row):
    n = row.shape[1]
    one = jnp.transpose(jnp.broadcast_to(row, (128, n)))
    return jnp.concatenate([one] * (n // 128), axis=1)


def arrivals(n_line, body):
    each = 2 * n_line - 1

    def step(t, carry):
        stage, r = t // each, lax.rem(t, each)
        body(stage, (r + 1) // 2, lax.rem(r + 1, 2))
        return carry

    lax.fori_loop(0, 2 * each, step, 0)


def attend_kernel(
    n_line, ready, x_ref, wq_ref, wk_ref, wv_ref, cos_ref, sin_ref, scale_ref, oc_ref, wg_ref, wu_ref, kp_ref,
    q_h, y_h, c_h, kv_h, oc_o, wg_o, wu_o, o_ref, mixed_ref, inv_ref,
    kv_ref, acc, total, place_q, q_ref, y_ref, c_ref, kv_o, kept, *sems,
):
    y, c, z, s = place()
    blk_greet(n_line)
    seqs, rows, wide = q_ref.shape
    heads = wide // 128
    chunk = 4 * LINE_CHUNKS
    cut = wu_ref.shape[-1] - wu_o.shape[-1]
    up = LineGather(
        n_line, lambda: wu_ref.at[:, slice(cut, wu_ref.shape[-1])], lambda zz: wu_o.at[zz], *sems[-4:]
    )
    up.start()
    ready()

    each = len(BlkGather.sems(n_line))
    picks = [
        (lambda i=i: kv_ref.at[i], lambda block, i=i: kv_o.at[block, i]) for i in range(seqs)
    ] + [(lambda: oc_ref, lambda block: oc_o.at[:, block])]
    jobs = [
        BlkGather(n_line, *pick, *sems[each * i : each * (i + 1)]) for i, pick in enumerate(picks)
    ]

    def make(t, carry):
        i, h = t // heads, lax.rem(t, heads)
        lanes = pl.ds(pl.multiple_of(h * 128, 128), 128)
        mine = pl.ds(pl.multiple_of(i * rows, rows), rows)
        wv = wv_ref[h]
        got = dot_nt(x_ref[mine], jnp.concatenate([wq_ref[h], wk_ref[h], jnp.zeros_like(wv), wv], axis=0))
        raw, value = got[:, :128], got[:, 128:]
        low = lanes_of(raw.shape) < HEAD_DIM
        turned = raw * cos_ref[mine] + turn(raw) * sin_ref[mine]
        norm = lax.rsqrt(halves(turned * turned) + HEAD_DIM * tiny_eps)
        unit = turned * norm
        both = unit * scale_ref[pl.ds(h, 1)]
        q_ref[i, :, lanes] = jnp.where(low, both, 0.0).astype(BF)
        kv_ref[i, :, lanes] = jnp.where(low, pltpu.roll(both, HEAD_DIM, 1), value).astype(BF)
        y_ref[mine, lanes] = unit
        c_ref[mine, lanes] = norm
        for j in range(seqs):
            pl.when(t == heads * (j + 1) - 1)(jobs[j].start)
        return carry

    lax.fori_loop(0, seqs * heads, make, 0)
    gates = line_gathers(
        n_line, wg_ref, lambda z: wg_o.at[z], sems[each * (seqs + 1) : each * (seqs + 1) + chunk]
    )
    jobs[-1].start()
    for job in gates:
        job.keep().start()
    n_blk = 2 * n_line
    keeps = [
        pltpu.make_async_copy(a, o, kept.at[n_blk + i])
        for i, (a, o) in enumerate(((q_ref, q_h), (y_ref, y_h), (c_ref, c_h)))
    ]
    for copy in keeps:
        copy.start()

    def keep_keys(block):
        return pltpu.make_async_copy(kv_o.at[block], kv_h.at[block], kept.at[block])

    acc[...] = jnp.zeros_like(acc)
    total[...] = jnp.zeros_like(total)
    for i in range(seqs):
        place_q[i] = down_columns(kp_ref[i, z * 2 + s])

    def attend_to(i, block, keys):
        allowed = kp_ref[i, block] <= place_q[i]
        for h in range(heads):
            lanes = slice(h * 128, (h + 1) * 128)
            kv = keys(lanes)
            p = jnp.where(allowed, jnp.exp(dot_nt(q_ref[i, :, lanes], kv)), 0.0)
            part = p[:, :128]
            for j in range(1, rows // 128):
                part = part + p[:, j * 128 : (j + 1) * 128]
            total[i, h] = total[i, h] + part
            acc[i, h] = acc[i, h] + dot_nn(p.astype(BF), kv)

    def body(stage, k, way):
        ahead = jnp.where(k == 0, 1, k + 1)

        @pl.when((stage == 1) & ((k == 0) | (way == 1)) & (ahead < n_line))
        def _():
            for job in gates + [up]:
                job.step(ahead)

        @pl.when((stage == 0) & (k > 0) & (way == 0))
        def _():
            for job in jobs:
                job.step(k)

        for w, last in ((0, z), (1, n_line - 1 - z)):
            @pl.when((stage == 0) & (k == last) & ((k == 0) | (way == 0)))
            def _():
                for job in gates:
                    pl.when(job.goes(w))(lambda: job.own(w).start())

        there = (k == 0) | jnp.where(way == 0, z >= k, z + k < n_line)

        @pl.when(there)
        def _():
            for job in jobs:
                for w in (0, 1):
                    pl.when((stage == 1) & (k > 0) & (way == w))(lambda: job.over(w, k).wait_recv())
                pl.when((stage == 1) & (k == 0))(lambda: job.own(2).wait_recv())
                pl.when((stage == 0) & (k == 0))(lambda: job.keep().wait())
            zz = jnp.where(way == 0, z - k, z + k)
            block = zz * 2 + jnp.where(stage == 0, s, 1 - s)
            keep_keys(block).start()

            for i in range(seqs):
                attend_to(i, block, lambda lanes: kv_o[block, i, :, lanes])

    arrivals(n_line, body)
    low = lanes_of((rows, 128)) < HEAD_DIM
    for i in range(seqs):
        outs = []
        for h in range(heads):
            inverse = 1.0 / jnp.broadcast_to(jnp.sum(total[i, h], axis=-1, keepdims=True), (rows, 128))
            out = acc[i, h] * inverse
            o_ref[i, h] = out
            inv_ref[i, h] = jnp.transpose(inverse)[:8]
            outs.append(out)
        for h in range(0, heads - 1, 2):
            mixed_ref[i, :, h * HEAD_DIM : (h + 2) * HEAD_DIM] = jnp.where(
                low, pltpu.roll(outs[h], HEAD_DIM, 1), outs[h + 1]
            ).astype(BF)
        if heads % 2 == 1:
            mixed_ref[i, :, (heads - 1) * HEAD_DIM :] = pltpu.roll(outs[-1], HEAD_DIM, 1)[:, :HEAD_DIM].astype(BF)
    for job in jobs:
        job.finish_sends()
    for job in gates + [up]:
        job.finish()
    for copy in keeps + [keep_keys(block) for block in range(n_blk)]:
        copy.wait()


def attend(n_line, seqs, x, wq, wk, wv, cos, sin, scale, oc, wg, wu, k_places):
    tokens, width = x.shape
    n_blk, heads, rows = 2 * n_line, wq.shape[0], tokens // seqs
    head, wide = (seqs, heads, rows, 128), (seqs, rows, heads * 128)
    flat = ((tokens, heads * 128), F32)
    first = lane_chunks(width)[0].stop
    return comm_call(
        functools.partial(attend_kernel, n_line), "attend", 5,
        (x, wq, wk, wv, cos, sin, scale, oc, wg, wu, k_places),
        [
            (wide, BF), flat, flat, ((n_blk,) + wide, BF), (oc.shape[:1] + (n_blk,) + oc.shape[1:], BF),
            ((n_line,) + wg.shape, BF), ((n_line, wu.shape[0], width - first), BF), (head, F32),
            ((seqs, rows, heads * HEAD_DIM), BF), ((seqs, heads, 8, rows), F32),
        ],
        [
            pltpu.VMEM(wide, BF), pltpu.VMEM(head, F32), pltpu.VMEM(head, F32), pltpu.VMEM((seqs, rows, rows), F32),
            pltpu.VMEM(wide, BF), pltpu.VMEM(*flat), pltpu.VMEM(*flat), pltpu.VMEM((n_blk,) + wide, BF),
            pltpu.SemaphoreType.DMA((n_blk + 3,)),
        ]
        + BlkGather.sems(n_line) * (seqs + 1) + line_gather_sems(n_line) + LineGather.sems(n_line),
        90, far_outs=(0, 1, 2, 3, 4, 5, 6), late=(0, 1, 2, 3, 4, 5),
    )


def attend_back_kernel(
    n_line, fits, ready, q_ref, low_ref, w_ref, mixed_ref, o_ref, inv_ref, kv_ref, kp_ref, gu_ref,
    dq_ref, dkv_ref, oc_ref, gu_o, dz, delta, dq, parts, oparts, key_s, key_sem, *scratch,
):
    y, c, z, s = place()
    blk_greet(n_line)
    seqs, rows, wide = q_ref.shape
    heads, width = wide // 128, low_ref.shape[-1]
    each = 6
    ups = line_reduces(n_line, gu_ref, scratch[each * (seqs + 1) :])
    for line_job, _ in ups:
        line_job.step(n_line - 1)
    ready()
    low_rows = low_ref[...].reshape(seqs * rows, width)
    grad = dot_tn(low_rows, mixed_ref[...].reshape(seqs * rows, mixed_ref.shape[-1])).astype(BF)
    n_blk, each_out = 2 * n_line, width // (8 * n_line)
    for b in range(n_blk):
        for v in range(4):
            at = (v * n_blk + b) * each_out
            oparts[b, v * each_out : (v + 1) * each_out] = grad[at : at + each_out]
    each = 6
    jobs = [BlkReduce(n_line, parts.at[:, i], *scratch[each * i : each * (i + 1)]) for i in range(seqs)]
    out_job = BlkReduce(n_line, oparts, *scratch[each * seqs : each * (seqs + 1)])
    for k in range(n_line - 1, -1, -1):
        out_job.start(k)
    low = lanes_of((rows, 128)) < HEAD_DIM
    for i in range(seqs):
        d = dot_nn(low_rows[i * rows : (i + 1) * rows], w_ref[...]).astype(BF).astype(F32)
        for h in range(heads):
            at = h // 2 * 128
            if h == heads - 1 and heads % 2 == 1:
                tile = jnp.concatenate([jnp.zeros((rows, HEAD_DIM), F32), d[:, at:]], axis=1)
            else:
                tile = d[:, at : at + 128]
                if h % 2 == 0:
                    tile = pltpu.roll(tile, HEAD_DIM, 1)
                tile = jnp.where(low, 0.0, tile)
            dz[i, h] = tile.astype(BF)
            row = jnp.sum(tile * o_ref[i, h], axis=-1, keepdims=True)
            delta[i, h] = jnp.transpose(jnp.broadcast_to(row, (rows, 128)))[:8]
    dq[...] = jnp.zeros_like(dq)

    def block_of(block):
        if fits:
            keys = kv_ref.at[block]
        else:
            keys = key_s
            copy = pltpu.make_async_copy(kv_ref.at[block], key_s, key_sem.at[0])
            copy.start()
            copy.wait()
        def one(i, carry):
            allowed = down_columns(kp_ref[i, block]) <= kp_ref[i, z * 2 + s]
            for h in range(heads):
                lanes = slice(h * 128, (h + 1) * 128)
                kv = keys[i, :, lanes]
                pair = jnp.concatenate([q_ref[i, :, lanes], dz[i, h]], axis=0)
                scores = dot_nt(kv, pair)
                p = jnp.where(allowed, jnp.exp(scores[:, :rows]) * inv_ref[i, h][:1], 0.0)
                ds = (p * (scores[:, rows:] - delta[i, h][:1])).astype(BF)
                parts[block, i, :, lanes] = dot_nn(
                    jnp.concatenate([ds, p.astype(BF)], axis=1), pair
                ).astype(BF)
                dq[i, h] = dq[i, h] + dot_tn(ds, kv)
            return carry

        lax.fori_loop(0, seqs, one, 0)

    def step(t, carry):
        k, r = n_line - 1 - t // 4, lax.rem(t, 4)
        way, stays = r // 2, lax.rem(r, 2)

        @pl.when((r == 0) & (k > 0) & (k < n_line - 1))
        def _():
            for line_job, _ in ups:
                line_job.step(k)

        there = jnp.where(k == 0, way == 0, jnp.where(way == 0, z + k < n_line, z >= k))

        @pl.when(there)
        def _():
            zz = jnp.where(way == 0, z + k, z - k)
            block_of(zz * 2 + jnp.where(stays == 0, 1 - s, s))

            @pl.when(stays == 0)
            def _():
                for job in jobs:
                    job.side(zz).start()

        @pl.when((r == 3) & (k + 1 < n_line))
        def _():
            for w in (0, 1):
                @pl.when(jobs[0].exists(w, k + 1))
                def _():
                    for job in jobs + [out_job]:
                        job.move_on(w, k + 1)

        return carry

    lax.fori_loop(0, 4 * n_line, step, 0)
    for i in range(seqs):
        for h in range(heads):
            dq_ref[i, :, h * 128 : (h + 1) * 128] = dq[i, h].astype(BF)
    out_job.result(oc_ref)
    for i, job in enumerate(jobs):
        job.result(dkv_ref.at[i])
    for job, cut in ups:
        job.result(gu_o.at[cut])
    for job in jobs + [out_job] + [job for job, _ in ups]:
        job.finish()


def attend_back(n_line, q, low, w, mixed, o, inv, kv, k_places, gu):
    seqs, rows, wide = q.shape
    n_blk, heads = 2 * n_line, wide // 128
    head = (seqs, heads, rows, 128)
    width, columns = w.shape
    out_shape = (width // n_blk, columns)
    one = jax.ShapeDtypeStruct((n_blk,) + kv.shape[2:], BF)
    out_one = jax.ShapeDtypeStruct((n_blk,) + out_shape, BF)
    fits = kv.size * 2 <= 8_000_000
    return comm_call(
        functools.partial(attend_back_kernel, n_line, fits), "attend_back", 7,
        (q, low, w, mixed, o, inv, kv, k_places, gu),
        [(q.shape, BF), (kv.shape[1:], BF), (out_shape, BF), (gu.shape[1:], F32)],
        [
            pltpu.VMEM(head, BF), pltpu.VMEM((seqs, heads, 8, rows), F32), pltpu.VMEM(head, F32),
            pltpu.VMEM(kv.shape, BF), pltpu.VMEM(out_one.shape, BF),
            pltpu.VMEM((16, 128) if fits else kv.shape[1:], BF), pltpu.SemaphoreType.DMA((1,)),
        ]
        + BlkReduce.scratch(n_line, one) * seqs + BlkReduce.scratch(n_line, out_one)
        + line_reduce_scratch(n_line, gu),
        75, 67_000_000, () if fits else (6,), late=(0, 1, 2, 3, 4) + (6,) * fits,
    )


def unit_of(x):
    c = lax.rsqrt(jnp.sum(x * x, axis=-1, keepdims=True) + x.shape[-1] * tiny_eps)
    return x * c, c


def unit_back(y, c, dy):
    return c * (dy - y * jnp.sum(y * dy, axis=-1, keepdims=True))


class Late:
    @staticmethod
    def scratch(arrays):
        return [pltpu.VMEM(a.shape, a.dtype) for a in arrays] + [pltpu.SemaphoreType.DMA((len(arrays),))]

    def __init__(self, refs, scratch):
        *self.bufs, sem = scratch
        self.copies = [
            pltpu.make_async_copy(ref, buf, sem.at[i]) for i, (ref, buf) in enumerate(zip(refs, self.bufs))
        ]
        for copy in self.copies:
            copy.start()

    def __call__(self, i):
        self.copies[i].wait()
        return self.bufs[i]


def attn_joint_kernel(
    n_line, ready, mixed, w, hid, rate, dc, first_o, ua_o, ca_o, cv_o, all_o, down_o, part, low, *scratch
):
    ends = line_ends(n_line)
    greet(plane_peers(), ends[:2])
    ready()
    split = len(UlyReduce.scratch(part))
    job = UlyReduce(part, *scratch[:split])
    out = PlaneGather(low, all_o, *scratch[split : split + 3])
    downs = line_gathers(n_line, dc, lambda z: down_o.at[:, z], scratch[split + 3 :])
    for line_job in downs:
        line_job.start()
    steps = [(k, line_job) for k in range(1, n_line) for line_job in downs]
    parts, _, rows, width = part.shape
    seqs = mixed.shape[0]
    each = parts // seqs
    for i in range(seqs):
        got = dot_nt(mixed[i], w[...]).astype(BF)
        for k in range(each):
            for u in range(4):
                at = (u * each + k) * rows
                part[i * each + k, u] = got[at : at + rows]
            for copy in job.near[i * each + k]:
                copy.start()
    job.middle()
    k, line_job = steps.pop(0)
    line_job.step(k)
    for i in range(parts):
        ua, ca = unit_of(job.result(i))
        h = hid[i].astype(F32)
        first, cv = unit_of(h + rate[0:1] * (ua - h))
        low[i] = first.astype(BF)
        out.start_part(i)
        first_o[i], ua_o[i] = first, ua
        ca_o[i] = jnp.broadcast_to(ca, (rows, 128))
        cv_o[i] = jnp.broadcast_to(cv, (rows, 128))
        if i > 0:
            out.forward_part(i - 1)
        if len(steps) > 0:
            k, line_job = steps.pop(0)
            line_job.step(k)
    out.forward_part(parts - 1)
    for k, line_job in steps:
        line_job.step(k)
    out.finish()
    job.finish()
    for line_job in downs:
        line_job.finish()


def attn_joint(n_line, mixed, w, hid, rate, dc):
    parts, rows, width = hid.shape
    part = jax.ShapeDtypeStruct((parts, 4, rows, width), BF)
    thin = ((parts, rows, 128), F32)
    return comm_call(
        functools.partial(attn_joint_kernel, n_line), "attn_joint", 1, (mixed, w, hid, rate, dc),
        [
            (hid.shape, F32), (hid.shape, F32), thin, thin, ((8, parts, rows, width), BF),
            (dc.shape[:1] + (n_line,) + dc.shape[1:], BF),
        ],
        [pltpu.VMEM(part.shape, BF), pltpu.VMEM(hid.shape, BF)]
        + UlyReduce.scratch(part) + PlaneGather.sems(parts) + line_gather_sems(n_line),
        25, far_outs=(4, 5), late=(0, 1, 2, 4),
    )


def plane_products(job, part, y, c, prepare, product):
    _, parts, rows, width = part.shape
    for yy, spots in ((1 - y, (0, 2)), (y, (1, 3))):
        def one(j, carry):
            cc = jnp.where(j == 0, 1 - c, c)
            prepare(yy, cc)
            got = product(yy, cc).astype(BF).reshape(2, parts, rows, width)
            for ss in (0, 1):
                part[plane_index(yy, cc, ss)] = got[ss]

            @pl.when(j == 0)
            def _():
                for k in spots:
                    for copy in job.near[k]:
                        copy.start()

            return carry

        lax.fori_loop(0, 2, one, 0)
        job.middle(spots[0] == 0)


def ff_joint_kernel(
    ready, x, wu, wu2, wg, rate, w, first, cot, out_o, d1_o, sum_o, all_o, inner_h, up_h, gate_h,
    part, low, inner, up_s, gate_s, kept, *scratch,
):
    y, c, z, s = place()
    greet(plane_peers())
    split = len(PlaneReduce.scratch(part))
    job = PlaneReduce(part, *scratch[:split])
    out = PlaneGather(low, all_o, *scratch[split:])
    _, seqs, rows, width = part.shape
    columns, tokens = inner.shape[-1], 2 * seqs * rows
    cut = wu.shape[1]

    def forward(yy, cc):
        block = x[yy, cc].reshape(tokens, width)
        up = dot_nt(block[:, :cut], wu[...]) + dot_nt(block[:, cut:], wu2[...])
        gate = dot_nt(block, wg[...])
        gz = gate * rate[3:4, :columns] * D**0.5
        got = gz / (1.0 + jnp.exp(-gz)) * (up * rate[2:3, :columns])
        inner[yy, cc] = got.astype(BF).reshape(inner.shape[2:])
        up_s[yy, cc] = up.reshape(up_s.shape[2:])
        gate_s[yy, cc] = gate.reshape(gate_s.shape[2:])

    ready()
    plane_products(
        job, part, y, c, forward, lambda yy, cc: dot_nt(inner[yy, cc].reshape(tokens, columns), w[...])
    )
    keeps = [
        pltpu.make_async_copy(a, o, kept.at[i])
        for i, (a, o) in enumerate(((inner, inner_h), (up_s, up_h), (gate_s, gate_h)))
    ]
    for copy in keeps:
        copy.start()
    job.last()
    for i in range(seqs):
        ub, cb = unit_of(job.result(i))
        f, b = first[i], rate[1:2]
        o, cw = unit_of(f + b * (ub - f))
        dw = unit_back(o, cw, cot[i].astype(F32))
        step = b * dw
        low[i] = unit_back(ub, cb, step).astype(BF)
        out.start_part(i)
        out_o[i] = o.astype(BF)
        d1_o[i] = dw - step
        total = jnp.sum(dw * (ub - f), axis=0, keepdims=True)
        sum_o[...] = total if i == 0 else sum_o[...] + total
        if i > 0:
            out.forward_part(i - 1)
    out.forward_part(seqs - 1)
    out.finish()
    job.finish()
    for copy in keeps:
        copy.wait()


def ff_joint(x, wu, wu2, wg, rate, w, first, cot):
    seqs, rows, width = first.shape
    part = jax.ShapeDtypeStruct((8, seqs, rows, width), BF)
    columns = wg.shape[0]
    wide = (2, 2, 2, seqs * rows, columns)
    return comm_call(
        ff_joint_kernel, "ff_joint", 2,
        (x.reshape(wide[:4] + (width,)), wu, wu2, wg, rate, w, first, cot),
        [
            (first.shape, BF), (first.shape, F32), ((1, width), F32), (part.shape, BF),
            (wide, BF), (wide, F32), (wide, F32),
        ],
        [
            pltpu.VMEM(part.shape, BF), pltpu.VMEM(first.shape, BF), pltpu.VMEM(wide, BF),
            pltpu.VMEM(wide, F32), pltpu.VMEM(wide, F32), pltpu.SemaphoreType.DMA((3,)),
        ]
        + PlaneReduce.scratch(part) + PlaneGather.sems(seqs),
        35, far_outs=(3, 4, 5, 6), late=(0, 1, 2, 3, 5),
    )


def back_joint_kernel(
    n_line, ready, d, inner, rate, d1, first, ua, ca, cv, hid, wd_h, up_h, gate_h, wu_h, wu2_h, wg_h, x_h,
    res_o, sum_o, ff_sum_o, all_o, up_o, gate_o, down_o, part, low, down_s, du, dg, *scratch,
):
    y, c, z, s = place()
    late = Late((wd_h, up_h, gate_h, wu_h, wu2_h, wg_h, x_h), scratch[:8])
    scratch = scratch[8:]
    greet(plane_peers(), line_ends(n_line)[:2])
    ready()
    split = len(PlaneReduce.scratch(part))
    job = PlaneReduce(part, *scratch[:split])
    _, parts, rows, width = part.shape
    columns = du.shape[-1]
    tokens = 8 * parts * rows
    each = parts // all_o.shape[0]
    out = UlyGather(
        low, all_o, *scratch[split : split + 3],
        pick=lambda i, u: all_o.at[i // each, u, pl.ds(i % each * rows, rows)],
    )
    downs = line_reduces(n_line, down_s, scratch[split + 3 :])
    flat = lambda ref: ref[...].reshape(tokens, ref.shape[-1])

    deep = width // (4 * n_line)
    inner_all = flat(inner)

    def down_half(i, carry):
        lanes = pl.ds(pl.multiple_of(i * (width // 2), 128), width // 2)
        grad = dot_tn(d[:, :, :, :, lanes].reshape(tokens, width // 2), inner_all).astype(BF)
        for v in (0, 1):
            for k in range(n_line):
                at = (v * n_line + k) * deep
                down_s[k, 2 * i + v] = grad[at : at + deep]
        return carry

    lax.fori_loop(0, 2, down_half, 0)
    for line_job, _ in downs:
        line_job.step(n_line - 1)

    wd, up_ref, gate_ref = late(0), late(1), late(2)
    u_scale, g_scale = rate[2:3, :columns], rate[3:4, :columns] * D**0.5

    ff_sum_o[...] = jnp.zeros_like(ff_sum_o)

    def gated_back(yy, cc):
        got = dot_nn(d[yy, cc].reshape(tokens // 4, width), wd[...])
        up, gate = up_ref[yy, cc].reshape(got.shape), gate_ref[yy, cc].reshape(got.shape)
        gz = gate * g_scale
        sig = 1.0 / (1.0 + jnp.exp(-gz))
        d_up = got * (gz * sig)
        d_gate = got * (up * u_scale) * sig * (1.0 + gz * (1.0 - sig))
        du[yy, cc] = (d_up * u_scale).astype(BF).reshape(du.shape[2:])
        dg[yy, cc] = (d_gate * g_scale).astype(BF).reshape(dg.shape[2:])
        ff_sum_o[0:1] = ff_sum_o[0:1] + jnp.sum(d_up * up, axis=0, keepdims=True)
        ff_sum_o[1:2] = ff_sum_o[1:2] + jnp.sum(d_gate * gate, axis=0, keepdims=True) * D**0.5

    wu, wu2, wg = late(3), late(4), late(5)

    def product(yy, cc):
        u, g = du[yy, cc].reshape(tokens // 4, columns), dg[yy, cc].reshape(tokens // 4, columns)
        got = jnp.concatenate([dot_nn(u, wu[...]), dot_nn(u, wu2[...])], axis=1)
        return got + dot_nn(g, wg[...])

    plane_products(job, part, y, c, gated_back, product)
    steps = [(k, line_job) for k in range(n_line - 2, 0, -1) for line_job, _ in downs]
    job.last()
    x = late(6)

    def by_line(o, ref):
        n, rows_all = columns // n_line, flat(ref)

        def half(i, carry):
            lanes = pl.ds(pl.multiple_of(i * (width // 2), 128), width // 2)
            grad = dot_tn(rows_all, x[:, lanes]).astype(BF)
            for k in range(n_line):
                o[k, :, lanes] = grad[k * n : (k + 1) * n]
            return carry

        lax.fori_loop(0, 2, half, 0)

    by_line(up_o, du)
    for i in range(parts):
        f, h, u, a = first[i], hid[i].astype(F32), ua[i], rate[0:1]
        dv = unit_back(f, cv[i][:, :1], d1[i] + job.result(i))
        step = a * dv
        low[i] = unit_back(u, ca[i][:, :1], step).astype(BF)
        out.start_part(i)
        res_o[i] = dv - step
        total = jnp.sum(dv * (u - h), axis=0, keepdims=True)
        sum_o[...] = total if i == 0 else sum_o[...] + total
        if len(steps) > 0:
            k, line_job = steps.pop(0)
            line_job.step(k)
    for k, line_job in steps:
        line_job.step(k)
    by_line(gate_o, dg)
    out.forward()
    out.finish()
    job.finish()
    for line_job, cut in downs:
        line_job.result(down_o.at[cut])
        line_job.finish()


def back_joint(n_line, seqs, d, wd, up, gate, rate, wu, wu2, wg, x, inner, d1, first, ua, ca, cv, hid):
    parts, rows, width = first.shape
    columns = wd.shape[1]
    part = jax.ShapeDtypeStruct((8, parts, rows, width), BF)
    down = jax.ShapeDtypeStruct((n_line, 4, width // (4 * n_line), columns), BF)
    by_line = ((n_line, columns // n_line, width), BF)
    wide = lambda a: a.reshape(2, 2, 2, parts * rows, a.shape[-1])
    thin = pltpu.VMEM((2, 2, 2, parts * rows, columns), BF)
    late = (wd, wide(up), wide(gate), wu, wu2, wg, x)
    return comm_call(
        functools.partial(back_joint_kernel, n_line), "back_joint", 3,
        (wide(d), wide(inner), rate, d1, first, ua, ca, cv, hid) + late,
        [
            (first.shape, F32), ((1, width), F32), ((2, columns), F32),
            ((seqs, 4, parts * rows // seqs, width), BF), by_line, by_line, (down.shape[1:], BF),
        ],
        [pltpu.VMEM(part.shape, BF), pltpu.VMEM(first.shape, BF), pltpu.VMEM(down.shape, BF), thin, thin]
        + Late.scratch(late) + PlaneReduce.scratch(part) + UlyGather.sems(parts)
        + line_reduce_scratch(n_line, down),
        40, VMEM_BYTES, tuple(range(9, 16)), far_outs=(3,), late=(0, 1),
    )


def settle_kernel(count, cuts, *refs):
    ins, sums = refs[:count], refs[count]
    outs, pieces = refs[count + 1 : 2 * count + 1], refs[2 * count + 1 : 2 * count + 1 + len(cuts)]
    *bufs, come, go = refs[2 * count + 1 + len(cuts) :]
    into = [pltpu.make_async_copy(x, b, come.at[i]) for i, (x, b) in enumerate(zip(ins, bufs))]
    out = [pltpu.make_async_copy(b, o, go.at[i]) for i, (b, o) in enumerate(zip(bufs, outs))]
    for copy in into:
        copy.start()
    for piece, (at, wide) in zip(pieces, cuts):
        piece[...] = sums[:, at : at + wide]
    for a, b in zip(into, out):
        a.wait()
        b.start()
    for copy in out:
        copy.wait()


def settle(sums, cuts, *arrays):
    count = len(arrays)
    anyway, vmem = pl.BlockSpec(memory_space=pl.ANY), pl.BlockSpec(memory_space=pltpu.VMEM)
    return pl.pallas_call(
        functools.partial(settle_kernel, count, cuts),
        out_shape=[jax.ShapeDtypeStruct(a.shape, a.dtype) for a in arrays]
        + [jax.ShapeDtypeStruct((1, wide), F32) for _, wide in cuts],
        in_specs=[anyway] * count + [vmem],
        out_specs=[anyway] * count + [vmem] * len(cuts),
        scratch_shapes=[pltpu.VMEM(a.shape, a.dtype) for a in arrays]
        + [pltpu.SemaphoreType.DMA((count,))] * 2,
        compiler_params=pltpu.CompilerParams(vmem_limit_bytes=VMEM_BYTES),
        name="settle",
    )(*arrays, sums)


def local(
    hidden, positions, w_query, w_key, w_value, w_out, w_up, w_gate, w_down,
    qk_scale, alpha_attn, alpha_mlp, up_scale, gate_scale, cotangent,
):
    seqs, rows_each, width = hidden.shape
    n_line = lax.axis_size("line")
    n_blk = 2 * n_line
    heads = HEADS // 4
    local_width = heads * HEAD_DIM
    group_rows = 4 * rows_each
    tokens = seqs * rows_each
    group_tokens = 4 * tokens
    plane_tokens = 8 * tokens
    attn_each, ff_each = w_query.shape[0], w_up.shape[0]
    ff_local = ff_each * n_line
    far, core, line, side = place()
    uly = far * 2 + core

    def row(x, wide):
        return jnp.pad(x, ((0, 0),) * (x.ndim - 1) + ((0, wide - x.shape[-1]),))

    pieces = [v.astype(F32) for v in (qk_scale, alpha_attn, alpha_mlp, up_scale, gate_scale)]
    pieces.append(positions.reshape(-1).astype(F32))
    rows_of = [-(-v.shape[0] // 128) for v in pieces]
    starts = [sum(rows_of[:i]) for i in range(len(pieces) + 1)]
    tall = starts[-1] + -starts[-1] % 8
    small = 0.0
    for v, start in zip(pieces, starts):
        small = small + jnp.pad(v, (start * 128, (tall - start) * 128 - v.shape[0]))
    small = small.reshape(tall, 128)

    sizes = tuple(v.shape[0] for v in pieces)
    assert ff_local <= width and tokens <= 128 and attn_each <= 64
    (
        hid_all, places, cos, sin, scale_both, rates, wq_all, wk_all, wv_all, out_cols, down_cols, up_first
    ) = entry(
        n_line, tuple(starts), sizes, hidden, small, w_query, w_key, w_value, w_out, w_down, w_up
    )
    up_first = up_first.reshape(ff_local, -1)

    group_hidden = hid_all.reshape(group_tokens, width)
    wq = wq_all.reshape(heads, HEAD_DIM, width)
    wk = wk_all.reshape(heads, HEAD_DIM, width)
    wv = wv_all.reshape(heads, HEAD_DIM, width)
    qz, y_both, c_both, kv_all, out_all, gate_full, up_last, attended, mixed, inverse = attend(
        n_line, seqs, group_hidden, wq, wk, wv, cos, sin, scale_both, out_cols, w_gate, w_up,
        places,
    )
    up_last = up_last.reshape(ff_local, -1)
    gate_full = gate_full.reshape(ff_local, width)
    out_full = out_all.reshape(width, local_width)

    fine = (2 * seqs, rows_each // 2, width)
    hidden_fine = hidden.reshape(fine)
    first, unit_att, att_c, first_c, mlp_in, down_full = attn_joint(
        n_line, mixed, out_full, hidden_fine, rates,
        down_cols.reshape(4, 2 * attn_each, ff_local),
    )
    down_full = down_full.reshape(width, ff_local)
    mlp_in = mlp_in.reshape(plane_tokens, width)
    layer_out, grad_first, grad_alpha_mlp, branch_low, inner, up_rows, gate_rows = ff_joint(
        mlp_in, up_first, up_last, gate_full, rates, down_full, first, cotangent.reshape(fine)
    )
    branch_low = branch_low.reshape(plane_tokens, width)
    grad_residual, grad_alpha_attn, ff_scales, att_low, grad_up, grad_gate, down_own = back_joint(
        n_line, seqs, branch_low, down_full, up_rows, gate_rows, rates, up_first, up_last, gate_full,
        mlp_in, inner, grad_first, first, unit_att, att_c, first_c, hidden_fine,
    )
    down_own = down_own.reshape(8, attn_each, ff_local)

    dq, dkv, out_own, up_own = attend_back(
        n_line, qz, att_low.reshape(seqs, group_rows, width), out_full, mixed, attended, inverse,
        kv_all, places, grad_up,
    )
    out_own = out_own.reshape(4, attn_each, local_width)
    gq, gk, gv, grad_hidden, out_gradient, down_gradient, sums, gate_own = leave(
        n_line, group_hidden, dq, dkv, y_both, c_both, cos, sin, scale_both, wq, wk, wv,
        grad_residual.reshape(seqs, rows_each, width), out_own, down_own,
        grad_alpha_attn, grad_alpha_mlp, ff_scales, grad_gate,
    )
    cuts = (
        (128, attn_each), (0, attn_each), (attn_each, attn_each), (256, ff_each), (256 + ff_each, ff_each)
    )
    settled = settle(
        sums, cuts,
        layer_out.reshape(hidden.shape), grad_hidden, gq, gk, gv, out_gradient, up_own, gate_own,
        down_gradient,
    )
    return tuple(settled[:9]) + tuple(piece.reshape(-1) for piece in settled[9:])


def solution(mesh):
    far = mesh.shape["uly"] // 2
    line = mesh.shape["blk"] // 2
    finer = Mesh(mesh.devices.reshape(far, 2, line, 2), AXES)
    rows, tokens, flat = P(AXES, None), P(None, AXES, None), P(AXES)
    return jax.shard_map(
        local,
        mesh=finer,
        in_specs=(tokens, P(None, AXES)) + (rows,) * 7 + (flat,) * 5 + (tokens,),
        out_specs=(tokens, tokens) + (rows,) * 7 + (flat,) * 5,
        check_vma=False,
    )
```
